32 devices in a mesh: day: 2 (over x), chan: 16 (over z, y, core).
Axes of the slice: x: 2, y: 2, z: 4, core: 2. Of those that a mesh axis runs over, the one named last changes fastest.
Arguments:
- records: bfloat16 [1024, 8, 3000], P(('day', 'chan')), parts along dimension 0, may hold values from -6 to 6
- live_mask: int32 [1024], P(('day', 'chan')), parts along dimension 0, may hold values 0 or 1
- offsets: int32 [16], replicated, may hold values from 1 to 511, as said below
Outputs:
- correlations: bfloat16 [1024, 16, 2048], P(('day', 'chan')), parts along dimension 0
The draws below stay inside these ranges and needn't reach their ends.
There are 2 independent parts, one for each index of `day`. The reference program is written for one: setup_inputs(seed, part) draws one part's arguments, and reference() takes and returns one part's arrays. A program takes and returns all parts, laid end to end along the dimension named above; an argument that names none is the same for every part. Nothing has to cross between parts.
Inputs may be any that keep to these rules, and one draw needn't show every extreme that they name: offsets[k] lies between k * 32 + 1 and (k + 1) * 32, and the last one equals 511.
All inputs are finite; a program needn't handle non-finite values. No bound on the sum of `live_mask` on one device may be relied on, other than what follows from the above.
Results may differ from the reference program's by a relative error of at most 0.0076.
Values may be sent and summed in bfloat16 or wider, within the bound.
A program may use at most 128 MiB of HBM per device.

```python
import math
import jax
import jax.numpy as jnp
from jax import lax

W = 8
L = 3000
F = 512
F0 = 6
LAGS = 2048
BAND = 512
K = 16
CH_TOTAL = 512


def draw_offsets(key, part):
    stride = BAND // K
    index = jnp.arange(K, dtype=jnp.int32)
    base = index * stride + 1
    jitter = jax.random.randint(key, (K,), 0, stride, dtype=jnp.int32)
    jitter = jnp.where(index == K - 1, stride - 2, jitter)
    return (base + jitter).astype(jnp.int32)


def place_ends(entries, own_key, low, largest):
    longest = entries.shape.index(max(entries.shape))
    spots = []
    for shift in (0, 1):
        where = [jax.random.randint(jax.random.fold_in(own_key, axis), (), 0, length) for axis, length in enumerate(entries.shape)]
        where[longest] = (where[longest] + shift) % entries.shape[longest]
        spots.append(tuple(where))
    return entries.at[spots[0]].set(low).at[spots[1]].set(largest)


def shard_levels(rng, dims, cuts, low, high):
    level = 1.0
    for dim, shards_of in cuts:
        steps = jax.random.uniform(jax.random.fold_in(jax.random.fold_in(rng, 6), dim), (shards_of,), jnp.float32, low / len(cuts), high / len(cuts))
        level = level * jnp.repeat(jnp.exp(steps), dims[dim] // shards_of).reshape((-1,) + (1,) * (len(dims) - 1 - dim))
    return level


def normal_values(rng, shape, deviation, bound, shards=(), kind=jnp.bfloat16):
    level = shard_levels(rng, shape, shards, -0.22, 0.18) if shards else 1.0
    drawn = jax.random.normal(rng, shape, jnp.float32) * deviation * level
    return jnp.minimum(jnp.maximum(drawn, -bound), bound).astype(kind)


def setup_inputs(seed: int = 0, part: int = 0) -> dict:
    streams_of = jax.random.split(jax.random.key(seed), 4)
    part_keys = jax.random.split(jax.random.fold_in(streams_of[3], part), 4)
    return {
        "records": normal_values(part_keys[0], (CH_TOTAL, W, L), 1.0, 6.0, ((0, 16),)),
        "live_mask": place_ends((jax.random.randint(part_keys[1], (CH_TOTAL,), 0, 10) < 9).astype(jnp.int32), jax.random.fold_in(part_keys[1], 1), 0, 1),
        "offsets": draw_offsets(jax.random.fold_in(streams_of[3], 71), part),
    }


def forward_table(length):
    samples = jnp.arange(length, dtype=jnp.int32)
    freqs = F0 + jnp.arange(F, dtype=jnp.int32)
    phase = jnp.mod(samples[:, None] * freqs[None, :], length).astype(jnp.float32)
    angle = 2.0 * math.pi / length * phase
    return jnp.concatenate([jnp.cos(angle), -jnp.sin(angle)], axis=1).astype(jnp.bfloat16)

def inverse_table(length):
    freqs = F0 + jnp.arange(F, dtype=jnp.int32)
    shifts = jnp.arange(LAGS, dtype=jnp.int32) - LAGS // 2
    phase = jnp.mod(freqs[:, None] * shifts[None, :], length).astype(jnp.float32)
    angle = 2.0 * math.pi / length * phase
    return jnp.concatenate([jnp.cos(angle), -jnp.sin(angle)], axis=0).astype(jnp.bfloat16)

def whiten(records, live_mask):
    count, windows, length = records.shape
    table = forward_table(length)
    spectrum = jnp.dot(records.reshape(count * windows, length), table, preferred_element_type=jnp.float32)
    power = lax.optimization_barrier(jnp.mean(spectrum * spectrum, axis=1, keepdims=True))
    gain = jnp.repeat(live_mask.astype(jnp.float32), windows)[:, None]
    white = spectrum * (gain * lax.rsqrt(power + 1e-06))
    return white.astype(jnp.bfloat16).reshape(count, windows, 2, spectrum.shape[1] // 2)

def stacked_cross(local_spec, extended, offsets):
    row_count, windows, paired, bin_count = local_spec.shape
    first = local_spec.astype(jnp.float32)

    def single(offset_value):
        partner = lax.dynamic_slice_in_dim(extended, offset_value, row_count, 0).astype(jnp.float32)
        real_part = lax.optimization_barrier(jnp.sum(first[:, :, 0] * partner[:, :, 0] + first[:, :, 1] * partner[:, :, 1], axis=1))
        imag_part = lax.optimization_barrier(jnp.sum(first[:, :, 1] * partner[:, :, 0] - first[:, :, 0] * partner[:, :, 1], axis=1))
        return jnp.stack([real_part, imag_part], axis=1) / float(windows)

    def grouped(group):
        return jax.vmap(single)(group)
    result = lax.map(grouped, offsets.reshape(-1, 8))
    result = result.reshape(offsets.shape[0], row_count, 2, bin_count)
    return jnp.transpose(result, (1, 0, 2, 3)).astype(jnp.bfloat16)

def lag_transform(cross, length):
    count, pairs, paired, bin_count = cross.shape
    table = inverse_table(length)
    result = jnp.dot(cross.reshape(count * pairs, 2 * bin_count), table, preferred_element_type=jnp.float32)
    result = result * (1.0 / math.sqrt(bin_count))
    return result.reshape(count, pairs, table.shape[1]).astype(jnp.bfloat16)

def reference(records, live_mask, offsets):
    spectra = whiten(records, live_mask)
    padding = jnp.zeros((BAND,) + spectra.shape[1:], jnp.bfloat16)
    extended = jnp.concatenate([spectra, padding], axis=0)
    cross = stacked_cross(spectra, extended, offsets)
    return lag_transform(cross, records.shape[2])
```

```python
import functools
import math

import jax
import jax.numpy as jnp
import numpy as np
from jax import lax
from jax.experimental import pallas as pl
from jax.experimental.pallas import tpu as pltpu
from jax.sharding import PartitionSpec as P

F = 512
F0 = 6
LAGS = 2048
LANES = 128
BAND = 512
PIECES = 4
LAYER_CHIPS = 4


def forward_table(length):
    samples = np.arange(length, dtype=np.int64)
    freqs = F0 + np.arange(F, dtype=np.int64)
    phase = np.mod(samples[:, None] * freqs[None, :], length)
    angle = 2.0 * math.pi / length * phase
    return np.concatenate([np.cos(angle), -np.sin(angle)], axis=1).astype(np.float32).astype(jnp.bfloat16)


def inverse_table(length):
    freqs = F0 + np.arange(F, dtype=np.int64)
    shifts = np.arange(LAGS, dtype=np.int64) - LAGS // 2
    phase = np.mod(freqs[:, None] * shifts[None, :], length)
    angle = 2.0 * math.pi / length * phase
    return np.concatenate([np.cos(angle), -np.sin(angle)], axis=0).astype(np.float32).astype(jnp.bfloat16)


def whiten(records, live_mask):
    count, windows, length = records.shape
    spectrum = jnp.dot(
        records.reshape(count * windows, length),
        jnp.asarray(forward_table(length)),
        preferred_element_type=jnp.float32,
    )
    power = jnp.mean(spectrum * spectrum, axis=1, keepdims=True)
    gain = jnp.repeat(live_mask.astype(jnp.float32), windows)[:, None]
    white = spectrum * (gain * lax.rsqrt(power + 1e-06))
    return white.astype(jnp.bfloat16)


def reach_kernel(shape, offsets_ref, white_ref, cross_ref, held, ext, own, swapped, made, back,
                 z_send, z_recv, c_send, c_recv, y_send, y_recv, d_send, d_recv, e_send, r_send, r_recv):
    layers, columns, depth, pieces, windows, fold = shape
    count, slab = white_ref.shape[0], white_ref.shape[1]
    pairs = offsets_ref.shape[0]
    wide = 2 * columns
    total = layers * wide * count
    me = lax.axis_index("chan")
    z, q = me // wide, me % wide
    y, c = q // 2, q % 2
    sibling = me + 1 - 2 * c
    sib_q = q + 1 - 2 * c
    mate = me + 2 - 4 * y
    mate_q = q + 2 - 4 * y
    far_q = sib_q + 2 - 4 * y
    step = count // pieces
    top, lifted = layers - 1, depth + 1

    barrier = pltpu.get_barrier_semaphore()

    def greet(device):
        pl.semaphore_signal(barrier, inc=1, device_id={"chan": device}, device_id_type=pl.DeviceIdType.MESH)

    greet(sibling)
    if columns == 2:
        greet(mate)

    @pl.when(z >= 1)
    def _():
        greet(me - wide)

    @pl.when(z < layers - 1)
    def _():
        greet(me + wide)

    below, above = jnp.minimum(z, 1), jnp.minimum(top - z, 1)
    peers = columns + below + above
    if fold:
        @pl.when(z == 0)
        def _():
            for i in range(wide):
                greet(top * wide + i)

        @pl.when(z == top)
        def _():
            for i in range(wide):
                greet(jnp.int32(i))

        peers = peers + wide * (2 - below - above)
    pl.semaphore_wait(barrier, peers)

    def rows(p):
        return pl.ds(p * step, step)

    def mine(dz, p):
        return white_ref.at[rows(p)] if dz == 0 else held.at[dz * wide + q, rows(p)]

    def copy(source, slot, p, send, recv, device):
        return pltpu.make_async_remote_copy(
            src_ref=source,
            dst_ref=held.at[slot, rows(p)],
            send_sem=send,
            recv_sem=recv,
            device_id={"chan": device},
            device_id_type=pl.DeviceIdType.MESH,
        )

    def down(dz, p):
        return copy(mine(dz, p), (dz + 1) * wide + q, p, z_send.at[dz, p], z_recv.at[dz + 1, p], me - wide)

    def from_above(dz, p):
        return copy(mine(dz, p), dz * wide + q, p, z_send.at[dz, p], z_recv.at[dz, p], me)

    def across(dz, p, slot):
        return copy(mine(dz, p), slot, p, c_send.at[dz, p], c_recv.at[dz, p], sibling)

    def over(dz, p, slot):
        return copy(mine(dz, p), slot, p, y_send.at[dz, p], y_recv.at[dz, p], mate)

    def onward(dz, p, slot):
        return copy(held.at[dz * wide + mate_q, rows(p)], slot, p, d_send.at[dz, p], d_recv.at[dz, p], sibling)

    def both(*conditions):
        joined = conditions[0]
        for condition in conditions[1:]:
            joined = jnp.logical_and(joined, condition)
        return joined

    def exists(dz):
        return z + dz < layers

    def goes(dz, at_start, at_end):
        if dz == lifted:
            return z == top
        if dz == 0:
            return at_start
        if fold and dz == depth:
            return both(exists(dz), at_end)
        return exists(dz)

    def z_tx(dz):
        if fold and dz + 1 == depth:
            return both(exists(dz), z >= 1, jnp.logical_or(z >= 2, q == 0))
        return both(exists(dz), z >= 1)

    def z_rx(dz):
        return goes(dz, None, q == 0)

    def c_tx(dz):
        return goes(dz, c == 1, q == 0)

    def c_rx(dz):
        return goes(dz, c == 0, q == 1)

    def y_tx(dz):
        return goes(dz, y == 1, q == 0)

    def y_rx(dz):
        return goes(dz, y == 0, q == 2)

    def detoured(dz, p):
        return fold and dz == depth - 1 and p == pieces - 1

    def over_tx(dz, p):
        if detoured(dz, p):
            return both(y_tx(dz), jnp.logical_or(z > 0, y == 0))
        if raised(dz, p):
            return both(y_tx(dz), y == 0)
        return y_tx(dz)

    def raised(dz, p):
        return fold and dz == lifted and p >= pieces // 2

    def lift_mate(p):
        return copy(held.at[mate_q, rows(p)], lifted * wide + mate_q, p,
                    e_send.at[lifted, p], y_recv.at[lifted, p], me + top * wide)

    def extra(dz, p):
        return copy(held.at[dz * wide + mate_q, rows(p)], (dz + 1) * wide + mate_q, p,
                    e_send.at[dz, p], y_recv.at[dz + 1, p], me - wide)

    def extra_tx():
        return both(z == 1, y == 0)

    def d_rx(dz):
        return goes(dz, y == 0, q == 3)

    def lift(p):
        return copy(white_ref.at[rows(p)], lifted * wide + q, p, z_send.at[lifted, p], z_recv.at[lifted, p],
                    me + top * wide)

    def sends(dz):
        for p in range(pieces):
            if dz > 0:
                @pl.when(z_rx(dz))
                def _():
                    from_above(dz, p).wait_recv()
            if dz < depth:
                @pl.when(z_tx(dz))
                def _():
                    down(dz, p).start()
            if columns == 2:
                @pl.when(over_tx(dz, p))
                def _():
                    over(dz, p, dz * wide + q).start()
            @pl.when(c_tx(dz))
            def _():
                across(dz, p, dz * wide + q).start()

    def passes(dz):
        if columns == 2:
            for p in range(pieces):
                @pl.when(y_rx(dz))
                def _():
                    over(dz, p, dz * wide + mate_q).wait_recv()
                    onward(dz, p, dz * wide + mate_q).start()
                if dz == 0 and raised(lifted, p):
                    @pl.when(both(z == 0, y == 0))
                    def _():
                        lift_mate(p).start()
                if detoured(dz + 1, p):
                    @pl.when(extra_tx())
                    def _():
                        extra(dz, p).start()

    def arrives(dz):
        for p in range(pieces):
            @pl.when(c_rx(dz))
            def _():
                across(dz, p, dz * wide + sib_q).wait_recv()
            if columns == 2:
                @pl.when(d_rx(dz))
                def _():
                    onward(dz, p, dz * wide + far_q).wait_recv()

    def finishes(dz):
        for p in range(pieces):
            if dz < depth:
                @pl.when(z_tx(dz))
                def _():
                    down(dz, p).wait_send()
            if columns == 2:
                @pl.when(over_tx(dz, p))
                def _():
                    over(dz, p, dz * wide + q).wait_send()
                if detoured(dz + 1, p):
                    @pl.when(extra_tx())
                    def _():
                        extra(dz, p).wait_send()
                @pl.when(y_rx(dz))
                def _():
                    onward(dz, p, dz * wide + mate_q).wait_send()
            @pl.when(c_tx(dz))
            def _():
                across(dz, p, dz * wide + q).wait_send()

    def answer(i):
        return pltpu.make_async_remote_copy(
            src_ref=made.at[i],
            dst_ref=back.at[q],
            send_sem=r_send.at[i],
            recv_sem=r_recv.at[q],
            device_id={"chan": jnp.int32(i)},
            device_id_type=pl.DeviceIdType.MESH,
        )

    def answered(i):
        return pltpu.make_async_remote_copy(
            src_ref=made.at[i],
            dst_ref=back.at[i],
            send_sem=r_send.at[i],
            recv_sem=r_recv.at[i],
            device_id={"chan": me},
            device_id_type=pl.DeviceIdType.MESH,
        )

    low = lax.broadcasted_iota(jnp.int32, (8, LANES), 0) < 4

    def prepare(i, carry):
        raw = white_ref[i]
        value = raw.astype(jnp.float32)
        own[i] = value
        ext[q * count + i] = raw
        for w in range(windows):
            swapped[i, w * 8 : w * 8 + 8] = pltpu.roll(value[w * 8 : w * 8 + 8], 4, 0)
        return carry

    def settle(dz):
        def one(l):
            def fill(i, carry):
                ext[(dz * wide + l) * count + i] = held[dz * wide + l, i]
                return carry
            lax.fori_loop(0, count, fill, 0, unroll=4)

        if dz == 0:
            for l in range(1, wide):
                @pl.when(q < l)
                def _():
                    one(l)
        else:
            @pl.when(exists(dz))
            def _():
                for l in range(1 if fold and dz == depth else wide):
                    one(l)

    live = jnp.minimum(layers * wide - me, pairs)

    def outside():
        def nothing(k, carry):
            for r in range(count):
                cross_ref[r, k] = jnp.zeros((8, LANES), jnp.float32)
            return carry

        lax.fori_loop(live, pairs, nothing, 0)

        @pl.when(layers - z <= depth)
        def _():
            def blank(i, carry):
                ext[(layers - z) * wide * count + i] = jnp.zeros((slab, LANES), jnp.bfloat16)
                return carry

            lax.fori_loop(0, 2 * count, blank, 0, unroll=4)

    def reached(dz):
        if dz < 0:
            return 0
        if dz == depth:
            return live
        return jnp.minimum((dz + 1) * wide - q - 1, live)

    def multiply(dz):
        def pair(k, carry):
            shift = offsets_ref[k]

            def channel(i, inner):
                place = me * count + i + shift
                keep = jnp.where(place < total, 1.0 / windows, 0.0)
                near = jnp.minimum(q * count + i + shift, ext.shape[0] - 1)
                partner = ext[near].astype(jnp.float32)
                straight = own[i, :8] * partner[:8]
                twisted = swapped[i, :8] * partner[:8]
                for w in range(1, windows):
                    part = slice(w * 8, w * 8 + 8)
                    straight += own[i, part] * partner[part]
                    twisted += swapped[i, part] * partner[part]
                joined = jnp.where(
                    low,
                    straight + pltpu.roll(straight, 4, 0),
                    pltpu.roll(twisted, 4, 0) - twisted,
                )
                cross_ref[i, k] = joined * keep
                return inner

            return lax.fori_loop(0, count, channel, carry, unroll=4)

        begin, end = reached(dz - 1), reached(dz)
        if fold and dz == depth:
            @pl.when(z == 0)
            def _():
                lax.fori_loop(begin, begin + 1, pair, 0)

            @pl.when(z > 0)
            def _():
                lax.fori_loop(begin, end, pair, 0)
        else:
            lax.fori_loop(begin, end, pair, 0)

    def reply():
        for i in range(wide):
            shift = offsets_ref[top * wide + q - i]

            def channel(r, carry):
                place = i * count + r + shift
                keep = jnp.where(place < total, 1.0 / windows, 0.0)
                near = jnp.clip(place - top * wide * count, 0, ext.shape[0] - 1)
                partner = ext[near].astype(jnp.float32)
                value = held[lifted * wide + i, r].astype(jnp.float32)
                straight = value[:8] * partner[:8]
                twisted = pltpu.roll(value[:8], 4, 0) * partner[:8]
                for w in range(1, windows):
                    part = slice(w * 8, w * 8 + 8)
                    straight += value[part] * partner[part]
                    twisted += pltpu.roll(value[part], 4, 0) * partner[part]
                joined = jnp.where(
                    low,
                    straight + pltpu.roll(straight, 4, 0),
                    pltpu.roll(twisted, 4, 0) - twisted,
                )
                made[i, r] = (joined * keep).astype(jnp.bfloat16)
                return carry

            lax.fori_loop(0, count, channel, 0, unroll=4)
        for i in range(wide):
            answer(i).start()

    sends(0)
    if fold:
        @pl.when(z == 0)
        def _():
            for p in range(pieces):
                lift(p).start()

    lax.fori_loop(0, count, prepare, 0)
    outside()
    for dz in range(depth + 1):
        if dz < depth:
            sends(dz + 1)
        if fold and dz == 0:
            sends(lifted)
        passes(dz)
        if fold and dz == 0:
            passes(lifted)
        arrives(dz)
        settle(dz)
        if fold and dz == 0:
            arrives(lifted)

            @pl.when(z == top)
            def _():
                reply()

        multiply(dz)

    if fold:
        @pl.when(z == 0)
        def _():
            for i in range(wide):
                answered(i).wait_recv()

                def take(r, carry):
                    cross_ref[r, top * wide - q + i] = back[i, r].astype(jnp.float32)
                    return carry

                lax.fori_loop(0, count, take, 0, unroll=4)
            for p in range(pieces):
                lift(p).wait_send()
                if raised(lifted, p):
                    @pl.when(y == 0)
                    def _():
                        lift_mate(p).wait_send()

        @pl.when(z == top)
        def _():
            for i in range(wide):
                answer(i).wait_send()

        finishes(lifted)
    for dz in range(depth + 1):
        finishes(dz)


def middle_kernel(shape, offsets_ref, white_ref, cross_ref, held, spec, made, back, joined,
                  x_send, f_send, s_recv, r_send, r_recv):
    layers, wide, windows = shape
    pairs = offsets_ref.shape[0]
    count = white_ref.shape[0] // windows
    parts = layers * wide
    pitch = spec.shape[0] // (2 * windows)
    half, top, last = layers // 2, layers - 1, parts - 1
    me = lax.axis_index("chan")
    z, q = me // wide, me % wide
    c = q % 2
    first = z * wide
    base = half * wide
    sib_q = q + 1 - 2 * c
    mate_q = (q + 2) % wide
    far_q = (sib_q + 2) % wide
    inner_low, inner_high = z == half - 1, z == half
    meets = jnp.logical_or(
        jnp.logical_and(inner_low, c == 0), jnp.logical_and(inner_high, c == 1))
    ships = jnp.logical_not(meets)
    neighbour = jnp.where(z < half, me + wide, me - wide)

    barrier = pltpu.get_barrier_semaphore()
    for i in range(parts):
        @pl.when(me != i)
        def _():
            pl.semaphore_signal(barrier, inc=1, device_id={"chan": jnp.int32(i)},
                                device_id_type=pl.DeviceIdType.MESH)
    pl.semaphore_wait(barrier, parts - 1)

    def remote(source, target, send, recv, device):
        return pltpu.make_async_remote_copy(
            src_ref=source, dst_ref=target, send_sem=send, recv_sem=recv,
            device_id={"chan": device}, device_id_type=pl.DeviceIdType.MESH,
        )

    def piece(ri, col):
        return white_ref.at[:, pl.ds(pl.multiple_of((ri * wide + col) * LANES, LANES), LANES)]

    def swap(j, ri, col):
        return remote(piece(ri, col), held.at[me, ri], x_send.at[j, ri], s_recv.at[me, ri], first + col)

    def ship_own(ri):
        return remote(piece(ri, q), held.at[me, ri], f_send.at[me, ri], s_recv.at[me, ri], neighbour)

    def ship(s, ri):
        return remote(held.at[s, ri], held.at[s, ri], f_send.at[s, ri], s_recv.at[s, ri], neighbour)

    def reply(d, k):
        return remote(made.at[d, k], back.at[k, q], r_send.at[d, k], r_recv.at[k, q], d)

    def replied(k, col):
        return remote(back.at[k, col], back.at[k, col], r_send.at[me, k], r_recv.at[k, col], me)

    behind = jnp.logical_and(z == top, q >= 2)
    ahead = jnp.logical_and(ships, jnp.logical_not(behind))

    @pl.when(ahead)
    def _():
        for ri in range(2):
            ship_own(ri).start()
    columns = (sib_q, mate_q, far_q)
    for j, col in enumerate(columns):
        for ri in range(2):
            swap(j, ri, col).start()

    def settle(s, load):
        for ri in range(2):
            def one(i, carry):
                value = load(ri, i).astype(jnp.float32)
                for part in range(2):
                    row = ri * windows * pitch + s * count + 2 * i + part
                    spec[pl.ds(row, windows, stride=pitch), :] = value[part * windows:(part + 1) * windows]
                return carry

            lax.fori_loop(0, count // 2, one, 0, unroll=4)

    def own_rows(ri, i):
        lanes = pl.ds(pl.multiple_of((ri * wide + q) * LANES, LANES), LANES)
        return white_ref[pl.ds(pl.multiple_of(i * 2 * windows, 2 * windows), 2 * windows), lanes]

    def take(s, onward):
        for ri in range(2):
            ship(s, ri).wait_recv()

        if onward is not False:
            @pl.when(onward)
            def _():
                for ri in range(2):
                    ship(s, ri).start()
        settle(s, lambda ri, i: held[s, ri, pl.ds(pl.multiple_of(i * 2 * windows, 2 * windows), 2 * windows)])

    def block(d, k):
        shift = offsets_ref[k]
        for g in range(count // 16):
            mine = d * count + g * 16
            real = imag = None
            for w in range(windows):
                cr = spec[pl.ds(pl.multiple_of(w * pitch + mine, 8), 16), :]
                ci = spec[pl.ds(pl.multiple_of((windows + w) * pitch + mine, 8), 16), :]
                pr = spec[pl.ds(w * pitch + mine + shift, 16), :]
                pi = spec[pl.ds((windows + w) * pitch + mine + shift, 16), :]
                re, im = cr * pr + ci * pi, ci * pr - cr * pi
                real, imag = (re, im) if w == 0 else (real + re, imag + im)
            rows = slice(g * 16, g * 16 + 16)
            made[d, k, 0, rows] = (real * (1.0 / windows)).astype(jnp.bfloat16)
            made[d, k, 1, rows] = (imag * (1.0 / windows)).astype(jnp.bfloat16)

    def blocks(d_begin, d_end, u_begin, u_end):
        def reach(u, carry):
            low, high = jnp.maximum(d_begin, u - pairs), jnp.minimum(d_end, u)

            def work(d, inner):
                block(d, u - 1 - d)
                return inner

            def give(d, inner):
                @pl.when(d != me)
                def _():
                    reply(d, u - 1 - d).start()
                return inner

            lax.fori_loop(low, high, work, 0)
            lax.fori_loop(low, high, give, 0)
            return carry

        lax.fori_loop(u_begin, u_end, reach, 0)

    for x in range(2 * windows):
        spec[pl.ds(x * pitch + parts * count, count), :] = jnp.zeros((count, LANES), jnp.float32)

    def clear(i, carry):
        joined[pl.ds(pl.multiple_of(i * 64, 64), 64), :] = jnp.zeros((64, LANES), jnp.float32)
        return carry

    lax.fori_loop(0, joined.shape[0] // 64, clear, 0)

    settle(me, own_rows)
    take(first + sib_q, ahead)
    take(first + mate_q, ships)
    take(first + far_q, ships)

    @pl.when(behind)
    def _():
        for ri in range(2):
            ship_own(ri).start()
            ship(first + sib_q, ri).start()

    def nearest(j):
        return jnp.where(j == 0, q, jnp.where(j == 1, sib_q, jnp.where(j == 2, mate_q, far_q)))

    blocks(first, first + wide, first + 1, first + wide + jnp.where(z == top, 1, 0))

    @pl.when(jnp.logical_and(inner_low, c == 0))
    def _():
        def step(s, carry):
            take(s, False)
            blocks(first, first + wide, s, s + 1)
            return carry
        lax.fori_loop(base, base + wide, step, 0)

    @pl.when(jnp.logical_and(inner_high, c == 1))
    def _():
        def step(j, carry):
            s = base - wide + nearest(j)
            take(s, False)
            blocks(s, s + 1, base + 1, base + wide)
            return carry
        lax.fori_loop(0, wide, step, 0)
        blocks(base - wide, base, base, base + 1)

    @pl.when(jnp.logical_or(inner_low, jnp.logical_and(inner_high, c == 1)))
    def _():
        begin = jnp.where(inner_low, first + 1, first)
        end = jnp.where(jnp.logical_and(inner_low, c == 0), base + wide, first + wide)

        def step(j, carry):
            s = nearest(j)
            take(s, ships)
            blocks(s, s + 1, begin, end)
            return carry
        lax.fori_loop(0, wide, step, 0)
        blocks(0, wide, first, begin)

    @pl.when(jnp.logical_or(inner_high, jnp.logical_and(inner_low, c == 0)))
    def _():
        begin = jnp.where(jnp.logical_and(inner_high, c == 0), first, 0)

        def step(s, carry):
            take(s, ships)
            blocks(begin, first + wide, s, s + 1 + jnp.where(s == last, 1, 0))
            return carry
        lax.fori_loop(top * wide, parts, step, 0)

    def unpack(source, k, col):
        for ri in range(2):
            for g in range(count // 16):
                value = source[ri, g * 16:g * 16 + 16].astype(jnp.float32)
                for part in range(2):
                    row = (ri * wide + col) * count * pairs + (g * 16 + part * 8) * pairs + k
                    joined[pl.ds(row, 8, stride=pairs), :] = value[part * 8:part * 8 + 8]

    def collect(k, carry):
        u = me + k + 1
        away = jnp.logical_or(
            jnp.logical_and(z == 0, u >= wide),
            jnp.logical_and(jnp.logical_and(inner_low, c == 1), u >= base))
        for col in range(wide):
            here = jnp.logical_and(q == col, jnp.logical_not(away))

            @pl.when(here)
            def _():
                unpack(made.at[me, k], k, col)

            @pl.when(jnp.logical_not(here))
            def _():
                replied(k, col).wait_recv()
                unpack(back.at[k, col], k, col)
        return carry

    lax.fori_loop(0, parts - me, collect, 0)

    def pack(i, carry):
        rows = pl.ds(pl.multiple_of(i * 16, 16), 16)
        for x in range(2 * wide):
            start = pl.multiple_of(x * count * pairs + i * 16, 16)
            cross_ref[rows, x * LANES:(x + 1) * LANES] = joined[pl.ds(start, 16), :].astype(jnp.bfloat16)
        return carry

    lax.fori_loop(0, count * pairs // 16, pack, 0, unroll=2)

    for j, col in enumerate(columns):
        for ri in range(2):
            swap(j, ri, col).wait_send()

    @pl.when(ships)
    def _():
        def sent(s, carry):
            for ri in range(2):
                ship(s, ri).wait_send()
            return carry

        lax.fori_loop(first, first + wide, sent, 0)

        @pl.when(jnp.logical_or(inner_low, inner_high))
        def _():
            begin = jnp.where(inner_low, 0, top * wide)
            lax.fori_loop(begin, begin + wide, sent, 0)

    d_begin = jnp.where(jnp.logical_or(z == top, jnp.logical_and(inner_high, c == 0)), first, 0)
    u_end = jnp.where(jnp.logical_or(z == 0, jnp.logical_and(inner_low, c == 1)), first + wide, parts + 1)

    def drained(u, carry):
        def one(d, inner):
            @pl.when(d != me)
            def _():
                reply(d, u - 1 - d).wait_send()
            return inner

        return lax.fori_loop(jnp.maximum(d_begin, u - pairs), jnp.minimum(first + wide, u), one, carry)

    lax.fori_loop(jnp.maximum(first, 1), u_end, drained, 0)


def meet(layers, wide, white, windows, offsets):
    pairs = offsets.shape[0]
    count = white.shape[0] // windows
    parts = layers * wide
    pitch = (parts + 1) * count
    return pl.pallas_call(
        functools.partial(middle_kernel, (layers, wide, windows)),
        out_shape=jax.ShapeDtypeStruct((count * pairs, 2 * F), jnp.bfloat16),
        in_specs=[
            pl.BlockSpec(memory_space=pltpu.SMEM),
            pl.BlockSpec(memory_space=pltpu.VMEM),
        ],
        out_specs=pl.BlockSpec(memory_space=pltpu.VMEM),
        scratch_shapes=[
            pltpu.VMEM((parts, 2, count * windows, LANES), jnp.bfloat16),
            pltpu.VMEM((2 * windows * pitch, LANES), jnp.float32),
            pltpu.VMEM((parts, pairs, 2, count, LANES), jnp.bfloat16),
            pltpu.VMEM((pairs, wide, 2, count, LANES), jnp.bfloat16),
            pltpu.VMEM((2 * wide * count * pairs, LANES), jnp.float32),
            pltpu.SemaphoreType.DMA((wide - 1, 2)),
            pltpu.SemaphoreType.DMA((parts, 2)),
            pltpu.SemaphoreType.DMA((parts, 2)),
            pltpu.SemaphoreType.DMA((parts, pairs)),
            pltpu.SemaphoreType.DMA((pairs, wide)),
        ],
        compiler_params=pltpu.CompilerParams(
            vmem_limit_bytes=40 * 1024 * 1024, collective_id=1, has_side_effects=True
        ),
    )(offsets, white)


def shards(columns, records, live_mask, offsets):
    count, windows, length = records.shape
    pairs = offsets.shape[0]
    wide = 2 * columns
    layers = lax.axis_size("chan") // wide
    reach = (BAND + count - 2) // count
    depth = min(layers - 1, (wide - 1 + reach) // wide)
    pieces = PIECES
    fold = columns == 2 and depth == layers - 1 and depth >= 2 and layers * wide == pairs and pairs * count == BAND
    white = whiten(records, live_mask)
    if (
        columns == 2 and layers == 4 and layers * wide == pairs and pairs * count == BAND
        and F == wide * LANES and windows == 8 and count % 16 == 0
    ):
        cross = meet(layers, wide, white, windows, offsets)
        return lags(cross, count, pairs, length)
    spectra = white.reshape(count, windows * 8, LANES)
    slots = (depth + 1) * wide
    cross = pl.pallas_call(
        functools.partial(reach_kernel, (layers, columns, depth, pieces, windows, fold)),
        out_shape=jax.ShapeDtypeStruct((count, pairs, 8, LANES), jnp.float32),
        in_specs=[
            pl.BlockSpec(memory_space=pltpu.SMEM),
            pl.BlockSpec(memory_space=pltpu.VMEM),
        ],
        out_specs=pl.BlockSpec(memory_space=pltpu.VMEM),
        scratch_shapes=[
            pltpu.VMEM((slots + wide, count, windows * 8, LANES), jnp.bfloat16),
            pltpu.VMEM((slots * count, windows * 8, LANES), jnp.bfloat16),
            pltpu.VMEM((count, windows * 8, LANES), jnp.float32),
            pltpu.VMEM((count, windows * 8, LANES), jnp.float32),
            pltpu.VMEM((wide, count, 8, LANES), jnp.bfloat16),
            pltpu.VMEM((wide, count, 8, LANES), jnp.bfloat16),
        ]
        + [pltpu.SemaphoreType.DMA((depth + 2, pieces))] * 9
        + [pltpu.SemaphoreType.DMA((wide,))] * 2,
        compiler_params=pltpu.CompilerParams(
            vmem_limit_bytes=40 * 1024 * 1024, collective_id=0, has_side_effects=True
        ),
    )(offsets, spectra)
    return lags(cross.astype(jnp.bfloat16).reshape(count * pairs, 8 * LANES), count, pairs, length)


def lags(cross, count, pairs, length):
    result = jnp.dot(cross, jnp.asarray(inverse_table(length)), preferred_element_type=jnp.float32)
    result = result * (1.0 / math.sqrt(F))
    return result.reshape(count, pairs, LAGS).astype(jnp.bfloat16)


def solution(mesh):
    in_specs = (P(("day", "chan"), None, None), P(("day", "chan")), P())
    out_specs = P(("day", "chan"), None, None)
    columns = max(1, LAYER_CHIPS // mesh.shape["day"])
    body = functools.partial(shards, columns)
    return jax.shard_map(body, mesh=mesh, in_specs=in_specs, out_specs=out_specs, check_vma=False)
```

```python
import functools
import math

import jax
import jax.numpy as jnp
import numpy as np
from jax import lax
from jax.experimental import pallas as pl
from jax.experimental.pallas import tpu as pltpu
from jax.sharding import PartitionSpec as P

F = 512
F0 = 6
LAGS = 2048
LANES = 128
BAND = 512
PIECES = 4
LAYER_CHIPS = 4


def forward_table(length):
    samples = np.arange(length, dtype=np.int64)
    freqs = F0 + np.arange(F, dtype=np.int64)
    phase = np.mod(samples[:, None] * freqs[None, :], length)
    angle = 2.0 * math.pi / length * phase
    return np.concatenate([np.cos(angle), -np.sin(angle)], axis=1).astype(np.float32).astype(jnp.bfloat16)


def inverse_table(length):
    freqs = F0 + np.arange(F, dtype=np.int64)
    shifts = np.arange(LAGS, dtype=np.int64) - LAGS // 2
    phase = np.mod(freqs[:, None] * shifts[None, :], length)
    angle = 2.0 * math.pi / length * phase
    return np.concatenate([np.cos(angle), -np.sin(angle)], axis=0).astype(np.float32).astype(jnp.bfloat16)


def whiten(records, live_mask):
    count, windows, length = records.shape
    spectrum = jnp.dot(
        records.reshape(count * windows, length),
        jnp.asarray(forward_table(length)),
        preferred_element_type=jnp.float32,
    )
    power = jnp.mean(spectrum * spectrum, axis=1, keepdims=True)
    gain = jnp.repeat(live_mask.astype(jnp.float32), windows)[:, None]
    white = spectrum * (gain * lax.rsqrt(power + 1e-06))
    return white.astype(jnp.bfloat16)


def reach_kernel(shape, offsets_ref, white_ref, cross_ref, held, ext, own, swapped, made, back,
                 z_send, z_recv, c_send, c_recv, y_send, y_recv, d_send, d_recv, e_send, r_send, r_recv):
    layers, columns, depth, pieces, windows, fold = shape
    count, slab = white_ref.shape[0], white_ref.shape[1]
    pairs = offsets_ref.shape[0]
    wide = 2 * columns
    total = layers * wide * count
    me = lax.axis_index("chan")
    z, q = me // wide, me % wide
    y, c = q // 2, q % 2
    sibling = me + 1 - 2 * c
    sib_q = q + 1 - 2 * c
    mate = me + 2 - 4 * y
    mate_q = q + 2 - 4 * y
    far_q = sib_q + 2 - 4 * y
    step = count // pieces
    top, lifted = layers - 1, depth + 1

    barrier = pltpu.get_barrier_semaphore()

    def greet(device):
        pl.semaphore_signal(barrier, inc=1, device_id={"chan": device}, device_id_type=pl.DeviceIdType.MESH)

    greet(sibling)
    if columns == 2:
        greet(mate)

    @pl.when(z >= 1)
    def _():
        greet(me - wide)

    @pl.when(z < layers - 1)
    def _():
        greet(me + wide)

    below, above = jnp.minimum(z, 1), jnp.minimum(top - z, 1)
    peers = columns + below + above
    if fold:
        @pl.when(z == 0)
        def _():
            for i in range(wide):
                greet(top * wide + i)

        @pl.when(z == top)
        def _():
            for i in range(wide):
                greet(jnp.int32(i))

        peers = peers + wide * (2 - below - above)
    pl.semaphore_wait(barrier, peers)

    def rows(p):
        return pl.ds(p * step, step)

    def mine(dz, p):
        return white_ref.at[rows(p)] if dz == 0 else held.at[dz * wide + q, rows(p)]

    def copy(source, slot, p, send, recv, device):
        return pltpu.make_async_remote_copy(
            src_ref=source,
            dst_ref=held.at[slot, rows(p)],
            send_sem=send,
            recv_sem=recv,
            device_id={"chan": device},
            device_id_type=pl.DeviceIdType.MESH,
        )

    def down(dz, p):
        return copy(mine(dz, p), (dz + 1) * wide + q, p, z_send.at[dz, p], z_recv.at[dz + 1, p], me - wide)

    def from_above(dz, p):
        return copy(mine(dz, p), dz * wide + q, p, z_send.at[dz, p], z_recv.at[dz, p], me)

    def across(dz, p, slot):
        return copy(mine(dz, p), slot, p, c_send.at[dz, p], c_recv.at[dz, p], sibling)

    def over(dz, p, slot):
        return copy(mine(dz, p), slot, p, y_send.at[dz, p], y_recv.at[dz, p], mate)

    def onward(dz, p, slot):
        return copy(held.at[dz * wide + mate_q, rows(p)], slot, p, d_send.at[dz, p], d_recv.at[dz, p], sibling)

    def both(*conditions):
        joined = conditions[0]
        for condition in conditions[1:]:
            joined = jnp.logical_and(joined, condition)
        return joined

    def exists(dz):
        return z + dz < layers

    def goes(dz, at_start, at_end):
        if dz == lifted:
            return z == top
        if dz == 0:
            return at_start
        if fold and dz == depth:
            return both(exists(dz), at_end)
        return exists(dz)

    def z_tx(dz):
        if fold and dz + 1 == depth:
            return both(exists(dz), z >= 1, jnp.logical_or(z >= 2, q == 0))
        return both(exists(dz), z >= 1)

    def z_rx(dz):
        return goes(dz, None, q == 0)

    def c_tx(dz):
        return goes(dz, c == 1, q == 0)

    def c_rx(dz):
        return goes(dz, c == 0, q == 1)

    def y_tx(dz):
        return goes(dz, y == 1, q == 0)

    def y_rx(dz):
        return goes(dz, y == 0, q == 2)

    def detoured(dz, p):
        return fold and dz == depth - 1 and p == pieces - 1

    def over_tx(dz, p):
        if detoured(dz, p):
            return both(y_tx(dz), jnp.logical_or(z > 0, y == 0))
        if raised(dz, p):
            return both(y_tx(dz), y == 0)
        return y_tx(dz)

    def raised(dz, p):
        return fold and dz == lifted and p >= pieces // 2

    def lift_mate(p):
        return copy(held.at[mate_q, rows(p)], lifted * wide + mate_q, p,
                    e_send.at[lifted, p], y_recv.at[lifted, p], me + top * wide)

    def extra(dz, p):
        return copy(held.at[dz * wide + mate_q, rows(p)], (dz + 1) * wide + mate_q, p,
                    e_send.at[dz, p], y_recv.at[dz + 1, p], me - wide)

    def extra_tx():
        return both(z == 1, y == 0)

    def d_rx(dz):
        return goes(dz, y == 0, q == 3)

    def lift(p):
        return copy(white_ref.at[rows(p)], lifted * wide + q, p, z_send.at[lifted, p], z_recv.at[lifted, p],
                    me + top * wide)

    def sends(dz):
        for p in range(pieces):
            if dz > 0:
                @pl.when(z_rx(dz))
                def _():
                    from_above(dz, p).wait_recv()
            if dz < depth:
                @pl.when(z_tx(dz))
                def _():
                    down(dz, p).start()
            if columns == 2:
                @pl.when(over_tx(dz, p))
                def _():
                    over(dz, p, dz * wide + q).start()
            @pl.when(c_tx(dz))
            def _():
                across(dz, p, dz * wide + q).start()

    def passes(dz):
        if columns == 2:
            for p in range(pieces):
                @pl.when(y_rx(dz))
                def _():
                    over(dz, p, dz * wide + mate_q).wait_recv()
                    onward(dz, p, dz * wide + mate_q).start()
                if dz == 0 and raised(lifted, p):
                    @pl.when(both(z == 0, y == 0))
                    def _():
                        lift_mate(p).start()
                if detoured(dz + 1, p):
                    @pl.when(extra_tx())
                    def _():
                        extra(dz, p).start()

    def arrives(dz):
        for p in range(pieces):
            @pl.when(c_rx(dz))
            def _():
                across(dz, p, dz * wide + sib_q).wait_recv()
            if columns == 2:
                @pl.when(d_rx(dz))
                def _():
                    onward(dz, p, dz * wide + far_q).wait_recv()

    def finishes(dz):
        for p in range(pieces):
            if dz < depth:
                @pl.when(z_tx(dz))
                def _():
                    down(dz, p).wait_send()
            if columns == 2:
                @pl.when(over_tx(dz, p))
                def _():
                    over(dz, p, dz * wide + q).wait_send()
                if detoured(dz + 1, p):
                    @pl.when(extra_tx())
                    def _():
                        extra(dz, p).wait_send()
                @pl.when(y_rx(dz))
                def _():
                    onward(dz, p, dz * wide + mate_q).wait_send()
            @pl.when(c_tx(dz))
            def _():
                across(dz, p, dz * wide + q).wait_send()

    def answer(i):
        return pltpu.make_async_remote_copy(
            src_ref=made.at[i],
            dst_ref=back.at[q],
            send_sem=r_send.at[i],
            recv_sem=r_recv.at[q],
            device_id={"chan": jnp.int32(i)},
            device_id_type=pl.DeviceIdType.MESH,
        )

    def answered(i):
        return pltpu.make_async_remote_copy(
            src_ref=made.at[i],
            dst_ref=back.at[i],
            send_sem=r_send.at[i],
            recv_sem=r_recv.at[i],
            device_id={"chan": me},
            device_id_type=pl.DeviceIdType.MESH,
        )

    low = lax.broadcasted_iota(jnp.int32, (8, LANES), 0) < 4

    def prepare(i, carry):
        raw = white_ref[i]
        value = raw.astype(jnp.float32)
        own[i] = value
        ext[q * count + i] = raw
        for w in range(windows):
            swapped[i, w * 8 : w * 8 + 8] = pltpu.roll(value[w * 8 : w * 8 + 8], 4, 0)
        return carry

    def settle(dz):
        def one(l):
            def fill(i, carry):
                ext[(dz * wide + l) * count + i] = held[dz * wide + l, i]
                return carry
            lax.fori_loop(0, count, fill, 0, unroll=4)

        if dz == 0:
            for l in range(1, wide):
                @pl.when(q < l)
                def _():
                    one(l)
        else:
            @pl.when(exists(dz))
            def _():
                for l in range(1 if fold and dz == depth else wide):
                    one(l)

    live = jnp.minimum(layers * wide - me, pairs)

    def outside():
        def nothing(k, carry):
            for r in range(count):
                cross_ref[r, k] = jnp.zeros((8, LANES), jnp.float32)
            return carry

        lax.fori_loop(live, pairs, nothing, 0)

        @pl.when(layers - z <= depth)
        def _():
            def blank(i, carry):
                ext[(layers - z) * wide * count + i] = jnp.zeros((slab, LANES), jnp.bfloat16)
                return carry

            lax.fori_loop(0, 2 * count, blank, 0, unroll=4)

    def reached(dz):
        if dz < 0:
            return 0
        if dz == depth:
            return live
        return jnp.minimum((dz + 1) * wide - q - 1, live)

    def multiply(dz):
        def pair(k, carry):
            shift = offsets_ref[k]

            def channel(i, inner):
                place = me * count + i + shift
                keep = jnp.where(place < total, 1.0 / windows, 0.0)
                near = jnp.minimum(q * count + i + shift, ext.shape[0] - 1)
                partner = ext[near].astype(jnp.float32)
                straight = own[i, :8] * partner[:8]
                twisted = swapped[i, :8] * partner[:8]
                for w in range(1, windows):
                    part = slice(w * 8, w * 8 + 8)
                    straight += own[i, part] * partner[part]
                    twisted += swapped[i, part] * partner[part]
                joined = jnp.where(
                    low,
                    straight + pltpu.roll(straight, 4, 0),
                    pltpu.roll(twisted, 4, 0) - twisted,
                )
                cross_ref[i, k] = joined * keep
                return inner

            return lax.fori_loop(0, count, channel, carry, unroll=4)

        begin, end = reached(dz - 1), reached(dz)
        if fold and dz == depth:
            @pl.when(z == 0)
            def _():
                lax.fori_loop(begin, begin + 1, pair, 0)

            @pl.when(z > 0)
            def _():
                lax.fori_loop(begin, end, pair, 0)
        else:
            lax.fori_loop(begin, end, pair, 0)

    def reply():
        for i in range(wide):
            shift = offsets_ref[top * wide + q - i]

            def channel(r, carry):
                place = i * count + r + shift
                keep = jnp.where(place < total, 1.0 / windows, 0.0)
                near = jnp.clip(place - top * wide * count, 0, ext.shape[0] - 1)
                partner = ext[near].astype(jnp.float32)
                value = held[lifted * wide + i, r].astype(jnp.float32)
                straight = value[:8] * partner[:8]
                twisted = pltpu.roll(value[:8], 4, 0) * partner[:8]
                for w in range(1, windows):
                    part = slice(w * 8, w * 8 + 8)
                    straight += value[part] * partner[part]
                    twisted += pltpu.roll(value[part], 4, 0) * partner[part]
                joined = jnp.where(
                    low,
                    straight + pltpu.roll(straight, 4, 0),
                    pltpu.roll(twisted, 4, 0) - twisted,
                )
                made[i, r] = (joined * keep).astype(jnp.bfloat16)
                return carry

            lax.fori_loop(0, count, channel, 0, unroll=4)
        for i in range(wide):
            answer(i).start()

    sends(0)
    if fold:
        @pl.when(z == 0)
        def _():
            for p in range(pieces):
                lift(p).start()

    lax.fori_loop(0, count, prepare, 0)
    outside()
    for dz in range(depth + 1):
        if dz < depth:
            sends(dz + 1)
        if fold and dz == 0:
            sends(lifted)
        passes(dz)
        if fold and dz == 0:
            passes(lifted)
        arrives(dz)
        settle(dz)
        if fold and dz == 0:
            arrives(lifted)

            @pl.when(z == top)
            def _():
                reply()

        multiply(dz)

    if fold:
        @pl.when(z == 0)
        def _():
            for i in range(wide):
                answered(i).wait_recv()

                def take(r, carry):
                    cross_ref[r, top * wide - q + i] = back[i, r].astype(jnp.float32)
                    return carry

                lax.fori_loop(0, count, take, 0, unroll=4)
            for p in range(pieces):
                lift(p).wait_send()
                if raised(lifted, p):
                    @pl.when(y == 0)
                    def _():
                        lift_mate(p).wait_send()

        @pl.when(z == top)
        def _():
            for i in range(wide):
                answer(i).wait_send()

        finishes(lifted)
    for dz in range(depth + 1):
        finishes(dz)


def middle_kernel(shape, offsets_ref, white_ref, cross_ref, held, spec, made, back, joined,
                  x_send, f_send, s_recv, r_send, r_recv):
    layers, wide, windows = shape
    pairs = offsets_ref.shape[0]
    count = white_ref.shape[0] // windows
    parts = layers * wide
    pitch = spec.shape[0] // (2 * windows)
    half, top, last = layers // 2, layers - 1, parts - 1
    me = lax.axis_index("chan")
    z, q = me // wide, me % wide
    c = q % 2
    first = z * wide
    base = half * wide
    sib_q = q + 1 - 2 * c
    mate_q = (q + 2) % wide
    far_q = (sib_q + 2) % wide
    near = c == 0
    inner_low, inner_high = z == half - 1, z == half
    neighbour = jnp.where(
        jnp.logical_or(z == 0, jnp.logical_and(inner_low, c == 1)), me + wide, me - wide)
    own_end = jnp.where(
        z == 0, jnp.where(near, base, wide),
        jnp.where(jnp.logical_and(inner_low, c == 1), base + wide, parts + 1))
    low_begin = jnp.where(
        inner_low, jnp.where(near, base, wide),
        jnp.where(jnp.logical_and(inner_high, c == 1), base + wide, 0))
    low_end = jnp.where(
        inner_low, own_end, jnp.where(jnp.logical_and(inner_high, c == 1), parts + 1, 0))

    barrier = pltpu.get_barrier_semaphore()

    def greet(device, condition):
        @pl.when(condition)
        def _():
            pl.semaphore_signal(barrier, inc=1, device_id={"chan": jnp.int32(device)},
                                device_id_type=pl.DeviceIdType.MESH)

    for col in (sib_q, mate_q, far_q):
        greet(first + col, z >= 0)
    for i in range(wide):
        odd = i % 2 == 1
        greet(wide + i, z == 0)
        if odd:
            greet(base + i, z < half)
        else:
            greet(base + i, jnp.logical_and(inner_low, q == i))
    greet(me - wide, jnp.logical_or(inner_low, jnp.logical_and(inner_high, c == 1)))
    greet(me + wide, inner_high)
    replies_far = jnp.where(inner_low, wide, jnp.where(jnp.logical_and(inner_high, c == 1), 2 * wide - 1, 0))
    ships_there = jnp.where(jnp.logical_and(inner_low, near), 0, 1)
    pl.semaphore_wait(barrier, wide - 1 + replies_far + ships_there)

    def remote(source, target, send, recv, device):
        return pltpu.make_async_remote_copy(
            src_ref=source, dst_ref=target, send_sem=send, recv_sem=recv,
            device_id={"chan": device}, device_id_type=pl.DeviceIdType.MESH,
        )

    def piece(ri, col):
        return white_ref.at[:, pl.ds(pl.multiple_of((ri * wide + col) * LANES, LANES), LANES)]

    def swap(j, ri, col):
        return remote(piece(ri, col), held.at[me, ri], x_send.at[j, ri], s_recv.at[me, ri], first + col)

    def ship_own(ri):
        return remote(piece(ri, q), held.at[me, ri], f_send.at[me, ri], s_recv.at[me, ri], neighbour)

    def ship(s, ri):
        return remote(held.at[s, ri], held.at[s, ri], f_send.at[s, ri], s_recv.at[s, ri], neighbour)

    def reply(d, k):
        return remote(made.at[d, k], back.at[k, q], r_send.at[d, k], r_recv.at[k, q], d)

    def replied(k, col):
        return remote(back.at[k, col], back.at[k, col], r_send.at[me, k], r_recv.at[k, col], me)

    for ri in range(2):
        ship_own(ri).start()
    columns = (sib_q, mate_q, far_q)
    for j, col in enumerate(columns):
        for ri in range(2):
            swap(j, ri, col).start()

    def settle(s, load):
        for ri in range(2):
            def one(i, carry):
                value = load(ri, i).astype(jnp.float32)
                for part in range(2):
                    row = ri * windows * pitch + s * count + 2 * i + part
                    spec[pl.ds(row, windows, stride=pitch), :] = value[part * windows:(part + 1) * windows]
                return carry

            lax.fori_loop(0, count // 2, one, 0, unroll=4)

    def own_rows(ri, i):
        lanes = pl.ds(pl.multiple_of((ri * wide + q) * LANES, LANES), LANES)
        return white_ref[pl.ds(pl.multiple_of(i * 2 * windows, 2 * windows), 2 * windows), lanes]

    def take(s, onward=None):
        for ri in range(2):
            ship(s, ri).wait_recv()
        if onward is not None:
            @pl.when(onward)
            def _():
                for ri in range(2):
                    ship(s, ri).start()
        settle(s, lambda ri, i: held[s, ri, pl.ds(pl.multiple_of(i * 2 * windows, 2 * windows), 2 * windows)])

    def block(d, k):
        shift = offsets_ref[k]
        for g in range(count // 16):
            mine = d * count + g * 16
            real = imag = None
            for w in range(windows):
                cr = spec[pl.ds(pl.multiple_of(w * pitch + mine, 8), 16), :]
                ci = spec[pl.ds(pl.multiple_of((windows + w) * pitch + mine, 8), 16), :]
                pr = spec[pl.ds(w * pitch + mine + shift, 16), :]
                pi = spec[pl.ds((windows + w) * pitch + mine + shift, 16), :]
                re, im = cr * pr + ci * pi, ci * pr - cr * pi
                real, imag = (re, im) if w == 0 else (real + re, imag + im)
            rows = slice(g * 16, g * 16 + 16)
            made[d, k, 0, rows] = (real * (1.0 / windows)).astype(jnp.bfloat16)
            made[d, k, 1, rows] = (imag * (1.0 / windows)).astype(jnp.bfloat16)

    def spans(d_begin, d_end, u_begin, u_end, visit):
        def reach(u, carry):
            def one(d, inner):
                visit(d, u - 1 - d)
                return inner

            return lax.fori_loop(jnp.maximum(d_begin, u - pairs), jnp.minimum(d_end, u), one, carry)

        lax.fori_loop(u_begin, u_end, reach, 0)

    def give(d, k):
        @pl.when(d != me)
        def _():
            reply(d, k).start()

    def gave(d, k):
        @pl.when(d != me)
        def _():
            reply(d, k).wait_send()

    def blocks(*span):
        spans(*span, block)
        spans(*span, give)

    for x in range(2 * windows):
        spec[pl.ds(x * pitch + parts * count, count), :] = jnp.zeros((count, LANES), jnp.float32)

    def clear(i, carry):
        joined[pl.ds(pl.multiple_of(i * 64, 64), 64), :] = jnp.zeros((64, LANES), jnp.float32)
        return carry

    lax.fori_loop(0, joined.shape[0] // 64, clear, 0)

    y = q // 2
    pair_1, pair_2 = (q, sib_q), (mate_q, far_q)

    def reached_1(start, more=0):
        return jnp.where(y == 0, start, start + 3), jnp.where(y == 0, start + 2, start + wide + more)

    def reached_2(start, more=0):
        return jnp.where(y == 0, start + 2, start), jnp.where(y == 0, start + wide + more, start + 3)

    settle(me, own_rows)
    for col in columns:
        take(first + col, z >= 0)
    blocks(first, first + wide, first + 1, first + wide + jnp.where(z == top, 1, 0))

    @pl.when(jnp.logical_and(z == 0, near))
    def _():
        for group, reached in ((pair_1, reached_1), (pair_2, reached_2)):
            for col in group:
                take(wide + col)
            blocks(0, wide, *reached(wide))

    @pl.when(inner_low)
    def _():
        def lower(group):
            for col in group:
                take(col, jnp.logical_not(near))

        lower(pair_1)
        for col in pair_1:
            take(base + col)
        blocks(wide, base, *reached_1(base))
        lower(pair_2)
        blocks(0, wide, *reached_1(base))

        @pl.when(jnp.logical_not(near))
        def _():
            blocks(0, wide, wide, base)
        for col in pair_2:
            take(base + col)
        blocks(0, base, *reached_2(base))

        @pl.when(near)
        def _():
            for group, reached in ((pair_1, reached_1), (pair_2, reached_2)):
                for col in group:
                    take(top * wide + col)
                blocks(0, base, *reached(top * wide, 1))

    @pl.when(inner_high)
    def _():
        for group, reached in ((pair_1, reached_1), (pair_2, reached_2)):
            for col in group:
                take(top * wide + col, near)
            blocks(base, base + wide, *reached(top * wide, 1))

        @pl.when(jnp.logical_not(near))
        def _():
            for col in pair_1 + pair_2:
                take(wide + col)
            for col in pair_1 + pair_2:
                take(col)
            blocks(0, base, top * wide, parts + 1)

    def unpack(source, k, col):
        for ri in range(2):
            for g in range(count // 16):
                value = source[ri, g * 16:g * 16 + 16].astype(jnp.float32)
                for part in range(2):
                    row = (ri * wide + col) * count * pairs + (g * 16 + part * 8) * pairs + k
                    joined[pl.ds(row, 8, stride=pairs), :] = value[part * 8:part * 8 + 8]

    def collect(k, carry):
        away = me + k + 1 >= own_end
        for col in range(wide):
            here = jnp.logical_and(q == col, jnp.logical_not(away))

            @pl.when(here)
            def _():
                unpack(made.at[me, k], k, col)

            @pl.when(jnp.logical_not(here))
            def _():
                replied(k, col).wait_recv()
                unpack(back.at[k, col], k, col)
        return carry

    lax.fori_loop(0, parts - me, collect, 0)

    def pack(i, carry):
        rows = pl.ds(pl.multiple_of(i * 16, 16), 16)
        for x in range(2 * wide):
            start = pl.multiple_of(x * count * pairs + i * 16, 16)
            cross_ref[rows, x * LANES:(x + 1) * LANES] = joined[pl.ds(start, 16), :].astype(jnp.bfloat16)
        return carry

    lax.fori_loop(0, count * pairs // 16, pack, 0, unroll=2)

    for j, col in enumerate(columns):
        for ri in range(2):
            swap(j, ri, col).wait_send()

    def sent(s, carry):
        for ri in range(2):
            ship(s, ri).wait_send()
        return carry

    lax.fori_loop(first, first + wide, sent, 0)

    @pl.when(jnp.logical_or(jnp.logical_and(inner_low, c == 1), jnp.logical_and(inner_high, near)))
    def _():
        begin = jnp.where(inner_low, 0, top * wide)
        lax.fori_loop(begin, begin + wide, sent, 0)

    spans(first, first + wide, first + 1, own_end, gave)
    spans(0, first, low_begin, low_end, gave)


def meet(layers, wide, white, windows, offsets):
    pairs = offsets.shape[0]
    count = white.shape[0] // windows
    parts = layers * wide
    pitch = (parts + 1) * count
    return pl.pallas_call(
        functools.partial(middle_kernel, (layers, wide, windows)),
        out_shape=jax.ShapeDtypeStruct((count * pairs, 2 * F), jnp.bfloat16),
        in_specs=[
            pl.BlockSpec(memory_space=pltpu.SMEM),
            pl.BlockSpec(memory_space=pltpu.VMEM),
        ],
        out_specs=pl.BlockSpec(memory_space=pltpu.VMEM),
        scratch_shapes=[
            pltpu.VMEM((parts, 2, count * windows, LANES), jnp.bfloat16),
            pltpu.VMEM((2 * windows * pitch, LANES), jnp.float32),
            pltpu.VMEM((parts, pairs, 2, count, LANES), jnp.bfloat16),
            pltpu.VMEM((pairs, wide, 2, count, LANES), jnp.bfloat16),
            pltpu.VMEM((2 * wide * count * pairs, LANES), jnp.float32),
            pltpu.SemaphoreType.DMA((wide - 1, 2)),
            pltpu.SemaphoreType.DMA((parts, 2)),
            pltpu.SemaphoreType.DMA((parts, 2)),
            pltpu.SemaphoreType.DMA((parts, pairs)),
            pltpu.SemaphoreType.DMA((pairs, wide)),
        ],
        compiler_params=pltpu.CompilerParams(
            vmem_limit_bytes=40 * 1024 * 1024, collective_id=1, has_side_effects=True
        ),
    )(offsets, white)


def shards(columns, records, live_mask, offsets):
    count, windows, length = records.shape
    pairs = offsets.shape[0]
    wide = 2 * columns
    layers = lax.axis_size("chan") // wide
    reach = (BAND + count - 2) // count
    depth = min(layers - 1, (wide - 1 + reach) // wide)
    pieces = PIECES
    fold = columns == 2 and depth == layers - 1 and depth >= 2 and layers * wide == pairs and pairs * count == BAND
    white = whiten(records, live_mask)
    if (
        columns == 2 and layers == 4 and layers * wide == pairs and pairs * count == BAND
        and F == wide * LANES and windows == 8 and count % 16 == 0
    ):
        cross = meet(layers, wide, white, windows, offsets)
        return lags(cross, count, pairs, length)
    spectra = white.reshape(count, windows * 8, LANES)
    slots = (depth + 1) * wide
    cross = pl.pallas_call(
        functools.partial(reach_kernel, (layers, columns, depth, pieces, windows, fold)),
        out_shape=jax.ShapeDtypeStruct((count, pairs, 8, LANES), jnp.float32),
        in_specs=[
            pl.BlockSpec(memory_space=pltpu.SMEM),
            pl.BlockSpec(memory_space=pltpu.VMEM),
        ],
        out_specs=pl.BlockSpec(memory_space=pltpu.VMEM),
        scratch_shapes=[
            pltpu.VMEM((slots + wide, count, windows * 8, LANES), jnp.bfloat16),
            pltpu.VMEM((slots * count, windows * 8, LANES), jnp.bfloat16),
            pltpu.VMEM((count, windows * 8, LANES), jnp.float32),
            pltpu.VMEM((count, windows * 8, LANES), jnp.float32),
            pltpu.VMEM((wide, count, 8, LANES), jnp.bfloat16),
            pltpu.VMEM((wide, count, 8, LANES), jnp.bfloat16),
        ]
        + [pltpu.SemaphoreType.DMA((depth + 2, pieces))] * 9
        + [pltpu.SemaphoreType.DMA((wide,))] * 2,
        compiler_params=pltpu.CompilerParams(
            vmem_limit_bytes=40 * 1024 * 1024, collective_id=0, has_side_effects=True
        ),
    )(offsets, spectra)
    return lags(cross.astype(jnp.bfloat16).reshape(count * pairs, 8 * LANES), count, pairs, length)


def lags(cross, count, pairs, length):
    result = jnp.dot(cross, jnp.asarray(inverse_table(length)), preferred_element_type=jnp.float32)
    result = result * (1.0 / math.sqrt(F))
    return result.reshape(count, pairs, LAGS).astype(jnp.bfloat16)


def solution(mesh):
    in_specs = (P(("day", "chan"), None, None), P(("day", "chan")), P())
    out_specs = P(("day", "chan"), None, None)
    columns = max(1, LAYER_CHIPS // mesh.shape["day"])
    body = functools.partial(shards, columns)
    return jax.shard_map(body, mesh=mesh, in_specs=in_specs, out_specs=out_specs, check_vma=False)
```

```python
import functools
import math

import jax
import jax.numpy as jnp
import numpy as np
from jax import lax
from jax.experimental import pallas as pl
from jax.experimental.pallas import tpu as pltpu
from jax.sharding import PartitionSpec as P

F = 512
F0 = 6
LAGS = 2048
LANES = 128
BAND = 512
PIECES = 4
LAYER_CHIPS = 4


def forward_table(length):
    samples = np.arange(length, dtype=np.int64)
    freqs = F0 + np.arange(F, dtype=np.int64)
    phase = np.mod(samples[:, None] * freqs[None, :], length)
    angle = 2.0 * math.pi / length * phase
    return np.concatenate([np.cos(angle), -np.sin(angle)], axis=1).astype(np.float32).astype(jnp.bfloat16)


def inverse_table(length):
    freqs = F0 + np.arange(F, dtype=np.int64)
    shifts = np.arange(LAGS, dtype=np.int64) - LAGS // 2
    phase = np.mod(freqs[:, None] * shifts[None, :], length)
    angle = 2.0 * math.pi / length * phase
    return np.concatenate([np.cos(angle), -np.sin(angle)], axis=0).astype(np.float32).astype(jnp.bfloat16)


def whiten(records, live_mask):
    count, windows, length = records.shape
    spectrum = jnp.dot(
        records.reshape(count * windows, length),
        jnp.asarray(forward_table(length)),
        preferred_element_type=jnp.float32,
    )
    power = jnp.mean(spectrum * spectrum, axis=1, keepdims=True)
    gain = jnp.repeat(live_mask.astype(jnp.float32), windows)[:, None]
    white = spectrum * (gain * lax.rsqrt(power + 1e-06))
    return white.astype(jnp.bfloat16)


def reach_kernel(shape, offsets_ref, white_ref, cross_ref, held, ext, own, swapped, made, back,
                 z_send, z_recv, c_send, c_recv, y_send, y_recv, d_send, d_recv, e_send, r_send, r_recv):
    layers, columns, depth, pieces, windows, fold = shape
    count, slab = white_ref.shape[0], white_ref.shape[1]
    pairs = offsets_ref.shape[0]
    wide = 2 * columns
    total = layers * wide * count
    me = lax.axis_index("chan")
    z, q = me // wide, me % wide
    y, c = q // 2, q % 2
    sibling = me + 1 - 2 * c
    sib_q = q + 1 - 2 * c
    mate = me + 2 - 4 * y
    mate_q = q + 2 - 4 * y
    far_q = sib_q + 2 - 4 * y
    step = count // pieces
    top, lifted = layers - 1, depth + 1

    barrier = pltpu.get_barrier_semaphore()

    def greet(device):
        pl.semaphore_signal(barrier, inc=1, device_id={"chan": device}, device_id_type=pl.DeviceIdType.MESH)

    greet(sibling)
    if columns == 2:
        greet(mate)

    @pl.when(z >= 1)
    def _():
        greet(me - wide)

    @pl.when(z < layers - 1)
    def _():
        greet(me + wide)

    below, above = jnp.minimum(z, 1), jnp.minimum(top - z, 1)
    peers = columns + below + above
    if fold:
        @pl.when(z == 0)
        def _():
            for i in range(wide):
                greet(top * wide + i)

        @pl.when(z == top)
        def _():
            for i in range(wide):
                greet(jnp.int32(i))

        peers = peers + wide * (2 - below - above)
    pl.semaphore_wait(barrier, peers)

    def rows(p):
        return pl.ds(p * step, step)

    def mine(dz, p):
        return white_ref.at[rows(p)] if dz == 0 else held.at[dz * wide + q, rows(p)]

    def copy(source, slot, p, send, recv, device):
        return pltpu.make_async_remote_copy(
            src_ref=source,
            dst_ref=held.at[slot, rows(p)],
            send_sem=send,
            recv_sem=recv,
            device_id={"chan": device},
            device_id_type=pl.DeviceIdType.MESH,
        )

    def down(dz, p):
        return copy(mine(dz, p), (dz + 1) * wide + q, p, z_send.at[dz, p], z_recv.at[dz + 1, p], me - wide)

    def from_above(dz, p):
        return copy(mine(dz, p), dz * wide + q, p, z_send.at[dz, p], z_recv.at[dz, p], me)

    def across(dz, p, slot):
        return copy(mine(dz, p), slot, p, c_send.at[dz, p], c_recv.at[dz, p], sibling)

    def over(dz, p, slot):
        return copy(mine(dz, p), slot, p, y_send.at[dz, p], y_recv.at[dz, p], mate)

    def onward(dz, p, slot):
        return copy(held.at[dz * wide + mate_q, rows(p)], slot, p, d_send.at[dz, p], d_recv.at[dz, p], sibling)

    def both(*conditions):
        joined = conditions[0]
        for condition in conditions[1:]:
            joined = jnp.logical_and(joined, condition)
        return joined

    def exists(dz):
        return z + dz < layers

    def goes(dz, at_start, at_end):
        if dz == lifted:
            return z == top
        if dz == 0:
            return at_start
        if fold and dz == depth:
            return both(exists(dz), at_end)
        return exists(dz)

    def z_tx(dz):
        if fold and dz + 1 == depth:
            return both(exists(dz), z >= 1, jnp.logical_or(z >= 2, q == 0))
        return both(exists(dz), z >= 1)

    def z_rx(dz):
        return goes(dz, None, q == 0)

    def c_tx(dz):
        return goes(dz, c == 1, q == 0)

    def c_rx(dz):
        return goes(dz, c == 0, q == 1)

    def y_tx(dz):
        return goes(dz, y == 1, q == 0)

    def y_rx(dz):
        return goes(dz, y == 0, q == 2)

    def detoured(dz, p):
        return fold and dz == depth - 1 and p == pieces - 1

    def over_tx(dz, p):
        if detoured(dz, p):
            return both(y_tx(dz), jnp.logical_or(z > 0, y == 0))
        if raised(dz, p):
            return both(y_tx(dz), y == 0)
        return y_tx(dz)

    def raised(dz, p):
        return fold and dz == lifted and p >= pieces // 2

    def lift_mate(p):
        return copy(held.at[mate_q, rows(p)], lifted * wide + mate_q, p,
                    e_send.at[lifted, p], y_recv.at[lifted, p], me + top * wide)

    def extra(dz, p):
        return copy(held.at[dz * wide + mate_q, rows(p)], (dz + 1) * wide + mate_q, p,
                    e_send.at[dz, p], y_recv.at[dz + 1, p], me - wide)

    def extra_tx():
        return both(z == 1, y == 0)

    def d_rx(dz):
        return goes(dz, y == 0, q == 3)

    def lift(p):
        return copy(white_ref.at[rows(p)], lifted * wide + q, p, z_send.at[lifted, p], z_recv.at[lifted, p],
                    me + top * wide)

    def sends(dz):
        for p in range(pieces):
            if dz > 0:
                @pl.when(z_rx(dz))
                def _():
                    from_above(dz, p).wait_recv()
            if dz < depth:
                @pl.when(z_tx(dz))
                def _():
                    down(dz, p).start()
            if columns == 2:
                @pl.when(over_tx(dz, p))
                def _():
                    over(dz, p, dz * wide + q).start()
            @pl.when(c_tx(dz))
            def _():
                across(dz, p, dz * wide + q).start()

    def passes(dz):
        if columns == 2:
            for p in range(pieces):
                @pl.when(y_rx(dz))
                def _():
                    over(dz, p, dz * wide + mate_q).wait_recv()
                    onward(dz, p, dz * wide + mate_q).start()
                if dz == 0 and raised(lifted, p):
                    @pl.when(both(z == 0, y == 0))
                    def _():
                        lift_mate(p).start()
                if detoured(dz + 1, p):
                    @pl.when(extra_tx())
                    def _():
                        extra(dz, p).start()

    def arrives(dz):
        for p in range(pieces):
            @pl.when(c_rx(dz))
            def _():
                across(dz, p, dz * wide + sib_q).wait_recv()
            if columns == 2:
                @pl.when(d_rx(dz))
                def _():
                    onward(dz, p, dz * wide + far_q).wait_recv()

    def finishes(dz):
        for p in range(pieces):
            if dz < depth:
                @pl.when(z_tx(dz))
                def _():
                    down(dz, p).wait_send()
            if columns == 2:
                @pl.when(over_tx(dz, p))
                def _():
                    over(dz, p, dz * wide + q).wait_send()
                if detoured(dz + 1, p):
                    @pl.when(extra_tx())
                    def _():
                        extra(dz, p).wait_send()
                @pl.when(y_rx(dz))
                def _():
                    onward(dz, p, dz * wide + mate_q).wait_send()
            @pl.when(c_tx(dz))
            def _():
                across(dz, p, dz * wide + q).wait_send()

    def answer(i):
        return pltpu.make_async_remote_copy(
            src_ref=made.at[i],
            dst_ref=back.at[q],
            send_sem=r_send.at[i],
            recv_sem=r_recv.at[q],
            device_id={"chan": jnp.int32(i)},
            device_id_type=pl.DeviceIdType.MESH,
        )

    def answered(i):
        return pltpu.make_async_remote_copy(
            src_ref=made.at[i],
            dst_ref=back.at[i],
            send_sem=r_send.at[i],
            recv_sem=r_recv.at[i],
            device_id={"chan": me},
            device_id_type=pl.DeviceIdType.MESH,
        )

    low = lax.broadcasted_iota(jnp.int32, (8, LANES), 0) < 4

    def prepare(i, carry):
        raw = white_ref[i]
        value = raw.astype(jnp.float32)
        own[i] = value
        ext[q * count + i] = raw
        for w in range(windows):
            swapped[i, w * 8 : w * 8 + 8] = pltpu.roll(value[w * 8 : w * 8 + 8], 4, 0)
        return carry

    def settle(dz):
        def one(l):
            def fill(i, carry):
                ext[(dz * wide + l) * count + i] = held[dz * wide + l, i]
                return carry
            lax.fori_loop(0, count, fill, 0, unroll=4)

        if dz == 0:
            for l in range(1, wide):
                @pl.when(q < l)
                def _():
                    one(l)
        else:
            @pl.when(exists(dz))
            def _():
                for l in range(1 if fold and dz == depth else wide):
                    one(l)

    live = jnp.minimum(layers * wide - me, pairs)

    def outside():
        def nothing(k, carry):
            for r in range(count):
                cross_ref[r, k] = jnp.zeros((8, LANES), jnp.float32)
            return carry

        lax.fori_loop(live, pairs, nothing, 0)

        @pl.when(layers - z <= depth)
        def _():
            def blank(i, carry):
                ext[(layers - z) * wide * count + i] = jnp.zeros((slab, LANES), jnp.bfloat16)
                return carry

            lax.fori_loop(0, 2 * count, blank, 0, unroll=4)

    def reached(dz):
        if dz < 0:
            return 0
        if dz == depth:
            return live
        return jnp.minimum((dz + 1) * wide - q - 1, live)

    def multiply(dz):
        def pair(k, carry):
            shift = offsets_ref[k]

            def channel(i, inner):
                place = me * count + i + shift
                keep = jnp.where(place < total, 1.0 / windows, 0.0)
                near = jnp.minimum(q * count + i + shift, ext.shape[0] - 1)
                partner = ext[near].astype(jnp.float32)
                straight = own[i, :8] * partner[:8]
                twisted = swapped[i, :8] * partner[:8]
                for w in range(1, windows):
                    part = slice(w * 8, w * 8 + 8)
                    straight += own[i, part] * partner[part]
                    twisted += swapped[i, part] * partner[part]
                joined = jnp.where(
                    low,
                    straight + pltpu.roll(straight, 4, 0),
                    pltpu.roll(twisted, 4, 0) - twisted,
                )
                cross_ref[i, k] = joined * keep
                return inner

            return lax.fori_loop(0, count, channel, carry, unroll=4)

        begin, end = reached(dz - 1), reached(dz)
        if fold and dz == depth:
            @pl.when(z == 0)
            def _():
                lax.fori_loop(begin, begin + 1, pair, 0)

            @pl.when(z > 0)
            def _():
                lax.fori_loop(begin, end, pair, 0)
        else:
            lax.fori_loop(begin, end, pair, 0)

    def reply():
        for i in range(wide):
            shift = offsets_ref[top * wide + q - i]

            def channel(r, carry):
                place = i * count + r + shift
                keep = jnp.where(place < total, 1.0 / windows, 0.0)
                near = jnp.clip(place - top * wide * count, 0, ext.shape[0] - 1)
                partner = ext[near].astype(jnp.float32)
                value = held[lifted * wide + i, r].astype(jnp.float32)
                straight = value[:8] * partner[:8]
                twisted = pltpu.roll(value[:8], 4, 0) * partner[:8]
                for w in range(1, windows):
                    part = slice(w * 8, w * 8 + 8)
                    straight += value[part] * partner[part]
                    twisted += pltpu.roll(value[part], 4, 0) * partner[part]
                joined = jnp.where(
                    low,
                    straight + pltpu.roll(straight, 4, 0),
                    pltpu.roll(twisted, 4, 0) - twisted,
                )
                made[i, r] = (joined * keep).astype(jnp.bfloat16)
                return carry

            lax.fori_loop(0, count, channel, 0, unroll=4)
        for i in range(wide):
            answer(i).start()

    sends(0)
    if fold:
        @pl.when(z == 0)
        def _():
            for p in range(pieces):
                lift(p).start()

    lax.fori_loop(0, count, prepare, 0)
    outside()
    for dz in range(depth + 1):
        if dz < depth:
            sends(dz + 1)
        if fold and dz == 0:
            sends(lifted)
        passes(dz)
        if fold and dz == 0:
            passes(lifted)
        arrives(dz)
        settle(dz)
        if fold and dz == 0:
            arrives(lifted)

            @pl.when(z == top)
            def _():
                reply()

        multiply(dz)

    if fold:
        @pl.when(z == 0)
        def _():
            for i in range(wide):
                answered(i).wait_recv()

                def take(r, carry):
                    cross_ref[r, top * wide - q + i] = back[i, r].astype(jnp.float32)
                    return carry

                lax.fori_loop(0, count, take, 0, unroll=4)
            for p in range(pieces):
                lift(p).wait_send()
                if raised(lifted, p):
                    @pl.when(y == 0)
                    def _():
                        lift_mate(p).wait_send()

        @pl.when(z == top)
        def _():
            for i in range(wide):
                answer(i).wait_send()

        finishes(lifted)
    for dz in range(depth + 1):
        finishes(dz)


def middle_kernel(shape, offsets_hbm, mask_hbm, records_hbm, table_hbm, cross_ref,
                  offsets_ref, mask_ref, records, table, spectrum, scale, white, held, spec, made, back, joined,
                  l_sem, x_send, f_send, s_recv, r_send, r_recv):
    layers, wide, windows = shape
    pairs = offsets_ref.shape[0]
    count = records.shape[0] // windows
    chunks, width = table.shape[0], table.shape[2]
    load = [pltpu.make_async_copy(records_hbm, records, l_sem.at[chunks])]
    for n in range(chunks):
        load.append(pltpu.make_async_copy(table_hbm.at[n], table.at[n], l_sem.at[n]))
    load.append(pltpu.make_async_copy(offsets_hbm, offsets_ref, l_sem.at[chunks + 1]))
    load.append(pltpu.make_async_copy(mask_hbm, mask_ref, l_sem.at[chunks + 2]))
    for one in load:
        one.start()
    parts = layers * wide
    pitch = spec.shape[0] // (2 * windows)
    half, top, last = layers // 2, layers - 1, parts - 1
    me = lax.axis_index("chan")
    z, q = me // wide, me % wide
    c = q % 2
    first = z * wide
    base = half * wide
    sib_q = q + 1 - 2 * c
    mate_q = (q + 2) % wide
    far_q = (sib_q + 2) % wide
    near = c == 0
    inner_low, inner_high = z == half - 1, z == half
    neighbour = jnp.where(
        jnp.logical_or(z == 0, jnp.logical_and(inner_low, c == 1)), me + wide, me - wide)
    own_end = jnp.where(
        z == 0, jnp.where(near, base, wide),
        jnp.where(jnp.logical_and(inner_low, c == 1), base + wide, parts + 1))
    low_begin = jnp.where(
        inner_low, jnp.where(near, base, wide),
        jnp.where(jnp.logical_and(inner_high, c == 1), base + wide, 0))
    low_end = jnp.where(
        inner_low, own_end, jnp.where(jnp.logical_and(inner_high, c == 1), parts + 1, 0))

    barrier = pltpu.get_barrier_semaphore()

    def greet(device, condition):
        @pl.when(condition)
        def _():
            pl.semaphore_signal(barrier, inc=1, device_id={"chan": jnp.int32(device)},
                                device_id_type=pl.DeviceIdType.MESH)

    for col in (sib_q, mate_q, far_q):
        greet(first + col, z >= 0)
    for i in range(wide):
        odd = i % 2 == 1
        greet(wide + i, z == 0)
        if odd:
            greet(base + i, z < half)
        else:
            greet(base + i, jnp.logical_and(inner_low, q == i))
    greet(me - wide, jnp.logical_or(inner_low, jnp.logical_and(inner_high, c == 1)))
    greet(me + wide, inner_high)
    replies_far = jnp.where(inner_low, wide, jnp.where(jnp.logical_and(inner_high, c == 1), 2 * wide - 1, 0))
    ships_there = jnp.where(jnp.logical_and(inner_low, near), 0, 1)

    load[0].wait()
    square = None
    for n in range(chunks):
        load[n + 1].wait()
        part = jnp.dot(records[...], table[n], preferred_element_type=jnp.float32)
        spectrum[:, n * width:(n + 1) * width] = part
        for lane in range(0, width, LANES):
            piece_square = part[:, lane:lane + LANES] * part[:, lane:lane + LANES]
            square = piece_square if square is None else square + piece_square
    power = jnp.sum(square, axis=1, keepdims=True) * (1.0 / (2 * F))
    scale[...] = jnp.broadcast_to(lax.rsqrt(power + 1e-06), scale.shape)

    for one in load[chunks + 1:]:
        one.wait()
    upper = lax.broadcasted_iota(jnp.int32, (2 * windows, LANES), 0) < windows

    def whitening(i, carry):
        rows = pl.ds(pl.multiple_of(i * 2 * windows, 2 * windows), 2 * windows)
        alive = jnp.where(upper, mask_ref[2 * i].astype(jnp.float32), mask_ref[2 * i + 1].astype(jnp.float32))
        gain = alive * scale[rows, :]
        for x in range(2 * wide):
            white[x, rows] = (spectrum[rows, x * LANES:(x + 1) * LANES] * gain).astype(jnp.bfloat16)
        return carry

    lax.fori_loop(0, count // 2, whitening, 0)
    pl.semaphore_wait(barrier, wide - 1 + replies_far + ships_there)

    def remote(source, target, send, recv, device):
        return pltpu.make_async_remote_copy(
            src_ref=source, dst_ref=target, send_sem=send, recv_sem=recv,
            device_id={"chan": device}, device_id_type=pl.DeviceIdType.MESH,
        )

    def piece(ri, col):
        return white.at[ri * wide + col]

    def swap(j, ri, col):
        return remote(piece(ri, col), held.at[me, ri], x_send.at[j, ri], s_recv.at[me, ri], first + col)

    def ship_own(ri):
        return remote(piece(ri, q), held.at[me, ri], f_send.at[me, ri], s_recv.at[me, ri], neighbour)

    def ship(s, ri):
        return remote(held.at[s, ri], held.at[s, ri], f_send.at[s, ri], s_recv.at[s, ri], neighbour)

    def reply(d, k):
        return remote(made.at[d, k], back.at[k, q], r_send.at[d, k], r_recv.at[k, q], d)

    def replied(k, col):
        return remote(back.at[k, col], back.at[k, col], r_send.at[me, k], r_recv.at[k, col], me)

    for ri in range(2):
        ship_own(ri).start()
    columns = (sib_q, mate_q, far_q)
    for j, col in enumerate(columns):
        for ri in range(2):
            swap(j, ri, col).start()

    def settle(s, load):
        for ri in range(2):
            def one(i, carry):
                value = load(ri, i).astype(jnp.float32)
                for part in range(2):
                    row = ri * windows * pitch + s * count + 2 * i + part
                    spec[pl.ds(row, windows, stride=pitch), :] = value[part * windows:(part + 1) * windows]
                return carry

            lax.fori_loop(0, count // 2, one, 0, unroll=4)

    def own_rows(ri, i):
        return white[ri * wide + q, pl.ds(pl.multiple_of(i * 2 * windows, 2 * windows), 2 * windows)]

    def take(s, onward=None):
        for ri in range(2):
            ship(s, ri).wait_recv()
        if onward is not None:
            @pl.when(onward)
            def _():
                for ri in range(2):
                    ship(s, ri).start()
        settle(s, lambda ri, i: held[s, ri, pl.ds(pl.multiple_of(i * 2 * windows, 2 * windows), 2 * windows)])

    def block(d, k):
        shift = offsets_ref[k]
        for g in range(count // 16):
            mine = d * count + g * 16
            real = imag = None
            for w in range(windows):
                cr = spec[pl.ds(pl.multiple_of(w * pitch + mine, 8), 16), :]
                ci = spec[pl.ds(pl.multiple_of((windows + w) * pitch + mine, 8), 16), :]
                pr = spec[pl.ds(w * pitch + mine + shift, 16), :]
                pi = spec[pl.ds((windows + w) * pitch + mine + shift, 16), :]
                re, im = cr * pr + ci * pi, ci * pr - cr * pi
                real, imag = (re, im) if w == 0 else (real + re, imag + im)
            rows = slice(g * 16, g * 16 + 16)
            made[d, k, 0, rows] = (real * (1.0 / windows)).astype(jnp.bfloat16)
            made[d, k, 1, rows] = (imag * (1.0 / windows)).astype(jnp.bfloat16)

    def spans(d_begin, d_end, u_begin, u_end, visit):
        def reach(u, carry):
            def one(d, inner):
                visit(d, u - 1 - d)
                return inner

            return lax.fori_loop(jnp.maximum(d_begin, u - pairs), jnp.minimum(d_end, u), one, carry)

        lax.fori_loop(u_begin, u_end, reach, 0)

    def give(d, k):
        @pl.when(d != me)
        def _():
            reply(d, k).start()

    def gave(d, k):
        @pl.when(d != me)
        def _():
            reply(d, k).wait_send()

    def blocks(*span):
        spans(*span, block)
        spans(*span, give)

    for x in range(2 * windows):
        spec[pl.ds(x * pitch + parts * count, count), :] = jnp.zeros((count, LANES), jnp.float32)

    def clear(i, carry):
        joined[pl.ds(pl.multiple_of(i * 64, 64), 64), :] = jnp.zeros((64, LANES), jnp.float32)
        return carry

    lax.fori_loop(0, joined.shape[0] // 64, clear, 0)

    y = q // 2
    pair_1, pair_2 = (q, sib_q), (mate_q, far_q)

    def reached_1(start, more=0):
        return jnp.where(y == 0, start, start + 3), jnp.where(y == 0, start + 2, start + wide + more)

    def reached_2(start, more=0):
        return jnp.where(y == 0, start + 2, start), jnp.where(y == 0, start + wide + more, start + 3)

    settle(me, own_rows)
    for col in columns:
        take(first + col, z >= 0)
    blocks(first, first + wide, first + 1, first + wide + jnp.where(z == top, 1, 0))

    @pl.when(jnp.logical_and(z == 0, near))
    def _():
        for group, reached in ((pair_1, reached_1), (pair_2, reached_2)):
            for col in group:
                take(wide + col)
            blocks(0, wide, *reached(wide))

    @pl.when(inner_low)
    def _():
        def lower(group):
            for col in group:
                take(col, jnp.logical_not(near))

        lower(pair_1)
        for col in pair_1:
            take(base + col)
        blocks(wide, base, *reached_1(base))
        lower(pair_2)
        blocks(0, wide, *reached_1(base))

        @pl.when(jnp.logical_not(near))
        def _():
            blocks(0, wide, wide, base)
        for col in pair_2:
            take(base + col)
        blocks(0, base, *reached_2(base))

        @pl.when(near)
        def _():
            for group, reached in ((pair_1, reached_1), (pair_2, reached_2)):
                for col in group:
                    take(top * wide + col)
                blocks(0, base, *reached(top * wide, 1))

    @pl.when(inner_high)
    def _():
        for group, reached in ((pair_1, reached_1), (pair_2, reached_2)):
            for col in group:
                take(top * wide + col, near)
            blocks(base, base + wide, *reached(top * wide, 1))

        @pl.when(jnp.logical_not(near))
        def _():
            for col in pair_1 + pair_2:
                take(wide + col)
            for col in pair_1 + pair_2:
                take(col)
            blocks(0, base, top * wide, parts + 1)

    def unpack(source, k, col):
        for ri in range(2):
            for g in range(count // 16):
                value = source[ri, g * 16:g * 16 + 16].astype(jnp.float32)
                for part in range(2):
                    row = (ri * wide + col) * count * pairs + (g * 16 + part * 8) * pairs + k
                    joined[pl.ds(row, 8, stride=pairs), :] = value[part * 8:part * 8 + 8]

    def collect(k, carry):
        away = me + k + 1 >= own_end
        for col in range(wide):
            here = jnp.logical_and(q == col, jnp.logical_not(away))

            @pl.when(here)
            def _():
                unpack(made.at[me, k], k, col)

            @pl.when(jnp.logical_not(here))
            def _():
                replied(k, col).wait_recv()
                unpack(back.at[k, col], k, col)
        return carry

    lax.fori_loop(0, parts - me, collect, 0)

    def pack(i, carry):
        rows = pl.ds(pl.multiple_of(i * 16, 16), 16)
        for x in range(2 * wide):
            start = pl.multiple_of(x * count * pairs + i * 16, 16)
            cross_ref[rows, x * LANES:(x + 1) * LANES] = joined[pl.ds(start, 16), :].astype(jnp.bfloat16)
        return carry

    lax.fori_loop(0, count * pairs // 16, pack, 0, unroll=2)

    for j, col in enumerate(columns):
        for ri in range(2):
            swap(j, ri, col).wait_send()

    def sent(s, carry):
        for ri in range(2):
            ship(s, ri).wait_send()
        return carry

    lax.fori_loop(first, first + wide, sent, 0)

    @pl.when(jnp.logical_or(jnp.logical_and(inner_low, c == 1), jnp.logical_and(inner_high, near)))
    def _():
        begin = jnp.where(inner_low, 0, top * wide)
        lax.fori_loop(begin, begin + wide, sent, 0)

    spans(first, first + wide, first + 1, own_end, gave)
    spans(0, first, low_begin, low_end, gave)


def meet(layers, wide, records, live_mask, offsets):
    pairs = offsets.shape[0]
    count, windows, length = records.shape
    parts = layers * wide
    pitch = (parts + 1) * count
    rows = count * windows
    width = 2 * LANES
    chunks = 2 * F // width
    table = np.ascontiguousarray(forward_table(length).reshape(length, chunks, width).transpose(1, 0, 2))
    return pl.pallas_call(
        functools.partial(middle_kernel, (layers, wide, windows)),
        out_shape=jax.ShapeDtypeStruct((count * pairs, 2 * F), jnp.bfloat16),
        in_specs=[
            pl.BlockSpec(memory_space=pltpu.HBM),
            pl.BlockSpec(memory_space=pltpu.HBM),
            pl.BlockSpec(memory_space=pltpu.HBM),
            pl.BlockSpec(memory_space=pltpu.HBM),
        ],
        out_specs=pl.BlockSpec(memory_space=pltpu.VMEM),
        scratch_shapes=[
            pltpu.SMEM((pairs,), jnp.int32),
            pltpu.SMEM((count,), jnp.int32),
            pltpu.VMEM((rows, length), jnp.bfloat16),
            pltpu.VMEM((chunks, length, width), jnp.bfloat16),
            pltpu.VMEM((rows, 2 * F), jnp.float32),
            pltpu.VMEM((rows, LANES), jnp.float32),
            pltpu.VMEM((2 * wide, rows, LANES), jnp.bfloat16),
            pltpu.VMEM((parts, 2, rows, LANES), jnp.bfloat16),
            pltpu.VMEM((2 * windows * pitch, LANES), jnp.float32),
            pltpu.VMEM((parts, pairs, 2, count, LANES), jnp.bfloat16),
            pltpu.VMEM((pairs, wide, 2, count, LANES), jnp.bfloat16),
            pltpu.VMEM((2 * wide * count * pairs, LANES), jnp.float32),
            pltpu.SemaphoreType.DMA((chunks + 3,)),
            pltpu.SemaphoreType.DMA((wide - 1, 2)),
            pltpu.SemaphoreType.DMA((parts, 2)),
            pltpu.SemaphoreType.DMA((parts, 2)),
            pltpu.SemaphoreType.DMA((parts, pairs)),
            pltpu.SemaphoreType.DMA((pairs, wide)),
        ],
        compiler_params=pltpu.CompilerParams(
            vmem_limit_bytes=36 * 1024 * 1024, collective_id=1, has_side_effects=True
        ),
    )(*[pltpu.with_memory_space_constraint(x, pltpu.HBM) for x in (offsets, live_mask, records.reshape(rows, length), jnp.asarray(table))])


def shards(columns, records, live_mask, offsets):
    count, windows, length = records.shape
    pairs = offsets.shape[0]
    wide = 2 * columns
    layers = lax.axis_size("chan") // wide
    reach = (BAND + count - 2) // count
    depth = min(layers - 1, (wide - 1 + reach) // wide)
    pieces = PIECES
    fold = columns == 2 and depth == layers - 1 and depth >= 2 and layers * wide == pairs and pairs * count == BAND
    if (
        columns == 2 and layers == 4 and layers * wide == pairs and pairs * count == BAND
        and F == wide * LANES and windows == 8 and count % 16 == 0
    ):
        cross = meet(layers, wide, records, live_mask, offsets)
        return lags(cross, count, pairs, length)
    spectra = whiten(records, live_mask).reshape(count, windows * 8, LANES)
    slots = (depth + 1) * wide
    cross = pl.pallas_call(
        functools.partial(reach_kernel, (layers, columns, depth, pieces, windows, fold)),
        out_shape=jax.ShapeDtypeStruct((count, pairs, 8, LANES), jnp.float32),
        in_specs=[
            pl.BlockSpec(memory_space=pltpu.SMEM),
            pl.BlockSpec(memory_space=pltpu.VMEM),
        ],
        out_specs=pl.BlockSpec(memory_space=pltpu.VMEM),
        scratch_shapes=[
            pltpu.VMEM((slots + wide, count, windows * 8, LANES), jnp.bfloat16),
            pltpu.VMEM((slots * count, windows * 8, LANES), jnp.bfloat16),
            pltpu.VMEM((count, windows * 8, LANES), jnp.float32),
            pltpu.VMEM((count, windows * 8, LANES), jnp.float32),
            pltpu.VMEM((wide, count, 8, LANES), jnp.bfloat16),
            pltpu.VMEM((wide, count, 8, LANES), jnp.bfloat16),
        ]
        + [pltpu.SemaphoreType.DMA((depth + 2, pieces))] * 9
        + [pltpu.SemaphoreType.DMA((wide,))] * 2,
        compiler_params=pltpu.CompilerParams(
            vmem_limit_bytes=40 * 1024 * 1024, collective_id=0, has_side_effects=True
        ),
    )(offsets, spectra)
    return lags(cross.astype(jnp.bfloat16).reshape(count * pairs, 8 * LANES), count, pairs, length)


def lags(cross, count, pairs, length):
    result = jnp.dot(cross, jnp.asarray(inverse_table(length)), preferred_element_type=jnp.float32)
    result = result * (1.0 / math.sqrt(F))
    return result.reshape(count, pairs, LAGS).astype(jnp.bfloat16)


def solution(mesh):
    in_specs = (P(("day", "chan"), None, None), P(("day", "chan")), P())
    out_specs = P(("day", "chan"), None, None)
    columns = max(1, LAYER_CHIPS // mesh.shape["day"])
    body = functools.partial(shards, columns)
    return jax.shard_map(body, mesh=mesh, in_specs=in_specs, out_specs=out_specs, check_vma=False)
```

```python
import functools
import math

import jax
import jax.numpy as jnp
import numpy as np
from jax import lax
from jax.experimental import pallas as pl
from jax.experimental.pallas import tpu as pltpu
from jax.sharding import PartitionSpec as P

F = 512
F0 = 6
LAGS = 2048
LANES = 128
BAND = 512
PIECES = 4
LAYER_CHIPS = 4


def forward_table(length):
    samples = np.arange(length, dtype=np.int64)
    freqs = F0 + np.arange(F, dtype=np.int64)
    phase = np.mod(samples[:, None] * freqs[None, :], length)
    angle = 2.0 * math.pi / length * phase
    return np.concatenate([np.cos(angle), -np.sin(angle)], axis=1).astype(np.float32).astype(jnp.bfloat16)


def inverse_table(length):
    freqs = F0 + np.arange(F, dtype=np.int64)
    shifts = np.arange(LAGS, dtype=np.int64) - LAGS // 2
    phase = np.mod(freqs[:, None] * shifts[None, :], length)
    angle = 2.0 * math.pi / length * phase
    return np.concatenate([np.cos(angle), -np.sin(angle)], axis=0).astype(np.float32).astype(jnp.bfloat16)


def whiten(records, live_mask):
    count, windows, length = records.shape
    spectrum = jnp.dot(
        records.reshape(count * windows, length),
        jnp.asarray(forward_table(length)),
        preferred_element_type=jnp.float32,
    )
    power = jnp.mean(spectrum * spectrum, axis=1, keepdims=True)
    gain = jnp.repeat(live_mask.astype(jnp.float32), windows)[:, None]
    white = spectrum * (gain * lax.rsqrt(power + 1e-06))
    return white.astype(jnp.bfloat16)


def reach_kernel(shape, offsets_ref, white_ref, cross_ref, held, ext, own, swapped, made, back,
                 z_send, z_recv, c_send, c_recv, y_send, y_recv, d_send, d_recv, e_send, r_send, r_recv):
    layers, columns, depth, pieces, windows, fold = shape
    count, slab = white_ref.shape[0], white_ref.shape[1]
    pairs = offsets_ref.shape[0]
    wide = 2 * columns
    total = layers * wide * count
    me = lax.axis_index("chan")
    z, q = me // wide, me % wide
    y, c = q // 2, q % 2
    sibling = me + 1 - 2 * c
    sib_q = q + 1 - 2 * c
    mate = me + 2 - 4 * y
    mate_q = q + 2 - 4 * y
    far_q = sib_q + 2 - 4 * y
    step = count // pieces
    top, lifted = layers - 1, depth + 1

    barrier = pltpu.get_barrier_semaphore()

    def greet(device):
        pl.semaphore_signal(barrier, inc=1, device_id={"chan": device}, device_id_type=pl.DeviceIdType.MESH)

    greet(sibling)
    if columns == 2:
        greet(mate)

    @pl.when(z >= 1)
    def _():
        greet(me - wide)

    @pl.when(z < layers - 1)
    def _():
        greet(me + wide)

    below, above = jnp.minimum(z, 1), jnp.minimum(top - z, 1)
    peers = columns + below + above
    if fold:
        @pl.when(z == 0)
        def _():
            for i in range(wide):
                greet(top * wide + i)

        @pl.when(z == top)
        def _():
            for i in range(wide):
                greet(jnp.int32(i))

        peers = peers + wide * (2 - below - above)
    pl.semaphore_wait(barrier, peers)

    def rows(p):
        return pl.ds(p * step, step)

    def mine(dz, p):
        return white_ref.at[rows(p)] if dz == 0 else held.at[dz * wide + q, rows(p)]

    def copy(source, slot, p, send, recv, device):
        return pltpu.make_async_remote_copy(
            src_ref=source,
            dst_ref=held.at[slot, rows(p)],
            send_sem=send,
            recv_sem=recv,
            device_id={"chan": device},
            device_id_type=pl.DeviceIdType.MESH,
        )

    def down(dz, p):
        return copy(mine(dz, p), (dz + 1) * wide + q, p, z_send.at[dz, p], z_recv.at[dz + 1, p], me - wide)

    def from_above(dz, p):
        return copy(mine(dz, p), dz * wide + q, p, z_send.at[dz, p], z_recv.at[dz, p], me)

    def across(dz, p, slot):
        return copy(mine(dz, p), slot, p, c_send.at[dz, p], c_recv.at[dz, p], sibling)

    def over(dz, p, slot):
        return copy(mine(dz, p), slot, p, y_send.at[dz, p], y_recv.at[dz, p], mate)

    def onward(dz, p, slot):
        return copy(held.at[dz * wide + mate_q, rows(p)], slot, p, d_send.at[dz, p], d_recv.at[dz, p], sibling)

    def both(*conditions):
        joined = conditions[0]
        for condition in conditions[1:]:
            joined = jnp.logical_and(joined, condition)
        return joined

    def exists(dz):
        return z + dz < layers

    def goes(dz, at_start, at_end):
        if dz == lifted:
            return z == top
        if dz == 0:
            return at_start
        if fold and dz == depth:
            return both(exists(dz), at_end)
        return exists(dz)

    def z_tx(dz):
        if fold and dz + 1 == depth:
            return both(exists(dz), z >= 1, jnp.logical_or(z >= 2, q == 0))
        return both(exists(dz), z >= 1)

    def z_rx(dz):
        return goes(dz, None, q == 0)

    def c_tx(dz):
        return goes(dz, c == 1, q == 0)

    def c_rx(dz):
        return goes(dz, c == 0, q == 1)

    def y_tx(dz):
        return goes(dz, y == 1, q == 0)

    def y_rx(dz):
        return goes(dz, y == 0, q == 2)

    def detoured(dz, p):
        return fold and dz == depth - 1 and p == pieces - 1

    def over_tx(dz, p):
        if detoured(dz, p):
            return both(y_tx(dz), jnp.logical_or(z > 0, y == 0))
        if raised(dz, p):
            return both(y_tx(dz), y == 0)
        return y_tx(dz)

    def raised(dz, p):
        return fold and dz == lifted and p >= pieces // 2

    def lift_mate(p):
        return copy(held.at[mate_q, rows(p)], lifted * wide + mate_q, p,
                    e_send.at[lifted, p], y_recv.at[lifted, p], me + top * wide)

    def extra(dz, p):
        return copy(held.at[dz * wide + mate_q, rows(p)], (dz + 1) * wide + mate_q, p,
                    e_send.at[dz, p], y_recv.at[dz + 1, p], me - wide)

    def extra_tx():
        return both(z == 1, y == 0)

    def d_rx(dz):
        return goes(dz, y == 0, q == 3)

    def lift(p):
        return copy(white_ref.at[rows(p)], lifted * wide + q, p, z_send.at[lifted, p], z_recv.at[lifted, p],
                    me + top * wide)

    def sends(dz):
        for p in range(pieces):
            if dz > 0:
                @pl.when(z_rx(dz))
                def _():
                    from_above(dz, p).wait_recv()
            if dz < depth:
                @pl.when(z_tx(dz))
                def _():
                    down(dz, p).start()
            if columns == 2:
                @pl.when(over_tx(dz, p))
                def _():
                    over(dz, p, dz * wide + q).start()
            @pl.when(c_tx(dz))
            def _():
                across(dz, p, dz * wide + q).start()

    def passes(dz):
        if columns == 2:
            for p in range(pieces):
                @pl.when(y_rx(dz))
                def _():
                    over(dz, p, dz * wide + mate_q).wait_recv()
                    onward(dz, p, dz * wide + mate_q).start()
                if dz == 0 and raised(lifted, p):
                    @pl.when(both(z == 0, y == 0))
                    def _():
                        lift_mate(p).start()
                if detoured(dz + 1, p):
                    @pl.when(extra_tx())
                    def _():
                        extra(dz, p).start()

    def arrives(dz):
        for p in range(pieces):
            @pl.when(c_rx(dz))
            def _():
                across(dz, p, dz * wide + sib_q).wait_recv()
            if columns == 2:
                @pl.when(d_rx(dz))
                def _():
                    onward(dz, p, dz * wide + far_q).wait_recv()

    def finishes(dz):
        for p in range(pieces):
            if dz < depth:
                @pl.when(z_tx(dz))
                def _():
                    down(dz, p).wait_send()
            if columns == 2:
                @pl.when(over_tx(dz, p))
                def _():
                    over(dz, p, dz * wide + q).wait_send()
                if detoured(dz + 1, p):
                    @pl.when(extra_tx())
                    def _():
                        extra(dz, p).wait_send()
                @pl.when(y_rx(dz))
                def _():
                    onward(dz, p, dz * wide + mate_q).wait_send()
            @pl.when(c_tx(dz))
            def _():
                across(dz, p, dz * wide + q).wait_send()

    def answer(i):
        return pltpu.make_async_remote_copy(
            src_ref=made.at[i],
            dst_ref=back.at[q],
            send_sem=r_send.at[i],
            recv_sem=r_recv.at[q],
            device_id={"chan": jnp.int32(i)},
            device_id_type=pl.DeviceIdType.MESH,
        )

    def answered(i):
        return pltpu.make_async_remote_copy(
            src_ref=made.at[i],
            dst_ref=back.at[i],
            send_sem=r_send.at[i],
            recv_sem=r_recv.at[i],
            device_id={"chan": me},
            device_id_type=pl.DeviceIdType.MESH,
        )

    low = lax.broadcasted_iota(jnp.int32, (8, LANES), 0) < 4

    def prepare(i, carry):
        raw = white_ref[i]
        value = raw.astype(jnp.float32)
        own[i] = value
        ext[q * count + i] = raw
        for w in range(windows):
            swapped[i, w * 8 : w * 8 + 8] = pltpu.roll(value[w * 8 : w * 8 + 8], 4, 0)
        return carry

    def settle(dz):
        def one(l):
            def fill(i, carry):
                ext[(dz * wide + l) * count + i] = held[dz * wide + l, i]
                return carry
            lax.fori_loop(0, count, fill, 0, unroll=4)

        if dz == 0:
            for l in range(1, wide):
                @pl.when(q < l)
                def _():
                    one(l)
        else:
            @pl.when(exists(dz))
            def _():
                for l in range(1 if fold and dz == depth else wide):
                    one(l)

    live = jnp.minimum(layers * wide - me, pairs)

    def outside():
        def nothing(k, carry):
            for r in range(count):
                cross_ref[r, k] = jnp.zeros((8, LANES), jnp.float32)
            return carry

        lax.fori_loop(live, pairs, nothing, 0)

        @pl.when(layers - z <= depth)
        def _():
            def blank(i, carry):
                ext[(layers - z) * wide * count + i] = jnp.zeros((slab, LANES), jnp.bfloat16)
                return carry

            lax.fori_loop(0, 2 * count, blank, 0, unroll=4)

    def reached(dz):
        if dz < 0:
            return 0
        if dz == depth:
            return live
        return jnp.minimum((dz + 1) * wide - q - 1, live)

    def multiply(dz):
        def pair(k, carry):
            shift = offsets_ref[k]

            def channel(i, inner):
                place = me * count + i + shift
                keep = jnp.where(place < total, 1.0 / windows, 0.0)
                near = jnp.minimum(q * count + i + shift, ext.shape[0] - 1)
                partner = ext[near].astype(jnp.float32)
                straight = own[i, :8] * partner[:8]
                twisted = swapped[i, :8] * partner[:8]
                for w in range(1, windows):
                    part = slice(w * 8, w * 8 + 8)
                    straight += own[i, part] * partner[part]
                    twisted += swapped[i, part] * partner[part]
                joined = jnp.where(
                    low,
                    straight + pltpu.roll(straight, 4, 0),
                    pltpu.roll(twisted, 4, 0) - twisted,
                )
                cross_ref[i, k] = joined * keep
                return inner

            return lax.fori_loop(0, count, channel, carry, unroll=4)

        begin, end = reached(dz - 1), reached(dz)
        if fold and dz == depth:
            @pl.when(z == 0)
            def _():
                lax.fori_loop(begin, begin + 1, pair, 0)

            @pl.when(z > 0)
            def _():
                lax.fori_loop(begin, end, pair, 0)
        else:
            lax.fori_loop(begin, end, pair, 0)

    def reply():
        for i in range(wide):
            shift = offsets_ref[top * wide + q - i]

            def channel(r, carry):
                place = i * count + r + shift
                keep = jnp.where(place < total, 1.0 / windows, 0.0)
                near = jnp.clip(place - top * wide * count, 0, ext.shape[0] - 1)
                partner = ext[near].astype(jnp.float32)
                value = held[lifted * wide + i, r].astype(jnp.float32)
                straight = value[:8] * partner[:8]
                twisted = pltpu.roll(value[:8], 4, 0) * partner[:8]
                for w in range(1, windows):
                    part = slice(w * 8, w * 8 + 8)
                    straight += value[part] * partner[part]
                    twisted += pltpu.roll(value[part], 4, 0) * partner[part]
                joined = jnp.where(
                    low,
                    straight + pltpu.roll(straight, 4, 0),
                    pltpu.roll(twisted, 4, 0) - twisted,
                )
                made[i, r] = (joined * keep).astype(jnp.bfloat16)
                return carry

            lax.fori_loop(0, count, channel, 0, unroll=4)
        for i in range(wide):
            answer(i).start()

    sends(0)
    if fold:
        @pl.when(z == 0)
        def _():
            for p in range(pieces):
                lift(p).start()

    lax.fori_loop(0, count, prepare, 0)
    outside()
    for dz in range(depth + 1):
        if dz < depth:
            sends(dz + 1)
        if fold and dz == 0:
            sends(lifted)
        passes(dz)
        if fold and dz == 0:
            passes(lifted)
        arrives(dz)
        settle(dz)
        if fold and dz == 0:
            arrives(lifted)

            @pl.when(z == top)
            def _():
                reply()

        multiply(dz)

    if fold:
        @pl.when(z == 0)
        def _():
            for i in range(wide):
                answered(i).wait_recv()

                def take(r, carry):
                    cross_ref[r, top * wide - q + i] = back[i, r].astype(jnp.float32)
                    return carry

                lax.fori_loop(0, count, take, 0, unroll=4)
            for p in range(pieces):
                lift(p).wait_send()
                if raised(lifted, p):
                    @pl.when(y == 0)
                    def _():
                        lift_mate(p).wait_send()

        @pl.when(z == top)
        def _():
            for i in range(wide):
                answer(i).wait_send()

        finishes(lifted)
    for dz in range(depth + 1):
        finishes(dz)


def middle_kernel(shape, offsets_hbm, mask_hbm, records_hbm, table_hbm, cross_ref,
                  offsets_ref, mask_ref, records, table, spectrum, scale, white, held, spec, made, back, joined,
                  l_sem, x_send, f_send, g_send, s_recv, r_send, r_recv):
    layers, wide, windows = shape
    pairs = offsets_ref.shape[0]
    count = records.shape[0] // windows
    chunks, width = table.shape[0], table.shape[2]
    load = [pltpu.make_async_copy(records_hbm, records, l_sem.at[chunks])]
    for n in range(chunks):
        load.append(pltpu.make_async_copy(table_hbm.at[n], table.at[n], l_sem.at[n]))
    load.append(pltpu.make_async_copy(offsets_hbm, offsets_ref, l_sem.at[chunks + 1]))
    load.append(pltpu.make_async_copy(mask_hbm, mask_ref, l_sem.at[chunks + 2]))
    for one in load:
        one.start()
    parts = layers * wide
    pitch = spec.shape[0] // (2 * windows)
    half, top, last = layers // 2, layers - 1, parts - 1
    me = lax.axis_index("chan")
    z, q = me // wide, me % wide
    c = q % 2
    first = z * wide
    base = half * wide
    sib_q = q + 1 - 2 * c
    mate_q = (q + 2) % wide
    far_q = (sib_q + 2) % wide
    near = c == 0
    inner_low, inner_high = z == half - 1, z == half
    neighbour = jnp.where(
        jnp.logical_or(z == 0, jnp.logical_and(inner_low, c == 1)), me + wide, me - wide)
    own_end = jnp.where(
        z == 0, base, jnp.where(jnp.logical_and(inner_low, c == 1), base + wide, parts + 1))
    low_begin = jnp.where(
        inner_low, base, jnp.where(jnp.logical_and(inner_high, c == 1), base + wide, 0))
    low_end = jnp.where(
        inner_low, own_end, jnp.where(jnp.logical_and(inner_high, c == 1), parts + 1, 0))

    barrier = pltpu.get_barrier_semaphore()

    def greet(device, condition):
        @pl.when(condition)
        def _():
            pl.semaphore_signal(barrier, inc=1, device_id={"chan": jnp.int32(device)},
                                device_id_type=pl.DeviceIdType.MESH)

    for col in (sib_q, mate_q, far_q):
        greet(first + col, z >= 0)
    for i in range(wide):
        odd = i % 2 == 1
        greet(wide + i, z == 0)
        if odd:
            greet(base + i, z < half)
        else:
            greet(base + i, jnp.logical_and(inner_low, q == i))
    greet(me - wide, jnp.logical_or(inner_low, jnp.logical_and(inner_high, c == 1)))
    greet(me + wide, inner_high)
    replies_far = jnp.where(inner_low, wide, jnp.where(jnp.logical_and(inner_high, c == 1), 2 * wide - 1, 0))
    ships_there = jnp.where(jnp.logical_and(inner_low, near), 0, 1)

    load[0].wait()
    square = None
    for n in range(chunks):
        load[n + 1].wait()
        part = jnp.dot(records[...], table[n], preferred_element_type=jnp.float32)
        spectrum[:, n * width:(n + 1) * width] = part
        for lane in range(0, width, LANES):
            piece_square = part[:, lane:lane + LANES] * part[:, lane:lane + LANES]
            square = piece_square if square is None else square + piece_square
    power = jnp.sum(square, axis=1, keepdims=True) * (1.0 / (2 * F))
    scale[...] = jnp.broadcast_to(lax.rsqrt(power + 1e-06), scale.shape)

    for one in load[chunks + 1:]:
        one.wait()
    upper = lax.broadcasted_iota(jnp.int32, (2 * windows, LANES), 0) < windows

    def whitening(i, carry):
        rows = pl.ds(pl.multiple_of(i * 2 * windows, 2 * windows), 2 * windows)
        alive = jnp.where(upper, mask_ref[2 * i].astype(jnp.float32), mask_ref[2 * i + 1].astype(jnp.float32))
        gain = alive * scale[rows, :]
        for x in range(2 * wide):
            white[x, rows] = (spectrum[rows, x * LANES:(x + 1) * LANES] * gain).astype(jnp.bfloat16)
        return carry

    lax.fori_loop(0, count // 2, whitening, 0)
    pl.semaphore_wait(barrier, wide - 1 + replies_far + ships_there)

    def remote(source, target, send, recv, device):
        return pltpu.make_async_remote_copy(
            src_ref=source, dst_ref=target, send_sem=send, recv_sem=recv,
            device_id={"chan": device}, device_id_type=pl.DeviceIdType.MESH,
        )

    def piece(ri, col):
        return white.at[ri * wide + col]

    def swap(j, ri, col):
        return remote(piece(ri, col), held.at[me, ri], x_send.at[j, ri], s_recv.at[me, ri], first + col)

    def ship_own(ri):
        return remote(piece(ri, q), held.at[me, ri], f_send.at[me, ri], s_recv.at[me, ri], neighbour)

    def ship(s, ri):
        return remote(held.at[s, ri], held.at[s, ri], f_send.at[s, ri], s_recv.at[s, ri], neighbour)

    both_ways = jnp.logical_and(inner_low, c == 1)

    def drop(s, ri, source):
        return remote(source, held.at[s, ri], g_send.at[s, ri], s_recv.at[s, ri], me - wide)

    def reply(d, k):
        return remote(made.at[d, k], back.at[k, q], r_send.at[d, k], r_recv.at[k, q], d)

    def replied(k, col):
        return remote(back.at[k, col], back.at[k, col], r_send.at[me, k], r_recv.at[k, col], me)

    for ri in range(2):
        ship_own(ri).start()

    @pl.when(both_ways)
    def _():
        for ri in range(2):
            drop(me, ri, piece(ri, q)).start()
    columns = (sib_q, mate_q, far_q)
    for j, col in enumerate(columns):
        for ri in range(2):
            swap(j, ri, col).start()

    def settle(s, load):
        for ri in range(2):
            def one(i, carry):
                value = load(ri, i).astype(jnp.float32)
                for part in range(2):
                    row = ri * windows * pitch + s * count + 2 * i + part
                    spec[pl.ds(row, windows, stride=pitch), :] = value[part * windows:(part + 1) * windows]
                return carry

            lax.fori_loop(0, count // 2, one, 0, unroll=4)

    def own_rows(ri, i):
        return white[ri * wide + q, pl.ds(pl.multiple_of(i * 2 * windows, 2 * windows), 2 * windows)]

    def take(s, onward=None, downward=None):
        for ri in range(2):
            ship(s, ri).wait_recv()
        if onward is not None:
            @pl.when(onward)
            def _():
                for ri in range(2):
                    ship(s, ri).start()
        if downward is not None:
            @pl.when(downward)
            def _():
                for ri in range(2):
                    drop(s, ri, held.at[s, ri]).start()
        settle(s, lambda ri, i: held[s, ri, pl.ds(pl.multiple_of(i * 2 * windows, 2 * windows), 2 * windows)])

    def block(d, k):
        shift = offsets_ref[k]
        for g in range(count // 16):
            mine = d * count + g * 16
            real = imag = None
            for w in range(windows):
                cr = spec[pl.ds(pl.multiple_of(w * pitch + mine, 8), 16), :]
                ci = spec[pl.ds(pl.multiple_of((windows + w) * pitch + mine, 8), 16), :]
                pr = spec[pl.ds(w * pitch + mine + shift, 16), :]
                pi = spec[pl.ds((windows + w) * pitch + mine + shift, 16), :]
                re, im = cr * pr + ci * pi, ci * pr - cr * pi
                real, imag = (re, im) if w == 0 else (real + re, imag + im)
            rows = slice(g * 16, g * 16 + 16)
            made[d, k, 0, rows] = (real * (1.0 / windows)).astype(jnp.bfloat16)
            made[d, k, 1, rows] = (imag * (1.0 / windows)).astype(jnp.bfloat16)

    def spans(d_begin, d_end, u_begin, u_end, visit):
        def reach(u, carry):
            def one(d, inner):
                visit(d, u - 1 - d)
                return inner

            return lax.fori_loop(jnp.maximum(d_begin, u - pairs), jnp.minimum(d_end, u), one, carry)

        lax.fori_loop(u_begin, u_end, reach, 0)

    def give(d, k):
        @pl.when(d != me)
        def _():
            reply(d, k).start()

    def gave(d, k):
        @pl.when(d != me)
        def _():
            reply(d, k).wait_send()

    def blocks(*span):
        spans(*span, block)
        spans(*span, give)

    for x in range(2 * windows):
        spec[pl.ds(x * pitch + parts * count, count), :] = jnp.zeros((count, LANES), jnp.float32)

    def clear(i, carry):
        joined[pl.ds(pl.multiple_of(i * 64, 64), 64), :] = jnp.zeros((64, LANES), jnp.float32)
        return carry

    lax.fori_loop(0, joined.shape[0] // 64, clear, 0)

    y = q // 2
    pair_1, pair_2 = (q, sib_q), (mate_q, far_q)

    def reached_1(start, more=0):
        return jnp.where(y == 0, start, start + 3), jnp.where(y == 0, start + 2, start + wide + more)

    def reached_2(start, more=0):
        return jnp.where(y == 0, start + 2, start), jnp.where(y == 0, start + wide + more, start + 3)

    settle(me, own_rows)
    for col in columns:
        take(first + col, z >= 0, both_ways)
    blocks(first, first + wide, first + 1, first + wide + jnp.where(z == top, 1, 0))

    @pl.when(z == 0)
    def _():
        for group, reached in ((pair_1, reached_1), (pair_2, reached_2)):
            for col in group:
                take(wide + col)
            blocks(0, wide, *reached(wide))

    @pl.when(inner_low)
    def _():
        def lower(group):
            for col in group:
                take(col, jnp.logical_not(near))

        lower(pair_1)
        for col in pair_1:
            take(base + col)
        blocks(2 * y, 2 * y + 2, *reached_1(base))
        blocks(wide, base, *reached_1(base))
        lower(pair_2)
        blocks(2 - 2 * y, wide - 2 * y, *reached_1(base))
        for col in pair_2:
            take(base + col)
        blocks(0, base, *reached_2(base))

        @pl.when(near)
        def _():
            for group, reached in ((pair_1, reached_1), (pair_2, reached_2)):
                for col in group:
                    take(top * wide + col)
                blocks(0, base, *reached(top * wide, 1))

    @pl.when(inner_high)
    def _():
        for group, reached in ((pair_1, reached_1), (pair_2, reached_2)):
            for col in group:
                take(top * wide + col, near)
            blocks(base, base + wide, *reached(top * wide, 1))

        @pl.when(jnp.logical_not(near))
        def _():
            for col in pair_1 + pair_2:
                take(wide + col)
            spans(wide, base, top * wide, parts + 1, block)
            for col in pair_1:
                take(col)
            blocks(2 * y, 2 * y + 2, top * wide, parts + 1)
            for col in pair_2:
                take(col)
            blocks(2 - 2 * y, wide - 2 * y, top * wide, parts + 1)
            spans(wide, base, top * wide, parts + 1, give)

    def unpack(source, k, col):
        for ri in range(2):
            for g in range(count // 16):
                value = source[ri, g * 16:g * 16 + 16].astype(jnp.float32)
                for part in range(2):
                    row = (ri * wide + col) * count * pairs + (g * 16 + part * 8) * pairs + k
                    joined[pl.ds(row, 8, stride=pairs), :] = value[part * 8:part * 8 + 8]

    def collect(k, carry):
        away = me + k + 1 >= own_end
        for col in range(wide):
            here = jnp.logical_and(q == col, jnp.logical_not(away))

            @pl.when(here)
            def _():
                unpack(made.at[me, k], k, col)

            @pl.when(jnp.logical_not(here))
            def _():
                replied(k, col).wait_recv()
                unpack(back.at[k, col], k, col)
        return carry

    lax.fori_loop(0, parts - me, collect, 0)

    def pack(i, carry):
        rows = pl.ds(pl.multiple_of(i * 16, 16), 16)
        for x in range(2 * wide):
            start = pl.multiple_of(x * count * pairs + i * 16, 16)
            cross_ref[rows, x * LANES:(x + 1) * LANES] = joined[pl.ds(start, 16), :].astype(jnp.bfloat16)
        return carry

    lax.fori_loop(0, count * pairs // 16, pack, 0, unroll=2)

    for j, col in enumerate(columns):
        for ri in range(2):
            swap(j, ri, col).wait_send()

    def sent(s, carry):
        for ri in range(2):
            ship(s, ri).wait_send()
        return carry

    lax.fori_loop(first, first + wide, sent, 0)

    @pl.when(both_ways)
    def _():
        def dropped(s, carry):
            for ri in range(2):
                drop(s, ri, held.at[s, ri]).wait_send()
            return carry

        lax.fori_loop(first, first + wide, dropped, 0)

    @pl.when(jnp.logical_or(jnp.logical_and(inner_low, c == 1), jnp.logical_and(inner_high, near)))
    def _():
        begin = jnp.where(inner_low, 0, top * wide)
        lax.fori_loop(begin, begin + wide, sent, 0)

    spans(first, first + wide, first + 1, own_end, gave)
    spans(0, first, low_begin, low_end, gave)


def meet(layers, wide, records, live_mask, offsets):
    pairs = offsets.shape[0]
    count, windows, length = records.shape
    parts = layers * wide
    pitch = (parts + 1) * count
    rows = count * windows
    width = 2 * LANES
    chunks = 2 * F // width
    table = np.ascontiguousarray(forward_table(length).reshape(length, chunks, width).transpose(1, 0, 2))
    return pl.pallas_call(
        functools.partial(middle_kernel, (layers, wide, windows)),
        out_shape=jax.ShapeDtypeStruct((count * pairs, 2 * F), jnp.bfloat16),
        in_specs=[
            pl.BlockSpec(memory_space=pltpu.HBM),
            pl.BlockSpec(memory_space=pltpu.HBM),
            pl.BlockSpec(memory_space=pltpu.HBM),
            pl.BlockSpec(memory_space=pltpu.HBM),
        ],
        out_specs=pl.BlockSpec(memory_space=pltpu.VMEM),
        scratch_shapes=[
            pltpu.SMEM((pairs,), jnp.int32),
            pltpu.SMEM((count,), jnp.int32),
            pltpu.VMEM((rows, length), jnp.bfloat16),
            pltpu.VMEM((chunks, length, width), jnp.bfloat16),
            pltpu.VMEM((rows, 2 * F), jnp.float32),
            pltpu.VMEM((rows, LANES), jnp.float32),
            pltpu.VMEM((2 * wide, rows, LANES), jnp.bfloat16),
            pltpu.VMEM((parts, 2, rows, LANES), jnp.bfloat16),
            pltpu.VMEM((2 * windows * pitch, LANES), jnp.float32),
            pltpu.VMEM((parts, pairs, 2, count, LANES), jnp.bfloat16),
            pltpu.VMEM((pairs, wide, 2, count, LANES), jnp.bfloat16),
            pltpu.VMEM((2 * wide * count * pairs, LANES), jnp.float32),
            pltpu.SemaphoreType.DMA((chunks + 3,)),
            pltpu.SemaphoreType.DMA((wide - 1, 2)),
            pltpu.SemaphoreType.DMA((parts, 2)),
            pltpu.SemaphoreType.DMA((parts, 2)),
            pltpu.SemaphoreType.DMA((parts, 2)),
            pltpu.SemaphoreType.DMA((parts, pairs)),
            pltpu.SemaphoreType.DMA((pairs, wide)),
        ],
        compiler_params=pltpu.CompilerParams(
            vmem_limit_bytes=36 * 1024 * 1024, collective_id=1, has_side_effects=True
        ),
    )(*[pltpu.with_memory_space_constraint(x, pltpu.HBM) for x in (offsets, live_mask, records.reshape(rows, length), jnp.asarray(table))])


def shards(columns, records, live_mask, offsets):
    count, windows, length = records.shape
    pairs = offsets.shape[0]
    wide = 2 * columns
    layers = lax.axis_size("chan") // wide
    reach = (BAND + count - 2) // count
    depth = min(layers - 1, (wide - 1 + reach) // wide)
    pieces = PIECES
    fold = columns == 2 and depth == layers - 1 and depth >= 2 and layers * wide == pairs and pairs * count == BAND
    if (
        columns == 2 and layers == 4 and layers * wide == pairs and pairs * count == BAND
        and F == wide * LANES and windows == 8 and count % 16 == 0
    ):
        cross = meet(layers, wide, records, live_mask, offsets)
        return lags(cross, count, pairs, length)
    spectra = whiten(records, live_mask).reshape(count, windows * 8, LANES)
    slots = (depth + 1) * wide
    cross = pl.pallas_call(
        functools.partial(reach_kernel, (layers, columns, depth, pieces, windows, fold)),
        out_shape=jax.ShapeDtypeStruct((count, pairs, 8, LANES), jnp.float32),
        in_specs=[
            pl.BlockSpec(memory_space=pltpu.SMEM),
            pl.BlockSpec(memory_space=pltpu.VMEM),
        ],
        out_specs=pl.BlockSpec(memory_space=pltpu.VMEM),
        scratch_shapes=[
            pltpu.VMEM((slots + wide, count, windows * 8, LANES), jnp.bfloat16),
            pltpu.VMEM((slots * count, windows * 8, LANES), jnp.bfloat16),
            pltpu.VMEM((count, windows * 8, LANES), jnp.float32),
            pltpu.VMEM((count, windows * 8, LANES), jnp.float32),
            pltpu.VMEM((wide, count, 8, LANES), jnp.bfloat16),
            pltpu.VMEM((wide, count, 8, LANES), jnp.bfloat16),
        ]
        + [pltpu.SemaphoreType.DMA((depth + 2, pieces))] * 9
        + [pltpu.SemaphoreType.DMA((wide,))] * 2,
        compiler_params=pltpu.CompilerParams(
            vmem_limit_bytes=40 * 1024 * 1024, collective_id=0, has_side_effects=True
        ),
    )(offsets, spectra)
    return lags(cross.astype(jnp.bfloat16).reshape(count * pairs, 8 * LANES), count, pairs, length)


def lags(cross, count, pairs, length):
    result = jnp.dot(cross, jnp.asarray(inverse_table(length)), preferred_element_type=jnp.float32)
    result = result * (1.0 / math.sqrt(F))
    return result.reshape(count, pairs, LAGS).astype(jnp.bfloat16)


def solution(mesh):
    in_specs = (P(("day", "chan"), None, None), P(("day", "chan")), P())
    out_specs = P(("day", "chan"), None, None)
    columns = max(1, LAYER_CHIPS // mesh.shape["day"])
    body = functools.partial(shards, columns)
    return jax.shard_map(body, mesh=mesh, in_specs=in_specs, out_specs=out_specs, check_vma=False)
```

```python
import functools
import math

import jax
import jax.numpy as jnp
import numpy as np
from jax import lax
from jax.experimental import pallas as pl
from jax.experimental.pallas import tpu as pltpu
from jax.sharding import PartitionSpec as P

F = 512
F0 = 6
LAGS = 2048
LANES = 128
BAND = 512
PIECES = 4
LAYER_CHIPS = 4


def forward_table(length):
    samples = np.arange(length, dtype=np.int64)
    freqs = F0 + np.arange(F, dtype=np.int64)
    phase = np.mod(samples[:, None] * freqs[None, :], length)
    angle = 2.0 * math.pi / length * phase
    return np.concatenate([np.cos(angle), -np.sin(angle)], axis=1).astype(np.float32).astype(jnp.bfloat16)


def inverse_table(length):
    freqs = F0 + np.arange(F, dtype=np.int64)
    shifts = np.arange(LAGS, dtype=np.int64) - LAGS // 2
    phase = np.mod(freqs[:, None] * shifts[None, :], length)
    angle = 2.0 * math.pi / length * phase
    return np.concatenate([np.cos(angle), -np.sin(angle)], axis=0).astype(np.float32).astype(jnp.bfloat16)


def whiten(records, live_mask):
    count, windows, length = records.shape
    spectrum = jnp.dot(
        records.reshape(count * windows, length),
        jnp.asarray(forward_table(length)),
        preferred_element_type=jnp.float32,
    )
    power = jnp.mean(spectrum * spectrum, axis=1, keepdims=True)
    gain = jnp.repeat(live_mask.astype(jnp.float32), windows)[:, None]
    white = spectrum * (gain * lax.rsqrt(power + 1e-06))
    return white.astype(jnp.bfloat16)


def reach_kernel(shape, offsets_ref, white_ref, cross_ref, held, ext, own, swapped, made, back,
                 z_send, z_recv, c_send, c_recv, y_send, y_recv, d_send, d_recv, e_send, r_send, r_recv):
    layers, columns, depth, pieces, windows, fold = shape
    count, slab = white_ref.shape[0], white_ref.shape[1]
    pairs = offsets_ref.shape[0]
    wide = 2 * columns
    total = layers * wide * count
    me = lax.axis_index("chan")
    z, q = me // wide, me % wide
    y, c = q // 2, q % 2
    sibling = me + 1 - 2 * c
    sib_q = q + 1 - 2 * c
    mate = me + 2 - 4 * y
    mate_q = q + 2 - 4 * y
    far_q = sib_q + 2 - 4 * y
    step = count // pieces
    top, lifted = layers - 1, depth + 1

    barrier = pltpu.get_barrier_semaphore()

    def greet(device):
        pl.semaphore_signal(barrier, inc=1, device_id={"chan": device}, device_id_type=pl.DeviceIdType.MESH)

    greet(sibling)
    if columns == 2:
        greet(mate)

    @pl.when(z >= 1)
    def _():
        greet(me - wide)

    @pl.when(z < layers - 1)
    def _():
        greet(me + wide)

    below, above = jnp.minimum(z, 1), jnp.minimum(top - z, 1)
    peers = columns + below + above
    if fold:
        @pl.when(z == 0)
        def _():
            for i in range(wide):
                greet(top * wide + i)

        @pl.when(z == top)
        def _():
            for i in range(wide):
                greet(jnp.int32(i))

        peers = peers + wide * (2 - below - above)
    pl.semaphore_wait(barrier, peers)

    def rows(p):
        return pl.ds(p * step, step)

    def mine(dz, p):
        return white_ref.at[rows(p)] if dz == 0 else held.at[dz * wide + q, rows(p)]

    def copy(source, slot, p, send, recv, device):
        return pltpu.make_async_remote_copy(
            src_ref=source,
            dst_ref=held.at[slot, rows(p)],
            send_sem=send,
            recv_sem=recv,
            device_id={"chan": device},
            device_id_type=pl.DeviceIdType.MESH,
        )

    def down(dz, p):
        return copy(mine(dz, p), (dz + 1) * wide + q, p, z_send.at[dz, p], z_recv.at[dz + 1, p], me - wide)

    def from_above(dz, p):
        return copy(mine(dz, p), dz * wide + q, p, z_send.at[dz, p], z_recv.at[dz, p], me)

    def across(dz, p, slot):
        return copy(mine(dz, p), slot, p, c_send.at[dz, p], c_recv.at[dz, p], sibling)

    def over(dz, p, slot):
        return copy(mine(dz, p), slot, p, y_send.at[dz, p], y_recv.at[dz, p], mate)

    def onward(dz, p, slot):
        return copy(held.at[dz * wide + mate_q, rows(p)], slot, p, d_send.at[dz, p], d_recv.at[dz, p], sibling)

    def both(*conditions):
        joined = conditions[0]
        for condition in conditions[1:]:
            joined = jnp.logical_and(joined, condition)
        return joined

    def exists(dz):
        return z + dz < layers

    def goes(dz, at_start, at_end):
        if dz == lifted:
            return z == top
        if dz == 0:
            return at_start
        if fold and dz == depth:
            return both(exists(dz), at_end)
        return exists(dz)

    def z_tx(dz):
        if fold and dz + 1 == depth:
            return both(exists(dz), z >= 1, jnp.logical_or(z >= 2, q == 0))
        return both(exists(dz), z >= 1)

    def z_rx(dz):
        return goes(dz, None, q == 0)

    def c_tx(dz):
        return goes(dz, c == 1, q == 0)

    def c_rx(dz):
        return goes(dz, c == 0, q == 1)

    def y_tx(dz):
        return goes(dz, y == 1, q == 0)

    def y_rx(dz):
        return goes(dz, y == 0, q == 2)

    def detoured(dz, p):
        return fold and dz == depth - 1 and p == pieces - 1

    def over_tx(dz, p):
        if detoured(dz, p):
            return both(y_tx(dz), jnp.logical_or(z > 0, y == 0))
        if raised(dz, p):
            return both(y_tx(dz), y == 0)
        return y_tx(dz)

    def raised(dz, p):
        return fold and dz == lifted and p >= pieces // 2

    def lift_mate(p):
        return copy(held.at[mate_q, rows(p)], lifted * wide + mate_q, p,
                    e_send.at[lifted, p], y_recv.at[lifted, p], me + top * wide)

    def extra(dz, p):
        return copy(held.at[dz * wide + mate_q, rows(p)], (dz + 1) * wide + mate_q, p,
                    e_send.at[dz, p], y_recv.at[dz + 1, p], me - wide)

    def extra_tx():
        return both(z == 1, y == 0)

    def d_rx(dz):
        return goes(dz, y == 0, q == 3)

    def lift(p):
        return copy(white_ref.at[rows(p)], lifted * wide + q, p, z_send.at[lifted, p], z_recv.at[lifted, p],
                    me + top * wide)

    def sends(dz):
        for p in range(pieces):
            if dz > 0:
                @pl.when(z_rx(dz))
                def _():
                    from_above(dz, p).wait_recv()
            if dz < depth:
                @pl.when(z_tx(dz))
                def _():
                    down(dz, p).start()
            if columns == 2:
                @pl.when(over_tx(dz, p))
                def _():
                    over(dz, p, dz * wide + q).start()
            @pl.when(c_tx(dz))
            def _():
                across(dz, p, dz * wide + q).start()

    def passes(dz):
        if columns == 2:
            for p in range(pieces):
                @pl.when(y_rx(dz))
                def _():
                    over(dz, p, dz * wide + mate_q).wait_recv()
                    onward(dz, p, dz * wide + mate_q).start()
                if dz == 0 and raised(lifted, p):
                    @pl.when(both(z == 0, y == 0))
                    def _():
                        lift_mate(p).start()
                if detoured(dz + 1, p):
                    @pl.when(extra_tx())
                    def _():
                        extra(dz, p).start()

    def arrives(dz):
        for p in range(pieces):
            @pl.when(c_rx(dz))
            def _():
                across(dz, p, dz * wide + sib_q).wait_recv()
            if columns == 2:
                @pl.when(d_rx(dz))
                def _():
                    onward(dz, p, dz * wide + far_q).wait_recv()

    def finishes(dz):
        for p in range(pieces):
            if dz < depth:
                @pl.when(z_tx(dz))
                def _():
                    down(dz, p).wait_send()
            if columns == 2:
                @pl.when(over_tx(dz, p))
                def _():
                    over(dz, p, dz * wide + q).wait_send()
                if detoured(dz + 1, p):
                    @pl.when(extra_tx())
                    def _():
                        extra(dz, p).wait_send()
                @pl.when(y_rx(dz))
                def _():
                    onward(dz, p, dz * wide + mate_q).wait_send()
            @pl.when(c_tx(dz))
            def _():
                across(dz, p, dz * wide + q).wait_send()

    def answer(i):
        return pltpu.make_async_remote_copy(
            src_ref=made.at[i],
            dst_ref=back.at[q],
            send_sem=r_send.at[i],
            recv_sem=r_recv.at[q],
            device_id={"chan": jnp.int32(i)},
            device_id_type=pl.DeviceIdType.MESH,
        )

    def answered(i):
        return pltpu.make_async_remote_copy(
            src_ref=made.at[i],
            dst_ref=back.at[i],
            send_sem=r_send.at[i],
            recv_sem=r_recv.at[i],
            device_id={"chan": me},
            device_id_type=pl.DeviceIdType.MESH,
        )

    low = lax.broadcasted_iota(jnp.int32, (8, LANES), 0) < 4

    def prepare(i, carry):
        raw = white_ref[i]
        value = raw.astype(jnp.float32)
        own[i] = value
        ext[q * count + i] = raw
        for w in range(windows):
            swapped[i, w * 8 : w * 8 + 8] = pltpu.roll(value[w * 8 : w * 8 + 8], 4, 0)
        return carry

    def settle(dz):
        def one(l):
            def fill(i, carry):
                ext[(dz * wide + l) * count + i] = held[dz * wide + l, i]
                return carry
            lax.fori_loop(0, count, fill, 0, unroll=4)

        if dz == 0:
            for l in range(1, wide):
                @pl.when(q < l)
                def _():
                    one(l)
        else:
            @pl.when(exists(dz))
            def _():
                for l in range(1 if fold and dz == depth else wide):
                    one(l)

    live = jnp.minimum(layers * wide - me, pairs)

    def outside():
        def nothing(k, carry):
            for r in range(count):
                cross_ref[r, k] = jnp.zeros((8, LANES), jnp.float32)
            return carry

        lax.fori_loop(live, pairs, nothing, 0)

        @pl.when(layers - z <= depth)
        def _():
            def blank(i, carry):
                ext[(layers - z) * wide * count + i] = jnp.zeros((slab, LANES), jnp.bfloat16)
                return carry

            lax.fori_loop(0, 2 * count, blank, 0, unroll=4)

    def reached(dz):
        if dz < 0:
            return 0
        if dz == depth:
            return live
        return jnp.minimum((dz + 1) * wide - q - 1, live)

    def multiply(dz):
        def pair(k, carry):
            shift = offsets_ref[k]

            def channel(i, inner):
                place = me * count + i + shift
                keep = jnp.where(place < total, 1.0 / windows, 0.0)
                near = jnp.minimum(q * count + i + shift, ext.shape[0] - 1)
                partner = ext[near].astype(jnp.float32)
                straight = own[i, :8] * partner[:8]
                twisted = swapped[i, :8] * partner[:8]
                for w in range(1, windows):
                    part = slice(w * 8, w * 8 + 8)
                    straight += own[i, part] * partner[part]
                    twisted += swapped[i, part] * partner[part]
                joined = jnp.where(
                    low,
                    straight + pltpu.roll(straight, 4, 0),
                    pltpu.roll(twisted, 4, 0) - twisted,
                )
                cross_ref[i, k] = joined * keep
                return inner

            return lax.fori_loop(0, count, channel, carry, unroll=4)

        begin, end = reached(dz - 1), reached(dz)
        if fold and dz == depth:
            @pl.when(z == 0)
            def _():
                lax.fori_loop(begin, begin + 1, pair, 0)

            @pl.when(z > 0)
            def _():
                lax.fori_loop(begin, end, pair, 0)
        else:
            lax.fori_loop(begin, end, pair, 0)

    def reply():
        for i in range(wide):
            shift = offsets_ref[top * wide + q - i]

            def channel(r, carry):
                place = i * count + r + shift
                keep = jnp.where(place < total, 1.0 / windows, 0.0)
                near = jnp.clip(place - top * wide * count, 0, ext.shape[0] - 1)
                partner = ext[near].astype(jnp.float32)
                value = held[lifted * wide + i, r].astype(jnp.float32)
                straight = value[:8] * partner[:8]
                twisted = pltpu.roll(value[:8], 4, 0) * partner[:8]
                for w in range(1, windows):
                    part = slice(w * 8, w * 8 + 8)
                    straight += value[part] * partner[part]
                    twisted += pltpu.roll(value[part], 4, 0) * partner[part]
                joined = jnp.where(
                    low,
                    straight + pltpu.roll(straight, 4, 0),
                    pltpu.roll(twisted, 4, 0) - twisted,
                )
                made[i, r] = (joined * keep).astype(jnp.bfloat16)
                return carry

            lax.fori_loop(0, count, channel, 0, unroll=4)
        for i in range(wide):
            answer(i).start()

    sends(0)
    if fold:
        @pl.when(z == 0)
        def _():
            for p in range(pieces):
                lift(p).start()

    lax.fori_loop(0, count, prepare, 0)
    outside()
    for dz in range(depth + 1):
        if dz < depth:
            sends(dz + 1)
        if fold and dz == 0:
            sends(lifted)
        passes(dz)
        if fold and dz == 0:
            passes(lifted)
        arrives(dz)
        settle(dz)
        if fold and dz == 0:
            arrives(lifted)

            @pl.when(z == top)
            def _():
                reply()

        multiply(dz)

    if fold:
        @pl.when(z == 0)
        def _():
            for i in range(wide):
                answered(i).wait_recv()

                def take(r, carry):
                    cross_ref[r, top * wide - q + i] = back[i, r].astype(jnp.float32)
                    return carry

                lax.fori_loop(0, count, take, 0, unroll=4)
            for p in range(pieces):
                lift(p).wait_send()
                if raised(lifted, p):
                    @pl.when(y == 0)
                    def _():
                        lift_mate(p).wait_send()

        @pl.when(z == top)
        def _():
            for i in range(wide):
                answer(i).wait_send()

        finishes(lifted)
    for dz in range(depth + 1):
        finishes(dz)


def middle_kernel(shape, offsets_hbm, mask_hbm, records_hbm, table_hbm, cross_ref,
                  offsets_ref, mask_ref, records, table, spectrum, scale, white, held, spec, made, back, joined,
                  l_sem, x_send, f_send, g_send, s_recv, r_send, r_recv):
    layers, wide, windows = shape
    pairs = offsets_ref.shape[0]
    count = records.shape[0] // windows
    chunks, width = table.shape[0], table.shape[2]
    load = [pltpu.make_async_copy(records_hbm, records, l_sem.at[chunks])]
    for n in range(chunks):
        load.append(pltpu.make_async_copy(table_hbm.at[n], table.at[n], l_sem.at[n]))
    load.append(pltpu.make_async_copy(offsets_hbm, offsets_ref, l_sem.at[chunks + 1]))
    load.append(pltpu.make_async_copy(mask_hbm, mask_ref, l_sem.at[chunks + 2]))
    for one in load:
        one.start()
    parts = layers * wide
    pitch = spec.shape[0] // (2 * windows)
    half, top, last = layers // 2, layers - 1, parts - 1
    me = lax.axis_index("chan")
    z, q = me // wide, me % wide
    c = q % 2
    first = z * wide
    base = half * wide
    sib_q = q + 1 - 2 * c
    mate_q = (q + 2) % wide
    far_q = (sib_q + 2) % wide
    near = c == 0
    inner_low, inner_high = z == half - 1, z == half
    neighbour = jnp.where(
        jnp.logical_or(z == 0, jnp.logical_and(inner_low, c == 1)), me + wide, me - wide)
    own_end = jnp.where(
        z == 0, base, jnp.where(jnp.logical_and(inner_low, c == 1), base + wide, parts + 1))
    barrier = pltpu.get_barrier_semaphore()

    def greet(device, condition):
        @pl.when(condition)
        def _():
            pl.semaphore_signal(barrier, inc=1, device_id={"chan": jnp.int32(device)},
                                device_id_type=pl.DeviceIdType.MESH)

    for col in (sib_q, mate_q, far_q):
        greet(first + col, z >= 0)
    for i in range(wide):
        odd = i % 2 == 1
        greet(wide + i, z == 0)
        if odd:
            greet(base + i, z < half)
        else:
            greet(base + i, jnp.logical_and(inner_low, q == i))
    greet(me - wide, jnp.logical_or(inner_low, jnp.logical_and(inner_high, c == 1)))
    greet(me + wide, inner_high)
    replies_far = jnp.where(inner_low, wide, jnp.where(jnp.logical_and(inner_high, c == 1), 2 * wide - 1, 0))
    ships_there = jnp.where(jnp.logical_and(inner_low, near), 0, 1)

    load[0].wait()
    square = None
    for n in range(chunks):
        load[n + 1].wait()
        part = jnp.dot(records[...], table[n], preferred_element_type=jnp.float32)
        spectrum[:, n * width:(n + 1) * width] = part
        for lane in range(0, width, LANES):
            piece_square = part[:, lane:lane + LANES] * part[:, lane:lane + LANES]
            square = piece_square if square is None else square + piece_square
    power = jnp.sum(square, axis=1, keepdims=True) * (1.0 / (2 * F))
    scale[...] = jnp.broadcast_to(lax.rsqrt(power + 1e-06), scale.shape)

    for one in load[chunks + 1:]:
        one.wait()
    upper = lax.broadcasted_iota(jnp.int32, (2 * windows, LANES), 0) < windows

    def whitening(i, carry):
        rows = pl.ds(pl.multiple_of(i * 2 * windows, 2 * windows), 2 * windows)
        alive = jnp.where(upper, mask_ref[2 * i].astype(jnp.float32), mask_ref[2 * i + 1].astype(jnp.float32))
        gain = alive * scale[rows, :]
        for x in range(2 * wide):
            white[x, rows] = (spectrum[rows, x * LANES:(x + 1) * LANES] * gain).astype(jnp.bfloat16)
        return carry

    lax.fori_loop(0, count // 2, whitening, 0)
    pl.semaphore_wait(barrier, wide - 1 + replies_far + ships_there)

    def remote(source, target, send, recv, device):
        return pltpu.make_async_remote_copy(
            src_ref=source, dst_ref=target, send_sem=send, recv_sem=recv,
            device_id={"chan": device}, device_id_type=pl.DeviceIdType.MESH,
        )

    def piece(ri, col):
        return white.at[ri * wide + col]

    def swap(ri, col):
        return remote(piece(ri, col), held.at[me, ri], x_send, s_recv.at[me], first + col)

    def ship_own(ri):
        return remote(piece(ri, q), held.at[me, ri], f_send, s_recv.at[me], neighbour)

    def ship(s):
        return remote(held.at[s], held.at[s], f_send, s_recv.at[s], neighbour)

    both_ways = jnp.logical_and(inner_low, c == 1)

    def drop_own(ri):
        return remote(piece(ri, q), held.at[me, ri], g_send, s_recv.at[me], me - wide)

    def drop(s):
        return remote(held.at[s], held.at[s], g_send, s_recv.at[s], me - wide)

    def made_at(d, k):
        return made.at[d * pairs + k]

    def reply(d, k):
        return remote(made_at(d, k), back.at[k, q], r_send, r_recv.at[k], d)

    def shipped(slots, send):
        remote(held.at[0:slots], held.at[0:slots], send, s_recv.at[0], neighbour).wait_send()

    for ri in range(2):
        ship_own(ri).start()

    @pl.when(both_ways)
    def _():
        for ri in range(2):
            drop_own(ri).start()
    columns = (sib_q, mate_q, far_q)
    for col in columns:
        for ri in range(2):
            swap(ri, col).start()

    def settle(s, load):
        for ri in range(2):
            def one(i, carry):
                value = load(ri, i).astype(jnp.float32)
                for part in range(2):
                    row = ri * windows * pitch + s * count + 2 * i + part
                    spec[pl.ds(row, windows, stride=pitch), :] = value[part * windows:(part + 1) * windows]
                return carry

            lax.fori_loop(0, count // 2, one, 0, unroll=4)

    def own_rows(ri, i):
        return white[ri * wide + q, pl.ds(pl.multiple_of(i * 2 * windows, 2 * windows), 2 * windows)]

    def take(s, onward=None, downward=None):
        ship(s).wait_recv()
        if onward is not None:
            @pl.when(onward)
            def _():
                ship(s).start()
        if downward is not None:
            @pl.when(downward)
            def _():
                drop(s).start()
        settle(s, lambda ri, i: held[s, ri, pl.ds(pl.multiple_of(i * 2 * windows, 2 * windows), 2 * windows)])

    def block(d, k):
        shift = offsets_ref[k]
        for g in range(count // 16):
            mine = d * count + g * 16
            real = imag = None
            for w in range(windows):
                cr = spec[pl.ds(pl.multiple_of(w * pitch + mine, 8), 16), :]
                ci = spec[pl.ds(pl.multiple_of((windows + w) * pitch + mine, 8), 16), :]
                pr = spec[pl.ds(w * pitch + mine + shift, 16), :]
                pi = spec[pl.ds((windows + w) * pitch + mine + shift, 16), :]
                re, im = cr * pr + ci * pi, ci * pr - cr * pi
                real, imag = (re, im) if w == 0 else (real + re, imag + im)
            rows = slice(g * 16, g * 16 + 16)
            made[d * pairs + k, 0, rows] = (real * (1.0 / windows)).astype(jnp.bfloat16)
            made[d * pairs + k, 1, rows] = (imag * (1.0 / windows)).astype(jnp.bfloat16)

    def spans(d_begin, d_end, u_begin, u_end, visit):
        def reach(u, carry):
            def one(d, inner):
                visit(d, u - 1 - d)
                return inner

            return lax.fori_loop(jnp.maximum(d_begin, u - pairs), jnp.minimum(d_end, u), one, carry)

        lax.fori_loop(u_begin, u_end, reach, 0)

    def give(d, k):
        @pl.when(d != me)
        def _():
            reply(d, k).start()

    def blocks(*span):
        spans(*span, block)
        spans(*span, give)

    for x in range(2 * windows):
        spec[pl.ds(x * pitch + parts * count, count), :] = jnp.zeros((count, LANES), jnp.float32)

    def clear(i, carry):
        joined[pl.ds(pl.multiple_of(i * 64, 64), 64), :] = jnp.zeros((64, LANES), jnp.float32)
        return carry

    lax.fori_loop(0, joined.shape[0] // 64, clear, 0)

    y = q // 2
    pair_1, pair_2 = (q, sib_q), (mate_q, far_q)

    def reached_1(start, more=0):
        return jnp.where(y == 0, start, start + 3), jnp.where(y == 0, start + 2, start + wide + more)

    def reached_2(start, more=0):
        return jnp.where(y == 0, start + 2, start), jnp.where(y == 0, start + wide + more, start + 3)

    settle(me, own_rows)
    for col in columns:
        take(first + col, z >= 0, both_ways)
    blocks(first, first + wide, first + 1, first + wide + jnp.where(z == top, 1, 0))

    @pl.when(z == 0)
    def _():
        for group, reached in ((pair_1, reached_1), (pair_2, reached_2)):
            for col in group:
                take(wide + col)
            blocks(0, wide, *reached(wide))

    @pl.when(inner_low)
    def _():
        def lower(group):
            for col in group:
                take(col, jnp.logical_not(near))

        lower(pair_1)
        for col in pair_1:
            take(base + col)
        blocks(2 * y, 2 * y + 2, *reached_1(base))
        blocks(wide, base, *reached_1(base))
        lower(pair_2)
        blocks(2 - 2 * y, wide - 2 * y, *reached_1(base))
        for col in pair_2:
            take(base + col)
        blocks(0, base, *reached_2(base))

        @pl.when(near)
        def _():
            for group, reached in ((pair_1, reached_1), (pair_2, reached_2)):
                for col in group:
                    take(top * wide + col)
                blocks(0, base, *reached(top * wide, 1))

    @pl.when(inner_high)
    def _():
        for group, reached in ((pair_1, reached_1), (pair_2, reached_2)):
            for col in group:
                take(top * wide + col, near)
            blocks(base, base + wide, *reached(top * wide, 1))

        @pl.when(jnp.logical_not(near))
        def _():
            for col in pair_1 + pair_2:
                take(wide + col)
            spans(wide, base, top * wide, parts + 1, block)
            for col in pair_1:
                take(col)
            blocks(2 * y, 2 * y + 2, top * wide, parts + 1)
            for col in pair_2:
                take(col)
            blocks(2 - 2 * y, wide - 2 * y, top * wide, parts + 1)
            spans(wide, base, top * wide, parts + 1, give)

    def unpack(source, k, col):
        for ri in range(2):
            for g in range(count // 16):
                value = source[ri, g * 16:g * 16 + 16].astype(jnp.float32)
                for part in range(2):
                    row = (ri * wide + col) * count * pairs + (g * 16 + part * 8) * pairs + k
                    joined[pl.ds(row, 8, stride=pairs), :] = value[part * 8:part * 8 + 8]

    def collect(k, carry):
        away = me + k + 1 >= own_end
        def received(cols):
            remote(back.at[k, 0:cols], back.at[k, 0:cols], r_send, r_recv.at[k], me).wait_recv()

        @pl.when(away)
        def _():
            received(wide)

        @pl.when(jnp.logical_not(away))
        def _():
            received(wide - 1)

        for col in range(wide):
            here = jnp.logical_and(q == col, jnp.logical_not(away))

            @pl.when(here)
            def _():
                unpack(made_at(me, k), k, col)

            @pl.when(jnp.logical_not(here))
            def _():
                unpack(back.at[k, col], k, col)
        return carry

    lax.fori_loop(0, parts - me, collect, 0)

    def pack(i, carry):
        rows = pl.ds(pl.multiple_of(i * 16, 16), 16)
        for x in range(2 * wide):
            start = pl.multiple_of(x * count * pairs + i * 16, 16)
            cross_ref[rows, x * LANES:(x + 1) * LANES] = joined[pl.ds(start, 16), :].astype(jnp.bfloat16)
        return carry

    lax.fori_loop(0, count * pairs // 16, pack, 0, unroll=2)

    shipped(wide - 1, x_send)
    forwards = jnp.logical_or(both_ways, jnp.logical_and(inner_high, near))

    @pl.when(forwards)
    def _():
        shipped(2 * wide, f_send)

    @pl.when(jnp.logical_not(forwards))
    def _():
        shipped(wide, f_send)

    @pl.when(both_ways)
    def _():
        shipped(wide, g_send)

    for i in range(parts):
        layer, odd = i // wide, i % 2 == 1
        ends = base if layer == 0 else base + wide if layer == half - 1 and odd else parts + 1
        replies = sum(
            min(ends, d + pairs + 1) - d - 1 for d in range(layer * wide, (layer + 1) * wide) if d != i)
        if layer == half - 1 or (layer == half and odd):
            begins = base if layer == half - 1 else base + wide
            replies += sum(min(ends, d + pairs + 1) - begins for d in range(layer * wide))

        @pl.when(me == i)
        def _():
            done = made.at[0:replies]
            remote(done, done, r_send, r_recv.at[0], me).wait_send()


def meet(layers, wide, records, live_mask, offsets):
    pairs = offsets.shape[0]
    count, windows, length = records.shape
    parts = layers * wide
    pitch = (parts + 1) * count
    rows = count * windows
    width = 2 * LANES
    chunks = 2 * F // width
    table = np.ascontiguousarray(forward_table(length).reshape(length, chunks, width).transpose(1, 0, 2))
    return pl.pallas_call(
        functools.partial(middle_kernel, (layers, wide, windows)),
        out_shape=jax.ShapeDtypeStruct((count * pairs, 2 * F), jnp.bfloat16),
        in_specs=[
            pl.BlockSpec(memory_space=pltpu.HBM),
            pl.BlockSpec(memory_space=pltpu.HBM),
            pl.BlockSpec(memory_space=pltpu.HBM),
            pl.BlockSpec(memory_space=pltpu.HBM),
        ],
        out_specs=pl.BlockSpec(memory_space=pltpu.VMEM),
        scratch_shapes=[
            pltpu.SMEM((pairs,), jnp.int32),
            pltpu.SMEM((count,), jnp.int32),
            pltpu.VMEM((rows, length), jnp.bfloat16),
            pltpu.VMEM((chunks, length, width), jnp.bfloat16),
            pltpu.VMEM((rows, 2 * F), jnp.float32),
            pltpu.VMEM((rows, LANES), jnp.float32),
            pltpu.VMEM((2 * wide, rows, LANES), jnp.bfloat16),
            pltpu.VMEM((parts, 2, rows, LANES), jnp.bfloat16),
            pltpu.VMEM((2 * windows * pitch, LANES), jnp.float32),
            pltpu.VMEM((parts * pairs, 2, count, LANES), jnp.bfloat16),
            pltpu.VMEM((pairs, wide, 2, count, LANES), jnp.bfloat16),
            pltpu.VMEM((2 * wide * count * pairs, LANES), jnp.float32),
            pltpu.SemaphoreType.DMA((chunks + 3,)),
            pltpu.SemaphoreType.DMA,
            pltpu.SemaphoreType.DMA,
            pltpu.SemaphoreType.DMA,
            pltpu.SemaphoreType.DMA((parts,)),
            pltpu.SemaphoreType.DMA,
            pltpu.SemaphoreType.DMA((pairs,)),
        ],
        compiler_params=pltpu.CompilerParams(
            vmem_limit_bytes=36 * 1024 * 1024, collective_id=1, has_side_effects=True
        ),
    )(*[pltpu.with_memory_space_constraint(x, pltpu.HBM) for x in (offsets, live_mask, records.reshape(rows, length), jnp.asarray(table))])


def shards(columns, records, live_mask, offsets):
    count, windows, length = records.shape
    pairs = offsets.shape[0]
    wide = 2 * columns
    layers = lax.axis_size("chan") // wide
    reach = (BAND + count - 2) // count
    depth = min(layers - 1, (wide - 1 + reach) // wide)
    pieces = PIECES
    fold = columns == 2 and depth == layers - 1 and depth >= 2 and layers * wide == pairs and pairs * count == BAND
    if (
        columns == 2 and layers == 4 and layers * wide == pairs and pairs * count == BAND
        and F == wide * LANES and windows == 8 and count % 16 == 0
    ):
        cross = meet(layers, wide, records, live_mask, offsets)
        return lags(cross, count, pairs, length)
    spectra = whiten(records, live_mask).reshape(count, windows * 8, LANES)
    slots = (depth + 1) * wide
    cross = pl.pallas_call(
        functools.partial(reach_kernel, (layers, columns, depth, pieces, windows, fold)),
        out_shape=jax.ShapeDtypeStruct((count, pairs, 8, LANES), jnp.float32),
        in_specs=[
            pl.BlockSpec(memory_space=pltpu.SMEM),
            pl.BlockSpec(memory_space=pltpu.VMEM),
        ],
        out_specs=pl.BlockSpec(memory_space=pltpu.VMEM),
        scratch_shapes=[
            pltpu.VMEM((slots + wide, count, windows * 8, LANES), jnp.bfloat16),
            pltpu.VMEM((slots * count, windows * 8, LANES), jnp.bfloat16),
            pltpu.VMEM((count, windows * 8, LANES), jnp.float32),
            pltpu.VMEM((count, windows * 8, LANES), jnp.float32),
            pltpu.VMEM((wide, count, 8, LANES), jnp.bfloat16),
            pltpu.VMEM((wide, count, 8, LANES), jnp.bfloat16),
        ]
        + [pltpu.SemaphoreType.DMA((depth + 2, pieces))] * 9
        + [pltpu.SemaphoreType.DMA((wide,))] * 2,
        compiler_params=pltpu.CompilerParams(
            vmem_limit_bytes=40 * 1024 * 1024, collective_id=0, has_side_effects=True
        ),
    )(offsets, spectra)
    return lags(cross.astype(jnp.bfloat16).reshape(count * pairs, 8 * LANES), count, pairs, length)


def lags(cross, count, pairs, length):
    result = jnp.dot(cross, jnp.asarray(inverse_table(length)), preferred_element_type=jnp.float32)
    result = result * (1.0 / math.sqrt(F))
    return result.reshape(count, pairs, LAGS).astype(jnp.bfloat16)


def solution(mesh):
    in_specs = (P(("day", "chan"), None, None), P(("day", "chan")), P())
    out_specs = P(("day", "chan"), None, None)
    columns = max(1, LAYER_CHIPS // mesh.shape["day"])
    body = functools.partial(shards, columns)
    return jax.shard_map(body, mesh=mesh, in_specs=in_specs, out_specs=out_specs, check_vma=False)
```

```python
import functools
import math

import jax
import jax.numpy as jnp
import numpy as np
from jax import lax
from jax.experimental import pallas as pl
from jax.experimental.pallas import tpu as pltpu
from jax.sharding import PartitionSpec as P

F = 512
F0 = 6
LAGS = 2048
LANES = 128
SPAN = 512
BAND = 512
PIECES = 4
LAYER_CHIPS = 4


def forward_table(length):
    samples = np.arange(length, dtype=np.int64)
    freqs = F0 + np.arange(F, dtype=np.int64)
    phase = np.mod(samples[:, None] * freqs[None, :], length)
    angle = 2.0 * math.pi / length * phase
    return np.concatenate([np.cos(angle), -np.sin(angle)], axis=1).astype(np.float32).astype(jnp.bfloat16)


def inverse_table(length):
    freqs = F0 + np.arange(F, dtype=np.int64)
    shifts = np.arange(LAGS, dtype=np.int64) - LAGS // 2
    phase = np.mod(freqs[:, None] * shifts[None, :], length)
    angle = 2.0 * math.pi / length * phase
    return np.concatenate([np.cos(angle), -np.sin(angle)], axis=0).astype(np.float32).astype(jnp.bfloat16)


def whiten(records, live_mask):
    count, windows, length = records.shape
    spectrum = jnp.dot(
        records.reshape(count * windows, length),
        jnp.asarray(forward_table(length)),
        preferred_element_type=jnp.float32,
    )
    power = jnp.mean(spectrum * spectrum, axis=1, keepdims=True)
    gain = jnp.repeat(live_mask.astype(jnp.float32), windows)[:, None]
    white = spectrum * (gain * lax.rsqrt(power + 1e-06))
    return white.astype(jnp.bfloat16)


def reach_kernel(shape, offsets_ref, white_ref, cross_ref, held, ext, own, swapped, made, back,
                 z_send, z_recv, c_send, c_recv, y_send, y_recv, d_send, d_recv, e_send, r_send, r_recv):
    layers, columns, depth, pieces, windows, fold = shape
    count, slab = white_ref.shape[0], white_ref.shape[1]
    pairs = offsets_ref.shape[0]
    wide = 2 * columns
    total = layers * wide * count
    me = lax.axis_index("chan")
    z, q = me // wide, me % wide
    y, c = q // 2, q % 2
    sibling = me + 1 - 2 * c
    sib_q = q + 1 - 2 * c
    mate = me + 2 - 4 * y
    mate_q = q + 2 - 4 * y
    far_q = sib_q + 2 - 4 * y
    step = count // pieces
    top, lifted = layers - 1, depth + 1

    barrier = pltpu.get_barrier_semaphore()

    def greet(device):
        pl.semaphore_signal(barrier, inc=1, device_id={"chan": device}, device_id_type=pl.DeviceIdType.MESH)

    greet(sibling)
    if columns == 2:
        greet(mate)

    @pl.when(z >= 1)
    def _():
        greet(me - wide)

    @pl.when(z < layers - 1)
    def _():
        greet(me + wide)

    below, above = jnp.minimum(z, 1), jnp.minimum(top - z, 1)
    peers = columns + below + above
    if fold:
        @pl.when(z == 0)
        def _():
            for i in range(wide):
                greet(top * wide + i)

        @pl.when(z == top)
        def _():
            for i in range(wide):
                greet(jnp.int32(i))

        peers = peers + wide * (2 - below - above)
    pl.semaphore_wait(barrier, peers)

    def rows(p):
        return pl.ds(p * step, step)

    def mine(dz, p):
        return white_ref.at[rows(p)] if dz == 0 else held.at[dz * wide + q, rows(p)]

    def copy(source, slot, p, send, recv, device):
        return pltpu.make_async_remote_copy(
            src_ref=source,
            dst_ref=held.at[slot, rows(p)],
            send_sem=send,
            recv_sem=recv,
            device_id={"chan": device},
            device_id_type=pl.DeviceIdType.MESH,
        )

    def down(dz, p):
        return copy(mine(dz, p), (dz + 1) * wide + q, p, z_send.at[dz, p], z_recv.at[dz + 1, p], me - wide)

    def from_above(dz, p):
        return copy(mine(dz, p), dz * wide + q, p, z_send.at[dz, p], z_recv.at[dz, p], me)

    def across(dz, p, slot):
        return copy(mine(dz, p), slot, p, c_send.at[dz, p], c_recv.at[dz, p], sibling)

    def over(dz, p, slot):
        return copy(mine(dz, p), slot, p, y_send.at[dz, p], y_recv.at[dz, p], mate)

    def onward(dz, p, slot):
        return copy(held.at[dz * wide + mate_q, rows(p)], slot, p, d_send.at[dz, p], d_recv.at[dz, p], sibling)

    def both(*conditions):
        joined = conditions[0]
        for condition in conditions[1:]:
            joined = jnp.logical_and(joined, condition)
        return joined

    def exists(dz):
        return z + dz < layers

    def goes(dz, at_start, at_end):
        if dz == lifted:
            return z == top
        if dz == 0:
            return at_start
        if fold and dz == depth:
            return both(exists(dz), at_end)
        return exists(dz)

    def z_tx(dz):
        if fold and dz + 1 == depth:
            return both(exists(dz), z >= 1, jnp.logical_or(z >= 2, q == 0))
        return both(exists(dz), z >= 1)

    def z_rx(dz):
        return goes(dz, None, q == 0)

    def c_tx(dz):
        return goes(dz, c == 1, q == 0)

    def c_rx(dz):
        return goes(dz, c == 0, q == 1)

    def y_tx(dz):
        return goes(dz, y == 1, q == 0)

    def y_rx(dz):
        return goes(dz, y == 0, q == 2)

    def detoured(dz, p):
        return fold and dz == depth - 1 and p == pieces - 1

    def over_tx(dz, p):
        if detoured(dz, p):
            return both(y_tx(dz), jnp.logical_or(z > 0, y == 0))
        if raised(dz, p):
            return both(y_tx(dz), y == 0)
        return y_tx(dz)

    def raised(dz, p):
        return fold and dz == lifted and p >= pieces // 2

    def lift_mate(p):
        return copy(held.at[mate_q, rows(p)], lifted * wide + mate_q, p,
                    e_send.at[lifted, p], y_recv.at[lifted, p], me + top * wide)

    def extra(dz, p):
        return copy(held.at[dz * wide + mate_q, rows(p)], (dz + 1) * wide + mate_q, p,
                    e_send.at[dz, p], y_recv.at[dz + 1, p], me - wide)

    def extra_tx():
        return both(z == 1, y == 0)

    def d_rx(dz):
        return goes(dz, y == 0, q == 3)

    def lift(p):
        return copy(white_ref.at[rows(p)], lifted * wide + q, p, z_send.at[lifted, p], z_recv.at[lifted, p],
                    me + top * wide)

    def sends(dz):
        for p in range(pieces):
            if dz > 0:
                @pl.when(z_rx(dz))
                def _():
                    from_above(dz, p).wait_recv()
            if dz < depth:
                @pl.when(z_tx(dz))
                def _():
                    down(dz, p).start()
            if columns == 2:
                @pl.when(over_tx(dz, p))
                def _():
                    over(dz, p, dz * wide + q).start()
            @pl.when(c_tx(dz))
            def _():
                across(dz, p, dz * wide + q).start()

    def passes(dz):
        if columns == 2:
            for p in range(pieces):
                @pl.when(y_rx(dz))
                def _():
                    over(dz, p, dz * wide + mate_q).wait_recv()
                    onward(dz, p, dz * wide + mate_q).start()
                if dz == 0 and raised(lifted, p):
                    @pl.when(both(z == 0, y == 0))
                    def _():
                        lift_mate(p).start()
                if detoured(dz + 1, p):
                    @pl.when(extra_tx())
                    def _():
                        extra(dz, p).start()

    def arrives(dz):
        for p in range(pieces):
            @pl.when(c_rx(dz))
            def _():
                across(dz, p, dz * wide + sib_q).wait_recv()
            if columns == 2:
                @pl.when(d_rx(dz))
                def _():
                    onward(dz, p, dz * wide + far_q).wait_recv()

    def finishes(dz):
        for p in range(pieces):
            if dz < depth:
                @pl.when(z_tx(dz))
                def _():
                    down(dz, p).wait_send()
            if columns == 2:
                @pl.when(over_tx(dz, p))
                def _():
                    over(dz, p, dz * wide + q).wait_send()
                if detoured(dz + 1, p):
                    @pl.when(extra_tx())
                    def _():
                        extra(dz, p).wait_send()
                @pl.when(y_rx(dz))
                def _():
                    onward(dz, p, dz * wide + mate_q).wait_send()
            @pl.when(c_tx(dz))
            def _():
                across(dz, p, dz * wide + q).wait_send()

    def answer(i):
        return pltpu.make_async_remote_copy(
            src_ref=made.at[i],
            dst_ref=back.at[q],
            send_sem=r_send.at[i],
            recv_sem=r_recv.at[q],
            device_id={"chan": jnp.int32(i)},
            device_id_type=pl.DeviceIdType.MESH,
        )

    def answered(i):
        return pltpu.make_async_remote_copy(
            src_ref=made.at[i],
            dst_ref=back.at[i],
            send_sem=r_send.at[i],
            recv_sem=r_recv.at[i],
            device_id={"chan": me},
            device_id_type=pl.DeviceIdType.MESH,
        )

    low = lax.broadcasted_iota(jnp.int32, (8, LANES), 0) < 4

    def prepare(i, carry):
        raw = white_ref[i]
        value = raw.astype(jnp.float32)
        own[i] = value
        ext[q * count + i] = raw
        for w in range(windows):
            swapped[i, w * 8 : w * 8 + 8] = pltpu.roll(value[w * 8 : w * 8 + 8], 4, 0)
        return carry

    def settle(dz):
        def one(l):
            def fill(i, carry):
                ext[(dz * wide + l) * count + i] = held[dz * wide + l, i]
                return carry
            lax.fori_loop(0, count, fill, 0, unroll=4)

        if dz == 0:
            for l in range(1, wide):
                @pl.when(q < l)
                def _():
                    one(l)
        else:
            @pl.when(exists(dz))
            def _():
                for l in range(1 if fold and dz == depth else wide):
                    one(l)

    live = jnp.minimum(layers * wide - me, pairs)

    def outside():
        def nothing(k, carry):
            for r in range(count):
                cross_ref[r, k] = jnp.zeros((8, LANES), jnp.float32)
            return carry

        lax.fori_loop(live, pairs, nothing, 0)

        @pl.when(layers - z <= depth)
        def _():
            def blank(i, carry):
                ext[(layers - z) * wide * count + i] = jnp.zeros((slab, LANES), jnp.bfloat16)
                return carry

            lax.fori_loop(0, 2 * count, blank, 0, unroll=4)

    def reached(dz):
        if dz < 0:
            return 0
        if dz == depth:
            return live
        return jnp.minimum((dz + 1) * wide - q - 1, live)

    def multiply(dz):
        def pair(k, carry):
            shift = offsets_ref[k]

            def channel(i, inner):
                place = me * count + i + shift
                keep = jnp.where(place < total, 1.0 / windows, 0.0)
                near = jnp.minimum(q * count + i + shift, ext.shape[0] - 1)
                partner = ext[near].astype(jnp.float32)
                straight = own[i, :8] * partner[:8]
                twisted = swapped[i, :8] * partner[:8]
                for w in range(1, windows):
                    part = slice(w * 8, w * 8 + 8)
                    straight += own[i, part] * partner[part]
                    twisted += swapped[i, part] * partner[part]
                joined = jnp.where(
                    low,
                    straight + pltpu.roll(straight, 4, 0),
                    pltpu.roll(twisted, 4, 0) - twisted,
                )
                cross_ref[i, k] = joined * keep
                return inner

            return lax.fori_loop(0, count, channel, carry, unroll=4)

        begin, end = reached(dz - 1), reached(dz)
        if fold and dz == depth:
            @pl.when(z == 0)
            def _():
                lax.fori_loop(begin, begin + 1, pair, 0)

            @pl.when(z > 0)
            def _():
                lax.fori_loop(begin, end, pair, 0)
        else:
            lax.fori_loop(begin, end, pair, 0)

    def reply():
        for i in range(wide):
            shift = offsets_ref[top * wide + q - i]

            def channel(r, carry):
                place = i * count + r + shift
                keep = jnp.where(place < total, 1.0 / windows, 0.0)
                near = jnp.clip(place - top * wide * count, 0, ext.shape[0] - 1)
                partner = ext[near].astype(jnp.float32)
                value = held[lifted * wide + i, r].astype(jnp.float32)
                straight = value[:8] * partner[:8]
                twisted = pltpu.roll(value[:8], 4, 0) * partner[:8]
                for w in range(1, windows):
                    part = slice(w * 8, w * 8 + 8)
                    straight += value[part] * partner[part]
                    twisted += pltpu.roll(value[part], 4, 0) * partner[part]
                joined = jnp.where(
                    low,
                    straight + pltpu.roll(straight, 4, 0),
                    pltpu.roll(twisted, 4, 0) - twisted,
                )
                made[i, r] = (joined * keep).astype(jnp.bfloat16)
                return carry

            lax.fori_loop(0, count, channel, 0, unroll=4)
        for i in range(wide):
            answer(i).start()

    sends(0)
    if fold:
        @pl.when(z == 0)
        def _():
            for p in range(pieces):
                lift(p).start()

    lax.fori_loop(0, count, prepare, 0)
    outside()
    for dz in range(depth + 1):
        if dz < depth:
            sends(dz + 1)
        if fold and dz == 0:
            sends(lifted)
        passes(dz)
        if fold and dz == 0:
            passes(lifted)
        arrives(dz)
        settle(dz)
        if fold and dz == 0:
            arrives(lifted)

            @pl.when(z == top)
            def _():
                reply()

        multiply(dz)

    if fold:
        @pl.when(z == 0)
        def _():
            for i in range(wide):
                answered(i).wait_recv()

                def take(r, carry):
                    cross_ref[r, top * wide - q + i] = back[i, r].astype(jnp.float32)
                    return carry

                lax.fori_loop(0, count, take, 0, unroll=4)
            for p in range(pieces):
                lift(p).wait_send()
                if raised(lifted, p):
                    @pl.when(y == 0)
                    def _():
                        lift_mate(p).wait_send()

        @pl.when(z == top)
        def _():
            for i in range(wide):
                answer(i).wait_send()

        finishes(lifted)
    for dz in range(depth + 1):
        finishes(dz)


def middle_kernel(shape, offsets_hbm, mask_hbm, records_hbm, table_hbm, inverse_hbm, half_ref, cross_ref, inverse,
                  offsets_ref, mask_ref, records, table, crossed, spectrum, white, held, spec, made, back, joined,
                  l_sem, x_send, f_send, g_send, s_recv, r_send, r_recv):
    layers, wide, windows = shape
    pairs = offsets_ref.shape[0]
    count = records.shape[0] // windows
    chunks, width = table.shape[0], table.shape[2]
    load = [pltpu.make_async_copy(records_hbm, records, l_sem.at[chunks])]
    for n in range(chunks):
        load.append(pltpu.make_async_copy(table_hbm.at[n], table.at[n], l_sem.at[n]))
    load.append(pltpu.make_async_copy(offsets_hbm, offsets_ref, l_sem.at[chunks + 1]))
    load.append(pltpu.make_async_copy(mask_hbm, mask_ref, l_sem.at[chunks + 2]))
    for one in load:
        one.start()
    parts = layers * wide
    pitch = spec.shape[0] // (2 * windows)
    half, top, last = layers // 2, layers - 1, parts - 1
    me = lax.axis_index("chan")
    z, q = me // wide, me % wide
    c = q % 2
    first = z * wide
    base = half * wide
    sib_q = q + 1 - 2 * c
    mate_q = (q + 2) % wide
    far_q = (sib_q + 2) % wide
    near = c == 0
    inner_low, inner_high = z == half - 1, z == half
    neighbour = jnp.where(
        jnp.logical_or(z == 0, jnp.logical_and(inner_low, c == 1)), me + wide, me - wide)
    own_end = jnp.where(
        z == 0, base, jnp.where(jnp.logical_and(inner_low, c == 1), base + wide, parts + 1))
    barrier = pltpu.get_barrier_semaphore()

    def greet(device, condition):
        @pl.when(condition)
        def _():
            pl.semaphore_signal(barrier, inc=1, device_id={"chan": jnp.int32(device)},
                                device_id_type=pl.DeviceIdType.MESH)

    for col in (sib_q, mate_q, far_q):
        greet(first + col, z >= 0)
    for i in range(wide):
        odd = i % 2 == 1
        greet(wide + i, z == 0)
        if odd:
            greet(base + i, z < half)
        else:
            greet(base + i, jnp.logical_and(inner_low, q == i))
    greet(me - wide, jnp.logical_or(inner_low, jnp.logical_and(inner_high, c == 1)))
    greet(me + wide, inner_high)
    replies_far = jnp.where(inner_low, wide, jnp.where(jnp.logical_and(inner_high, c == 1), 2 * wide - 1, 0))
    ships_there = jnp.where(jnp.logical_and(inner_low, near), 0, 1)

    load[0].wait()
    for n in range(chunks):
        load[n + 1].wait()
        spectrum[:, n * width:(n + 1) * width] = jnp.dot(
            records[...], table[n], preferred_element_type=jnp.float32)
    for one in load[chunks + 1:]:
        one.wait()
    upper = lax.broadcasted_iota(jnp.int32, (2 * windows, 1), 0) < windows

    def whitening(i, carry):
        rows = pl.ds(pl.multiple_of(i * 2 * windows, 2 * windows), 2 * windows)
        values = [spectrum[rows, x * LANES:(x + 1) * LANES] for x in range(2 * wide)]
        square = values[0] * values[0]
        for value in values[1:]:
            square += value * value
        power = jnp.sum(square, axis=1, keepdims=True) * (1.0 / (2 * F))
        alive = jnp.where(upper, mask_ref[2 * i].astype(jnp.float32), mask_ref[2 * i + 1].astype(jnp.float32))
        gain = alive * lax.rsqrt(power + 1e-06)
        for x, value in enumerate(values):
            white[x, rows] = (value * gain).astype(jnp.bfloat16)
        return carry

    lax.fori_loop(0, count // 2, whitening, 0, unroll=4)
    fetch = pltpu.make_async_copy(inverse_hbm, inverse, l_sem.at[0])
    fetch.start()
    pl.semaphore_wait(barrier, wide - 1 + replies_far + ships_there)

    def remote(source, target, send, recv, device):
        return pltpu.make_async_remote_copy(
            src_ref=source, dst_ref=target, send_sem=send, recv_sem=recv,
            device_id={"chan": device}, device_id_type=pl.DeviceIdType.MESH,
        )

    def piece(ri, col):
        return white.at[ri * wide + col]

    def swap(ri, col):
        return remote(piece(ri, col), held.at[me, ri], x_send, s_recv.at[me], first + col)

    def ship_own(ri):
        return remote(piece(ri, q), held.at[me, ri], f_send, s_recv.at[me], neighbour)

    def ship(s):
        return remote(held.at[s], held.at[s], f_send, s_recv.at[s], neighbour)

    both_ways = jnp.logical_and(inner_low, c == 1)

    def drop_own(ri):
        return remote(piece(ri, q), held.at[me, ri], g_send, s_recv.at[me], me - wide)

    def drop(s):
        return remote(held.at[s], held.at[s], g_send, s_recv.at[s], me - wide)

    def made_at(d, k):
        return made.at[d * pairs + k]

    def reply(d, k):
        return remote(made_at(d, k), back.at[k, q], r_send, r_recv.at[k], d)

    def shipped(slots, send):
        remote(held.at[0:slots], held.at[0:slots], send, s_recv.at[0], neighbour).wait_send()

    for ri in range(2):
        ship_own(ri).start()

    @pl.when(both_ways)
    def _():
        for ri in range(2):
            drop_own(ri).start()
    columns = (sib_q, mate_q, far_q)
    for col in columns:
        for ri in range(2):
            swap(ri, col).start()

    def settle(s, load):
        for ri in range(2):
            def one(i, carry):
                value = load(ri, i).astype(jnp.float32)
                for part in range(2):
                    row = ri * windows * pitch + s * count + 2 * i + part
                    spec[pl.ds(row, windows, stride=pitch), :] = value[part * windows:(part + 1) * windows]
                return carry

            lax.fori_loop(0, count // 2, one, 0, unroll=4)

    def own_rows(ri, i):
        return white[ri * wide + q, pl.ds(pl.multiple_of(i * 2 * windows, 2 * windows), 2 * windows)]

    def take(s, onward=None, downward=None):
        ship(s).wait_recv()
        if onward is not None:
            @pl.when(onward)
            def _():
                ship(s).start()
        if downward is not None:
            @pl.when(downward)
            def _():
                drop(s).start()
        settle(s, lambda ri, i: held[s, ri, pl.ds(pl.multiple_of(i * 2 * windows, 2 * windows), 2 * windows)])

    def block(d, k):
        shift = offsets_ref[k]
        for g in range(count // 16):
            mine = d * count + g * 16
            real = imag = None
            for w in range(windows):
                cr = spec[pl.ds(pl.multiple_of(w * pitch + mine, 8), 16), :]
                ci = spec[pl.ds(pl.multiple_of((windows + w) * pitch + mine, 8), 16), :]
                pr = spec[pl.ds(w * pitch + mine + shift, 16), :]
                pi = spec[pl.ds((windows + w) * pitch + mine + shift, 16), :]
                re, im = cr * pr + ci * pi, ci * pr - cr * pi
                real, imag = (re, im) if w == 0 else (real + re, imag + im)
            rows = slice(g * 16, g * 16 + 16)
            made[d * pairs + k, 0, rows] = (real * (1.0 / windows)).astype(jnp.bfloat16)
            made[d * pairs + k, 1, rows] = (imag * (1.0 / windows)).astype(jnp.bfloat16)

    def spans(d_begin, d_end, u_begin, u_end, visit):
        def reach(u, carry):
            def one(d, inner):
                visit(d, u - 1 - d)
                return inner

            return lax.fori_loop(jnp.maximum(d_begin, u - pairs), jnp.minimum(d_end, u), one, carry)

        lax.fori_loop(u_begin, u_end, reach, 0)

    def give(d, k):
        @pl.when(d != me)
        def _():
            reply(d, k).start()

    def blocks(*span):
        spans(*span, block)
        spans(*span, give)

    for x in range(2 * windows):
        spec[pl.ds(x * pitch + parts * count, count), :] = jnp.zeros((count, LANES), jnp.float32)

    def clear(i, carry):
        joined[pl.ds(pl.multiple_of(i * 64, 64), 64), :] = jnp.zeros((64, LANES), jnp.float32)
        return carry

    lax.fori_loop(0, joined.shape[0] // 64, clear, 0)

    y = q // 2
    pair_1, pair_2 = (q, sib_q), (mate_q, far_q)

    def reached_1(start, more=0):
        return jnp.where(y == 0, start, start + 3), jnp.where(y == 0, start + 2, start + wide + more)

    def reached_2(start, more=0):
        return jnp.where(y == 0, start + 2, start), jnp.where(y == 0, start + wide + more, start + 3)

    settle(me, own_rows)
    for col in columns:
        take(first + col, z >= 0, both_ways)
    blocks(first, first + wide, first + 1, first + wide + jnp.where(z == top, 1, 0))

    @pl.when(z == 0)
    def _():
        for group, reached in ((pair_1, reached_1), (pair_2, reached_2)):
            for col in group:
                take(wide + col)
            blocks(0, wide, *reached(wide))

    @pl.when(inner_low)
    def _():
        def lower(group):
            for col in group:
                take(col, jnp.logical_not(near))

        lower(pair_1)
        for col in pair_1:
            take(base + col)
        blocks(2 * y, 2 * y + 2, *reached_1(base))
        blocks(wide, base, *reached_1(base))
        lower(pair_2)
        blocks(2 - 2 * y, wide - 2 * y, *reached_1(base))
        for col in pair_2:
            take(base + col)
        blocks(0, base, *reached_2(base))

        @pl.when(near)
        def _():
            for group, reached in ((pair_1, reached_1), (pair_2, reached_2)):
                for col in group:
                    take(top * wide + col)
                blocks(0, base, *reached(top * wide, 1))

    @pl.when(inner_high)
    def _():
        for group, reached in ((pair_1, reached_1), (pair_2, reached_2)):
            for col in group:
                take(top * wide + col, near)
            blocks(base, base + wide, *reached(top * wide, 1))

        @pl.when(jnp.logical_not(near))
        def _():
            for col in pair_1 + pair_2:
                take(wide + col)
            spans(wide, base, top * wide, parts + 1, block)
            for col in pair_1:
                take(col)
            blocks(2 * y, 2 * y + 2, top * wide, parts + 1)
            for col in pair_2:
                take(col)
            blocks(2 - 2 * y, wide - 2 * y, top * wide, parts + 1)
            spans(wide, base, top * wide, parts + 1, give)

    group = pairs // 2

    def unpack(source, k, col):
        for ri in range(2):
            for g in range(count // 16):
                value = source[ri, g * 16:g * 16 + 16].astype(jnp.float32)
                for part in range(2):
                    seg = (k // group) * 2 * wide + ri * wide + col
                    row = (seg * count + g * 16 + part * 8) * group + k % group
                    joined[pl.ds(row, 8, stride=group), :] = value[part * 8:part * 8 + 8]

    def collect(k, carry):
        away = me + k + 1 >= own_end
        def received(cols):
            remote(back.at[k, 0:cols], back.at[k, 0:cols], r_send, r_recv.at[k], me).wait_recv()

        @pl.when(away)
        def _():
            received(wide)

        @pl.when(jnp.logical_not(away))
        def _():
            received(wide - 1)

        for col in range(wide):
            here = jnp.logical_and(q == col, jnp.logical_not(away))

            @pl.when(here)
            def _():
                unpack(made_at(me, k), k, col)

            @pl.when(jnp.logical_not(here))
            def _():
                unpack(back.at[k, col], k, col)
        return carry

    def pack(which, target):
        def one(i, carry):
            rows = pl.ds(pl.multiple_of(i * 16, 16), 16)
            for x in range(2 * wide):
                start = pl.multiple_of((which * 2 * wide + x) * count * group + i * 16, 16)
                target[rows, x * LANES:(x + 1) * LANES] = joined[pl.ds(start, 16), :].astype(jnp.bfloat16)
            return carry

        lax.fori_loop(0, count * group // 16, one, 0, unroll=2)

    lax.fori_loop(0, jnp.minimum(group, parts - me), collect, 0)
    pack(0, crossed)
    fetch.wait()
    for n in range(0, LAGS, SPAN):
        lagged = jnp.dot(crossed[...], inverse[:, n:n + SPAN], preferred_element_type=jnp.float32)
        half_ref[:, n:n + SPAN] = (lagged * (1.0 / math.sqrt(F))).astype(jnp.bfloat16)
    lax.fori_loop(group, parts - me, collect, 0)
    pack(1, cross_ref)

    shipped(wide - 1, x_send)
    forwards = jnp.logical_or(both_ways, jnp.logical_and(inner_high, near))

    @pl.when(forwards)
    def _():
        shipped(2 * wide, f_send)

    @pl.when(jnp.logical_not(forwards))
    def _():
        shipped(wide, f_send)

    @pl.when(both_ways)
    def _():
        shipped(wide, g_send)

    for i in range(parts):
        layer, odd = i // wide, i % 2 == 1
        ends = base if layer == 0 else base + wide if layer == half - 1 and odd else parts + 1
        replies = sum(
            min(ends, d + pairs + 1) - d - 1 for d in range(layer * wide, (layer + 1) * wide) if d != i)
        if layer == half - 1 or (layer == half and odd):
            begins = base if layer == half - 1 else base + wide
            replies += sum(min(ends, d + pairs + 1) - begins for d in range(layer * wide))

        @pl.when(me == i)
        def _():
            done = made.at[0:replies]
            remote(done, done, r_send, r_recv.at[0], me).wait_send()


def meet(layers, wide, records, live_mask, offsets):
    pairs = offsets.shape[0]
    count, windows, length = records.shape
    parts = layers * wide
    pitch = (parts + 1) * count
    rows = count * windows
    width = 2 * LANES
    chunks = 2 * F // width
    table = np.ascontiguousarray(forward_table(length).reshape(length, chunks, width).transpose(1, 0, 2))
    return pl.pallas_call(
        functools.partial(middle_kernel, (layers, wide, windows)),
        out_shape=[
            jax.ShapeDtypeStruct((count * pairs // 2, LAGS), jnp.bfloat16),
            jax.ShapeDtypeStruct((count * pairs // 2, 2 * F), jnp.bfloat16),
            jax.ShapeDtypeStruct((2 * F, LAGS), jnp.bfloat16),
        ],
        in_specs=[
            pl.BlockSpec(memory_space=pltpu.HBM),
            pl.BlockSpec(memory_space=pltpu.HBM),
            pl.BlockSpec(memory_space=pltpu.HBM),
            pl.BlockSpec(memory_space=pltpu.HBM),
            pl.BlockSpec(memory_space=pltpu.HBM),
        ],
        out_specs=[pl.BlockSpec(memory_space=pltpu.VMEM)] * 3,
        scratch_shapes=[
            pltpu.SMEM((pairs,), jnp.int32),
            pltpu.SMEM((count,), jnp.int32),
            pltpu.VMEM((rows, length), jnp.bfloat16),
            pltpu.VMEM((chunks, length, width), jnp.bfloat16),
            pltpu.VMEM((count * pairs // 2, 2 * F), jnp.bfloat16),
            pltpu.VMEM((rows, 2 * F), jnp.float32),
            pltpu.VMEM((2 * wide, rows, LANES), jnp.bfloat16),
            pltpu.VMEM((parts, 2, rows, LANES), jnp.bfloat16),
            pltpu.VMEM((2 * windows * pitch, LANES), jnp.float32),
            pltpu.VMEM((parts * pairs, 2, count, LANES), jnp.bfloat16),
            pltpu.VMEM((pairs, wide, 2, count, LANES), jnp.bfloat16),
            pltpu.VMEM((2 * wide * count * pairs, LANES), jnp.float32),
            pltpu.SemaphoreType.DMA((chunks + 3,)),
            pltpu.SemaphoreType.DMA,
            pltpu.SemaphoreType.DMA,
            pltpu.SemaphoreType.DMA,
            pltpu.SemaphoreType.DMA((parts,)),
            pltpu.SemaphoreType.DMA,
            pltpu.SemaphoreType.DMA((pairs,)),
        ],
        compiler_params=pltpu.CompilerParams(
            vmem_limit_bytes=36 * 1024 * 1024, collective_id=1, has_side_effects=True
        ),
    )(*[
        pltpu.with_memory_space_constraint(x, pltpu.HBM)
        for x in (offsets, live_mask, records.reshape(rows, length), jnp.asarray(table),
                  jnp.asarray(inverse_table(length)))
    ])


def finish_kernel(half_ref, cross_ref, table_ref, out_hbm, stage, sem):
    group = out_hbm.shape[1] // 2
    copies = [pltpu.make_async_copy(half_ref, out_hbm.at[:, 0:group], sem.at[0])]
    copies[0].start()
    for i, n in enumerate(range(0, LAGS, SPAN)):
        lagged = jnp.dot(cross_ref[...], table_ref[:, n:n + SPAN], preferred_element_type=jnp.float32)
        lagged = (lagged * (1.0 / math.sqrt(F))).astype(jnp.bfloat16)
        stage[:, :, n:n + SPAN] = lagged.reshape(stage.shape[0], group, SPAN)
        copies.append(pltpu.make_async_copy(
            stage.at[:, :, n:n + SPAN], out_hbm.at[:, group:2 * group, n:n + SPAN], sem.at[i + 1]))
        copies[-1].start()
    for one in copies:
        one.wait()


def finish(half, cross, table, count, pairs):
    return pl.pallas_call(
        finish_kernel,
        out_shape=jax.ShapeDtypeStruct((count, pairs, LAGS), jnp.bfloat16),
        in_specs=[pl.BlockSpec(memory_space=pltpu.VMEM)] * 3,
        out_specs=pl.BlockSpec(memory_space=pltpu.HBM),
        scratch_shapes=[
            pltpu.VMEM((count, pairs // 2, LAGS), jnp.bfloat16),
            pltpu.SemaphoreType.DMA((LAGS // SPAN + 1,)),
        ],
        compiler_params=pltpu.CompilerParams(vmem_limit_bytes=16 * 1024 * 1024),
    )(half.reshape(count, pairs // 2, LAGS), cross, table)


def shards(columns, records, live_mask, offsets):
    count, windows, length = records.shape
    pairs = offsets.shape[0]
    wide = 2 * columns
    layers = lax.axis_size("chan") // wide
    reach = (BAND + count - 2) // count
    depth = min(layers - 1, (wide - 1 + reach) // wide)
    pieces = PIECES
    fold = columns == 2 and depth == layers - 1 and depth >= 2 and layers * wide == pairs and pairs * count == BAND
    if (
        columns == 2 and layers == 4 and layers * wide == pairs and pairs * count == BAND
        and F == wide * LANES and windows == 8 and count % 16 == 0
    ):
        half, cross, inverse = meet(layers, wide, records, live_mask, offsets)
        return finish(half, cross, inverse, count, pairs)
    spectra = whiten(records, live_mask).reshape(count, windows * 8, LANES)
    slots = (depth + 1) * wide
    cross = pl.pallas_call(
        functools.partial(reach_kernel, (layers, columns, depth, pieces, windows, fold)),
        out_shape=jax.ShapeDtypeStruct((count, pairs, 8, LANES), jnp.float32),
        in_specs=[
            pl.BlockSpec(memory_space=pltpu.SMEM),
            pl.BlockSpec(memory_space=pltpu.VMEM),
        ],
        out_specs=pl.BlockSpec(memory_space=pltpu.VMEM),
        scratch_shapes=[
            pltpu.VMEM((slots + wide, count, windows * 8, LANES), jnp.bfloat16),
            pltpu.VMEM((slots * count, windows * 8, LANES), jnp.bfloat16),
            pltpu.VMEM((count, windows * 8, LANES), jnp.float32),
            pltpu.VMEM((count, windows * 8, LANES), jnp.float32),
            pltpu.VMEM((wide, count, 8, LANES), jnp.bfloat16),
            pltpu.VMEM((wide, count, 8, LANES), jnp.bfloat16),
        ]
        + [pltpu.SemaphoreType.DMA((depth + 2, pieces))] * 9
        + [pltpu.SemaphoreType.DMA((wide,))] * 2,
        compiler_params=pltpu.CompilerParams(
            vmem_limit_bytes=40 * 1024 * 1024, collective_id=0, has_side_effects=True
        ),
    )(offsets, spectra)
    return lags(cross.astype(jnp.bfloat16).reshape(count * pairs, 8 * LANES), count, pairs, length)


def lags(cross, count, pairs, length):
    result = jnp.dot(cross, jnp.asarray(inverse_table(length)), preferred_element_type=jnp.float32)
    result = result * (1.0 / math.sqrt(F))
    return result.reshape(count, pairs, LAGS).astype(jnp.bfloat16)


def solution(mesh):
    in_specs = (P(("day", "chan"), None, None), P(("day", "chan")), P())
    out_specs = P(("day", "chan"), None, None)
    columns = max(1, LAYER_CHIPS // mesh.shape["day"])
    body = functools.partial(shards, columns)
    return jax.shard_map(body, mesh=mesh, in_specs=in_specs, out_specs=out_specs, check_vma=False)
```

```python
import functools
import math

import jax
import jax.numpy as jnp
import numpy as np
from jax import lax
from jax.experimental import pallas as pl
from jax.experimental.pallas import tpu as pltpu
from jax.sharding import PartitionSpec as P

F = 512
F0 = 6
LAGS = 2048
LANES = 128
SPAN = 512
BAND = 512
PIECES = 4
LAYER_CHIPS = 4


def forward_table(length):
    samples = np.arange(length, dtype=np.int64)
    freqs = F0 + np.arange(F, dtype=np.int64)
    phase = np.mod(samples[:, None] * freqs[None, :], length)
    angle = 2.0 * math.pi / length * phase
    return np.concatenate([np.cos(angle), -np.sin(angle)], axis=1).astype(np.float32).astype(jnp.bfloat16)


def inverse_table(length):
    freqs = F0 + np.arange(F, dtype=np.int64)
    shifts = np.arange(LAGS, dtype=np.int64) - LAGS // 2
    phase = np.mod(freqs[:, None] * shifts[None, :], length)
    angle = 2.0 * math.pi / length * phase
    return np.concatenate([np.cos(angle), -np.sin(angle)], axis=0).astype(np.float32).astype(jnp.bfloat16)


def whiten(records, live_mask):
    count, windows, length = records.shape
    spectrum = jnp.dot(
        records.reshape(count * windows, length),
        jnp.asarray(forward_table(length)),
        preferred_element_type=jnp.float32,
    )
    power = jnp.mean(spectrum * spectrum, axis=1, keepdims=True)
    gain = jnp.repeat(live_mask.astype(jnp.float32), windows)[:, None]
    white = spectrum * (gain * lax.rsqrt(power + 1e-06))
    return white.astype(jnp.bfloat16)


def reach_kernel(shape, offsets_ref, white_ref, cross_ref, held, ext, own, swapped, made, back,
                 z_send, z_recv, c_send, c_recv, y_send, y_recv, d_send, d_recv, e_send, r_send, r_recv):
    layers, columns, depth, pieces, windows, fold = shape
    count, slab = white_ref.shape[0], white_ref.shape[1]
    pairs = offsets_ref.shape[0]
    wide = 2 * columns
    total = layers * wide * count
    me = lax.axis_index("chan")
    z, q = me // wide, me % wide
    y, c = q // 2, q % 2
    sibling = me + 1 - 2 * c
    sib_q = q + 1 - 2 * c
    mate = me + 2 - 4 * y
    mate_q = q + 2 - 4 * y
    far_q = sib_q + 2 - 4 * y
    step = count // pieces
    top, lifted = layers - 1, depth + 1

    barrier = pltpu.get_barrier_semaphore()

    def greet(device):
        pl.semaphore_signal(barrier, inc=1, device_id={"chan": device}, device_id_type=pl.DeviceIdType.MESH)

    greet(sibling)
    if columns == 2:
        greet(mate)

    @pl.when(z >= 1)
    def _():
        greet(me - wide)

    @pl.when(z < layers - 1)
    def _():
        greet(me + wide)

    below, above = jnp.minimum(z, 1), jnp.minimum(top - z, 1)
    peers = columns + below + above
    if fold:
        @pl.when(z == 0)
        def _():
            for i in range(wide):
                greet(top * wide + i)

        @pl.when(z == top)
        def _():
            for i in range(wide):
                greet(jnp.int32(i))

        peers = peers + wide * (2 - below - above)
    pl.semaphore_wait(barrier, peers)

    def rows(p):
        return pl.ds(p * step, step)

    def mine(dz, p):
        return white_ref.at[rows(p)] if dz == 0 else held.at[dz * wide + q, rows(p)]

    def copy(source, slot, p, send, recv, device):
        return pltpu.make_async_remote_copy(
            src_ref=source,
            dst_ref=held.at[slot, rows(p)],
            send_sem=send,
            recv_sem=recv,
            device_id={"chan": device},
            device_id_type=pl.DeviceIdType.MESH,
        )

    def down(dz, p):
        return copy(mine(dz, p), (dz + 1) * wide + q, p, z_send.at[dz, p], z_recv.at[dz + 1, p], me - wide)

    def from_above(dz, p):
        return copy(mine(dz, p), dz * wide + q, p, z_send.at[dz, p], z_recv.at[dz, p], me)

    def across(dz, p, slot):
        return copy(mine(dz, p), slot, p, c_send.at[dz, p], c_recv.at[dz, p], sibling)

    def over(dz, p, slot):
        return copy(mine(dz, p), slot, p, y_send.at[dz, p], y_recv.at[dz, p], mate)

    def onward(dz, p, slot):
        return copy(held.at[dz * wide + mate_q, rows(p)], slot, p, d_send.at[dz, p], d_recv.at[dz, p], sibling)

    def both(*conditions):
        joined = conditions[0]
        for condition in conditions[1:]:
            joined = jnp.logical_and(joined, condition)
        return joined

    def exists(dz):
        return z + dz < layers

    def goes(dz, at_start, at_end):
        if dz == lifted:
            return z == top
        if dz == 0:
            return at_start
        if fold and dz == depth:
            return both(exists(dz), at_end)
        return exists(dz)

    def z_tx(dz):
        if fold and dz + 1 == depth:
            return both(exists(dz), z >= 1, jnp.logical_or(z >= 2, q == 0))
        return both(exists(dz), z >= 1)

    def z_rx(dz):
        return goes(dz, None, q == 0)

    def c_tx(dz):
        return goes(dz, c == 1, q == 0)

    def c_rx(dz):
        return goes(dz, c == 0, q == 1)

    def y_tx(dz):
        return goes(dz, y == 1, q == 0)

    def y_rx(dz):
        return goes(dz, y == 0, q == 2)

    def detoured(dz, p):
        return fold and dz == depth - 1 and p == pieces - 1

    def over_tx(dz, p):
        if detoured(dz, p):
            return both(y_tx(dz), jnp.logical_or(z > 0, y == 0))
        if raised(dz, p):
            return both(y_tx(dz), y == 0)
        return y_tx(dz)

    def raised(dz, p):
        return fold and dz == lifted and p >= pieces // 2

    def lift_mate(p):
        return copy(held.at[mate_q, rows(p)], lifted * wide + mate_q, p,
                    e_send.at[lifted, p], y_recv.at[lifted, p], me + top * wide)

    def extra(dz, p):
        return copy(held.at[dz * wide + mate_q, rows(p)], (dz + 1) * wide + mate_q, p,
                    e_send.at[dz, p], y_recv.at[dz + 1, p], me - wide)

    def extra_tx():
        return both(z == 1, y == 0)

    def d_rx(dz):
        return goes(dz, y == 0, q == 3)

    def lift(p):
        return copy(white_ref.at[rows(p)], lifted * wide + q, p, z_send.at[lifted, p], z_recv.at[lifted, p],
                    me + top * wide)

    def sends(dz):
        for p in range(pieces):
            if dz > 0:
                @pl.when(z_rx(dz))
                def _():
                    from_above(dz, p).wait_recv()
            if dz < depth:
                @pl.when(z_tx(dz))
                def _():
                    down(dz, p).start()
            if columns == 2:
                @pl.when(over_tx(dz, p))
                def _():
                    over(dz, p, dz * wide + q).start()
            @pl.when(c_tx(dz))
            def _():
                across(dz, p, dz * wide + q).start()

    def passes(dz):
        if columns == 2:
            for p in range(pieces):
                @pl.when(y_rx(dz))
                def _():
                    over(dz, p, dz * wide + mate_q).wait_recv()
                    onward(dz, p, dz * wide + mate_q).start()
                if dz == 0 and raised(lifted, p):
                    @pl.when(both(z == 0, y == 0))
                    def _():
                        lift_mate(p).start()
                if detoured(dz + 1, p):
                    @pl.when(extra_tx())
                    def _():
                        extra(dz, p).start()

    def arrives(dz):
        for p in range(pieces):
            @pl.when(c_rx(dz))
            def _():
                across(dz, p, dz * wide + sib_q).wait_recv()
            if columns == 2:
                @pl.when(d_rx(dz))
                def _():
                    onward(dz, p, dz * wide + far_q).wait_recv()

    def finishes(dz):
        for p in range(pieces):
            if dz < depth:
                @pl.when(z_tx(dz))
                def _():
                    down(dz, p).wait_send()
            if columns == 2:
                @pl.when(over_tx(dz, p))
                def _():
                    over(dz, p, dz * wide + q).wait_send()
                if detoured(dz + 1, p):
                    @pl.when(extra_tx())
                    def _():
                        extra(dz, p).wait_send()
                @pl.when(y_rx(dz))
                def _():
                    onward(dz, p, dz * wide + mate_q).wait_send()
            @pl.when(c_tx(dz))
            def _():
                across(dz, p, dz * wide + q).wait_send()

    def answer(i):
        return pltpu.make_async_remote_copy(
            src_ref=made.at[i],
            dst_ref=back.at[q],
            send_sem=r_send.at[i],
            recv_sem=r_recv.at[q],
            device_id={"chan": jnp.int32(i)},
            device_id_type=pl.DeviceIdType.MESH,
        )

    def answered(i):
        return pltpu.make_async_remote_copy(
            src_ref=made.at[i],
            dst_ref=back.at[i],
            send_sem=r_send.at[i],
            recv_sem=r_recv.at[i],
            device_id={"chan": me},
            device_id_type=pl.DeviceIdType.MESH,
        )

    low = lax.broadcasted_iota(jnp.int32, (8, LANES), 0) < 4

    def prepare(i, carry):
        raw = white_ref[i]
        value = raw.astype(jnp.float32)
        own[i] = value
        ext[q * count + i] = raw
        for w in range(windows):
            swapped[i, w * 8 : w * 8 + 8] = pltpu.roll(value[w * 8 : w * 8 + 8], 4, 0)
        return carry

    def settle(dz):
        def one(l):
            def fill(i, carry):
                ext[(dz * wide + l) * count + i] = held[dz * wide + l, i]
                return carry
            lax.fori_loop(0, count, fill, 0, unroll=4)

        if dz == 0:
            for l in range(1, wide):
                @pl.when(q < l)
                def _():
                    one(l)
        else:
            @pl.when(exists(dz))
            def _():
                for l in range(1 if fold and dz == depth else wide):
                    one(l)

    live = jnp.minimum(layers * wide - me, pairs)

    def outside():
        def nothing(k, carry):
            for r in range(count):
                cross_ref[r, k] = jnp.zeros((8, LANES), jnp.float32)
            return carry

        lax.fori_loop(live, pairs, nothing, 0)

        @pl.when(layers - z <= depth)
        def _():
            def blank(i, carry):
                ext[(layers - z) * wide * count + i] = jnp.zeros((slab, LANES), jnp.bfloat16)
                return carry

            lax.fori_loop(0, 2 * count, blank, 0, unroll=4)

    def reached(dz):
        if dz < 0:
            return 0
        if dz == depth:
            return live
        return jnp.minimum((dz + 1) * wide - q - 1, live)

    def multiply(dz):
        def pair(k, carry):
            shift = offsets_ref[k]

            def channel(i, inner):
                place = me * count + i + shift
                keep = jnp.where(place < total, 1.0 / windows, 0.0)
                near = jnp.minimum(q * count + i + shift, ext.shape[0] - 1)
                partner = ext[near].astype(jnp.float32)
                straight = own[i, :8] * partner[:8]
                twisted = swapped[i, :8] * partner[:8]
                for w in range(1, windows):
                    part = slice(w * 8, w * 8 + 8)
                    straight += own[i, part] * partner[part]
                    twisted += swapped[i, part] * partner[part]
                joined = jnp.where(
                    low,
                    straight + pltpu.roll(straight, 4, 0),
                    pltpu.roll(twisted, 4, 0) - twisted,
                )
                cross_ref[i, k] = joined * keep
                return inner

            return lax.fori_loop(0, count, channel, carry, unroll=4)

        begin, end = reached(dz - 1), reached(dz)
        if fold and dz == depth:
            @pl.when(z == 0)
            def _():
                lax.fori_loop(begin, begin + 1, pair, 0)

            @pl.when(z > 0)
            def _():
                lax.fori_loop(begin, end, pair, 0)
        else:
            lax.fori_loop(begin, end, pair, 0)

    def reply():
        for i in range(wide):
            shift = offsets_ref[top * wide + q - i]

            def channel(r, carry):
                place = i * count + r + shift
                keep = jnp.where(place < total, 1.0 / windows, 0.0)
                near = jnp.clip(place - top * wide * count, 0, ext.shape[0] - 1)
                partner = ext[near].astype(jnp.float32)
                value = held[lifted * wide + i, r].astype(jnp.float32)
                straight = value[:8] * partner[:8]
                twisted = pltpu.roll(value[:8], 4, 0) * partner[:8]
                for w in range(1, windows):
                    part = slice(w * 8, w * 8 + 8)
                    straight += value[part] * partner[part]
                    twisted += pltpu.roll(value[part], 4, 0) * partner[part]
                joined = jnp.where(
                    low,
                    straight + pltpu.roll(straight, 4, 0),
                    pltpu.roll(twisted, 4, 0) - twisted,
                )
                made[i, r] = (joined * keep).astype(jnp.bfloat16)
                return carry

            lax.fori_loop(0, count, channel, 0, unroll=4)
        for i in range(wide):
            answer(i).start()

    sends(0)
    if fold:
        @pl.when(z == 0)
        def _():
            for p in range(pieces):
                lift(p).start()

    lax.fori_loop(0, count, prepare, 0)
    outside()
    for dz in range(depth + 1):
        if dz < depth:
            sends(dz + 1)
        if fold and dz == 0:
            sends(lifted)
        passes(dz)
        if fold and dz == 0:
            passes(lifted)
        arrives(dz)
        settle(dz)
        if fold and dz == 0:
            arrives(lifted)

            @pl.when(z == top)
            def _():
                reply()

        multiply(dz)

    if fold:
        @pl.when(z == 0)
        def _():
            for i in range(wide):
                answered(i).wait_recv()

                def take(r, carry):
                    cross_ref[r, top * wide - q + i] = back[i, r].astype(jnp.float32)
                    return carry

                lax.fori_loop(0, count, take, 0, unroll=4)
            for p in range(pieces):
                lift(p).wait_send()
                if raised(lifted, p):
                    @pl.when(y == 0)
                    def _():
                        lift_mate(p).wait_send()

        @pl.when(z == top)
        def _():
            for i in range(wide):
                answer(i).wait_send()

        finishes(lifted)
    for dz in range(depth + 1):
        finishes(dz)


def middle_kernel(shape, offsets_hbm, mask_hbm, records_hbm, table_hbm, inverse_hbm, half_ref, cross_ref, inverse,
                  offsets_ref, mask_ref, records, table, crossed, spectrum, white, held, spec, made, back, joined,
                  l_sem, x_send, f_send, g_send, s_recv, r_send, r_recv):
    layers, wide, windows = shape
    pairs = offsets_ref.shape[0]
    count = records.shape[0] // windows
    chunks, width = table.shape[0], table.shape[2]
    load = [pltpu.make_async_copy(records_hbm, records, l_sem.at[chunks])]
    for n in range(chunks):
        load.append(pltpu.make_async_copy(table_hbm.at[n], table.at[n], l_sem.at[n]))
    load.append(pltpu.make_async_copy(offsets_hbm, offsets_ref, l_sem.at[chunks + 1]))
    load.append(pltpu.make_async_copy(mask_hbm, mask_ref, l_sem.at[chunks + 2]))
    for one in load:
        one.start()
    parts = layers * wide
    pitch = spec.shape[0] // (2 * windows)
    half, top, last = layers // 2, layers - 1, parts - 1
    me = lax.axis_index("chan")
    z, q = me // wide, me % wide
    c = q % 2
    first = z * wide
    base = half * wide
    sib_q = q + 1 - 2 * c
    mate_q = (q + 2) % wide
    far_q = (sib_q + 2) % wide
    near = c == 0
    inner_low, inner_high = z == half - 1, z == half
    neighbour = jnp.where(
        jnp.logical_or(z == 0, jnp.logical_and(inner_low, c == 1)), me + wide, me - wide)
    own_end = jnp.where(
        z == 0, base, jnp.where(jnp.logical_and(inner_low, c == 1), base + wide, parts + 1))
    barrier = pltpu.get_barrier_semaphore()

    def greet(device, condition):
        @pl.when(condition)
        def _():
            pl.semaphore_signal(barrier, inc=1, device_id={"chan": jnp.int32(device)},
                                device_id_type=pl.DeviceIdType.MESH)

    for col in (sib_q, mate_q, far_q):
        greet(first + col, z >= 0)
    for i in range(wide):
        odd = i % 2 == 1
        greet(wide + i, z == 0)
        if odd:
            greet(base + i, z < half)
        else:
            greet(base + i, jnp.logical_and(inner_low, q == i))
    greet(me - wide, jnp.logical_or(inner_low, jnp.logical_and(inner_high, c == 1)))
    greet(me + wide, inner_high)
    replies_far = jnp.where(inner_low, wide, jnp.where(jnp.logical_and(inner_high, c == 1), 2 * wide - 1, 0))
    ships_there = jnp.where(jnp.logical_and(inner_low, near), 0, 1)

    load[0].wait()
    def transform(n, carry):
        pltpu.make_async_copy(table_hbm.at[n], table.at[n], l_sem.at[n]).wait()
        spectrum[n] = jnp.dot(records[...], table[n], preferred_element_type=jnp.float32)
        return carry

    lax.fori_loop(0, chunks, transform, 0)
    for one in load[chunks + 1:]:
        one.wait()
    upper = lax.broadcasted_iota(jnp.int32, (2 * windows, 1), 0) < windows

    def whitening(i, carry):
        rows = pl.ds(pl.multiple_of(i * 2 * windows, 2 * windows), 2 * windows)
        values = [
            spectrum[x * LANES // width, rows, x * LANES % width:x * LANES % width + LANES]
            for x in range(2 * wide)]
        square = values[0] * values[0]
        for value in values[1:]:
            square += value * value
        power = jnp.sum(square, axis=1, keepdims=True) * (1.0 / (2 * F))
        alive = jnp.where(upper, mask_ref[2 * i].astype(jnp.float32), mask_ref[2 * i + 1].astype(jnp.float32))
        gain = alive * lax.rsqrt(power + 1e-06)
        for x, value in enumerate(values):
            white[x, rows] = (value * gain).astype(jnp.bfloat16)
        return carry

    lax.fori_loop(0, count // 2, whitening, 0, unroll=4)
    fetch = pltpu.make_async_copy(inverse_hbm, inverse, l_sem.at[0])
    fetch.start()
    pl.semaphore_wait(barrier, wide - 1 + replies_far + ships_there)

    def remote(source, target, send, recv, device):
        return pltpu.make_async_remote_copy(
            src_ref=source, dst_ref=target, send_sem=send, recv_sem=recv,
            device_id={"chan": device}, device_id_type=pl.DeviceIdType.MESH,
        )

    def piece(ri, col):
        return white.at[ri * wide + col]

    def swap(ri, col):
        return remote(piece(ri, col), held.at[me, ri], x_send, s_recv.at[me], first + col)

    def ship_own(ri):
        return remote(piece(ri, q), held.at[me, ri], f_send, s_recv.at[me], neighbour)

    def ship(s):
        return remote(held.at[s], held.at[s], f_send, s_recv.at[s], neighbour)

    both_ways = jnp.logical_and(inner_low, c == 1)

    def drop_own(ri):
        return remote(piece(ri, q), held.at[me, ri], g_send, s_recv.at[me], me - wide)

    def drop(s):
        return remote(held.at[s], held.at[s], g_send, s_recv.at[s], me - wide)

    def made_at(d, k):
        return made.at[d * pairs + k]

    def reply(d, k):
        return remote(made_at(d, k), back.at[k, q], r_send, r_recv.at[k], d)

    def shipped(slots, send):
        remote(held.at[0:slots], held.at[0:slots], send, s_recv.at[0], neighbour).wait_send()

    for ri in range(2):
        ship_own(ri).start()

    @pl.when(both_ways)
    def _():
        for ri in range(2):
            drop_own(ri).start()
    columns = (sib_q, mate_q, far_q)
    for col in columns:
        for ri in range(2):
            swap(ri, col).start()

    def settle(s, load):
        for ri in range(2):
            def one(i, carry):
                value = load(ri, i).astype(jnp.float32)
                for part in range(2):
                    row = ri * windows * pitch + s * count + 2 * i + part
                    spec[pl.ds(row, windows, stride=pitch), :] = value[part * windows:(part + 1) * windows]
                return carry

            lax.fori_loop(0, count // 2, one, 0, unroll=4)

    def own_rows(ri, i):
        return white[ri * wide + q, pl.ds(pl.multiple_of(i * 2 * windows, 2 * windows), 2 * windows)]

    def take(s, onward=None, downward=None):
        ship(s).wait_recv()
        if onward is not None:
            @pl.when(onward)
            def _():
                ship(s).start()
        if downward is not None:
            @pl.when(downward)
            def _():
                drop(s).start()
        settle(s, lambda ri, i: held[s, ri, pl.ds(pl.multiple_of(i * 2 * windows, 2 * windows), 2 * windows)])

    def block(d, k):
        shift = offsets_ref[k]
        for g in range(count // 16):
            mine = d * count + g * 16
            real = imag = None
            for w in range(windows):
                cr = spec[pl.ds(pl.multiple_of(w * pitch + mine, 8), 16), :]
                ci = spec[pl.ds(pl.multiple_of((windows + w) * pitch + mine, 8), 16), :]
                pr = spec[pl.ds(w * pitch + mine + shift, 16), :]
                pi = spec[pl.ds((windows + w) * pitch + mine + shift, 16), :]
                re, im = cr * pr + ci * pi, ci * pr - cr * pi
                real, imag = (re, im) if w == 0 else (real + re, imag + im)
            rows = slice(g * 16, g * 16 + 16)
            made[d * pairs + k, 0, rows] = (real * (1.0 / windows)).astype(jnp.bfloat16)
            made[d * pairs + k, 1, rows] = (imag * (1.0 / windows)).astype(jnp.bfloat16)

    def spans(d_begin, d_end, u_begin, u_end, visit):
        def reach(u, carry):
            def one(d, inner):
                visit(d, u - 1 - d)
                return inner

            return lax.fori_loop(jnp.maximum(d_begin, u - pairs), jnp.minimum(d_end, u), one, carry)

        lax.fori_loop(u_begin, u_end, reach, 0)

    def give(d, k):
        @pl.when(d != me)
        def _():
            reply(d, k).start()

    def blocks(*span):
        spans(*span, block)
        spans(*span, give)

    for x in range(2 * windows):
        spec[pl.ds(x * pitch + parts * count, count), :] = jnp.zeros((count, LANES), jnp.float32)

    def clear(i, carry):
        joined[pl.ds(pl.multiple_of(i * 64, 64), 64), :] = jnp.zeros((64, LANES), jnp.float32)
        return carry

    lax.fori_loop(0, joined.shape[0] // 64, clear, 0)

    y = q // 2
    pair_1, pair_2 = (q, sib_q), (mate_q, far_q)

    def reached_1(start, more=0):
        return jnp.where(y == 0, start, start + 3), jnp.where(y == 0, start + 2, start + wide + more)

    def reached_2(start, more=0):
        return jnp.where(y == 0, start + 2, start), jnp.where(y == 0, start + wide + more, start + 3)

    settle(me, own_rows)
    for col in columns:
        take(first + col, z >= 0, both_ways)
    blocks(first, first + wide, first + 1, first + wide + jnp.where(z == top, 1, 0))

    @pl.when(z == 0)
    def _():
        for group, reached in ((pair_1, reached_1), (pair_2, reached_2)):
            for col in group:
                take(wide + col)
            blocks(0, wide, *reached(wide))

    @pl.when(inner_low)
    def _():
        def lower(group):
            for col in group:
                take(col, jnp.logical_not(near))

        lower(pair_1)
        for col in pair_1:
            take(base + col)
        blocks(2 * y, 2 * y + 2, *reached_1(base))
        blocks(wide, base, *reached_1(base))
        lower(pair_2)
        blocks(2 - 2 * y, wide - 2 * y, *reached_1(base))
        for col in pair_2:
            take(base + col)
        blocks(0, base, *reached_2(base))

        @pl.when(near)
        def _():
            for group, reached in ((pair_1, reached_1), (pair_2, reached_2)):
                for col in group:
                    take(top * wide + col)
                blocks(0, base, *reached(top * wide, 1))

    @pl.when(inner_high)
    def _():
        for group, reached in ((pair_1, reached_1), (pair_2, reached_2)):
            for col in group:
                take(top * wide + col, near)
            blocks(base, base + wide, *reached(top * wide, 1))

        @pl.when(jnp.logical_not(near))
        def _():
            for col in pair_1 + pair_2:
                take(wide + col)
            spans(wide, base, top * wide, parts + 1, block)
            for col in pair_1:
                take(col)
            blocks(2 * y, 2 * y + 2, top * wide, parts + 1)
            for col in pair_2:
                take(col)
            blocks(2 - 2 * y, wide - 2 * y, top * wide, parts + 1)
            spans(wide, base, top * wide, parts + 1, give)

    group = pairs // 2

    def unpack(source, k, col):
        for ri in range(2):
            for g in range(count // 16):
                value = source[ri, g * 16:g * 16 + 16].astype(jnp.float32)
                for part in range(2):
                    seg = (k // group) * 2 * wide + ri * wide + col
                    row = (seg * count + g * 16 + part * 8) * group + k % group
                    joined[pl.ds(row, 8, stride=group), :] = value[part * 8:part * 8 + 8]

    def collect(k, carry):
        away = me + k + 1 >= own_end
        def received(cols):
            remote(back.at[k, 0:cols], back.at[k, 0:cols], r_send, r_recv.at[k], me).wait_recv()

        @pl.when(away)
        def _():
            received(wide)

        @pl.when(jnp.logical_not(away))
        def _():
            received(wide - 1)

        for col in range(wide):
            here = jnp.logical_and(q == col, jnp.logical_not(away))

            @pl.when(here)
            def _():
                unpack(made_at(me, k), k, col)

            @pl.when(jnp.logical_not(here))
            def _():
                unpack(back.at[k, col], k, col)
        return carry

    def pack(which, target):
        def one(i, carry):
            rows = pl.ds(pl.multiple_of(i * 16, 16), 16)
            for x in range(2 * wide):
                start = pl.multiple_of((which * 2 * wide + x) * count * group + i * 16, 16)
                target[rows, x * LANES:(x + 1) * LANES] = joined[pl.ds(start, 16), :].astype(jnp.bfloat16)
            return carry

        lax.fori_loop(0, count * group // 16, one, 0, unroll=2)

    lax.fori_loop(0, jnp.minimum(group, parts - me), collect, 0)
    pack(0, crossed)
    fetch.wait()

    def invert(n, carry):
        span = pl.ds(pl.multiple_of(n * SPAN, SPAN), SPAN)
        lagged = jnp.dot(crossed[...], inverse[:, span], preferred_element_type=jnp.float32)
        half_ref[:, span] = (lagged * (1.0 / math.sqrt(F))).astype(jnp.bfloat16)
        return carry

    lax.fori_loop(0, LAGS // SPAN, invert, 0)
    lax.fori_loop(group, parts - me, collect, 0)
    pack(1, cross_ref)

    shipped(wide - 1, x_send)
    forwards = jnp.logical_or(both_ways, jnp.logical_and(inner_high, near))

    @pl.when(forwards)
    def _():
        shipped(2 * wide, f_send)

    @pl.when(jnp.logical_not(forwards))
    def _():
        shipped(wide, f_send)

    @pl.when(both_ways)
    def _():
        shipped(wide, g_send)

    for i in range(parts):
        layer, odd = i // wide, i % 2 == 1
        ends = base if layer == 0 else base + wide if layer == half - 1 and odd else parts + 1
        replies = sum(
            min(ends, d + pairs + 1) - d - 1 for d in range(layer * wide, (layer + 1) * wide) if d != i)
        if layer == half - 1 or (layer == half and odd):
            begins = base if layer == half - 1 else base + wide
            replies += sum(min(ends, d + pairs + 1) - begins for d in range(layer * wide))

        @pl.when(me == i)
        def _():
            done = made.at[0:replies]
            remote(done, done, r_send, r_recv.at[0], me).wait_send()


def meet(layers, wide, records, live_mask, offsets):
    pairs = offsets.shape[0]
    count, windows, length = records.shape
    parts = layers * wide
    pitch = (parts + 1) * count
    rows = count * windows
    width = 2 * LANES
    chunks = 2 * F // width
    table = np.ascontiguousarray(forward_table(length).reshape(length, chunks, width).transpose(1, 0, 2))
    return pl.pallas_call(
        functools.partial(middle_kernel, (layers, wide, windows)),
        out_shape=[
            jax.ShapeDtypeStruct((count * pairs // 2, LAGS), jnp.bfloat16),
            jax.ShapeDtypeStruct((count * pairs // 2, 2 * F), jnp.bfloat16),
            jax.ShapeDtypeStruct((2 * F, LAGS), jnp.bfloat16),
        ],
        in_specs=[
            pl.BlockSpec(memory_space=pltpu.HBM),
            pl.BlockSpec(memory_space=pltpu.HBM),
            pl.BlockSpec(memory_space=pltpu.HBM),
            pl.BlockSpec(memory_space=pltpu.HBM),
            pl.BlockSpec(memory_space=pltpu.HBM),
        ],
        out_specs=[pl.BlockSpec(memory_space=pltpu.VMEM)] * 3,
        scratch_shapes=[
            pltpu.SMEM((pairs,), jnp.int32),
            pltpu.SMEM((count,), jnp.int32),
            pltpu.VMEM((rows, length), jnp.bfloat16),
            pltpu.VMEM((chunks, length, width), jnp.bfloat16),
            pltpu.VMEM((count * pairs // 2, 2 * F), jnp.bfloat16),
            pltpu.VMEM((chunks, rows, width), jnp.float32),
            pltpu.VMEM((2 * wide, rows, LANES), jnp.bfloat16),
            pltpu.VMEM((parts, 2, rows, LANES), jnp.bfloat16),
            pltpu.VMEM((2 * windows * pitch, LANES), jnp.float32),
            pltpu.VMEM((parts * pairs, 2, count, LANES), jnp.bfloat16),
            pltpu.VMEM((pairs, wide, 2, count, LANES), jnp.bfloat16),
            pltpu.VMEM((2 * wide * count * pairs, LANES), jnp.float32),
            pltpu.SemaphoreType.DMA((chunks + 3,)),
            pltpu.SemaphoreType.DMA,
            pltpu.SemaphoreType.DMA,
            pltpu.SemaphoreType.DMA,
            pltpu.SemaphoreType.DMA((parts,)),
            pltpu.SemaphoreType.DMA,
            pltpu.SemaphoreType.DMA((pairs,)),
        ],
        compiler_params=pltpu.CompilerParams(
            vmem_limit_bytes=36 * 1024 * 1024, collective_id=1, has_side_effects=True
        ),
    )(*[
        pltpu.with_memory_space_constraint(x, pltpu.HBM)
        for x in (offsets, live_mask, records.reshape(rows, length), jnp.asarray(table),
                  jnp.asarray(inverse_table(length)))
    ])


def finish_kernel(half_ref, cross_ref, table_ref, out_hbm, stage, sem):
    group = out_hbm.shape[1] // 2
    copies = [pltpu.make_async_copy(half_ref, out_hbm.at[:, 0:group], sem.at[0])]
    copies[0].start()
    for i, n in enumerate(range(0, LAGS, SPAN)):
        lagged = jnp.dot(cross_ref[...], table_ref[:, n:n + SPAN], preferred_element_type=jnp.float32)
        lagged = (lagged * (1.0 / math.sqrt(F))).astype(jnp.bfloat16)
        stage[:, :, n:n + SPAN] = lagged.reshape(stage.shape[0], group, SPAN)
        copies.append(pltpu.make_async_copy(
            stage.at[:, :, n:n + SPAN], out_hbm.at[:, group:2 * group, n:n + SPAN], sem.at[i + 1]))
        copies[-1].start()
    for one in copies:
        one.wait()


def finish(half, cross, table, count, pairs):
    return pl.pallas_call(
        finish_kernel,
        out_shape=jax.ShapeDtypeStruct((count, pairs, LAGS), jnp.bfloat16),
        in_specs=[pl.BlockSpec(memory_space=pltpu.VMEM)] * 3,
        out_specs=pl.BlockSpec(memory_space=pltpu.HBM),
        scratch_shapes=[
            pltpu.VMEM((count, pairs // 2, LAGS), jnp.bfloat16),
            pltpu.SemaphoreType.DMA((LAGS // SPAN + 1,)),
        ],
        compiler_params=pltpu.CompilerParams(vmem_limit_bytes=16 * 1024 * 1024),
    )(half.reshape(count, pairs // 2, LAGS), cross, table)


def shards(columns, records, live_mask, offsets):
    count, windows, length = records.shape
    pairs = offsets.shape[0]
    wide = 2 * columns
    layers = lax.axis_size("chan") // wide
    reach = (BAND + count - 2) // count
    depth = min(layers - 1, (wide - 1 + reach) // wide)
    pieces = PIECES
    fold = columns == 2 and depth == layers - 1 and depth >= 2 and layers * wide == pairs and pairs * count == BAND
    if (
        columns == 2 and layers == 4 and layers * wide == pairs and pairs * count == BAND
        and F == wide * LANES and windows == 8 and count % 16 == 0
    ):
        half, cross, inverse = meet(layers, wide, records, live_mask, offsets)
        return finish(half, cross, inverse, count, pairs)
    spectra = whiten(records, live_mask).reshape(count, windows * 8, LANES)
    slots = (depth + 1) * wide
    cross = pl.pallas_call(
        functools.partial(reach_kernel, (layers, columns, depth, pieces, windows, fold)),
        out_shape=jax.ShapeDtypeStruct((count, pairs, 8, LANES), jnp.float32),
        in_specs=[
            pl.BlockSpec(memory_space=pltpu.SMEM),
            pl.BlockSpec(memory_space=pltpu.VMEM),
        ],
        out_specs=pl.BlockSpec(memory_space=pltpu.VMEM),
        scratch_shapes=[
            pltpu.VMEM((slots + wide, count, windows * 8, LANES), jnp.bfloat16),
            pltpu.VMEM((slots * count, windows * 8, LANES), jnp.bfloat16),
            pltpu.VMEM((count, windows * 8, LANES), jnp.float32),
            pltpu.VMEM((count, windows * 8, LANES), jnp.float32),
            pltpu.VMEM((wide, count, 8, LANES), jnp.bfloat16),
            pltpu.VMEM((wide, count, 8, LANES), jnp.bfloat16),
        ]
        + [pltpu.SemaphoreType.DMA((depth + 2, pieces))] * 9
        + [pltpu.SemaphoreType.DMA((wide,))] * 2,
        compiler_params=pltpu.CompilerParams(
            vmem_limit_bytes=40 * 1024 * 1024, collective_id=0, has_side_effects=True
        ),
    )(offsets, spectra)
    return lags(cross.astype(jnp.bfloat16).reshape(count * pairs, 8 * LANES), count, pairs, length)


def lags(cross, count, pairs, length):
    result = jnp.dot(cross, jnp.asarray(inverse_table(length)), preferred_element_type=jnp.float32)
    result = result * (1.0 / math.sqrt(F))
    return result.reshape(count, pairs, LAGS).astype(jnp.bfloat16)


def solution(mesh):
    in_specs = (P(("day", "chan"), None, None), P(("day", "chan")), P())
    out_specs = P(("day", "chan"), None, None)
    columns = max(1, LAYER_CHIPS // mesh.shape["day"])
    body = functools.partial(shards, columns)
    return jax.shard_map(body, mesh=mesh, in_specs=in_specs, out_specs=out_specs, check_vma=False)
```

```python
import functools
import math

import jax
import jax.numpy as jnp
import numpy as np
from jax import lax
from jax.experimental import pallas as pl
from jax.experimental.pallas import tpu as pltpu
from jax.sharding import PartitionSpec as P

F = 512
F0 = 6
LAGS = 2048
LANES = 128
SPAN = 512
BAND = 512
PIECES = 4
LAYER_CHIPS = 4


def forward_table(length):
    samples = np.arange(length, dtype=np.int64)
    freqs = F0 + np.arange(F, dtype=np.int64)
    phase = np.mod(samples[:, None] * freqs[None, :], length)
    angle = 2.0 * math.pi / length * phase
    return np.concatenate([np.cos(angle), -np.sin(angle)], axis=1).astype(np.float32).astype(jnp.bfloat16)


def inverse_table(length):
    freqs = F0 + np.arange(F, dtype=np.int64)
    shifts = np.arange(LAGS, dtype=np.int64) - LAGS // 2
    phase = np.mod(freqs[:, None] * shifts[None, :], length)
    angle = 2.0 * math.pi / length * phase
    return np.concatenate([np.cos(angle), -np.sin(angle)], axis=0).astype(np.float32).astype(jnp.bfloat16)


def whiten(records, live_mask):
    count, windows, length = records.shape
    spectrum = jnp.dot(
        records.reshape(count * windows, length),
        jnp.asarray(forward_table(length)),
        preferred_element_type=jnp.float32,
    )
    power = jnp.mean(spectrum * spectrum, axis=1, keepdims=True)
    gain = jnp.repeat(live_mask.astype(jnp.float32), windows)[:, None]
    white = spectrum * (gain * lax.rsqrt(power + 1e-06))
    return white.astype(jnp.bfloat16)


def reach_kernel(shape, offsets_ref, white_ref, cross_ref, held, ext, own, swapped, made, back,
                 z_send, z_recv, c_send, c_recv, y_send, y_recv, d_send, d_recv, e_send, r_send, r_recv):
    layers, columns, depth, pieces, windows, fold = shape
    count, slab = white_ref.shape[0], white_ref.shape[1]
    pairs = offsets_ref.shape[0]
    wide = 2 * columns
    total = layers * wide * count
    me = lax.axis_index("chan")
    z, q = me // wide, me % wide
    y, c = q // 2, q % 2
    sibling = me + 1 - 2 * c
    sib_q = q + 1 - 2 * c
    mate = me + 2 - 4 * y
    mate_q = q + 2 - 4 * y
    far_q = sib_q + 2 - 4 * y
    step = count // pieces
    top, lifted = layers - 1, depth + 1

    barrier = pltpu.get_barrier_semaphore()

    def greet(device):
        pl.semaphore_signal(barrier, inc=1, device_id={"chan": device}, device_id_type=pl.DeviceIdType.MESH)

    greet(sibling)
    if columns == 2:
        greet(mate)

    @pl.when(z >= 1)
    def _():
        greet(me - wide)

    @pl.when(z < layers - 1)
    def _():
        greet(me + wide)

    below, above = jnp.minimum(z, 1), jnp.minimum(top - z, 1)
    peers = columns + below + above
    if fold:
        @pl.when(z == 0)
        def _():
            for i in range(wide):
                greet(top * wide + i)

        @pl.when(z == top)
        def _():
            for i in range(wide):
                greet(jnp.int32(i))

        peers = peers + wide * (2 - below - above)
    pl.semaphore_wait(barrier, peers)

    def rows(p):
        return pl.ds(p * step, step)

    def mine(dz, p):
        return white_ref.at[rows(p)] if dz == 0 else held.at[dz * wide + q, rows(p)]

    def copy(source, slot, p, send, recv, device):
        return pltpu.make_async_remote_copy(
            src_ref=source,
            dst_ref=held.at[slot, rows(p)],
            send_sem=send,
            recv_sem=recv,
            device_id={"chan": device},
            device_id_type=pl.DeviceIdType.MESH,
        )

    def down(dz, p):
        return copy(mine(dz, p), (dz + 1) * wide + q, p, z_send.at[dz, p], z_recv.at[dz + 1, p], me - wide)

    def from_above(dz, p):
        return copy(mine(dz, p), dz * wide + q, p, z_send.at[dz, p], z_recv.at[dz, p], me)

    def across(dz, p, slot):
        return copy(mine(dz, p), slot, p, c_send.at[dz, p], c_recv.at[dz, p], sibling)

    def over(dz, p, slot):
        return copy(mine(dz, p), slot, p, y_send.at[dz, p], y_recv.at[dz, p], mate)

    def onward(dz, p, slot):
        return copy(held.at[dz * wide + mate_q, rows(p)], slot, p, d_send.at[dz, p], d_recv.at[dz, p], sibling)

    def both(*conditions):
        joined = conditions[0]
        for condition in conditions[1:]:
            joined = jnp.logical_and(joined, condition)
        return joined

    def exists(dz):
        return z + dz < layers

    def goes(dz, at_start, at_end):
        if dz == lifted:
            return z == top
        if dz == 0:
            return at_start
        if fold and dz == depth:
            return both(exists(dz), at_end)
        return exists(dz)

    def z_tx(dz):
        if fold and dz + 1 == depth:
            return both(exists(dz), z >= 1, jnp.logical_or(z >= 2, q == 0))
        return both(exists(dz), z >= 1)

    def z_rx(dz):
        return goes(dz, None, q == 0)

    def c_tx(dz):
        return goes(dz, c == 1, q == 0)

    def c_rx(dz):
        return goes(dz, c == 0, q == 1)

    def y_tx(dz):
        return goes(dz, y == 1, q == 0)

    def y_rx(dz):
        return goes(dz, y == 0, q == 2)

    def detoured(dz, p):
        return fold and dz == depth - 1 and p == pieces - 1

    def over_tx(dz, p):
        if detoured(dz, p):
            return both(y_tx(dz), jnp.logical_or(z > 0, y == 0))
        if raised(dz, p):
            return both(y_tx(dz), y == 0)
        return y_tx(dz)

    def raised(dz, p):
        return fold and dz == lifted and p >= pieces // 2

    def lift_mate(p):
        return copy(held.at[mate_q, rows(p)], lifted * wide + mate_q, p,
                    e_send.at[lifted, p], y_recv.at[lifted, p], me + top * wide)

    def extra(dz, p):
        return copy(held.at[dz * wide + mate_q, rows(p)], (dz + 1) * wide + mate_q, p,
                    e_send.at[dz, p], y_recv.at[dz + 1, p], me - wide)

    def extra_tx():
        return both(z == 1, y == 0)

    def d_rx(dz):
        return goes(dz, y == 0, q == 3)

    def lift(p):
        return copy(white_ref.at[rows(p)], lifted * wide + q, p, z_send.at[lifted, p], z_recv.at[lifted, p],
                    me + top * wide)

    def sends(dz):
        for p in range(pieces):
            if dz > 0:
                @pl.when(z_rx(dz))
                def _():
                    from_above(dz, p).wait_recv()
            if dz < depth:
                @pl.when(z_tx(dz))
                def _():
                    down(dz, p).start()
            if columns == 2:
                @pl.when(over_tx(dz, p))
                def _():
                    over(dz, p, dz * wide + q).start()
            @pl.when(c_tx(dz))
            def _():
                across(dz, p, dz * wide + q).start()

    def passes(dz):
        if columns == 2:
            for p in range(pieces):
                @pl.when(y_rx(dz))
                def _():
                    over(dz, p, dz * wide + mate_q).wait_recv()
                    onward(dz, p, dz * wide + mate_q).start()
                if dz == 0 and raised(lifted, p):
                    @pl.when(both(z == 0, y == 0))
                    def _():
                        lift_mate(p).start()
                if detoured(dz + 1, p):
                    @pl.when(extra_tx())
                    def _():
                        extra(dz, p).start()

    def arrives(dz):
        for p in range(pieces):
            @pl.when(c_rx(dz))
            def _():
                across(dz, p, dz * wide + sib_q).wait_recv()
            if columns == 2:
                @pl.when(d_rx(dz))
                def _():
                    onward(dz, p, dz * wide + far_q).wait_recv()

    def finishes(dz):
        for p in range(pieces):
            if dz < depth:
                @pl.when(z_tx(dz))
                def _():
                    down(dz, p).wait_send()
            if columns == 2:
                @pl.when(over_tx(dz, p))
                def _():
                    over(dz, p, dz * wide + q).wait_send()
                if detoured(dz + 1, p):
                    @pl.when(extra_tx())
                    def _():
                        extra(dz, p).wait_send()
                @pl.when(y_rx(dz))
                def _():
                    onward(dz, p, dz * wide + mate_q).wait_send()
            @pl.when(c_tx(dz))
            def _():
                across(dz, p, dz * wide + q).wait_send()

    def answer(i):
        return pltpu.make_async_remote_copy(
            src_ref=made.at[i],
            dst_ref=back.at[q],
            send_sem=r_send.at[i],
            recv_sem=r_recv.at[q],
            device_id={"chan": jnp.int32(i)},
            device_id_type=pl.DeviceIdType.MESH,
        )

    def answered(i):
        return pltpu.make_async_remote_copy(
            src_ref=made.at[i],
            dst_ref=back.at[i],
            send_sem=r_send.at[i],
            recv_sem=r_recv.at[i],
            device_id={"chan": me},
            device_id_type=pl.DeviceIdType.MESH,
        )

    low = lax.broadcasted_iota(jnp.int32, (8, LANES), 0) < 4

    def prepare(i, carry):
        raw = white_ref[i]
        value = raw.astype(jnp.float32)
        own[i] = value
        ext[q * count + i] = raw
        for w in range(windows):
            swapped[i, w * 8 : w * 8 + 8] = pltpu.roll(value[w * 8 : w * 8 + 8], 4, 0)
        return carry

    def settle(dz):
        def one(l):
            def fill(i, carry):
                ext[(dz * wide + l) * count + i] = held[dz * wide + l, i]
                return carry
            lax.fori_loop(0, count, fill, 0, unroll=4)

        if dz == 0:
            for l in range(1, wide):
                @pl.when(q < l)
                def _():
                    one(l)
        else:
            @pl.when(exists(dz))
            def _():
                for l in range(1 if fold and dz == depth else wide):
                    one(l)

    live = jnp.minimum(layers * wide - me, pairs)

    def outside():
        def nothing(k, carry):
            for r in range(count):
                cross_ref[r, k] = jnp.zeros((8, LANES), jnp.float32)
            return carry

        lax.fori_loop(live, pairs, nothing, 0)

        @pl.when(layers - z <= depth)
        def _():
            def blank(i, carry):
                ext[(layers - z) * wide * count + i] = jnp.zeros((slab, LANES), jnp.bfloat16)
                return carry

            lax.fori_loop(0, 2 * count, blank, 0, unroll=4)

    def reached(dz):
        if dz < 0:
            return 0
        if dz == depth:
            return live
        return jnp.minimum((dz + 1) * wide - q - 1, live)

    def multiply(dz):
        def pair(k, carry):
            shift = offsets_ref[k]

            def channel(i, inner):
                place = me * count + i + shift
                keep = jnp.where(place < total, 1.0 / windows, 0.0)
                near = jnp.minimum(q * count + i + shift, ext.shape[0] - 1)
                partner = ext[near].astype(jnp.float32)
                straight = own[i, :8] * partner[:8]
                twisted = swapped[i, :8] * partner[:8]
                for w in range(1, windows):
                    part = slice(w * 8, w * 8 + 8)
                    straight += own[i, part] * partner[part]
                    twisted += swapped[i, part] * partner[part]
                joined = jnp.where(
                    low,
                    straight + pltpu.roll(straight, 4, 0),
                    pltpu.roll(twisted, 4, 0) - twisted,
                )
                cross_ref[i, k] = joined * keep
                return inner

            return lax.fori_loop(0, count, channel, carry, unroll=4)

        begin, end = reached(dz - 1), reached(dz)
        if fold and dz == depth:
            @pl.when(z == 0)
            def _():
                lax.fori_loop(begin, begin + 1, pair, 0)

            @pl.when(z > 0)
            def _():
                lax.fori_loop(begin, end, pair, 0)
        else:
            lax.fori_loop(begin, end, pair, 0)

    def reply():
        for i in range(wide):
            shift = offsets_ref[top * wide + q - i]

            def channel(r, carry):
                place = i * count + r + shift
                keep = jnp.where(place < total, 1.0 / windows, 0.0)
                near = jnp.clip(place - top * wide * count, 0, ext.shape[0] - 1)
                partner = ext[near].astype(jnp.float32)
                value = held[lifted * wide + i, r].astype(jnp.float32)
                straight = value[:8] * partner[:8]
                twisted = pltpu.roll(value[:8], 4, 0) * partner[:8]
                for w in range(1, windows):
                    part = slice(w * 8, w * 8 + 8)
                    straight += value[part] * partner[part]
                    twisted += pltpu.roll(value[part], 4, 0) * partner[part]
                joined = jnp.where(
                    low,
                    straight + pltpu.roll(straight, 4, 0),
                    pltpu.roll(twisted, 4, 0) - twisted,
                )
                made[i, r] = (joined * keep).astype(jnp.bfloat16)
                return carry

            lax.fori_loop(0, count, channel, 0, unroll=4)
        for i in range(wide):
            answer(i).start()

    sends(0)
    if fold:
        @pl.when(z == 0)
        def _():
            for p in range(pieces):
                lift(p).start()

    lax.fori_loop(0, count, prepare, 0)
    outside()
    for dz in range(depth + 1):
        if dz < depth:
            sends(dz + 1)
        if fold and dz == 0:
            sends(lifted)
        passes(dz)
        if fold and dz == 0:
            passes(lifted)
        arrives(dz)
        settle(dz)
        if fold and dz == 0:
            arrives(lifted)

            @pl.when(z == top)
            def _():
                reply()

        multiply(dz)

    if fold:
        @pl.when(z == 0)
        def _():
            for i in range(wide):
                answered(i).wait_recv()

                def take(r, carry):
                    cross_ref[r, top * wide - q + i] = back[i, r].astype(jnp.float32)
                    return carry

                lax.fori_loop(0, count, take, 0, unroll=4)
            for p in range(pieces):
                lift(p).wait_send()
                if raised(lifted, p):
                    @pl.when(y == 0)
                    def _():
                        lift_mate(p).wait_send()

        @pl.when(z == top)
        def _():
            for i in range(wide):
                answer(i).wait_send()

        finishes(lifted)
    for dz in range(depth + 1):
        finishes(dz)


def middle_kernel(shape, offsets_hbm, mask_hbm, records_hbm, table_hbm, inverse_hbm, half_ref, cross_ref, inverse,
                  offsets_ref, mask_ref, records, table, crossed, spectrum, square, white, gains, column, held, spec, made, back, joined,
                  l_sem, x_send, f_send, g_send, s_recv, r_send, r_recv):
    layers, wide, windows = shape
    pairs = offsets_ref.shape[0]
    count = records.shape[0] // windows
    chunks, width = table.shape[0], table.shape[2]
    rows = count * windows
    parts = layers * wide
    pitch = spec.shape[0] // (2 * windows)
    half, top, last = layers // 2, layers - 1, parts - 1
    me = lax.axis_index("chan")
    z, q = me // wide, me % wide
    c = q % 2
    first = z * wide
    base = half * wide
    sib_q = q + 1 - 2 * c
    mate_q = (q + 2) % wide
    far_q = (sib_q + 2) % wide
    near = c == 0

    def nearest(j):
        return jnp.where(j == 0, q, jnp.where(j == 1, sib_q, jnp.where(j == 2, mate_q, far_q)))

    def chunk(j):
        return pltpu.make_async_copy(table_hbm.at[nearest(j)], table.at[j], l_sem.at[j])

    load = [
        pltpu.make_async_copy(records_hbm, records, l_sem.at[chunks]),
        pltpu.make_async_copy(offsets_hbm, offsets_ref, l_sem.at[chunks + 1]),
        pltpu.make_async_copy(mask_hbm, mask_ref, l_sem.at[chunks + 2]),
    ]
    load[0].start()
    for n in range(chunks):
        chunk(n).start()
    for one in load[1:]:
        one.start()
    inner_low, inner_high = z == half - 1, z == half
    neighbour = jnp.where(
        jnp.logical_or(z == 0, jnp.logical_and(inner_low, c == 1)), me + wide, me - wide)
    own_end = jnp.where(
        z == 0, base, jnp.where(jnp.logical_and(inner_low, c == 1), base + wide, parts + 1))
    barrier = pltpu.get_barrier_semaphore()

    def greet(device, condition):
        @pl.when(condition)
        def _():
            pl.semaphore_signal(barrier, inc=1, device_id={"chan": jnp.int32(device)},
                                device_id_type=pl.DeviceIdType.MESH)

    for col in (sib_q, mate_q, far_q):
        greet(first + col, z >= 0)
    for i in range(wide):
        odd = i % 2 == 1
        greet(wide + i, z == 0)
        if odd:
            greet(base + i, z < half)
        else:
            greet(base + i, jnp.logical_and(inner_low, q == i))
    greet(me - wide, jnp.logical_or(inner_low, jnp.logical_and(inner_high, c == 1)))
    greet(me + wide, inner_high)
    replies_far = jnp.where(inner_low, wide, jnp.where(jnp.logical_and(inner_high, c == 1), 2 * wide - 1, 0))
    ships_there = jnp.where(jnp.logical_and(inner_low, near), 0, 1)

    def remote(source, target, send, recv, device):
        return pltpu.make_async_remote_copy(
            src_ref=source, dst_ref=target, send_sem=send, recv_sem=recv,
            device_id={"chan": device}, device_id_type=pl.DeviceIdType.MESH,
        )

    def piece(ri, col):
        return white.at[ri * wide + col]

    def swap(ri, col):
        return remote(piece(ri, col), held.at[me, pl.ds(ri * rows, rows)], x_send, s_recv.at[me], first + col)

    def ship_own(ri):
        return remote(piece(ri, q), held.at[me, pl.ds(ri * rows, rows)], f_send, s_recv.at[me], neighbour)

    def ship(s):
        return remote(held.at[s], held.at[s], f_send, s_recv.at[s], neighbour)

    both_ways = jnp.logical_and(inner_low, c == 1)

    def drop_own(ri):
        return remote(piece(ri, q), held.at[me, pl.ds(ri * rows, rows)], g_send, s_recv.at[me], me - wide)

    def drop(s):
        return remote(held.at[s], held.at[s], g_send, s_recv.at[s], me - wide)

    def made_at(d, k):
        return made.at[d * pairs + k]

    def reply(d, k):
        return remote(made_at(d, k), back.at[k, q], r_send, r_recv.at[k], d)

    def shipped(slots, send):
        remote(held.at[0:slots], held.at[0:slots], send, s_recv.at[0], neighbour).wait_send()

    def gain_to(send, device):
        return remote(gains, held.at[me, pl.ds(2 * rows, 16)], send, s_recv.at[me], device)

    def clear(i, carry):
        joined[pl.ds(pl.multiple_of(i * 64, 64), 64), :] = jnp.zeros((64, LANES), jnp.float32)
        return carry

    lax.fori_loop(0, joined.shape[0] // 64, clear, 0)

    def blank(x, carry):
        spec[pl.ds(pl.multiple_of(x * pitch + parts * count, 8), count), :] = jnp.zeros((count, LANES), jnp.float32)
        return carry

    lax.fori_loop(0, 2 * windows, blank, 0)
    square[...] = jnp.zeros(square.shape, jnp.float32)
    load[0].wait()

    def transform(j, carry):
        col = nearest(j)
        chunk(j).wait()
        spectrum[...] = jnp.dot(records[...], table[j], preferred_element_type=jnp.float32)

        def narrow(i, inner):
            some = pl.ds(pl.multiple_of(i * 16, 16), 16)
            real, imag = spectrum[some, :LANES], spectrum[some, LANES:]
            white[col, some] = real.astype(jnp.bfloat16)
            white[wide + col, some] = imag.astype(jnp.bfloat16)
            square[some, :] += real * real + imag * imag
            return inner

        lax.fori_loop(0, rows // 16, narrow, 0, unroll=4)

        @pl.when(j == 0)
        def _():
            pl.semaphore_wait(barrier, wide - 1 + replies_far + ships_there)
            for ri in range(2):
                ship_own(ri).start()

            @pl.when(both_ways)
            def _():
                for ri in range(2):
                    drop_own(ri).start()

        @pl.when(j > 0)
        def _():
            for ri in range(2):
                swap(ri, col).start()
        return carry

    lax.fori_loop(0, chunks, transform, 0)
    for one in load[1:]:
        one.wait()
    place = lax.broadcasted_iota(jnp.int32, (16, LANES), 0)
    channel = lax.broadcasted_iota(jnp.int32, (8, LANES), 1) // windows
    terms = jnp.zeros((16, LANES), jnp.float32)
    for part in range(rows // LANES):
        total = jnp.sum(square[part * LANES:(part + 1) * LANES, :], axis=1, keepdims=True)
        scale = jnp.broadcast_to(lax.rsqrt(total * (1.0 / (2 * F)) + 1e-06), (LANES, LANES)).T[:8]
        alive = jnp.zeros((8, LANES), jnp.float32)
        for n in range(LANES // windows):
            alive = jnp.where(channel == n, mask_ref[part * (LANES // windows) + n].astype(jnp.float32), alive)
        rest = (scale * alive)[:1]
        for term in range(3):
            kept = rest.astype(jnp.bfloat16).astype(jnp.float32)
            terms = jnp.where(place == part * 3 + term, kept, terms)
            rest = rest - kept
    gains[...] = terms.astype(jnp.bfloat16)
    fetch = pltpu.make_async_copy(inverse_hbm, inverse, l_sem.at[0])
    fetch.start()

    def settle(s, gain, piece_of):
        for part in range(rows // LANES):
            scale = sum(gain[part * 3 + term:part * 3 + term + 1].astype(jnp.float32) for term in range(3))
            column[part * LANES:(part + 1) * LANES, :] = jnp.broadcast_to(scale, (LANES, LANES)).T

        def one(i, carry):
            some = pl.ds(pl.multiple_of(i * 2 * windows, 2 * windows), 2 * windows)
            factor = column[some, :]
            for ri in range(2):
                value = piece_of(ri, i).astype(jnp.float32) * factor
                for part in range(2):
                    row = ri * windows * pitch + s * count + 2 * i + part
                    spec[pl.ds(row, windows, stride=pitch), :] = value[part * windows:(part + 1) * windows]
            return carry

        lax.fori_loop(0, count // 2, one, 0, unroll=4)

    def own_rows(ri, i):
        return white[ri * wide + q, pl.ds(pl.multiple_of(i * 2 * windows, 2 * windows), 2 * windows)]

    def take(s, onward=None, downward=None):
        ship(s).wait_recv()
        if onward is not None:
            @pl.when(onward)
            def _():
                ship(s).start()
        if downward is not None:
            @pl.when(downward)
            def _():
                drop(s).start()
        settle(
            s, held[s, 2 * rows:2 * rows + 16],
            lambda ri, i: held[s, pl.ds(pl.multiple_of(ri * rows + i * 2 * windows, 2 * windows), 2 * windows)])

    def takes(start, begin, end, onward=None, downward=None):
        def one(j, carry):
            take(start + nearest(j), onward, downward)
            return carry

        lax.fori_loop(begin, end, one, 0)

    def block(d, k):
        shift = offsets_ref[k]
        for g in range(count // 16):
            mine = d * count + g * 16
            real = imag = None
            for w in range(windows):
                cr = spec[pl.ds(pl.multiple_of(w * pitch + mine, 8), 16), :]
                ci = spec[pl.ds(pl.multiple_of((windows + w) * pitch + mine, 8), 16), :]
                pr = spec[pl.ds(w * pitch + mine + shift, 16), :]
                pi = spec[pl.ds((windows + w) * pitch + mine + shift, 16), :]
                re, im = cr * pr + ci * pi, ci * pr - cr * pi
                real, imag = (re, im) if w == 0 else (real + re, imag + im)
            rows = slice(g * 16, g * 16 + 16)
            made[d * pairs + k, 0, rows] = (real * (1.0 / windows)).astype(jnp.bfloat16)
            made[d * pairs + k, 1, rows] = (imag * (1.0 / windows)).astype(jnp.bfloat16)

    def spans(d_begin, d_end, u_begin, u_end, visit):
        def reach(u, carry):
            def one(d, inner):
                visit(d, u - 1 - d)
                return inner

            return lax.fori_loop(jnp.maximum(d_begin, u - pairs), jnp.minimum(d_end, u), one, carry)

        lax.fori_loop(u_begin, u_end, reach, 0)

    def give(d, k):
        @pl.when(d != me)
        def _():
            reply(d, k).start()

    def blocks(*span):
        spans(*span, block)
        spans(*span, give)

    y = q // 2
    def reached_1(start, more=0):
        return jnp.where(y == 0, start, start + 3), jnp.where(y == 0, start + 2, start + wide + more)

    def reached_2(start, more=0):
        return jnp.where(y == 0, start + 2, start), jnp.where(y == 0, start + wide + more, start + 3)

    settle(me, gains[...], own_rows)
    gain_to(f_send, neighbour).start()

    @pl.when(both_ways)
    def _():
        gain_to(g_send, me - wide).start()
    for col in (sib_q, mate_q, far_q):
        gain_to(x_send, first + col).start()
    takes(first, 1, wide, z >= 0, both_ways)
    blocks(first, first + wide, first + 1, first + wide + jnp.where(z == top, 1, 0))

    @pl.when(z == 0)
    def _():
        for begin, reached in ((0, reached_1), (2, reached_2)):
            takes(wide, begin, begin + 2)
            blocks(0, wide, *reached(wide))

    @pl.when(inner_low)
    def _():
        takes(0, 0, 2, jnp.logical_not(near))
        takes(base, 0, 2)
        blocks(2 * y, 2 * y + 2, *reached_1(base))
        blocks(wide, base, *reached_1(base))
        takes(0, 2, wide, jnp.logical_not(near))
        blocks(2 - 2 * y, wide - 2 * y, *reached_1(base))
        takes(base, 2, wide)
        blocks(0, base, *reached_2(base))

        @pl.when(near)
        def _():
            for begin, reached in ((0, reached_1), (2, reached_2)):
                takes(top * wide, begin, begin + 2)
                blocks(0, base, *reached(top * wide, 1))

    @pl.when(inner_high)
    def _():
        for begin, reached in ((0, reached_1), (2, reached_2)):
            takes(top * wide, begin, begin + 2, near)
            blocks(base, base + wide, *reached(top * wide, 1))

        @pl.when(jnp.logical_not(near))
        def _():
            takes(wide, 0, wide)
            spans(wide, base, top * wide, parts + 1, block)
            takes(0, 0, 2)
            blocks(2 * y, 2 * y + 2, top * wide, parts + 1)
            takes(0, 2, wide)
            blocks(2 - 2 * y, wide - 2 * y, top * wide, parts + 1)
            spans(wide, base, top * wide, parts + 1, give)

    group = pairs // 2

    def unpack(source, k, col):
        for ri in range(2):
            for g in range(count // 16):
                value = source[ri, g * 16:g * 16 + 16].astype(jnp.float32)
                for part in range(2):
                    seg = (k // group) * 2 * wide + ri * wide + col
                    row = (seg * count + g * 16 + part * 8) * group + k % group
                    joined[pl.ds(row, 8, stride=group), :] = value[part * 8:part * 8 + 8]

    def collect(k, carry):
        away = me + k + 1 >= own_end
        def received(cols):
            remote(back.at[k, 0:cols], back.at[k, 0:cols], r_send, r_recv.at[k], me).wait_recv()

        @pl.when(away)
        def _():
            received(wide)

        @pl.when(jnp.logical_not(away))
        def _():
            received(wide - 1)

        for col in range(wide):
            here = jnp.logical_and(q == col, jnp.logical_not(away))

            @pl.when(here)
            def _():
                unpack(made_at(me, k), k, col)

            @pl.when(jnp.logical_not(here))
            def _():
                unpack(back.at[k, col], k, col)
        return carry

    def pack(which, target):
        def one(i, carry):
            rows = pl.ds(pl.multiple_of(i * 16, 16), 16)
            for x in range(2 * wide):
                start = pl.multiple_of((which * 2 * wide + x) * count * group + i * 16, 16)
                target[rows, x * LANES:(x + 1) * LANES] = joined[pl.ds(start, 16), :].astype(jnp.bfloat16)
            return carry

        lax.fori_loop(0, count * group // 16, one, 0, unroll=2)

    lax.fori_loop(0, jnp.minimum(group, parts - me), collect, 0)
    pack(0, crossed)
    fetch.wait()

    def invert(n, carry):
        span = pl.ds(pl.multiple_of(n * SPAN, SPAN), SPAN)
        lagged = jnp.dot(crossed[...], inverse[:, span], preferred_element_type=jnp.float32)
        half_ref[:, span] = (lagged * (1.0 / math.sqrt(F))).astype(jnp.bfloat16)
        return carry

    lax.fori_loop(0, LAGS // SPAN, invert, 0)
    lax.fori_loop(group, parts - me, collect, 0)
    pack(1, cross_ref)

    shipped(wide - 1, x_send)
    forwards = jnp.logical_or(both_ways, jnp.logical_and(inner_high, near))

    @pl.when(forwards)
    def _():
        shipped(2 * wide, f_send)

    @pl.when(jnp.logical_not(forwards))
    def _():
        shipped(wide, f_send)

    @pl.when(both_ways)
    def _():
        shipped(wide, g_send)

    for i in range(parts):
        layer, odd = i // wide, i % 2 == 1
        ends = base if layer == 0 else base + wide if layer == half - 1 and odd else parts + 1
        replies = sum(
            min(ends, d + pairs + 1) - d - 1 for d in range(layer * wide, (layer + 1) * wide) if d != i)
        if layer == half - 1 or (layer == half and odd):
            begins = base if layer == half - 1 else base + wide
            replies += sum(min(ends, d + pairs + 1) - begins for d in range(layer * wide))

        @pl.when(me == i)
        def _():
            done = made.at[0:replies]
            remote(done, done, r_send, r_recv.at[0], me).wait_send()


def meet(layers, wide, records, live_mask, offsets):
    pairs = offsets.shape[0]
    count, windows, length = records.shape
    parts = layers * wide
    pitch = (parts + 1) * count
    rows = count * windows
    width = 2 * LANES
    chunks = 2 * F // width
    table = np.ascontiguousarray(
        forward_table(length).reshape(length, 2, chunks, LANES).transpose(2, 0, 1, 3).reshape(chunks, length, width))
    return pl.pallas_call(
        functools.partial(middle_kernel, (layers, wide, windows)),
        out_shape=[
            jax.ShapeDtypeStruct((count * pairs // 2, LAGS), jnp.bfloat16),
            jax.ShapeDtypeStruct((count * pairs // 2, 2 * F), jnp.bfloat16),
            jax.ShapeDtypeStruct((2 * F, LAGS), jnp.bfloat16),
        ],
        in_specs=[
            pl.BlockSpec(memory_space=pltpu.HBM),
            pl.BlockSpec(memory_space=pltpu.HBM),
            pl.BlockSpec(memory_space=pltpu.HBM),
            pl.BlockSpec(memory_space=pltpu.HBM),
            pl.BlockSpec(memory_space=pltpu.HBM),
        ],
        out_specs=[pl.BlockSpec(memory_space=pltpu.VMEM)] * 3,
        scratch_shapes=[
            pltpu.SMEM((pairs,), jnp.int32),
            pltpu.SMEM((count,), jnp.int32),
            pltpu.VMEM((rows, length), jnp.bfloat16),
            pltpu.VMEM((chunks, length, width), jnp.bfloat16),
            pltpu.VMEM((count * pairs // 2, 2 * F), jnp.bfloat16),
            pltpu.VMEM((rows, width), jnp.float32),
            pltpu.VMEM((rows, LANES), jnp.float32),
            pltpu.VMEM((2 * wide, rows, LANES), jnp.bfloat16),
            pltpu.VMEM((16, LANES), jnp.bfloat16),
            pltpu.VMEM((rows, LANES), jnp.float32),
            pltpu.VMEM((parts, 2 * rows + 16, LANES), jnp.bfloat16),
            pltpu.VMEM((2 * windows * pitch, LANES), jnp.float32),
            pltpu.VMEM((parts * pairs, 2, count, LANES), jnp.bfloat16),
            pltpu.VMEM((pairs, wide, 2, count, LANES), jnp.bfloat16),
            pltpu.VMEM((2 * wide * count * pairs, LANES), jnp.float32),
            pltpu.SemaphoreType.DMA((chunks + 3,)),
            pltpu.SemaphoreType.DMA,
            pltpu.SemaphoreType.DMA,
            pltpu.SemaphoreType.DMA,
            pltpu.SemaphoreType.DMA((parts,)),
            pltpu.SemaphoreType.DMA,
            pltpu.SemaphoreType.DMA((pairs,)),
        ],
        compiler_params=pltpu.CompilerParams(
            vmem_limit_bytes=36 * 1024 * 1024, collective_id=1, has_side_effects=True
        ),
    )(*[
        pltpu.with_memory_space_constraint(x, pltpu.HBM)
        for x in (offsets, live_mask, records.reshape(rows, length), jnp.asarray(table),
                  jnp.asarray(inverse_table(length)))
    ])


def finish_kernel(half_ref, cross_ref, table_ref, out_hbm, stage, sem):
    group = out_hbm.shape[1] // 2
    copies = [pltpu.make_async_copy(half_ref, out_hbm.at[:, 0:group], sem.at[0])]
    copies[0].start()
    for i, n in enumerate(range(0, LAGS, SPAN)):
        lagged = jnp.dot(cross_ref[...], table_ref[:, n:n + SPAN], preferred_element_type=jnp.float32)
        lagged = (lagged * (1.0 / math.sqrt(F))).astype(jnp.bfloat16)
        stage[:, :, n:n + SPAN] = lagged.reshape(stage.shape[0], group, SPAN)
        copies.append(pltpu.make_async_copy(
            stage.at[:, :, n:n + SPAN], out_hbm.at[:, group:2 * group, n:n + SPAN], sem.at[i + 1]))
        copies[-1].start()
    for one in copies:
        one.wait()


def finish(half, cross, table, count, pairs):
    return pl.pallas_call(
        finish_kernel,
        out_shape=jax.ShapeDtypeStruct((count, pairs, LAGS), jnp.bfloat16),
        in_specs=[pl.BlockSpec(memory_space=pltpu.VMEM)] * 3,
        out_specs=pl.BlockSpec(memory_space=pltpu.HBM),
        scratch_shapes=[
            pltpu.VMEM((count, pairs // 2, LAGS), jnp.bfloat16),
            pltpu.SemaphoreType.DMA((LAGS // SPAN + 1,)),
        ],
        compiler_params=pltpu.CompilerParams(vmem_limit_bytes=16 * 1024 * 1024),
    )(half.reshape(count, pairs // 2, LAGS), cross, table)


def shards(columns, records, live_mask, offsets):
    count, windows, length = records.shape
    pairs = offsets.shape[0]
    wide = 2 * columns
    layers = lax.axis_size("chan") // wide
    reach = (BAND + count - 2) // count
    depth = min(layers - 1, (wide - 1 + reach) // wide)
    pieces = PIECES
    fold = columns == 2 and depth == layers - 1 and depth >= 2 and layers * wide == pairs and pairs * count == BAND
    if (
        columns == 2 and layers == 4 and layers * wide == pairs and pairs * count == BAND
        and F == wide * LANES and windows == 8 and count % 16 == 0
    ):
        half, cross, inverse = meet(layers, wide, records, live_mask, offsets)
        return finish(half, cross, inverse, count, pairs)
    spectra = whiten(records, live_mask).reshape(count, windows * 8, LANES)
    slots = (depth + 1) * wide
    cross = pl.pallas_call(
        functools.partial(reach_kernel, (layers, columns, depth, pieces, windows, fold)),
        out_shape=jax.ShapeDtypeStruct((count, pairs, 8, LANES), jnp.float32),
        in_specs=[
            pl.BlockSpec(memory_space=pltpu.SMEM),
            pl.BlockSpec(memory_space=pltpu.VMEM),
        ],
        out_specs=pl.BlockSpec(memory_space=pltpu.VMEM),
        scratch_shapes=[
            pltpu.VMEM((slots + wide, count, windows * 8, LANES), jnp.bfloat16),
            pltpu.VMEM((slots * count, windows * 8, LANES), jnp.bfloat16),
            pltpu.VMEM((count, windows * 8, LANES), jnp.float32),
            pltpu.VMEM((count, windows * 8, LANES), jnp.float32),
            pltpu.VMEM((wide, count, 8, LANES), jnp.bfloat16),
            pltpu.VMEM((wide, count, 8, LANES), jnp.bfloat16),
        ]
        + [pltpu.SemaphoreType.DMA((depth + 2, pieces))] * 9
        + [pltpu.SemaphoreType.DMA((wide,))] * 2,
        compiler_params=pltpu.CompilerParams(
            vmem_limit_bytes=40 * 1024 * 1024, collective_id=0, has_side_effects=True
        ),
    )(offsets, spectra)
    return lags(cross.astype(jnp.bfloat16).reshape(count * pairs, 8 * LANES), count, pairs, length)


def lags(cross, count, pairs, length):
    result = jnp.dot(cross, jnp.asarray(inverse_table(length)), preferred_element_type=jnp.float32)
    result = result * (1.0 / math.sqrt(F))
    return result.reshape(count, pairs, LAGS).astype(jnp.bfloat16)


def solution(mesh):
    in_specs = (P(("day", "chan"), None, None), P(("day", "chan")), P())
    out_specs = P(("day", "chan"), None, None)
    columns = max(1, LAYER_CHIPS // mesh.shape["day"])
    body = functools.partial(shards, columns)
    return jax.shard_map(body, mesh=mesh, in_specs=in_specs, out_specs=out_specs, check_vma=False)
```

```python
import functools
import math

import jax
import jax.numpy as jnp
import numpy as np
from jax import lax
from jax.experimental import pallas as pl
from jax.experimental.pallas import tpu as pltpu
from jax.sharding import PartitionSpec as P

F = 512
F0 = 6
LAGS = 2048
LANES = 128
SPAN = 512
BAND = 512
PIECES = 4
LAYER_CHIPS = 4


def forward_table(length):
    samples = np.arange(length, dtype=np.int64)
    freqs = F0 + np.arange(F, dtype=np.int64)
    phase = np.mod(samples[:, None] * freqs[None, :], length)
    angle = 2.0 * math.pi / length * phase
    return np.concatenate([np.cos(angle), -np.sin(angle)], axis=1).astype(np.float32).astype(jnp.bfloat16)


def inverse_table(length):
    freqs = F0 + np.arange(F, dtype=np.int64)
    shifts = np.arange(LAGS, dtype=np.int64) - LAGS // 2
    phase = np.mod(freqs[:, None] * shifts[None, :], length)
    angle = 2.0 * math.pi / length * phase
    return np.concatenate([np.cos(angle), -np.sin(angle)], axis=0).astype(np.float32).astype(jnp.bfloat16)


def whiten(records, live_mask):
    count, windows, length = records.shape
    spectrum = jnp.dot(
        records.reshape(count * windows, length),
        jnp.asarray(forward_table(length)),
        preferred_element_type=jnp.float32,
    )
    power = jnp.mean(spectrum * spectrum, axis=1, keepdims=True)
    gain = jnp.repeat(live_mask.astype(jnp.float32), windows)[:, None]
    white = spectrum * (gain * lax.rsqrt(power + 1e-06))
    return white.astype(jnp.bfloat16)


def reach_kernel(shape, offsets_ref, white_ref, cross_ref, held, ext, own, swapped, made, back,
                 z_send, z_recv, c_send, c_recv, y_send, y_recv, d_send, d_recv, e_send, r_send, r_recv):
    layers, columns, depth, pieces, windows, fold = shape
    count, slab = white_ref.shape[0], white_ref.shape[1]
    pairs = offsets_ref.shape[0]
    wide = 2 * columns
    total = layers * wide * count
    me = lax.axis_index("chan")
    z, q = me // wide, me % wide
    y, c = q // 2, q % 2
    sibling = me + 1 - 2 * c
    sib_q = q + 1 - 2 * c
    mate = me + 2 - 4 * y
    mate_q = q + 2 - 4 * y
    far_q = sib_q + 2 - 4 * y
    step = count // pieces
    top, lifted = layers - 1, depth + 1

    barrier = pltpu.get_barrier_semaphore()

    def greet(device):
        pl.semaphore_signal(barrier, inc=1, device_id={"chan": device}, device_id_type=pl.DeviceIdType.MESH)

    greet(sibling)
    if columns == 2:
        greet(mate)

    @pl.when(z >= 1)
    def _():
        greet(me - wide)

    @pl.when(z < layers - 1)
    def _():
        greet(me + wide)

    below, above = jnp.minimum(z, 1), jnp.minimum(top - z, 1)
    peers = columns + below + above
    if fold:
        @pl.when(z == 0)
        def _():
            for i in range(wide):
                greet(top * wide + i)

        @pl.when(z == top)
        def _():
            for i in range(wide):
                greet(jnp.int32(i))

        peers = peers + wide * (2 - below - above)
    pl.semaphore_wait(barrier, peers)

    def rows(p):
        return pl.ds(p * step, step)

    def mine(dz, p):
        return white_ref.at[rows(p)] if dz == 0 else held.at[dz * wide + q, rows(p)]

    def copy(source, slot, p, send, recv, device):
        return pltpu.make_async_remote_copy(
            src_ref=source,
            dst_ref=held.at[slot, rows(p)],
            send_sem=send,
            recv_sem=recv,
            device_id={"chan": device},
            device_id_type=pl.DeviceIdType.MESH,
        )

    def down(dz, p):
        return copy(mine(dz, p), (dz + 1) * wide + q, p, z_send.at[dz, p], z_recv.at[dz + 1, p], me - wide)

    def from_above(dz, p):
        return copy(mine(dz, p), dz * wide + q, p, z_send.at[dz, p], z_recv.at[dz, p], me)

    def across(dz, p, slot):
        return copy(mine(dz, p), slot, p, c_send.at[dz, p], c_recv.at[dz, p], sibling)

    def over(dz, p, slot):
        return copy(mine(dz, p), slot, p, y_send.at[dz, p], y_recv.at[dz, p], mate)

    def onward(dz, p, slot):
        return copy(held.at[dz * wide + mate_q, rows(p)], slot, p, d_send.at[dz, p], d_recv.at[dz, p], sibling)

    def both(*conditions):
        joined = conditions[0]
        for condition in conditions[1:]:
            joined = jnp.logical_and(joined, condition)
        return joined

    def exists(dz):
        return z + dz < layers

    def goes(dz, at_start, at_end):
        if dz == lifted:
            return z == top
        if dz == 0:
            return at_start
        if fold and dz == depth:
            return both(exists(dz), at_end)
        return exists(dz)

    def z_tx(dz):
        if fold and dz + 1 == depth:
            return both(exists(dz), z >= 1, jnp.logical_or(z >= 2, q == 0))
        return both(exists(dz), z >= 1)

    def z_rx(dz):
        return goes(dz, None, q == 0)

    def c_tx(dz):
        return goes(dz, c == 1, q == 0)

    def c_rx(dz):
        return goes(dz, c == 0, q == 1)

    def y_tx(dz):
        return goes(dz, y == 1, q == 0)

    def y_rx(dz):
        return goes(dz, y == 0, q == 2)

    def detoured(dz, p):
        return fold and dz == depth - 1 and p == pieces - 1

    def over_tx(dz, p):
        if detoured(dz, p):
            return both(y_tx(dz), jnp.logical_or(z > 0, y == 0))
        if raised(dz, p):
            return both(y_tx(dz), y == 0)
        return y_tx(dz)

    def raised(dz, p):
        return fold and dz == lifted and p >= pieces // 2

    def lift_mate(p):
        return copy(held.at[mate_q, rows(p)], lifted * wide + mate_q, p,
                    e_send.at[lifted, p], y_recv.at[lifted, p], me + top * wide)

    def extra(dz, p):
        return copy(held.at[dz * wide + mate_q, rows(p)], (dz + 1) * wide + mate_q, p,
                    e_send.at[dz, p], y_recv.at[dz + 1, p], me - wide)

    def extra_tx():
        return both(z == 1, y == 0)

    def d_rx(dz):
        return goes(dz, y == 0, q == 3)

    def lift(p):
        return copy(white_ref.at[rows(p)], lifted * wide + q, p, z_send.at[lifted, p], z_recv.at[lifted, p],
                    me + top * wide)

    def sends(dz):
        for p in range(pieces):
            if dz > 0:
                @pl.when(z_rx(dz))
                def _():
                    from_above(dz, p).wait_recv()
            if dz < depth:
                @pl.when(z_tx(dz))
                def _():
                    down(dz, p).start()
            if columns == 2:
                @pl.when(over_tx(dz, p))
                def _():
                    over(dz, p, dz * wide + q).start()
            @pl.when(c_tx(dz))
            def _():
                across(dz, p, dz * wide + q).start()

    def passes(dz):
        if columns == 2:
            for p in range(pieces):
                @pl.when(y_rx(dz))
                def _():
                    over(dz, p, dz * wide + mate_q).wait_recv()
                    onward(dz, p, dz * wide + mate_q).start()
                if dz == 0 and raised(lifted, p):
                    @pl.when(both(z == 0, y == 0))
                    def _():
                        lift_mate(p).start()
                if detoured(dz + 1, p):
                    @pl.when(extra_tx())
                    def _():
                        extra(dz, p).start()

    def arrives(dz):
        for p in range(pieces):
            @pl.when(c_rx(dz))
            def _():
                across(dz, p, dz * wide + sib_q).wait_recv()
            if columns == 2:
                @pl.when(d_rx(dz))
                def _():
                    onward(dz, p, dz * wide + far_q).wait_recv()

    def finishes(dz):
        for p in range(pieces):
            if dz < depth:
                @pl.when(z_tx(dz))
                def _():
                    down(dz, p).wait_send()
            if columns == 2:
                @pl.when(over_tx(dz, p))
                def _():
                    over(dz, p, dz * wide + q).wait_send()
                if detoured(dz + 1, p):
                    @pl.when(extra_tx())
                    def _():
                        extra(dz, p).wait_send()
                @pl.when(y_rx(dz))
                def _():
                    onward(dz, p, dz * wide + mate_q).wait_send()
            @pl.when(c_tx(dz))
            def _():
                across(dz, p, dz * wide + q).wait_send()

    def answer(i):
        return pltpu.make_async_remote_copy(
            src_ref=made.at[i],
            dst_ref=back.at[q],
            send_sem=r_send.at[i],
            recv_sem=r_recv.at[q],
            device_id={"chan": jnp.int32(i)},
            device_id_type=pl.DeviceIdType.MESH,
        )

    def answered(i):
        return pltpu.make_async_remote_copy(
            src_ref=made.at[i],
            dst_ref=back.at[i],
            send_sem=r_send.at[i],
            recv_sem=r_recv.at[i],
            device_id={"chan": me},
            device_id_type=pl.DeviceIdType.MESH,
        )

    low = lax.broadcasted_iota(jnp.int32, (8, LANES), 0) < 4

    def prepare(i, carry):
        raw = white_ref[i]
        value = raw.astype(jnp.float32)
        own[i] = value
        ext[q * count + i] = raw
        for w in range(windows):
            swapped[i, w * 8 : w * 8 + 8] = pltpu.roll(value[w * 8 : w * 8 + 8], 4, 0)
        return carry

    def settle(dz):
        def one(l):
            def fill(i, carry):
                ext[(dz * wide + l) * count + i] = held[dz * wide + l, i]
                return carry
            lax.fori_loop(0, count, fill, 0, unroll=4)

        if dz == 0:
            for l in range(1, wide):
                @pl.when(q < l)
                def _():
                    one(l)
        else:
            @pl.when(exists(dz))
            def _():
                for l in range(1 if fold and dz == depth else wide):
                    one(l)

    live = jnp.minimum(layers * wide - me, pairs)

    def outside():
        def nothing(k, carry):
            for r in range(count):
                cross_ref[r, k] = jnp.zeros((8, LANES), jnp.float32)
            return carry

        lax.fori_loop(live, pairs, nothing, 0)

        @pl.when(layers - z <= depth)
        def _():
            def blank(i, carry):
                ext[(layers - z) * wide * count + i] = jnp.zeros((slab, LANES), jnp.bfloat16)
                return carry

            lax.fori_loop(0, 2 * count, blank, 0, unroll=4)

    def reached(dz):
        if dz < 0:
            return 0
        if dz == depth:
            return live
        return jnp.minimum((dz + 1) * wide - q - 1, live)

    def multiply(dz):
        def pair(k, carry):
            shift = offsets_ref[k]

            def channel(i, inner):
                place = me * count + i + shift
                keep = jnp.where(place < total, 1.0 / windows, 0.0)
                near = jnp.minimum(q * count + i + shift, ext.shape[0] - 1)
                partner = ext[near].astype(jnp.float32)
                straight = own[i, :8] * partner[:8]
                twisted = swapped[i, :8] * partner[:8]
                for w in range(1, windows):
                    part = slice(w * 8, w * 8 + 8)
                    straight += own[i, part] * partner[part]
                    twisted += swapped[i, part] * partner[part]
                joined = jnp.where(
                    low,
                    straight + pltpu.roll(straight, 4, 0),
                    pltpu.roll(twisted, 4, 0) - twisted,
                )
                cross_ref[i, k] = joined * keep
                return inner

            return lax.fori_loop(0, count, channel, carry, unroll=4)

        begin, end = reached(dz - 1), reached(dz)
        if fold and dz == depth:
            @pl.when(z == 0)
            def _():
                lax.fori_loop(begin, begin + 1, pair, 0)

            @pl.when(z > 0)
            def _():
                lax.fori_loop(begin, end, pair, 0)
        else:
            lax.fori_loop(begin, end, pair, 0)

    def reply():
        for i in range(wide):
            shift = offsets_ref[top * wide + q - i]

            def channel(r, carry):
                place = i * count + r + shift
                keep = jnp.where(place < total, 1.0 / windows, 0.0)
                near = jnp.clip(place - top * wide * count, 0, ext.shape[0] - 1)
                partner = ext[near].astype(jnp.float32)
                value = held[lifted * wide + i, r].astype(jnp.float32)
                straight = value[:8] * partner[:8]
                twisted = pltpu.roll(value[:8], 4, 0) * partner[:8]
                for w in range(1, windows):
                    part = slice(w * 8, w * 8 + 8)
                    straight += value[part] * partner[part]
                    twisted += pltpu.roll(value[part], 4, 0) * partner[part]
                joined = jnp.where(
                    low,
                    straight + pltpu.roll(straight, 4, 0),
                    pltpu.roll(twisted, 4, 0) - twisted,
                )
                made[i, r] = (joined * keep).astype(jnp.bfloat16)
                return carry

            lax.fori_loop(0, count, channel, 0, unroll=4)
        for i in range(wide):
            answer(i).start()

    sends(0)
    if fold:
        @pl.when(z == 0)
        def _():
            for p in range(pieces):
                lift(p).start()

    lax.fori_loop(0, count, prepare, 0)
    outside()
    for dz in range(depth + 1):
        if dz < depth:
            sends(dz + 1)
        if fold and dz == 0:
            sends(lifted)
        passes(dz)
        if fold and dz == 0:
            passes(lifted)
        arrives(dz)
        settle(dz)
        if fold and dz == 0:
            arrives(lifted)

            @pl.when(z == top)
            def _():
                reply()

        multiply(dz)

    if fold:
        @pl.when(z == 0)
        def _():
            for i in range(wide):
                answered(i).wait_recv()

                def take(r, carry):
                    cross_ref[r, top * wide - q + i] = back[i, r].astype(jnp.float32)
                    return carry

                lax.fori_loop(0, count, take, 0, unroll=4)
            for p in range(pieces):
                lift(p).wait_send()
                if raised(lifted, p):
                    @pl.when(y == 0)
                    def _():
                        lift_mate(p).wait_send()

        @pl.when(z == top)
        def _():
            for i in range(wide):
                answer(i).wait_send()

        finishes(lifted)
    for dz in range(depth + 1):
        finishes(dz)


def middle_kernel(shape, offsets_hbm, mask_hbm, records_hbm, table_hbm, inverse_hbm, half_ref, cross_ref, inverse,
                  offsets_ref, mask_ref, records, table, crossed, spectrum, square, white, gains, column, scales, held, spec, made, back, joined,
                  l_sem, x_send, f_send, g_send, n_send, n_recv, s_recv, r_send, r_recv):
    layers, wide, windows = shape
    pairs = offsets_ref.shape[0]
    count = records.shape[0] // windows
    chunks, width = table.shape[0], table.shape[2]
    rows = count * windows
    parts = layers * wide
    pitch = spec.shape[0] // (2 * windows)
    half, top, last = layers // 2, layers - 1, parts - 1
    me = lax.axis_index("chan")
    z, q = me // wide, me % wide
    c = q % 2
    first = z * wide
    base = half * wide
    sib_q = q + 1 - 2 * c
    mate_q = (q + 2) % wide
    far_q = (sib_q + 2) % wide
    near = c == 0

    def nearest(j):
        return jnp.where(j == 0, q, jnp.where(j == 1, sib_q, jnp.where(j == 2, mate_q, far_q)))

    def chunk(j):
        return pltpu.make_async_copy(table_hbm.at[nearest(j)], table.at[j], l_sem.at[j])

    load = [
        pltpu.make_async_copy(records_hbm, records, l_sem.at[chunks]),
        pltpu.make_async_copy(offsets_hbm, offsets_ref, l_sem.at[chunks + 1]),
        pltpu.make_async_copy(mask_hbm, mask_ref, l_sem.at[chunks + 2]),
    ]
    load[0].start()
    for n in range(chunks):
        chunk(n).start()
    for one in load[1:]:
        one.start()
    inner_low, inner_high = z == half - 1, z == half
    neighbour = jnp.where(
        jnp.logical_or(z == 0, jnp.logical_and(inner_low, c == 1)), me + wide, me - wide)
    own_end = jnp.where(
        z == 0, base, jnp.where(jnp.logical_and(inner_low, c == 1), base + wide, parts + 1))
    barrier = pltpu.get_barrier_semaphore()

    def greet(device, condition):
        @pl.when(condition)
        def _():
            pl.semaphore_signal(barrier, inc=1, device_id={"chan": jnp.int32(device)},
                                device_id_type=pl.DeviceIdType.MESH)

    for col in (sib_q, mate_q, far_q):
        greet(first + col, z >= 0)
    for i in range(wide):
        odd = i % 2 == 1
        greet(wide + i, z == 0)
        if odd:
            greet(base + i, z < half)
        else:
            greet(base + i, jnp.logical_and(inner_low, q == i))
    greet(me - wide, jnp.logical_or(inner_low, jnp.logical_and(inner_high, c == 1)))
    greet(me + wide, inner_high)
    replies_far = jnp.where(inner_low, wide, jnp.where(jnp.logical_and(inner_high, c == 1), 2 * wide - 1, 0))
    ships_there = jnp.where(jnp.logical_and(inner_low, near), 0, 1)

    def remote(source, target, send, recv, device):
        return pltpu.make_async_remote_copy(
            src_ref=source, dst_ref=target, send_sem=send, recv_sem=recv,
            device_id={"chan": device}, device_id_type=pl.DeviceIdType.MESH,
        )

    def piece(ri, col):
        return white.at[ri * wide + col]

    def swap(ri, col):
        return remote(piece(ri, col), held.at[me, pl.ds(ri * rows, rows)], x_send, s_recv.at[me], first + col)

    def ship_own(ri):
        return remote(piece(ri, q), held.at[me, pl.ds(ri * rows, rows)], f_send, s_recv.at[me], neighbour)

    def ship(s):
        return remote(held.at[s], held.at[s], f_send, s_recv.at[s], neighbour)

    both_ways = jnp.logical_and(inner_low, c == 1)

    def drop_own(ri):
        return remote(piece(ri, q), held.at[me, pl.ds(ri * rows, rows)], g_send, s_recv.at[me], me - wide)

    def drop(s):
        return remote(held.at[s], held.at[s], g_send, s_recv.at[s], me - wide)

    def made_at(d, k):
        return made.at[d * pairs + k]

    def reply(d, k):
        return remote(made_at(d, k), back.at[k, q], r_send, r_recv.at[k], d)

    def shipped(slots, send):
        remote(held.at[0:slots], held.at[0:slots], send, s_recv.at[0], neighbour).wait_send()

    def gain_to(device):
        return remote(gains, scales.at[me], n_send, n_recv.at[me], device)

    def gain_on(s, device):
        return remote(scales.at[s], scales.at[s], n_send, n_recv.at[s], device)

    def clear(i, carry):
        joined[pl.ds(pl.multiple_of(i * 64, 64), 64), :] = jnp.zeros((64, LANES), jnp.float32)
        return carry

    lax.fori_loop(0, joined.shape[0] // 64, clear, 0)

    def blank(x, carry):
        spec[pl.ds(pl.multiple_of(x * pitch + parts * count, 8), count), :] = jnp.zeros((count, LANES), jnp.float32)
        return carry

    lax.fori_loop(0, 2 * windows, blank, 0)
    square[...] = jnp.zeros(square.shape, jnp.float32)
    load[0].wait()

    def transform(j, carry):
        col = nearest(j)
        chunk(j).wait()
        spectrum[...] = jnp.dot(records[...], table[j], preferred_element_type=jnp.float32)

        def narrow(i, inner):
            some = pl.ds(pl.multiple_of(i * 16, 16), 16)
            real, imag = spectrum[some, :LANES], spectrum[some, LANES:]
            white[col, some] = real.astype(jnp.bfloat16)
            white[wide + col, some] = imag.astype(jnp.bfloat16)
            square[some, :] += real * real + imag * imag
            return inner

        lax.fori_loop(0, rows // 16, narrow, 0, unroll=4)

        @pl.when(j == 0)
        def _():
            pl.semaphore_wait(barrier, wide - 1 + replies_far + ships_there)
            for ri in range(2):
                ship_own(ri).start()

            @pl.when(both_ways)
            def _():
                for ri in range(2):
                    drop_own(ri).start()

        @pl.when(j > 0)
        def _():
            for ri in range(2):
                swap(ri, col).start()
        return carry

    lax.fori_loop(0, chunks, transform, 0)
    for one in load[1:]:
        one.wait()
    place = lax.broadcasted_iota(jnp.int32, (16, LANES), 0)
    channel = lax.broadcasted_iota(jnp.int32, (8, LANES), 1) // windows
    terms = jnp.zeros((16, LANES), jnp.float32)
    for part in range(rows // LANES):
        total = jnp.sum(square[part * LANES:(part + 1) * LANES, :], axis=1, keepdims=True)
        scale = jnp.broadcast_to(lax.rsqrt(total * (1.0 / (2 * F)) + 1e-06), (LANES, LANES)).T[:8]
        alive = jnp.zeros((8, LANES), jnp.float32)
        for n in range(LANES // windows):
            alive = jnp.where(channel == n, mask_ref[part * (LANES // windows) + n].astype(jnp.float32), alive)
        rest = (scale * alive)[:1]
        for term in range(3):
            kept = rest.astype(jnp.bfloat16).astype(jnp.float32)
            terms = jnp.where(place == part * 3 + term, kept, terms)
            rest = rest - kept
    gains[...] = terms.astype(jnp.bfloat16)
    fetch = pltpu.make_async_copy(inverse_hbm, inverse, l_sem.at[0])
    fetch.start()

    def settle(s, gain, piece_of):
        for part in range(rows // LANES):
            scale = sum(gain[part * 3 + term:part * 3 + term + 1].astype(jnp.float32) for term in range(3))
            column[part * LANES:(part + 1) * LANES, :] = jnp.broadcast_to(scale, (LANES, LANES)).T

        def one(i, carry):
            some = pl.ds(pl.multiple_of(i * 2 * windows, 2 * windows), 2 * windows)
            factor = column[some, :]
            for ri in range(2):
                value = piece_of(ri, i).astype(jnp.float32) * factor
                for part in range(2):
                    row = ri * windows * pitch + s * count + 2 * i + part
                    spec[pl.ds(row, windows, stride=pitch), :] = value[part * windows:(part + 1) * windows]
            return carry

        lax.fori_loop(0, count // 2, one, 0, unroll=4)

    def own_rows(ri, i):
        return white[ri * wide + q, pl.ds(pl.multiple_of(i * 2 * windows, 2 * windows), 2 * windows)]

    def arrive(s, onward, downward):
        ship(s).wait_recv()
        if onward is not None:
            @pl.when(onward)
            def _():
                ship(s).start()
        if downward is not None:
            @pl.when(downward)
            def _():
                drop(s).start()

    def unfold(s, onward, downward):
        gain_on(s, me).wait_recv()
        if onward is not None:
            @pl.when(onward)
            def _():
                gain_on(s, neighbour).start()
        if downward is not None:
            @pl.when(downward)
            def _():
                gain_on(s, me - wide).start()
        settle(
            s, scales[s],
            lambda ri, i: held[s, pl.ds(pl.multiple_of(ri * rows + i * 2 * windows, 2 * windows), 2 * windows)])

    def takes(start, begin, end, onward=None, downward=None):
        def one(j, carry):
            arrive(start + nearest(j), onward, downward)
            return carry

        def two(j, carry):
            unfold(start + nearest(j), onward, downward)
            return carry

        lax.fori_loop(begin, end, one, 0)
        lax.fori_loop(begin, end, two, 0)

    def block(d, k):
        shift = offsets_ref[k]
        for g in range(count // 16):
            mine = d * count + g * 16
            real = imag = None
            for w in range(windows):
                cr = spec[pl.ds(pl.multiple_of(w * pitch + mine, 8), 16), :]
                ci = spec[pl.ds(pl.multiple_of((windows + w) * pitch + mine, 8), 16), :]
                pr = spec[pl.ds(w * pitch + mine + shift, 16), :]
                pi = spec[pl.ds((windows + w) * pitch + mine + shift, 16), :]
                re, im = cr * pr + ci * pi, ci * pr - cr * pi
                real, imag = (re, im) if w == 0 else (real + re, imag + im)
            rows = slice(g * 16, g * 16 + 16)
            made[d * pairs + k, 0, rows] = (real * (1.0 / windows)).astype(jnp.bfloat16)
            made[d * pairs + k, 1, rows] = (imag * (1.0 / windows)).astype(jnp.bfloat16)

    def spans(d_begin, d_end, u_begin, u_end, visit):
        def reach(u, carry):
            def one(d, inner):
                visit(d, u - 1 - d)
                return inner

            return lax.fori_loop(jnp.maximum(d_begin, u - pairs), jnp.minimum(d_end, u), one, carry)

        lax.fori_loop(u_begin, u_end, reach, 0)

    def give(d, k):
        @pl.when(d != me)
        def _():
            reply(d, k).start()

    def blocks(*span):
        spans(*span, block)
        spans(*span, give)

    y = q // 2
    def reached_1(start, more=0):
        return jnp.where(y == 0, start, start + 3), jnp.where(y == 0, start + 2, start + wide + more)

    def reached_2(start, more=0):
        return jnp.where(y == 0, start + 2, start), jnp.where(y == 0, start + wide + more, start + 3)

    settle(me, gains[...], own_rows)
    gain_to(neighbour).start()

    @pl.when(both_ways)
    def _():
        gain_to(me - wide).start()
    for col in (sib_q, mate_q, far_q):
        gain_to(first + col).start()
    takes(first, 1, 2, z >= 0, both_ways)
    takes(first, 2, wide, z >= 0, both_ways)
    blocks(first, first + wide, first + 1, first + wide + jnp.where(z == top, 1, 0))

    @pl.when(z == 0)
    def _():
        for begin, reached in ((0, reached_1), (2, reached_2)):
            takes(wide, begin, begin + 2)
            blocks(0, wide, *reached(wide))

    @pl.when(inner_low)
    def _():
        takes(0, 0, 2, jnp.logical_not(near))
        takes(base, 0, 2)
        blocks(2 * y, 2 * y + 2, *reached_1(base))
        blocks(wide, base, *reached_1(base))
        takes(0, 2, wide, jnp.logical_not(near))
        blocks(2 - 2 * y, wide - 2 * y, *reached_1(base))
        takes(base, 2, wide)
        blocks(0, base, *reached_2(base))

        @pl.when(near)
        def _():
            for begin, reached in ((0, reached_1), (2, reached_2)):
                takes(top * wide, begin, begin + 2)
                blocks(0, base, *reached(top * wide, 1))

    @pl.when(inner_high)
    def _():
        for begin, reached in ((0, reached_1), (2, reached_2)):
            takes(top * wide, begin, begin + 2, near)
            blocks(base, base + wide, *reached(top * wide, 1))

        @pl.when(jnp.logical_not(near))
        def _():
            takes(wide, 0, wide)
            spans(wide, base, top * wide, parts + 1, block)
            takes(0, 0, 2)
            blocks(2 * y, 2 * y + 2, top * wide, parts + 1)
            takes(0, 2, wide)
            blocks(2 - 2 * y, wide - 2 * y, top * wide, parts + 1)
            spans(wide, base, top * wide, parts + 1, give)

    group = pairs // 2

    def unpack(source, k, col):
        for ri in range(2):
            for g in range(count // 16):
                value = source[ri, g * 16:g * 16 + 16].astype(jnp.float32)
                for part in range(2):
                    seg = (k // group) * 2 * wide + ri * wide + col
                    row = (seg * count + g * 16 + part * 8) * group + k % group
                    joined[pl.ds(row, 8, stride=group), :] = value[part * 8:part * 8 + 8]

    def collect(k, carry):
        away = me + k + 1 >= own_end
        def received(cols):
            remote(back.at[k, 0:cols], back.at[k, 0:cols], r_send, r_recv.at[k], me).wait_recv()

        @pl.when(away)
        def _():
            received(wide)

        @pl.when(jnp.logical_not(away))
        def _():
            received(wide - 1)

        for col in range(wide):
            here = jnp.logical_and(q == col, jnp.logical_not(away))

            @pl.when(here)
            def _():
                unpack(made_at(me, k), k, col)

            @pl.when(jnp.logical_not(here))
            def _():
                unpack(back.at[k, col], k, col)
        return carry

    def pack(which, target):
        def one(i, carry):
            rows = pl.ds(pl.multiple_of(i * 16, 16), 16)
            for x in range(2 * wide):
                start = pl.multiple_of((which * 2 * wide + x) * count * group + i * 16, 16)
                target[rows, x * LANES:(x + 1) * LANES] = joined[pl.ds(start, 16), :].astype(jnp.bfloat16)
            return carry

        lax.fori_loop(0, count * group // 16, one, 0, unroll=2)

    lax.fori_loop(0, jnp.minimum(group, parts - me), collect, 0)
    pack(0, crossed)
    fetch.wait()
    for n in range(0, LAGS, SPAN):
        lagged = jnp.dot(crossed[...], inverse[:, n:n + SPAN], preferred_element_type=jnp.float32)
        half_ref[:, n:n + SPAN] = (lagged * (1.0 / math.sqrt(F))).astype(jnp.bfloat16)
    lax.fori_loop(group, parts - me, collect, 0)
    pack(1, cross_ref)

    shipped(wide - 1, x_send)
    forwards = jnp.logical_or(both_ways, jnp.logical_and(inner_high, near))

    def told(slots):
        remote(scales.at[0:slots], scales.at[0:slots], n_send, n_recv.at[0], me).wait_send()

    @pl.when(both_ways)
    def _():
        shipped(wide, g_send)
        shipped(2 * wide, f_send)
        told(4 * wide - 1)

    @pl.when(jnp.logical_and(inner_high, near))
    def _():
        shipped(2 * wide, f_send)
        told(3 * wide - 1)

    @pl.when(jnp.logical_not(forwards))
    def _():
        shipped(wide, f_send)
        told(2 * wide - 1)

    for i in range(parts):
        layer, odd = i // wide, i % 2 == 1
        ends = base if layer == 0 else base + wide if layer == half - 1 and odd else parts + 1
        replies = sum(
            min(ends, d + pairs + 1) - d - 1 for d in range(layer * wide, (layer + 1) * wide) if d != i)
        if layer == half - 1 or (layer == half and odd):
            begins = base if layer == half - 1 else base + wide
            replies += sum(min(ends, d + pairs + 1) - begins for d in range(layer * wide))

        @pl.when(me == i)
        def _():
            done = made.at[0:replies]
            remote(done, done, r_send, r_recv.at[0], me).wait_send()


def meet(layers, wide, records, live_mask, offsets):
    pairs = offsets.shape[0]
    count, windows, length = records.shape
    parts = layers * wide
    pitch = (parts + 1) * count
    rows = count * windows
    width = 2 * LANES
    chunks = 2 * F // width
    table = np.ascontiguousarray(
        forward_table(length).reshape(length, 2, chunks, LANES).transpose(2, 0, 1, 3).reshape(chunks, length, width))
    return pl.pallas_call(
        functools.partial(middle_kernel, (layers, wide, windows)),
        out_shape=[
            jax.ShapeDtypeStruct((count * pairs // 2, LAGS), jnp.bfloat16),
            jax.ShapeDtypeStruct((count * pairs // 2, 2 * F), jnp.bfloat16),
            jax.ShapeDtypeStruct((2 * F, LAGS), jnp.bfloat16),
        ],
        in_specs=[
            pl.BlockSpec(memory_space=pltpu.HBM),
            pl.BlockSpec(memory_space=pltpu.HBM),
            pl.BlockSpec(memory_space=pltpu.HBM),
            pl.BlockSpec(memory_space=pltpu.HBM),
            pl.BlockSpec(memory_space=pltpu.HBM),
        ],
        out_specs=[pl.BlockSpec(memory_space=pltpu.VMEM)] * 3,
        scratch_shapes=[
            pltpu.SMEM((pairs,), jnp.int32),
            pltpu.SMEM((count,), jnp.int32),
            pltpu.VMEM((rows, length), jnp.bfloat16),
            pltpu.VMEM((chunks, length, width), jnp.bfloat16),
            pltpu.VMEM((count * pairs // 2, 2 * F), jnp.bfloat16),
            pltpu.VMEM((rows, width), jnp.float32),
            pltpu.VMEM((rows, LANES), jnp.float32),
            pltpu.VMEM((2 * wide, rows, LANES), jnp.bfloat16),
            pltpu.VMEM((16, LANES), jnp.bfloat16),
            pltpu.VMEM((rows, LANES), jnp.float32),
            pltpu.VMEM((parts, 16, LANES), jnp.bfloat16),
            pltpu.VMEM((parts, 2 * rows, LANES), jnp.bfloat16),
            pltpu.VMEM((2 * windows * pitch, LANES), jnp.float32),
            pltpu.VMEM((parts * pairs, 2, count, LANES), jnp.bfloat16),
            pltpu.VMEM((pairs, wide, 2, count, LANES), jnp.bfloat16),
            pltpu.VMEM((2 * wide * count * pairs, LANES), jnp.float32),
            pltpu.SemaphoreType.DMA((chunks + 3,)),
            pltpu.SemaphoreType.DMA,
            pltpu.SemaphoreType.DMA,
            pltpu.SemaphoreType.DMA,
            pltpu.SemaphoreType.DMA,
            pltpu.SemaphoreType.DMA((parts,)),
            pltpu.SemaphoreType.DMA((parts,)),
            pltpu.SemaphoreType.DMA,
            pltpu.SemaphoreType.DMA((pairs,)),
        ],
        compiler_params=pltpu.CompilerParams(
            vmem_limit_bytes=36 * 1024 * 1024, collective_id=1, has_side_effects=True
        ),
    )(*[
        pltpu.with_memory_space_constraint(x, pltpu.HBM)
        for x in (offsets, live_mask, records.reshape(rows, length), jnp.asarray(table),
                  jnp.asarray(inverse_table(length)))
    ])


def finish_kernel(half_ref, cross_ref, table_ref, out_hbm, stage, sem):
    group = out_hbm.shape[1] // 2
    copies = [pltpu.make_async_copy(half_ref, out_hbm.at[:, 0:group], sem.at[0])]
    copies[0].start()
    for i, n in enumerate(range(0, LAGS, SPAN)):
        lagged = jnp.dot(cross_ref[...], table_ref[:, n:n + SPAN], preferred_element_type=jnp.float32)
        lagged = (lagged * (1.0 / math.sqrt(F))).astype(jnp.bfloat16)
        stage[:, :, n:n + SPAN] = lagged.reshape(stage.shape[0], group, SPAN)
        copies.append(pltpu.make_async_copy(
            stage.at[:, :, n:n + SPAN], out_hbm.at[:, group:2 * group, n:n + SPAN], sem.at[i + 1]))
        copies[-1].start()
    for one in copies:
        one.wait()


def finish(half, cross, table, count, pairs):
    return pl.pallas_call(
        finish_kernel,
        out_shape=jax.ShapeDtypeStruct((count, pairs, LAGS), jnp.bfloat16),
        in_specs=[pl.BlockSpec(memory_space=pltpu.VMEM)] * 3,
        out_specs=pl.BlockSpec(memory_space=pltpu.HBM),
        scratch_shapes=[
            pltpu.VMEM((count, pairs // 2, LAGS), jnp.bfloat16),
            pltpu.SemaphoreType.DMA((LAGS // SPAN + 1,)),
        ],
        compiler_params=pltpu.CompilerParams(vmem_limit_bytes=16 * 1024 * 1024),
    )(half.reshape(count, pairs // 2, LAGS), cross, table)


def shards(columns, records, live_mask, offsets):
    count, windows, length = records.shape
    pairs = offsets.shape[0]
    wide = 2 * columns
    layers = lax.axis_size("chan") // wide
    reach = (BAND + count - 2) // count
    depth = min(layers - 1, (wide - 1 + reach) // wide)
    pieces = PIECES
    fold = columns == 2 and depth == layers - 1 and depth >= 2 and layers * wide == pairs and pairs * count == BAND
    if (
        columns == 2 and layers == 4 and layers * wide == pairs and pairs * count == BAND
        and F == wide * LANES and windows == 8 and count % 16 == 0
    ):
        half, cross, inverse = meet(layers, wide, records, live_mask, offsets)
        return finish(half, cross, inverse, count, pairs)
    spectra = whiten(records, live_mask).reshape(count, windows * 8, LANES)
    slots = (depth + 1) * wide
    cross = pl.pallas_call(
        functools.partial(reach_kernel, (layers, columns, depth, pieces, windows, fold)),
        out_shape=jax.ShapeDtypeStruct((count, pairs, 8, LANES), jnp.float32),
        in_specs=[
            pl.BlockSpec(memory_space=pltpu.SMEM),
            pl.BlockSpec(memory_space=pltpu.VMEM),
        ],
        out_specs=pl.BlockSpec(memory_space=pltpu.VMEM),
        scratch_shapes=[
            pltpu.VMEM((slots + wide, count, windows * 8, LANES), jnp.bfloat16),
            pltpu.VMEM((slots * count, windows * 8, LANES), jnp.bfloat16),
            pltpu.VMEM((count, windows * 8, LANES), jnp.float32),
            pltpu.VMEM((count, windows * 8, LANES), jnp.float32),
            pltpu.VMEM((wide, count, 8, LANES), jnp.bfloat16),
            pltpu.VMEM((wide, count, 8, LANES), jnp.bfloat16),
        ]
        + [pltpu.SemaphoreType.DMA((depth + 2, pieces))] * 9
        + [pltpu.SemaphoreType.DMA((wide,))] * 2,
        compiler_params=pltpu.CompilerParams(
            vmem_limit_bytes=40 * 1024 * 1024, collective_id=0, has_side_effects=True
        ),
    )(offsets, spectra)
    return lags(cross.astype(jnp.bfloat16).reshape(count * pairs, 8 * LANES), count, pairs, length)


def lags(cross, count, pairs, length):
    result = jnp.dot(cross, jnp.asarray(inverse_table(length)), preferred_element_type=jnp.float32)
    result = result * (1.0 / math.sqrt(F))
    return result.reshape(count, pairs, LAGS).astype(jnp.bfloat16)


def solution(mesh):
    in_specs = (P(("day", "chan"), None, None), P(("day", "chan")), P())
    out_specs = P(("day", "chan"), None, None)
    columns = max(1, LAYER_CHIPS // mesh.shape["day"])
    body = functools.partial(shards, columns)
    return jax.shard_map(body, mesh=mesh, in_specs=in_specs, out_specs=out_specs, check_vma=False)
```

```python
import functools
import math

import jax
import jax.numpy as jnp
import numpy as np
from jax import lax
from jax.experimental import pallas as pl
from jax.experimental.pallas import tpu as pltpu
from jax.sharding import PartitionSpec as P

F = 512
F0 = 6
LAGS = 2048
LANES = 128
SPAN = 512
BAND = 512
PIECES = 4
LAYER_CHIPS = 4


def forward_table(length):
    samples = np.arange(length, dtype=np.int64)
    freqs = F0 + np.arange(F, dtype=np.int64)
    phase = np.mod(samples[:, None] * freqs[None, :], length)
    angle = 2.0 * math.pi / length * phase
    return np.concatenate([np.cos(angle), -np.sin(angle)], axis=1).astype(np.float32).astype(jnp.bfloat16)


def inverse_table(length):
    freqs = F0 + np.arange(F, dtype=np.int64)
    shifts = np.arange(LAGS, dtype=np.int64) - LAGS // 2
    phase = np.mod(freqs[:, None] * shifts[None, :], length)
    angle = 2.0 * math.pi / length * phase
    return np.concatenate([np.cos(angle), -np.sin(angle)], axis=0).astype(np.float32).astype(jnp.bfloat16)


def whiten(records, live_mask):
    count, windows, length = records.shape
    spectrum = jnp.dot(
        records.reshape(count * windows, length),
        jnp.asarray(forward_table(length)),
        preferred_element_type=jnp.float32,
    )
    power = jnp.mean(spectrum * spectrum, axis=1, keepdims=True)
    gain = jnp.repeat(live_mask.astype(jnp.float32), windows)[:, None]
    white = spectrum * (gain * lax.rsqrt(power + 1e-06))
    return white.astype(jnp.bfloat16)


def reach_kernel(shape, offsets_ref, white_ref, cross_ref, held, ext, own, swapped, made, back,
                 z_send, z_recv, c_send, c_recv, y_send, y_recv, d_send, d_recv, e_send, r_send, r_recv):
    layers, columns, depth, pieces, windows, fold = shape
    count, slab = white_ref.shape[0], white_ref.shape[1]
    pairs = offsets_ref.shape[0]
    wide = 2 * columns
    total = layers * wide * count
    me = lax.axis_index("chan")
    z, q = me // wide, me % wide
    y, c = q // 2, q % 2
    sibling = me + 1 - 2 * c
    sib_q = q + 1 - 2 * c
    mate = me + 2 - 4 * y
    mate_q = q + 2 - 4 * y
    far_q = sib_q + 2 - 4 * y
    step = count // pieces
    top, lifted = layers - 1, depth + 1

    barrier = pltpu.get_barrier_semaphore()

    def greet(device):
        pl.semaphore_signal(barrier, inc=1, device_id={"chan": device}, device_id_type=pl.DeviceIdType.MESH)

    greet(sibling)
    if columns == 2:
        greet(mate)

    @pl.when(z >= 1)
    def _():
        greet(me - wide)

    @pl.when(z < layers - 1)
    def _():
        greet(me + wide)

    below, above = jnp.minimum(z, 1), jnp.minimum(top - z, 1)
    peers = columns + below + above
    if fold:
        @pl.when(z == 0)
        def _():
            for i in range(wide):
                greet(top * wide + i)

        @pl.when(z == top)
        def _():
            for i in range(wide):
                greet(jnp.int32(i))

        peers = peers + wide * (2 - below - above)
    pl.semaphore_wait(barrier, peers)

    def rows(p):
        return pl.ds(p * step, step)

    def mine(dz, p):
        return white_ref.at[rows(p)] if dz == 0 else held.at[dz * wide + q, rows(p)]

    def copy(source, slot, p, send, recv, device):
        return pltpu.make_async_remote_copy(
            src_ref=source,
            dst_ref=held.at[slot, rows(p)],
            send_sem=send,
            recv_sem=recv,
            device_id={"chan": device},
            device_id_type=pl.DeviceIdType.MESH,
        )

    def down(dz, p):
        return copy(mine(dz, p), (dz + 1) * wide + q, p, z_send.at[dz, p], z_recv.at[dz + 1, p], me - wide)

    def from_above(dz, p):
        return copy(mine(dz, p), dz * wide + q, p, z_send.at[dz, p], z_recv.at[dz, p], me)

    def across(dz, p, slot):
        return copy(mine(dz, p), slot, p, c_send.at[dz, p], c_recv.at[dz, p], sibling)

    def over(dz, p, slot):
        return copy(mine(dz, p), slot, p, y_send.at[dz, p], y_recv.at[dz, p], mate)

    def onward(dz, p, slot):
        return copy(held.at[dz * wide + mate_q, rows(p)], slot, p, d_send.at[dz, p], d_recv.at[dz, p], sibling)

    def both(*conditions):
        joined = conditions[0]
        for condition in conditions[1:]:
            joined = jnp.logical_and(joined, condition)
        return joined

    def exists(dz):
        return z + dz < layers

    def goes(dz, at_start, at_end):
        if dz == lifted:
            return z == top
        if dz == 0:
            return at_start
        if fold and dz == depth:
            return both(exists(dz), at_end)
        return exists(dz)

    def z_tx(dz):
        if fold and dz + 1 == depth:
            return both(exists(dz), z >= 1, jnp.logical_or(z >= 2, q == 0))
        return both(exists(dz), z >= 1)

    def z_rx(dz):
        return goes(dz, None, q == 0)

    def c_tx(dz):
        return goes(dz, c == 1, q == 0)

    def c_rx(dz):
        return goes(dz, c == 0, q == 1)

    def y_tx(dz):
        return goes(dz, y == 1, q == 0)

    def y_rx(dz):
        return goes(dz, y == 0, q == 2)

    def detoured(dz, p):
        return fold and dz == depth - 1 and p == pieces - 1

    def over_tx(dz, p):
        if detoured(dz, p):
            return both(y_tx(dz), jnp.logical_or(z > 0, y == 0))
        if raised(dz, p):
            return both(y_tx(dz), y == 0)
        return y_tx(dz)

    def raised(dz, p):
        return fold and dz == lifted and p >= pieces // 2

    def lift_mate(p):
        return copy(held.at[mate_q, rows(p)], lifted * wide + mate_q, p,
                    e_send.at[lifted, p], y_recv.at[lifted, p], me + top * wide)

    def extra(dz, p):
        return copy(held.at[dz * wide + mate_q, rows(p)], (dz + 1) * wide + mate_q, p,
                    e_send.at[dz, p], y_recv.at[dz + 1, p], me - wide)

    def extra_tx():
        return both(z == 1, y == 0)

    def d_rx(dz):
        return goes(dz, y == 0, q == 3)

    def lift(p):
        return copy(white_ref.at[rows(p)], lifted * wide + q, p, z_send.at[lifted, p], z_recv.at[lifted, p],
                    me + top * wide)

    def sends(dz):
        for p in range(pieces):
            if dz > 0:
                @pl.when(z_rx(dz))
                def _():
                    from_above(dz, p).wait_recv()
            if dz < depth:
                @pl.when(z_tx(dz))
                def _():
                    down(dz, p).start()
            if columns == 2:
                @pl.when(over_tx(dz, p))
                def _():
                    over(dz, p, dz * wide + q).start()
            @pl.when(c_tx(dz))
            def _():
                across(dz, p, dz * wide + q).start()

    def passes(dz):
        if columns == 2:
            for p in range(pieces):
                @pl.when(y_rx(dz))
                def _():
                    over(dz, p, dz * wide + mate_q).wait_recv()
                    onward(dz, p, dz * wide + mate_q).start()
                if dz == 0 and raised(lifted, p):
                    @pl.when(both(z == 0, y == 0))
                    def _():
                        lift_mate(p).start()
                if detoured(dz + 1, p):
                    @pl.when(extra_tx())
                    def _():
                        extra(dz, p).start()

    def arrives(dz):
        for p in range(pieces):
            @pl.when(c_rx(dz))
            def _():
                across(dz, p, dz * wide + sib_q).wait_recv()
            if columns == 2:
                @pl.when(d_rx(dz))
                def _():
                    onward(dz, p, dz * wide + far_q).wait_recv()

    def finishes(dz):
        for p in range(pieces):
            if dz < depth:
                @pl.when(z_tx(dz))
                def _():
                    down(dz, p).wait_send()
            if columns == 2:
                @pl.when(over_tx(dz, p))
                def _():
                    over(dz, p, dz * wide + q).wait_send()
                if detoured(dz + 1, p):
                    @pl.when(extra_tx())
                    def _():
                        extra(dz, p).wait_send()
                @pl.when(y_rx(dz))
                def _():
                    onward(dz, p, dz * wide + mate_q).wait_send()
            @pl.when(c_tx(dz))
            def _():
                across(dz, p, dz * wide + q).wait_send()

    def answer(i):
        return pltpu.make_async_remote_copy(
            src_ref=made.at[i],
            dst_ref=back.at[q],
            send_sem=r_send.at[i],
            recv_sem=r_recv.at[q],
            device_id={"chan": jnp.int32(i)},
            device_id_type=pl.DeviceIdType.MESH,
        )

    def answered(i):
        return pltpu.make_async_remote_copy(
            src_ref=made.at[i],
            dst_ref=back.at[i],
            send_sem=r_send.at[i],
            recv_sem=r_recv.at[i],
            device_id={"chan": me},
            device_id_type=pl.DeviceIdType.MESH,
        )

    low = lax.broadcasted_iota(jnp.int32, (8, LANES), 0) < 4

    def prepare(i, carry):
        raw = white_ref[i]
        value = raw.astype(jnp.float32)
        own[i] = value
        ext[q * count + i] = raw
        for w in range(windows):
            swapped[i, w * 8 : w * 8 + 8] = pltpu.roll(value[w * 8 : w * 8 + 8], 4, 0)
        return carry

    def settle(dz):
        def one(l):
            def fill(i, carry):
                ext[(dz * wide + l) * count + i] = held[dz * wide + l, i]
                return carry
            lax.fori_loop(0, count, fill, 0, unroll=4)

        if dz == 0:
            for l in range(1, wide):
                @pl.when(q < l)
                def _():
                    one(l)
        else:
            @pl.when(exists(dz))
            def _():
                for l in range(1 if fold and dz == depth else wide):
                    one(l)

    live = jnp.minimum(layers * wide - me, pairs)

    def outside():
        def nothing(k, carry):
            for r in range(count):
                cross_ref[r, k] = jnp.zeros((8, LANES), jnp.float32)
            return carry

        lax.fori_loop(live, pairs, nothing, 0)

        @pl.when(layers - z <= depth)
        def _():
            def blank(i, carry):
                ext[(layers - z) * wide * count + i] = jnp.zeros((slab, LANES), jnp.bfloat16)
                return carry

            lax.fori_loop(0, 2 * count, blank, 0, unroll=4)

    def reached(dz):
        if dz < 0:
            return 0
        if dz == depth:
            return live
        return jnp.minimum((dz + 1) * wide - q - 1, live)

    def multiply(dz):
        def pair(k, carry):
            shift = offsets_ref[k]

            def channel(i, inner):
                place = me * count + i + shift
                keep = jnp.where(place < total, 1.0 / windows, 0.0)
                near = jnp.minimum(q * count + i + shift, ext.shape[0] - 1)
                partner = ext[near].astype(jnp.float32)
                straight = own[i, :8] * partner[:8]
                twisted = swapped[i, :8] * partner[:8]
                for w in range(1, windows):
                    part = slice(w * 8, w * 8 + 8)
                    straight += own[i, part] * partner[part]
                    twisted += swapped[i, part] * partner[part]
                joined = jnp.where(
                    low,
                    straight + pltpu.roll(straight, 4, 0),
                    pltpu.roll(twisted, 4, 0) - twisted,
                )
                cross_ref[i, k] = joined * keep
                return inner

            return lax.fori_loop(0, count, channel, carry, unroll=4)

        begin, end = reached(dz - 1), reached(dz)
        if fold and dz == depth:
            @pl.when(z == 0)
            def _():
                lax.fori_loop(begin, begin + 1, pair, 0)

            @pl.when(z > 0)
            def _():
                lax.fori_loop(begin, end, pair, 0)
        else:
            lax.fori_loop(begin, end, pair, 0)

    def reply():
        for i in range(wide):
            shift = offsets_ref[top * wide + q - i]

            def channel(r, carry):
                place = i * count + r + shift
                keep = jnp.where(place < total, 1.0 / windows, 0.0)
                near = jnp.clip(place - top * wide * count, 0, ext.shape[0] - 1)
                partner = ext[near].astype(jnp.float32)
                value = held[lifted * wide + i, r].astype(jnp.float32)
                straight = value[:8] * partner[:8]
                twisted = pltpu.roll(value[:8], 4, 0) * partner[:8]
                for w in range(1, windows):
                    part = slice(w * 8, w * 8 + 8)
                    straight += value[part] * partner[part]
                    twisted += pltpu.roll(value[part], 4, 0) * partner[part]
                joined = jnp.where(
                    low,
                    straight + pltpu.roll(straight, 4, 0),
                    pltpu.roll(twisted, 4, 0) - twisted,
                )
                made[i, r] = (joined * keep).astype(jnp.bfloat16)
                return carry

            lax.fori_loop(0, count, channel, 0, unroll=4)
        for i in range(wide):
            answer(i).start()

    sends(0)
    if fold:
        @pl.when(z == 0)
        def _():
            for p in range(pieces):
                lift(p).start()

    lax.fori_loop(0, count, prepare, 0)
    outside()
    for dz in range(depth + 1):
        if dz < depth:
            sends(dz + 1)
        if fold and dz == 0:
            sends(lifted)
        passes(dz)
        if fold and dz == 0:
            passes(lifted)
        arrives(dz)
        settle(dz)
        if fold and dz == 0:
            arrives(lifted)

            @pl.when(z == top)
            def _():
                reply()

        multiply(dz)

    if fold:
        @pl.when(z == 0)
        def _():
            for i in range(wide):
                answered(i).wait_recv()

                def take(r, carry):
                    cross_ref[r, top * wide - q + i] = back[i, r].astype(jnp.float32)
                    return carry

                lax.fori_loop(0, count, take, 0, unroll=4)
            for p in range(pieces):
                lift(p).wait_send()
                if raised(lifted, p):
                    @pl.when(y == 0)
                    def _():
                        lift_mate(p).wait_send()

        @pl.when(z == top)
        def _():
            for i in range(wide):
                answer(i).wait_send()

        finishes(lifted)
    for dz in range(depth + 1):
        finishes(dz)


def middle_kernel(shape, offsets_hbm, mask_hbm, records_hbm, table_hbm, inverse_hbm, half_ref, cross_ref, inverse,
                  offsets_ref, mask_ref, records, table, crossed, spectrum, square, white, gains, column, scales, held, spec, made, back, joined,
                  l_sem, x_send, f_send, g_send, n_send, n_recv, s_recv, r_send, r_recv):
    layers, wide, windows = shape
    pairs = offsets_ref.shape[0]
    count = records.shape[0] // windows
    chunks, width = table.shape[0], table.shape[2]
    rows = count * windows
    parts = layers * wide
    pitch = spec.shape[0] // (2 * windows)
    half, top, last = layers // 2, layers - 1, parts - 1
    me = lax.axis_index("chan")
    z, q = me // wide, me % wide
    c = q % 2
    first = z * wide
    base = half * wide
    sib_q = q + 1 - 2 * c
    mate_q = (q + 2) % wide
    far_q = (sib_q + 2) % wide
    near = c == 0

    def nearest(j):
        return jnp.where(j == 0, q, jnp.where(j == 1, sib_q, jnp.where(j == 2, mate_q, far_q)))

    def slowest(j):
        return jnp.where(j == 0, q, jnp.where(j == 1, mate_q, jnp.where(j == 2, sib_q, far_q)))

    def chunk(j):
        return pltpu.make_async_copy(table_hbm.at[slowest(j)], table.at[j], l_sem.at[j])

    load = [
        pltpu.make_async_copy(records_hbm, records, l_sem.at[chunks]),
        pltpu.make_async_copy(offsets_hbm, offsets_ref, l_sem.at[chunks + 1]),
        pltpu.make_async_copy(mask_hbm, mask_ref, l_sem.at[chunks + 2]),
    ]
    load[0].start()
    for n in range(chunks):
        chunk(n).start()
    for one in load[1:]:
        one.start()
    inner_low, inner_high = z == half - 1, z == half
    neighbour = jnp.where(
        jnp.logical_or(z == 0, jnp.logical_and(inner_low, c == 1)), me + wide, me - wide)
    own_end = jnp.where(
        z == 0, jnp.where(near, base, jnp.where(q < 2, wide + 2, wide)),
        jnp.where(jnp.logical_and(inner_low, c == 1), base + wide, parts + 1))
    barrier = pltpu.get_barrier_semaphore()

    def greet(device, condition):
        @pl.when(condition)
        def _():
            pl.semaphore_signal(barrier, inc=1, device_id={"chan": jnp.int32(device)},
                                device_id_type=pl.DeviceIdType.MESH)

    for col in (sib_q, mate_q, far_q):
        greet(first + col, z >= 0)
    for i in range(wide):
        odd = i % 2 == 1
        greet(wide + i, z == 0)
        if odd:
            greet(base + i, z < half)
        else:
            greet(base + i, jnp.logical_and(inner_low, q == i))
    greet(me - wide, jnp.logical_or(inner_low, jnp.logical_and(inner_high, c == 1)))
    greet(me + wide, inner_high)
    replies_far = jnp.where(inner_low, wide, jnp.where(jnp.logical_and(inner_high, c == 1), 2 * wide - 1, 0))
    ships_there = jnp.where(jnp.logical_and(inner_low, near), 0, 1)

    def remote(source, target, send, recv, device):
        return pltpu.make_async_remote_copy(
            src_ref=source, dst_ref=target, send_sem=send, recv_sem=recv,
            device_id={"chan": device}, device_id_type=pl.DeviceIdType.MESH,
        )

    def piece(ri, col):
        return white.at[ri * wide + col]

    def swap(ri, col):
        return remote(piece(ri, col), held.at[me, pl.ds(ri * rows, rows)], x_send, s_recv.at[me], first + col)

    def ship_own(ri):
        return remote(piece(ri, q), held.at[me, pl.ds(ri * rows, rows)], f_send, s_recv.at[me], neighbour)

    def ship(s):
        return remote(held.at[s], held.at[s], f_send, s_recv.at[s], neighbour)

    both_ways = jnp.logical_and(inner_low, c == 1)

    def drop_own(ri):
        return remote(piece(ri, q), held.at[me, pl.ds(ri * rows, rows)], g_send, s_recv.at[me], me - wide)

    def drop(s):
        return remote(held.at[s], held.at[s], g_send, s_recv.at[s], me - wide)

    def made_at(d, k):
        return made.at[d * pairs + k]

    def reply(d, k):
        return remote(made_at(d, k), back.at[k, q], r_send, r_recv.at[k], d)

    def shipped(slots, send):
        remote(held.at[0:slots], held.at[0:slots], send, s_recv.at[0], neighbour).wait_send()

    def gain_to(device):
        return remote(gains, scales.at[me], n_send, n_recv.at[me], device)

    def gain_on(s, device):
        return remote(scales.at[s], scales.at[s], n_send, n_recv.at[s], device)

    def clear(i, carry):
        joined[pl.ds(pl.multiple_of(i * 64, 64), 64), :] = jnp.zeros((64, LANES), jnp.float32)
        return carry

    lax.fori_loop(0, joined.shape[0] // 64, clear, 0)

    def blank(x, carry):
        spec[pl.ds(pl.multiple_of(x * pitch + parts * count, 8), count), :] = jnp.zeros((count, LANES), jnp.float32)
        return carry

    lax.fori_loop(0, 2 * windows, blank, 0)
    square[...] = jnp.zeros(square.shape, jnp.float32)
    load[0].wait()

    def transform(j, carry):
        col = slowest(j)
        chunk(j).wait()
        spectrum[...] = jnp.dot(records[...], table[j], preferred_element_type=jnp.float32)

        def narrow(i, inner):
            some = pl.ds(pl.multiple_of(i * 16, 16), 16)
            real, imag = spectrum[some, :LANES], spectrum[some, LANES:]
            white[col, some] = real.astype(jnp.bfloat16)
            white[wide + col, some] = imag.astype(jnp.bfloat16)
            square[some, :] += real * real + imag * imag
            return inner

        lax.fori_loop(0, rows // 16, narrow, 0, unroll=4)

        @pl.when(j == 0)
        def _():
            pl.semaphore_wait(barrier, wide - 1 + replies_far + ships_there)
            for ri in range(2):
                ship_own(ri).start()

            @pl.when(both_ways)
            def _():
                for ri in range(2):
                    drop_own(ri).start()

        @pl.when(j > 0)
        def _():
            for ri in range(2):
                swap(ri, col).start()
        return carry

    lax.fori_loop(0, chunks, transform, 0)
    for one in load[1:]:
        one.wait()
    place = lax.broadcasted_iota(jnp.int32, (16, LANES), 0)
    channel = lax.broadcasted_iota(jnp.int32, (8, LANES), 1) // windows
    terms = jnp.zeros((16, LANES), jnp.float32)
    for part in range(rows // LANES):
        total = jnp.sum(square[part * LANES:(part + 1) * LANES, :], axis=1, keepdims=True)
        scale = jnp.broadcast_to(lax.rsqrt(total * (1.0 / (2 * F)) + 1e-06), (LANES, LANES)).T[:8]
        alive = jnp.zeros((8, LANES), jnp.float32)
        for n in range(LANES // windows):
            alive = jnp.where(channel == n, mask_ref[part * (LANES // windows) + n].astype(jnp.float32), alive)
        rest = (scale * alive)[:1]
        for term in range(3):
            kept = rest.astype(jnp.bfloat16).astype(jnp.float32)
            terms = jnp.where(place == part * 3 + term, kept, terms)
            rest = rest - kept
    gains[...] = terms.astype(jnp.bfloat16)
    fetch = pltpu.make_async_copy(inverse_hbm, inverse, l_sem.at[0])
    fetch.start()

    def settle(s, gain, piece_of):
        for part in range(rows // LANES):
            scale = sum(gain[part * 3 + term:part * 3 + term + 1].astype(jnp.float32) for term in range(3))
            column[part * LANES:(part + 1) * LANES, :] = jnp.broadcast_to(scale, (LANES, LANES)).T

        def one(i, carry):
            some = pl.ds(pl.multiple_of(i * 2 * windows, 2 * windows), 2 * windows)
            factor = column[some, :]
            for ri in range(2):
                value = piece_of(ri, i).astype(jnp.float32) * factor
                for part in range(2):
                    row = ri * windows * pitch + s * count + 2 * i + part
                    spec[pl.ds(row, windows, stride=pitch), :] = value[part * windows:(part + 1) * windows]
            return carry

        lax.fori_loop(0, count // 2, one, 0, unroll=4)

    def own_rows(ri, i):
        return white[ri * wide + q, pl.ds(pl.multiple_of(i * 2 * windows, 2 * windows), 2 * windows)]

    def arrive(s, onward):
        ship(s).wait_recv()
        if onward is not None:
            @pl.when(onward)
            def _():
                ship(s).start()

    def unfold(s, onward):
        gain_on(s, me).wait_recv()
        if onward is not None:
            @pl.when(onward)
            def _():
                gain_on(s, neighbour).start()
        settle(
            s, scales[s],
            lambda ri, i: held[s, pl.ds(pl.multiple_of(ri * rows + i * 2 * windows, 2 * windows), 2 * windows)])

    def takes(start, begin, end, onward=None):
        def one(j, carry):
            arrive(start + nearest(j), onward)
            return carry

        def two(j, carry):
            unfold(start + nearest(j), onward)
            return carry

        lax.fori_loop(begin, end, one, 0)
        lax.fori_loop(begin, end, two, 0)

    def block(d, k):
        shift = offsets_ref[k]
        for g in range(count // 16):
            mine = d * count + g * 16
            real = imag = None
            for w in range(windows):
                cr = spec[pl.ds(pl.multiple_of(w * pitch + mine, 8), 16), :]
                ci = spec[pl.ds(pl.multiple_of((windows + w) * pitch + mine, 8), 16), :]
                pr = spec[pl.ds(w * pitch + mine + shift, 16), :]
                pi = spec[pl.ds((windows + w) * pitch + mine + shift, 16), :]
                re, im = cr * pr + ci * pi, ci * pr - cr * pi
                real, imag = (re, im) if w == 0 else (real + re, imag + im)
            rows = slice(g * 16, g * 16 + 16)
            made[d * pairs + k, 0, rows] = (real * (1.0 / windows)).astype(jnp.bfloat16)
            made[d * pairs + k, 1, rows] = (imag * (1.0 / windows)).astype(jnp.bfloat16)

    def spans(d_begin, d_end, u_begin, u_end, visit):
        def reach(u, carry):
            def one(d, inner):
                visit(d, u - 1 - d)
                return inner

            return lax.fori_loop(jnp.maximum(d_begin, u - pairs), jnp.minimum(d_end, u), one, carry)

        lax.fori_loop(u_begin, u_end, reach, 0)

    def give(d, k):
        @pl.when(d != me)
        def _():
            reply(d, k).start()

    def blocks(d_begin, d_end, u_begin, u_end):
        def reach(u, carry):
            spans(d_begin, d_end, u, u + 1, block)
            spans(d_begin, d_end, u, u + 1, give)
            return carry

        lax.fori_loop(u_begin, u_end, reach, 0)

    y = q // 2
    def reached_1(start, more=0):
        return jnp.where(y == 0, start, start + 3), jnp.where(y == 0, start + 2, start + wide + more)

    def reached_2(start, more=0):
        return jnp.where(y == 0, start + 2, start), jnp.where(y == 0, start + wide + more, start + 3)

    settle(me, gains[...], own_rows)
    gain_to(neighbour).start()
    for col in (sib_q, mate_q, far_q):
        gain_to(first + col).start()
    arrive(first + sib_q, z >= 0)

    @pl.when(both_ways)
    def _():
        drop(first + sib_q).start()
        gain_to(me - wide).start()
    unfold(first + sib_q, z >= 0)

    @pl.when(both_ways)
    def _():
        gain_on(first + sib_q, me - wide).start()
    takes(first, 2, wide, z >= 0)
    blocks(first, first + wide, first + 1, first + wide + jnp.where(z == top, 1, 0))

    @pl.when(z == 0)
    def _():
        takes(wide, 0, 2)
        blocks(0, wide, *reached_1(wide))

        @pl.when(near)
        def _():
            takes(wide, 2, wide)
            blocks(0, wide, *reached_2(wide))

    @pl.when(inner_low)
    def _():
        takes(0, 0, 2, jnp.logical_not(near))

        @pl.when(jnp.logical_not(near))
        def _():
            blocks(2 * y, 2 * y + 2, jnp.where(y == 0, wide + 2, wide + 1), jnp.where(y == 0, base, base - 1))
        takes(base, 0, 2)
        blocks(2 * y, 2 * y + 2, *reached_1(base))
        blocks(wide, base, *reached_1(base))
        takes(0, 2, wide, jnp.logical_not(near))

        @pl.when(jnp.logical_not(near))
        def _():
            blocks(0, wide, wide, jnp.where(y == 0, wide, wide + 1))
            blocks(2 - 2 * y, wide - 2 * y, jnp.where(y == 0, wide + 2, wide + 1), jnp.where(y == 0, base, base - 1))
        blocks(2 - 2 * y, wide - 2 * y, *reached_1(base))
        takes(base, 2, wide)
        blocks(0, base, *reached_2(base))

        @pl.when(near)
        def _():
            for begin, reached in ((0, reached_1), (2, reached_2)):
                takes(top * wide, begin, begin + 2)
                blocks(0, base, *reached(top * wide, 1))

    @pl.when(inner_high)
    def _():
        for begin, reached in ((0, reached_1), (2, reached_2)):
            takes(top * wide, begin, begin + 2, near)
            blocks(base, base + wide, *reached(top * wide, 1))

        @pl.when(jnp.logical_not(near))
        def _():
            takes(wide, 0, wide)
            blocks(wide, base, *reached_1(top * wide, 1))
            spans(wide, base, *reached_2(top * wide, 1), block)
            takes(0, 0, 2)
            blocks(2 * y, 2 * y + 2, top * wide, parts + 1)
            takes(0, 2, wide)
            blocks(2 - 2 * y, wide - 2 * y, top * wide, parts + 1)
            spans(wide, base, *reached_2(top * wide, 1), give)

    group = pairs // 2

    def unpack(source, k, col):
        for ri in range(2):
            for g in range(count // 16):
                value = source[ri, g * 16:g * 16 + 16].astype(jnp.float32)
                for part in range(2):
                    seg = (k // group) * 2 * wide + ri * wide + col
                    row = (seg * count + g * 16 + part * 8) * group + k % group
                    joined[pl.ds(row, 8, stride=group), :] = value[part * 8:part * 8 + 8]

    def collect(k, carry):
        u = me + k + 1
        kept = jnp.logical_and(jnp.logical_and(z == 0, q == wide - 1), u == base - 1)
        away = jnp.logical_and(u >= own_end, jnp.logical_not(kept))
        def received(cols):
            remote(back.at[k, 0:cols], back.at[k, 0:cols], r_send, r_recv.at[k], me).wait_recv()

        @pl.when(away)
        def _():
            received(wide)

        @pl.when(jnp.logical_not(away))
        def _():
            received(wide - 1)

        for col in range(wide):
            here = jnp.logical_and(q == col, jnp.logical_not(away))

            @pl.when(here)
            def _():
                unpack(made_at(me, k), k, col)

            @pl.when(jnp.logical_not(here))
            def _():
                unpack(back.at[k, col], k, col)
        return carry

    def pack(which, target):
        def one(i, carry):
            rows = pl.ds(pl.multiple_of(i * 16, 16), 16)
            for x in range(2 * wide):
                start = pl.multiple_of((which * 2 * wide + x) * count * group + i * 16, 16)
                target[rows, x * LANES:(x + 1) * LANES] = joined[pl.ds(start, 16), :].astype(jnp.bfloat16)
            return carry

        lax.fori_loop(0, count * group // 16, one, 0, unroll=2)

    lax.fori_loop(0, jnp.minimum(group, parts - me), collect, 0)
    pack(0, crossed)
    fetch.wait()
    for n in range(0, LAGS, SPAN):
        lagged = jnp.dot(crossed[...], inverse[:, n:n + SPAN], preferred_element_type=jnp.float32)
        half_ref[:, n:n + SPAN] = (lagged * (1.0 / math.sqrt(F))).astype(jnp.bfloat16)
    lax.fori_loop(group, parts - me, collect, 0)
    pack(1, cross_ref)

    shipped(wide - 1, x_send)
    forwards = jnp.logical_or(jnp.logical_and(inner_low, c == 1), jnp.logical_and(inner_high, near))

    def told(slots):
        remote(scales.at[0:slots], scales.at[0:slots], n_send, n_recv.at[0], me).wait_send()

    @pl.when(forwards)
    def _():
        shipped(2 * wide, f_send)

    @pl.when(both_ways)
    def _():
        shipped(2, g_send)
        told(3 * wide + 1)

    @pl.when(jnp.logical_and(inner_high, near))
    def _():
        told(3 * wide - 1)

    @pl.when(jnp.logical_not(forwards))
    def _():
        shipped(wide, f_send)
        told(2 * wide - 1)

    def owners(z, q, u):
        c, early = q % 2, u in ((wide, wide + 1) if q < 2 else (base - 1,))
        layer = min(u, last) // wide
        if z == 0:
            return (0,) if layer == 0 or (layer == 1 and (c == 0 or early)) else ()
        if z == half - 1:
            if layer == 1:
                return (1,) if c == 0 or early else (0, 1)
            return (0, 1) if layer == half or (layer == top and c == 0) else ()
        if z == half:
            return (0, 1, half) if layer == top and c == 1 else (half,) if layer >= half else ()
        return (top,) if layer == top else ()

    for i in range(parts):
        replies = sum(
            d // wide in owners(i // wide, i % wide, u) and d != i and 0 <= u - 1 - d < pairs
            for u in range(1, parts + 1) for d in range(parts))

        @pl.when(me == i)
        def _():
            done = made.at[0:replies]
            remote(done, done, r_send, r_recv.at[0], me).wait_send()


def meet(layers, wide, records, live_mask, offsets):
    pairs = offsets.shape[0]
    count, windows, length = records.shape
    parts = layers * wide
    pitch = (parts + 1) * count
    rows = count * windows
    width = 2 * LANES
    chunks = 2 * F // width
    table = np.ascontiguousarray(
        forward_table(length).reshape(length, 2, chunks, LANES).transpose(2, 0, 1, 3).reshape(chunks, length, width))
    return pl.pallas_call(
        functools.partial(middle_kernel, (layers, wide, windows)),
        out_shape=[
            jax.ShapeDtypeStruct((count * pairs // 2, LAGS), jnp.bfloat16),
            jax.ShapeDtypeStruct((count * pairs // 2, 2 * F), jnp.bfloat16),
            jax.ShapeDtypeStruct((2 * F, LAGS), jnp.bfloat16),
        ],
        in_specs=[
            pl.BlockSpec(memory_space=pltpu.HBM),
            pl.BlockSpec(memory_space=pltpu.HBM),
            pl.BlockSpec(memory_space=pltpu.HBM),
            pl.BlockSpec(memory_space=pltpu.HBM),
            pl.BlockSpec(memory_space=pltpu.HBM),
        ],
        out_specs=[pl.BlockSpec(memory_space=pltpu.VMEM)] * 3,
        scratch_shapes=[
            pltpu.SMEM((pairs,), jnp.int32),
            pltpu.SMEM((count,), jnp.int32),
            pltpu.VMEM((rows, length), jnp.bfloat16),
            pltpu.VMEM((chunks, length, width), jnp.bfloat16),
            pltpu.VMEM((count * pairs // 2, 2 * F), jnp.bfloat16),
            pltpu.VMEM((rows, width), jnp.float32),
            pltpu.VMEM((rows, LANES), jnp.float32),
            pltpu.VMEM((2 * wide, rows, LANES), jnp.bfloat16),
            pltpu.VMEM((16, LANES), jnp.bfloat16),
            pltpu.VMEM((rows, LANES), jnp.float32),
            pltpu.VMEM((parts, 16, LANES), jnp.bfloat16),
            pltpu.VMEM((parts, 2 * rows, LANES), jnp.bfloat16),
            pltpu.VMEM((2 * windows * pitch, LANES), jnp.float32),
            pltpu.VMEM((parts * pairs, 2, count, LANES), jnp.bfloat16),
            pltpu.VMEM((pairs, wide, 2, count, LANES), jnp.bfloat16),
            pltpu.VMEM((2 * wide * count * pairs, LANES), jnp.float32),
            pltpu.SemaphoreType.DMA((chunks + 3,)),
            pltpu.SemaphoreType.DMA,
            pltpu.SemaphoreType.DMA,
            pltpu.SemaphoreType.DMA,
            pltpu.SemaphoreType.DMA,
            pltpu.SemaphoreType.DMA((parts,)),
            pltpu.SemaphoreType.DMA((parts,)),
            pltpu.SemaphoreType.DMA,
            pltpu.SemaphoreType.DMA((pairs,)),
        ],
        compiler_params=pltpu.CompilerParams(
            vmem_limit_bytes=36 * 1024 * 1024, collective_id=1, has_side_effects=True
        ),
    )(*[
        pltpu.with_memory_space_constraint(x, pltpu.HBM)
        for x in (offsets, live_mask, records.reshape(rows, length), jnp.asarray(table),
                  jnp.asarray(inverse_table(length)))
    ])


def finish_kernel(half_ref, cross_ref, table_ref, out_hbm, stage, sem):
    group = out_hbm.shape[1] // 2
    copies = [pltpu.make_async_copy(half_ref, out_hbm.at[:, 0:group], sem.at[0])]
    copies[0].start()
    for i, n in enumerate(range(0, LAGS, SPAN)):
        lagged = jnp.dot(cross_ref[...], table_ref[:, n:n + SPAN], preferred_element_type=jnp.float32)
        lagged = (lagged * (1.0 / math.sqrt(F))).astype(jnp.bfloat16)
        stage[:, :, n:n + SPAN] = lagged.reshape(stage.shape[0], group, SPAN)
        copies.append(pltpu.make_async_copy(
            stage.at[:, :, n:n + SPAN], out_hbm.at[:, group:2 * group, n:n + SPAN], sem.at[i + 1]))
        copies[-1].start()
    for one in copies:
        one.wait()


def finish(half, cross, table, count, pairs):
    return pl.pallas_call(
        finish_kernel,
        out_shape=jax.ShapeDtypeStruct((count, pairs, LAGS), jnp.bfloat16),
        in_specs=[pl.BlockSpec(memory_space=pltpu.VMEM)] * 3,
        out_specs=pl.BlockSpec(memory_space=pltpu.HBM),
        scratch_shapes=[
            pltpu.VMEM((count, pairs // 2, LAGS), jnp.bfloat16),
            pltpu.SemaphoreType.DMA((LAGS // SPAN + 1,)),
        ],
        compiler_params=pltpu.CompilerParams(vmem_limit_bytes=16 * 1024 * 1024),
    )(half.reshape(count, pairs // 2, LAGS), cross, table)


def shards(columns, records, live_mask, offsets):
    count, windows, length = records.shape
    pairs = offsets.shape[0]
    wide = 2 * columns
    layers = lax.axis_size("chan") // wide
    reach = (BAND + count - 2) // count
    depth = min(layers - 1, (wide - 1 + reach) // wide)
    pieces = PIECES
    fold = columns == 2 and depth == layers - 1 and depth >= 2 and layers * wide == pairs and pairs * count == BAND
    if (
        columns == 2 and layers == 4 and layers * wide == pairs and pairs * count == BAND
        and F == wide * LANES and windows == 8 and count % 16 == 0
    ):
        half, cross, inverse = meet(layers, wide, records, live_mask, offsets)
        return finish(half, cross, inverse, count, pairs)
    spectra = whiten(records, live_mask).reshape(count, windows * 8, LANES)
    slots = (depth + 1) * wide
    cross = pl.pallas_call(
        functools.partial(reach_kernel, (layers, columns, depth, pieces, windows, fold)),
        out_shape=jax.ShapeDtypeStruct((count, pairs, 8, LANES), jnp.float32),
        in_specs=[
            pl.BlockSpec(memory_space=pltpu.SMEM),
            pl.BlockSpec(memory_space=pltpu.VMEM),
        ],
        out_specs=pl.BlockSpec(memory_space=pltpu.VMEM),
        scratch_shapes=[
            pltpu.VMEM((slots + wide, count, windows * 8, LANES), jnp.bfloat16),
            pltpu.VMEM((slots * count, windows * 8, LANES), jnp.bfloat16),
            pltpu.VMEM((count, windows * 8, LANES), jnp.float32),
            pltpu.VMEM((count, windows * 8, LANES), jnp.float32),
            pltpu.VMEM((wide, count, 8, LANES), jnp.bfloat16),
            pltpu.VMEM((wide, count, 8, LANES), jnp.bfloat16),
        ]
        + [pltpu.SemaphoreType.DMA((depth + 2, pieces))] * 9
        + [pltpu.SemaphoreType.DMA((wide,))] * 2,
        compiler_params=pltpu.CompilerParams(
            vmem_limit_bytes=40 * 1024 * 1024, collective_id=0, has_side_effects=True
        ),
    )(offsets, spectra)
    return lags(cross.astype(jnp.bfloat16).reshape(count * pairs, 8 * LANES), count, pairs, length)


def lags(cross, count, pairs, length):
    result = jnp.dot(cross, jnp.asarray(inverse_table(length)), preferred_element_type=jnp.float32)
    result = result * (1.0 / math.sqrt(F))
    return result.reshape(count, pairs, LAGS).astype(jnp.bfloat16)


def solution(mesh):
    in_specs = (P(("day", "chan"), None, None), P(("day", "chan")), P())
    out_specs = P(("day", "chan"), None, None)
    columns = max(1, LAYER_CHIPS // mesh.shape["day"])
    body = functools.partial(shards, columns)
    return jax.shard_map(body, mesh=mesh, in_specs=in_specs, out_specs=out_specs, check_vma=False)
```

```python
import functools
import math

import jax
import jax.numpy as jnp
import numpy as np
from jax import lax
from jax.experimental import pallas as pl
from jax.experimental.pallas import tpu as pltpu
from jax.sharding import PartitionSpec as P

F = 512
F0 = 6
LAGS = 2048
LANES = 128
SPAN = 512
BAND = 512
PIECES = 4
LAYER_CHIPS = 4


def forward_table(length):
    samples = np.arange(length, dtype=np.int64)
    freqs = F0 + np.arange(F, dtype=np.int64)
    phase = np.mod(samples[:, None] * freqs[None, :], length)
    angle = 2.0 * math.pi / length * phase
    return np.concatenate([np.cos(angle), -np.sin(angle)], axis=1).astype(np.float32).astype(jnp.bfloat16)


def inverse_table(length):
    freqs = F0 + np.arange(F, dtype=np.int64)
    shifts = np.arange(LAGS, dtype=np.int64) - LAGS // 2
    phase = np.mod(freqs[:, None] * shifts[None, :], length)
    angle = 2.0 * math.pi / length * phase
    return np.concatenate([np.cos(angle), -np.sin(angle)], axis=0).astype(np.float32).astype(jnp.bfloat16)


def whiten(records, live_mask):
    count, windows, length = records.shape
    spectrum = jnp.dot(
        records.reshape(count * windows, length),
        jnp.asarray(forward_table(length)),
        preferred_element_type=jnp.float32,
    )
    power = jnp.mean(spectrum * spectrum, axis=1, keepdims=True)
    gain = jnp.repeat(live_mask.astype(jnp.float32), windows)[:, None]
    white = spectrum * (gain * lax.rsqrt(power + 1e-06))
    return white.astype(jnp.bfloat16)


def reach_kernel(shape, offsets_ref, white_ref, cross_ref, held, ext, own, swapped, made, back,
                 z_send, z_recv, c_send, c_recv, y_send, y_recv, d_send, d_recv, e_send, r_send, r_recv):
    layers, columns, depth, pieces, windows, fold = shape
    count, slab = white_ref.shape[0], white_ref.shape[1]
    pairs = offsets_ref.shape[0]
    wide = 2 * columns
    total = layers * wide * count
    me = lax.axis_index("chan")
    z, q = me // wide, me % wide
    y, c = q // 2, q % 2
    sibling = me + 1 - 2 * c
    sib_q = q + 1 - 2 * c
    mate = me + 2 - 4 * y
    mate_q = q + 2 - 4 * y
    far_q = sib_q + 2 - 4 * y
    step = count // pieces
    top, lifted = layers - 1, depth + 1

    barrier = pltpu.get_barrier_semaphore()

    def greet(device):
        pl.semaphore_signal(barrier, inc=1, device_id={"chan": device}, device_id_type=pl.DeviceIdType.MESH)

    greet(sibling)
    if columns == 2:
        greet(mate)

    @pl.when(z >= 1)
    def _():
        greet(me - wide)

    @pl.when(z < layers - 1)
    def _():
        greet(me + wide)

    below, above = jnp.minimum(z, 1), jnp.minimum(top - z, 1)
    peers = columns + below + above
    if fold:
        @pl.when(z == 0)
        def _():
            for i in range(wide):
                greet(top * wide + i)

        @pl.when(z == top)
        def _():
            for i in range(wide):
                greet(jnp.int32(i))

        peers = peers + wide * (2 - below - above)
    pl.semaphore_wait(barrier, peers)

    def rows(p):
        return pl.ds(p * step, step)

    def mine(dz, p):
        return white_ref.at[rows(p)] if dz == 0 else held.at[dz * wide + q, rows(p)]

    def copy(source, slot, p, send, recv, device):
        return pltpu.make_async_remote_copy(
            src_ref=source,
            dst_ref=held.at[slot, rows(p)],
            send_sem=send,
            recv_sem=recv,
            device_id={"chan": device},
            device_id_type=pl.DeviceIdType.MESH,
        )

    def down(dz, p):
        return copy(mine(dz, p), (dz + 1) * wide + q, p, z_send.at[dz, p], z_recv.at[dz + 1, p], me - wide)

    def from_above(dz, p):
        return copy(mine(dz, p), dz * wide + q, p, z_send.at[dz, p], z_recv.at[dz, p], me)

    def across(dz, p, slot):
        return copy(mine(dz, p), slot, p, c_send.at[dz, p], c_recv.at[dz, p], sibling)

    def over(dz, p, slot):
        return copy(mine(dz, p), slot, p, y_send.at[dz, p], y_recv.at[dz, p], mate)

    def onward(dz, p, slot):
        return copy(held.at[dz * wide + mate_q, rows(p)], slot, p, d_send.at[dz, p], d_recv.at[dz, p], sibling)

    def both(*conditions):
        joined = conditions[0]
        for condition in conditions[1:]:
            joined = jnp.logical_and(joined, condition)
        return joined

    def exists(dz):
        return z + dz < layers

    def goes(dz, at_start, at_end):
        if dz == lifted:
            return z == top
        if dz == 0:
            return at_start
        if fold and dz == depth:
            return both(exists(dz), at_end)
        return exists(dz)

    def z_tx(dz):
        if fold and dz + 1 == depth:
            return both(exists(dz), z >= 1, jnp.logical_or(z >= 2, q == 0))
        return both(exists(dz), z >= 1)

    def z_rx(dz):
        return goes(dz, None, q == 0)

    def c_tx(dz):
        return goes(dz, c == 1, q == 0)

    def c_rx(dz):
        return goes(dz, c == 0, q == 1)

    def y_tx(dz):
        return goes(dz, y == 1, q == 0)

    def y_rx(dz):
        return goes(dz, y == 0, q == 2)

    def detoured(dz, p):
        return fold and dz == depth - 1 and p == pieces - 1

    def over_tx(dz, p):
        if detoured(dz, p):
            return both(y_tx(dz), jnp.logical_or(z > 0, y == 0))
        if raised(dz, p):
            return both(y_tx(dz), y == 0)
        return y_tx(dz)

    def raised(dz, p):
        return fold and dz == lifted and p >= pieces // 2

    def lift_mate(p):
        return copy(held.at[mate_q, rows(p)], lifted * wide + mate_q, p,
                    e_send.at[lifted, p], y_recv.at[lifted, p], me + top * wide)

    def extra(dz, p):
        return copy(held.at[dz * wide + mate_q, rows(p)], (dz + 1) * wide + mate_q, p,
                    e_send.at[dz, p], y_recv.at[dz + 1, p], me - wide)

    def extra_tx():
        return both(z == 1, y == 0)

    def d_rx(dz):
        return goes(dz, y == 0, q == 3)

    def lift(p):
        return copy(white_ref.at[rows(p)], lifted * wide + q, p, z_send.at[lifted, p], z_recv.at[lifted, p],
                    me + top * wide)

    def sends(dz):
        for p in range(pieces):
            if dz > 0:
                @pl.when(z_rx(dz))
                def _():
                    from_above(dz, p).wait_recv()
            if dz < depth:
                @pl.when(z_tx(dz))
                def _():
                    down(dz, p).start()
            if columns == 2:
                @pl.when(over_tx(dz, p))
                def _():
                    over(dz, p, dz * wide + q).start()
            @pl.when(c_tx(dz))
            def _():
                across(dz, p, dz * wide + q).start()

    def passes(dz):
        if columns == 2:
            for p in range(pieces):
                @pl.when(y_rx(dz))
                def _():
                    over(dz, p, dz * wide + mate_q).wait_recv()
                    onward(dz, p, dz * wide + mate_q).start()
                if dz == 0 and raised(lifted, p):
                    @pl.when(both(z == 0, y == 0))
                    def _():
                        lift_mate(p).start()
                if detoured(dz + 1, p):
                    @pl.when(extra_tx())
                    def _():
                        extra(dz, p).start()

    def arrives(dz):
        for p in range(pieces):
            @pl.when(c_rx(dz))
            def _():
                across(dz, p, dz * wide + sib_q).wait_recv()
            if columns == 2:
                @pl.when(d_rx(dz))
                def _():
                    onward(dz, p, dz * wide + far_q).wait_recv()

    def finishes(dz):
        for p in range(pieces):
            if dz < depth:
                @pl.when(z_tx(dz))
                def _():
                    down(dz, p).wait_send()
            if columns == 2:
                @pl.when(over_tx(dz, p))
                def _():
                    over(dz, p, dz * wide + q).wait_send()
                if detoured(dz + 1, p):
                    @pl.when(extra_tx())
                    def _():
                        extra(dz, p).wait_send()
                @pl.when(y_rx(dz))
                def _():
                    onward(dz, p, dz * wide + mate_q).wait_send()
            @pl.when(c_tx(dz))
            def _():
                across(dz, p, dz * wide + q).wait_send()

    def answer(i):
        return pltpu.make_async_remote_copy(
            src_ref=made.at[i],
            dst_ref=back.at[q],
            send_sem=r_send.at[i],
            recv_sem=r_recv.at[q],
            device_id={"chan": jnp.int32(i)},
            device_id_type=pl.DeviceIdType.MESH,
        )

    def answered(i):
        return pltpu.make_async_remote_copy(
            src_ref=made.at[i],
            dst_ref=back.at[i],
            send_sem=r_send.at[i],
            recv_sem=r_recv.at[i],
            device_id={"chan": me},
            device_id_type=pl.DeviceIdType.MESH,
        )

    low = lax.broadcasted_iota(jnp.int32, (8, LANES), 0) < 4

    def prepare(i, carry):
        raw = white_ref[i]
        value = raw.astype(jnp.float32)
        own[i] = value
        ext[q * count + i] = raw
        for w in range(windows):
            swapped[i, w * 8 : w * 8 + 8] = pltpu.roll(value[w * 8 : w * 8 + 8], 4, 0)
        return carry

    def settle(dz):
        def one(l):
            def fill(i, carry):
                ext[(dz * wide + l) * count + i] = held[dz * wide + l, i]
                return carry
            lax.fori_loop(0, count, fill, 0, unroll=4)

        if dz == 0:
            for l in range(1, wide):
                @pl.when(q < l)
                def _():
                    one(l)
        else:
            @pl.when(exists(dz))
            def _():
                for l in range(1 if fold and dz == depth else wide):
                    one(l)

    live = jnp.minimum(layers * wide - me, pairs)

    def outside():
        def nothing(k, carry):
            for r in range(count):
                cross_ref[r, k] = jnp.zeros((8, LANES), jnp.float32)
            return carry

        lax.fori_loop(live, pairs, nothing, 0)

        @pl.when(layers - z <= depth)
        def _():
            def blank(i, carry):
                ext[(layers - z) * wide * count + i] = jnp.zeros((slab, LANES), jnp.bfloat16)
                return carry

            lax.fori_loop(0, 2 * count, blank, 0, unroll=4)

    def reached(dz):
        if dz < 0:
            return 0
        if dz == depth:
            return live
        return jnp.minimum((dz + 1) * wide - q - 1, live)

    def multiply(dz):
        def pair(k, carry):
            shift = offsets_ref[k]

            def channel(i, inner):
                place = me * count + i + shift
                keep = jnp.where(place < total, 1.0 / windows, 0.0)
                near = jnp.minimum(q * count + i + shift, ext.shape[0] - 1)
                partner = ext[near].astype(jnp.float32)
                straight = own[i, :8] * partner[:8]
                twisted = swapped[i, :8] * partner[:8]
                for w in range(1, windows):
                    part = slice(w * 8, w * 8 + 8)
                    straight += own[i, part] * partner[part]
                    twisted += swapped[i, part] * partner[part]
                joined = jnp.where(
                    low,
                    straight + pltpu.roll(straight, 4, 0),
                    pltpu.roll(twisted, 4, 0) - twisted,
                )
                cross_ref[i, k] = joined * keep
                return inner

            return lax.fori_loop(0, count, channel, carry, unroll=4)

        begin, end = reached(dz - 1), reached(dz)
        if fold and dz == depth:
            @pl.when(z == 0)
            def _():
                lax.fori_loop(begin, begin + 1, pair, 0)

            @pl.when(z > 0)
            def _():
                lax.fori_loop(begin, end, pair, 0)
        else:
            lax.fori_loop(begin, end, pair, 0)

    def reply():
        for i in range(wide):
            shift = offsets_ref[top * wide + q - i]

            def channel(r, carry):
                place = i * count + r + shift
                keep = jnp.where(place < total, 1.0 / windows, 0.0)
                near = jnp.clip(place - top * wide * count, 0, ext.shape[0] - 1)
                partner = ext[near].astype(jnp.float32)
                value = held[lifted * wide + i, r].astype(jnp.float32)
                straight = value[:8] * partner[:8]
                twisted = pltpu.roll(value[:8], 4, 0) * partner[:8]
                for w in range(1, windows):
                    part = slice(w * 8, w * 8 + 8)
                    straight += value[part] * partner[part]
                    twisted += pltpu.roll(value[part], 4, 0) * partner[part]
                joined = jnp.where(
                    low,
                    straight + pltpu.roll(straight, 4, 0),
                    pltpu.roll(twisted, 4, 0) - twisted,
                )
                made[i, r] = (joined * keep).astype(jnp.bfloat16)
                return carry

            lax.fori_loop(0, count, channel, 0, unroll=4)
        for i in range(wide):
            answer(i).start()

    sends(0)
    if fold:
        @pl.when(z == 0)
        def _():
            for p in range(pieces):
                lift(p).start()

    lax.fori_loop(0, count, prepare, 0)
    outside()
    for dz in range(depth + 1):
        if dz < depth:
            sends(dz + 1)
        if fold and dz == 0:
            sends(lifted)
        passes(dz)
        if fold and dz == 0:
            passes(lifted)
        arrives(dz)
        settle(dz)
        if fold and dz == 0:
            arrives(lifted)

            @pl.when(z == top)
            def _():
                reply()

        multiply(dz)

    if fold:
        @pl.when(z == 0)
        def _():
            for i in range(wide):
                answered(i).wait_recv()

                def take(r, carry):
                    cross_ref[r, top * wide - q + i] = back[i, r].astype(jnp.float32)
                    return carry

                lax.fori_loop(0, count, take, 0, unroll=4)
            for p in range(pieces):
                lift(p).wait_send()
                if raised(lifted, p):
                    @pl.when(y == 0)
                    def _():
                        lift_mate(p).wait_send()

        @pl.when(z == top)
        def _():
            for i in range(wide):
                answer(i).wait_send()

        finishes(lifted)
    for dz in range(depth + 1):
        finishes(dz)


def middle_kernel(shape, offsets_hbm, mask_hbm, records_hbm, table_hbm, inverse_hbm, half_ref, cross_ref, inverse,
                  offsets_ref, mask_ref, records, table, crossed, spectrum, square, white, gains, column, scales, held, spec, made, back, joined,
                  l_sem, x_send, f_send, g_send, n_send, n_recv, s_recv, r_send, r_recv):
    layers, wide, windows = shape
    pairs = offsets_ref.shape[0]
    count = records.shape[0] // windows
    chunks, width = table.shape[0], table.shape[2]
    rows = count * windows
    parts = layers * wide
    pitch = spec.shape[0] // (2 * windows)
    half, top, last = layers // 2, layers - 1, parts - 1
    me = lax.axis_index("chan")
    z, q = me // wide, me % wide
    c = q % 2
    first = z * wide
    base = half * wide
    sib_q = q + 1 - 2 * c
    mate_q = (q + 2) % wide
    far_q = (sib_q + 2) % wide
    near = c == 0

    def nearest(j):
        return jnp.where(j == 0, q, jnp.where(j == 1, sib_q, jnp.where(j == 2, mate_q, far_q)))

    def slowest(j):
        return jnp.where(j == 0, q, jnp.where(j == 1, mate_q, jnp.where(j == 2, sib_q, far_q)))

    def chunk(j):
        return pltpu.make_async_copy(table_hbm.at[slowest(j)], table.at[j], l_sem.at[j])

    load = [
        pltpu.make_async_copy(records_hbm, records, l_sem.at[chunks]),
        pltpu.make_async_copy(offsets_hbm, offsets_ref, l_sem.at[chunks + 1]),
        pltpu.make_async_copy(mask_hbm, mask_ref, l_sem.at[chunks + 2]),
    ]
    load[0].start()
    for n in range(chunks):
        chunk(n).start()
    for one in load[1:]:
        one.start()
    inner_low, inner_high = z == half - 1, z == half
    neighbour = jnp.where(
        jnp.logical_or(z == 0, jnp.logical_and(inner_low, c == 1)), me + wide, me - wide)
    own_end = jnp.where(
        z == 0, jnp.where(near, base, jnp.where(q < 2, wide + 2, wide)),
        jnp.where(jnp.logical_and(inner_low, c == 1), base + wide, parts + 1))
    barrier = pltpu.get_barrier_semaphore()

    def greet(device, condition):
        @pl.when(condition)
        def _():
            pl.semaphore_signal(barrier, inc=1, device_id={"chan": jnp.int32(device)},
                                device_id_type=pl.DeviceIdType.MESH)

    for col in (sib_q, mate_q, far_q):
        greet(first + col, z >= 0)
    for i in range(wide):
        odd = i % 2 == 1
        greet(wide + i, z == 0)
        if odd:
            greet(base + i, z < half)
        else:
            greet(base + i, jnp.logical_and(inner_low, q == i))
    greet(me - wide, jnp.logical_or(inner_low, jnp.logical_and(inner_high, c == 1)))
    greet(me + wide, inner_high)
    replies_far = jnp.where(inner_low, wide, jnp.where(jnp.logical_and(inner_high, c == 1), 2 * wide - 1, 0))
    ships_there = jnp.where(jnp.logical_and(inner_low, near), 0, 1)

    def remote(source, target, send, recv, device):
        return pltpu.make_async_remote_copy(
            src_ref=source, dst_ref=target, send_sem=send, recv_sem=recv,
            device_id={"chan": device}, device_id_type=pl.DeviceIdType.MESH,
        )

    def piece(ri, col):
        return white.at[ri * wide + col]

    def swap(ri, col):
        return remote(piece(ri, col), held.at[me, pl.ds(ri * rows, rows)], x_send, s_recv.at[me], first + col)

    def ship_own(ri):
        return remote(piece(ri, q), held.at[me, pl.ds(ri * rows, rows)], f_send, s_recv.at[me], neighbour)

    def ship(s):
        return remote(held.at[s], held.at[s], f_send, s_recv.at[s], neighbour)

    both_ways = jnp.logical_and(inner_low, c == 1)

    def drop_own(ri):
        return remote(piece(ri, q), held.at[me, pl.ds(ri * rows, rows)], g_send, s_recv.at[me], me - wide)

    def drop(s):
        return remote(held.at[s], held.at[s], g_send, s_recv.at[s], me - wide)

    def made_at(d, k):
        return made.at[d * pairs + k]

    def reply(d, k):
        return remote(made_at(d, k), back.at[k, q], r_send, r_recv.at[k], d)

    def shipped(slots, send):
        remote(held.at[0:slots], held.at[0:slots], send, s_recv.at[0], neighbour).wait_send()

    def gain_to(device):
        return remote(gains, scales.at[me], n_send, n_recv.at[me], device)

    def gain_on(s, device):
        return remote(scales.at[s], scales.at[s], n_send, n_recv.at[s], device)

    def clear(i, carry):
        joined[pl.ds(pl.multiple_of(i * 64, 64), 64), :] = jnp.zeros((64, LANES), jnp.float32)
        return carry

    lax.fori_loop(0, joined.shape[0] // 64, clear, 0)

    def blank(x, carry):
        spec[pl.ds(pl.multiple_of(x * pitch + parts * count, 8), count), :] = jnp.zeros((count, LANES), jnp.float32)
        return carry

    lax.fori_loop(0, 2 * windows, blank, 0)
    square[...] = jnp.zeros(square.shape, jnp.float32)
    load[0].wait()

    def transform(j, carry):
        col = slowest(j)
        chunk(j).wait()
        spectrum[...] = jnp.dot(records[...], table[j], preferred_element_type=jnp.float32)

        def narrow(i, inner):
            some = pl.ds(pl.multiple_of(i * 16, 16), 16)
            real, imag = spectrum[some, :LANES], spectrum[some, LANES:]
            white[col, some] = real.astype(jnp.bfloat16)
            white[wide + col, some] = imag.astype(jnp.bfloat16)
            square[some, :] += real * real + imag * imag
            return inner

        lax.fori_loop(0, rows // 16, narrow, 0, unroll=4)

        @pl.when(j == 0)
        def _():
            pl.semaphore_wait(barrier, wide - 1 + replies_far + ships_there)
            for ri in range(2):
                ship_own(ri).start()

            @pl.when(both_ways)
            def _():
                for ri in range(2):
                    drop_own(ri).start()

        @pl.when(j > 0)
        def _():
            for ri in range(2):
                swap(ri, col).start()
        return carry

    lax.fori_loop(0, chunks, transform, 0)
    for one in load[1:]:
        one.wait()
    place = lax.broadcasted_iota(jnp.int32, (16, LANES), 0)
    channel = lax.broadcasted_iota(jnp.int32, (8, LANES), 1) // windows
    terms = jnp.zeros((16, LANES), jnp.float32)
    for part in range(rows // LANES):
        total = jnp.sum(square[part * LANES:(part + 1) * LANES, :], axis=1, keepdims=True)
        scale = jnp.broadcast_to(lax.rsqrt(total * (1.0 / (2 * F)) + 1e-06), (LANES, LANES)).T[:8]
        alive = jnp.zeros((8, LANES), jnp.float32)
        for n in range(LANES // windows):
            alive = jnp.where(channel == n, mask_ref[part * (LANES // windows) + n].astype(jnp.float32), alive)
        rest = (scale * alive)[:1]
        for term in range(3):
            kept = rest.astype(jnp.bfloat16).astype(jnp.float32)
            terms = jnp.where(place == part * 3 + term, kept, terms)
            rest = rest - kept
    gains[...] = terms.astype(jnp.bfloat16)
    fetch = pltpu.make_async_copy(inverse_hbm, inverse, l_sem.at[0])
    fetch.start()

    def settle(s, gain, piece_of):
        for part in range(rows // LANES):
            scale = sum(gain[part * 3 + term:part * 3 + term + 1].astype(jnp.float32) for term in range(3))
            column[part * LANES:(part + 1) * LANES, :] = jnp.broadcast_to(scale, (LANES, LANES)).T

        def one(i, carry):
            some = pl.ds(pl.multiple_of(i * 2 * windows, 2 * windows), 2 * windows)
            factor = column[some, :]
            for ri in range(2):
                value = piece_of(ri, i).astype(jnp.float32) * factor
                for part in range(2):
                    row = ri * windows * pitch + s * count + 2 * i + part
                    spec[pl.ds(row, windows, stride=pitch), :] = value[part * windows:(part + 1) * windows]
            return carry

        lax.fori_loop(0, count // 2, one, 0, unroll=4)

    def own_rows(ri, i):
        return white[ri * wide + q, pl.ds(pl.multiple_of(i * 2 * windows, 2 * windows), 2 * windows)]

    def arrive(s, onward):
        ship(s).wait_recv()
        if onward is not None:
            @pl.when(onward)
            def _():
                ship(s).start()

    def unfold(s, onward):
        gain_on(s, me).wait_recv()
        if onward is not None:
            @pl.when(onward)
            def _():
                gain_on(s, neighbour).start()
        settle(
            s, scales[s],
            lambda ri, i: held[s, pl.ds(pl.multiple_of(ri * rows + i * 2 * windows, 2 * windows), 2 * windows)])

    def takes(start, begin, end, onward=None):
        def one(j, carry):
            arrive(start + nearest(j), onward)
            return carry

        def two(j, carry):
            unfold(start + nearest(j), onward)
            return carry

        lax.fori_loop(begin, end, one, 0)
        lax.fori_loop(begin, end, two, 0)

    def block(d, k):
        shift = offsets_ref[k]
        for g in range(count // 16):
            mine = d * count + g * 16
            real = imag = None
            for w in range(windows):
                cr = spec[pl.ds(pl.multiple_of(w * pitch + mine, 8), 16), :]
                ci = spec[pl.ds(pl.multiple_of((windows + w) * pitch + mine, 8), 16), :]
                pr = spec[pl.ds(w * pitch + mine + shift, 16), :]
                pi = spec[pl.ds((windows + w) * pitch + mine + shift, 16), :]
                re, im = cr * pr + ci * pi, ci * pr - cr * pi
                real, imag = (re, im) if w == 0 else (real + re, imag + im)
            rows = slice(g * 16, g * 16 + 16)
            made[d * pairs + k, 0, rows] = (real * (1.0 / windows)).astype(jnp.bfloat16)
            made[d * pairs + k, 1, rows] = (imag * (1.0 / windows)).astype(jnp.bfloat16)

    def spans(d_begin, d_end, u_begin, u_end, visit):
        def reach(u, carry):
            def one(d, inner):
                visit(d, u - 1 - d)
                return inner

            return lax.fori_loop(jnp.maximum(d_begin, u - pairs), jnp.minimum(d_end, u), one, carry)

        lax.fori_loop(u_begin, u_end, reach, 0)

    def give(d, k):
        @pl.when(d != me)
        def _():
            reply(d, k).start()

    def blocks(d_begin, d_end, u_begin, u_end):
        def reach(u, carry):
            spans(d_begin, d_end, u, u + 1, block)
            spans(d_begin, d_end, u, u + 1, give)
            return carry

        lax.fori_loop(u_begin, u_end, reach, 0)

    y = q // 2
    def reached_1(start, more=0):
        return jnp.where(y == 0, start, start + 3), jnp.where(y == 0, start + 2, start + wide + more)

    def reached_2(start, more=0):
        return jnp.where(y == 0, start + 2, start), jnp.where(y == 0, start + wide + more, start + 3)

    settle(me, gains[...], own_rows)
    gain_to(neighbour).start()
    for col in (sib_q, mate_q, far_q):
        gain_to(first + col).start()
    arrive(first + sib_q, z >= 0)

    @pl.when(both_ways)
    def _():
        drop(first + sib_q).start()
        gain_to(me - wide).start()
    unfold(first + sib_q, z >= 0)

    @pl.when(both_ways)
    def _():
        gain_on(first + sib_q, me - wide).start()
    takes(first, 2, wide, z >= 0)
    blocks(first, first + wide, first + 1, first + wide + jnp.where(z == top, 1, 0))

    @pl.when(z == 0)
    def _():
        takes(wide, 0, 2)
        blocks(0, wide, *reached_1(wide))

        @pl.when(near)
        def _():
            takes(wide, 2, wide)
            blocks(0, wide, *reached_2(wide))

    @pl.when(inner_low)
    def _():
        takes(0, 0, 2, jnp.logical_not(near))

        @pl.when(jnp.logical_not(near))
        def _():
            blocks(2 * y, 2 * y + 2, jnp.where(y == 0, wide + 2, wide + 1), jnp.where(y == 0, base, base - 1))
        takes(base, 0, 2)
        blocks(2 * y, 2 * y + 2, *reached_1(base))
        blocks(wide, base, *reached_1(base))
        takes(0, 2, wide, jnp.logical_not(near))

        @pl.when(jnp.logical_not(near))
        def _():
            blocks(0, wide, wide, jnp.where(y == 0, wide, wide + 1))
            blocks(2 - 2 * y, wide - 2 * y, jnp.where(y == 0, wide + 2, wide + 1), jnp.where(y == 0, base, base - 1))
        blocks(2 - 2 * y, wide - 2 * y, *reached_1(base))
        takes(base, 2, wide)
        blocks(0, wide, *reached_2(base))
        blocks(wide, base, *reached_2(base))

        @pl.when(near)
        def _():
            for begin, reached in ((0, reached_1), (2, reached_2)):
                takes(top * wide, begin, begin + 2)
                blocks(0, wide, *reached(top * wide, 1))
                blocks(wide, base, *reached(top * wide, 1))

    @pl.when(inner_high)
    def _():
        for begin, reached in ((0, reached_1), (2, reached_2)):
            takes(top * wide, begin, begin + 2, near)
            blocks(base, base + wide, *reached(top * wide, 1))

        @pl.when(jnp.logical_not(near))
        def _():
            takes(wide, 0, wide)
            blocks(wide, base, *reached_1(top * wide, 1))
            spans(wide, base, *reached_2(top * wide, 1), block)
            takes(0, 0, 2)
            blocks(2 * y, 2 * y + 2, top * wide, parts + 1)
            takes(0, 2, wide)
            blocks(2 - 2 * y, wide - 2 * y, top * wide, parts + 1)
            spans(wide, base, *reached_2(top * wide, 1), give)

    group = pairs // 2

    def unpack(source, k, col):
        for ri in range(2):
            for g in range(count // 16):
                value = source[ri, g * 16:g * 16 + 16].astype(jnp.float32)
                for part in range(2):
                    seg = (k // group) * 2 * wide + ri * wide + col
                    row = (seg * count + g * 16 + part * 8) * group + k % group
                    joined[pl.ds(row, 8, stride=group), :] = value[part * 8:part * 8 + 8]

    def collect(k, carry):
        u = me + k + 1
        kept = jnp.logical_and(jnp.logical_and(z == 0, q == wide - 1), u == base - 1)
        away = jnp.logical_and(u >= own_end, jnp.logical_not(kept))
        def received(cols):
            remote(back.at[k, 0:cols], back.at[k, 0:cols], r_send, r_recv.at[k], me).wait_recv()

        @pl.when(away)
        def _():
            received(wide)

        @pl.when(jnp.logical_not(away))
        def _():
            received(wide - 1)

        for col in range(wide):
            here = jnp.logical_and(q == col, jnp.logical_not(away))

            @pl.when(here)
            def _():
                unpack(made_at(me, k), k, col)

            @pl.when(jnp.logical_not(here))
            def _():
                unpack(back.at[k, col], k, col)
        return carry

    def pack(which, target):
        def one(i, carry):
            rows = pl.ds(pl.multiple_of(i * 16, 16), 16)
            for x in range(2 * wide):
                start = pl.multiple_of((which * 2 * wide + x) * count * group + i * 16, 16)
                target[rows, x * LANES:(x + 1) * LANES] = joined[pl.ds(start, 16), :].astype(jnp.bfloat16)
            return carry

        lax.fori_loop(0, count * group // 16, one, 0, unroll=2)

    lax.fori_loop(0, jnp.minimum(group, parts - me), collect, 0)
    pack(0, crossed)
    fetch.wait()
    for n in range(0, LAGS, SPAN):
        lagged = jnp.dot(crossed[...], inverse[:, n:n + SPAN], preferred_element_type=jnp.float32)
        half_ref[:, n:n + SPAN] = (lagged * (1.0 / math.sqrt(F))).astype(jnp.bfloat16)
    lax.fori_loop(group, parts - me, collect, 0)
    pack(1, cross_ref)

    shipped(wide - 1, x_send)
    forwards = jnp.logical_or(jnp.logical_and(inner_low, c == 1), jnp.logical_and(inner_high, near))

    def told(slots):
        remote(scales.at[0:slots], scales.at[0:slots], n_send, n_recv.at[0], me).wait_send()

    @pl.when(forwards)
    def _():
        shipped(2 * wide, f_send)

    @pl.when(both_ways)
    def _():
        shipped(2, g_send)
        told(3 * wide + 1)

    @pl.when(jnp.logical_and(inner_high, near))
    def _():
        told(3 * wide - 1)

    @pl.when(jnp.logical_not(forwards))
    def _():
        shipped(wide, f_send)
        told(2 * wide - 1)

    def owners(z, q, u):
        c, early = q % 2, u in ((wide, wide + 1) if q < 2 else (base - 1,))
        layer = min(u, last) // wide
        if z == 0:
            return (0,) if layer == 0 or (layer == 1 and (c == 0 or early)) else ()
        if z == half - 1:
            if layer == 1:
                return (1,) if c == 0 or early else (0, 1)
            return (0, 1) if layer == half or (layer == top and c == 0) else ()
        if z == half:
            return (0, 1, half) if layer == top and c == 1 else (half,) if layer >= half else ()
        return (top,) if layer == top else ()

    for i in range(parts):
        replies = sum(
            d // wide in owners(i // wide, i % wide, u) and d != i and 0 <= u - 1 - d < pairs
            for u in range(1, parts + 1) for d in range(parts))

        @pl.when(me == i)
        def _():
            done = made.at[0:replies]
            remote(done, done, r_send, r_recv.at[0], me).wait_send()


def meet(layers, wide, records, live_mask, offsets):
    pairs = offsets.shape[0]
    count, windows, length = records.shape
    parts = layers * wide
    pitch = (parts + 1) * count
    rows = count * windows
    width = 2 * LANES
    chunks = 2 * F // width
    table = np.ascontiguousarray(
        forward_table(length).reshape(length, 2, chunks, LANES).transpose(2, 0, 1, 3).reshape(chunks, length, width))
    return pl.pallas_call(
        functools.partial(middle_kernel, (layers, wide, windows)),
        out_shape=[
            jax.ShapeDtypeStruct((count * pairs // 2, LAGS), jnp.bfloat16),
            jax.ShapeDtypeStruct((count * pairs // 2, 2 * F), jnp.bfloat16),
            jax.ShapeDtypeStruct((2 * F, LAGS), jnp.bfloat16),
        ],
        in_specs=[
            pl.BlockSpec(memory_space=pltpu.HBM),
            pl.BlockSpec(memory_space=pltpu.HBM),
            pl.BlockSpec(memory_space=pltpu.HBM),
            pl.BlockSpec(memory_space=pltpu.HBM),
            pl.BlockSpec(memory_space=pltpu.HBM),
        ],
        out_specs=[pl.BlockSpec(memory_space=pltpu.VMEM)] * 3,
        scratch_shapes=[
            pltpu.SMEM((pairs,), jnp.int32),
            pltpu.SMEM((count,), jnp.int32),
            pltpu.VMEM((rows, length), jnp.bfloat16),
            pltpu.VMEM((chunks, length, width), jnp.bfloat16),
            pltpu.VMEM((count * pairs // 2, 2 * F), jnp.bfloat16),
            pltpu.VMEM((rows, width), jnp.float32),
            pltpu.VMEM((rows, LANES), jnp.float32),
            pltpu.VMEM((2 * wide, rows, LANES), jnp.bfloat16),
            pltpu.VMEM((16, LANES), jnp.bfloat16),
            pltpu.VMEM((rows, LANES), jnp.float32),
            pltpu.VMEM((parts, 16, LANES), jnp.bfloat16),
            pltpu.VMEM((parts, 2 * rows, LANES), jnp.bfloat16),
            pltpu.VMEM((2 * windows * pitch, LANES), jnp.float32),
            pltpu.VMEM((parts * pairs, 2, count, LANES), jnp.bfloat16),
            pltpu.VMEM((pairs, wide, 2, count, LANES), jnp.bfloat16),
            pltpu.VMEM((2 * wide * count * pairs, LANES), jnp.float32),
            pltpu.SemaphoreType.DMA((chunks + 3,)),
            pltpu.SemaphoreType.DMA,
            pltpu.SemaphoreType.DMA,
            pltpu.SemaphoreType.DMA,
            pltpu.SemaphoreType.DMA,
            pltpu.SemaphoreType.DMA((parts,)),
            pltpu.SemaphoreType.DMA((parts,)),
            pltpu.SemaphoreType.DMA,
            pltpu.SemaphoreType.DMA((pairs,)),
        ],
        compiler_params=pltpu.CompilerParams(
            vmem_limit_bytes=36 * 1024 * 1024, collective_id=1, has_side_effects=True
        ),
    )(*[
        pltpu.with_memory_space_constraint(x, pltpu.HBM)
        for x in (offsets, live_mask, records.reshape(rows, length), jnp.asarray(table),
                  jnp.asarray(inverse_table(length)))
    ])


def finish_kernel(half_ref, cross_ref, table_ref, out_hbm, stage, sem):
    group = out_hbm.shape[1] // 2
    copies = [pltpu.make_async_copy(half_ref, out_hbm.at[:, 0:group], sem.at[0])]
    copies[0].start()
    for i, n in enumerate(range(0, LAGS, SPAN)):
        lagged = jnp.dot(cross_ref[...], table_ref[:, n:n + SPAN], preferred_element_type=jnp.float32)
        lagged = (lagged * (1.0 / math.sqrt(F))).astype(jnp.bfloat16)
        stage[:, :, n:n + SPAN] = lagged.reshape(stage.shape[0], group, SPAN)
        copies.append(pltpu.make_async_copy(
            stage.at[:, :, n:n + SPAN], out_hbm.at[:, group:2 * group, n:n + SPAN], sem.at[i + 1]))
        copies[-1].start()
    for one in copies:
        one.wait()


def finish(half, cross, table, count, pairs):
    return pl.pallas_call(
        finish_kernel,
        out_shape=jax.ShapeDtypeStruct((count, pairs, LAGS), jnp.bfloat16),
        in_specs=[pl.BlockSpec(memory_space=pltpu.VMEM)] * 3,
        out_specs=pl.BlockSpec(memory_space=pltpu.HBM),
        scratch_shapes=[
            pltpu.VMEM((count, pairs // 2, LAGS), jnp.bfloat16),
            pltpu.SemaphoreType.DMA((LAGS // SPAN + 1,)),
        ],
        compiler_params=pltpu.CompilerParams(vmem_limit_bytes=16 * 1024 * 1024),
    )(half.reshape(count, pairs // 2, LAGS), cross, table)


def shards(columns, records, live_mask, offsets):
    count, windows, length = records.shape
    pairs = offsets.shape[0]
    wide = 2 * columns
    layers = lax.axis_size("chan") // wide
    reach = (BAND + count - 2) // count
    depth = min(layers - 1, (wide - 1 + reach) // wide)
    pieces = PIECES
    fold = columns == 2 and depth == layers - 1 and depth >= 2 and layers * wide == pairs and pairs * count == BAND
    if (
        columns == 2 and layers == 4 and layers * wide == pairs and pairs * count == BAND
        and F == wide * LANES and windows == 8 and count % 16 == 0
    ):
        half, cross, inverse = meet(layers, wide, records, live_mask, offsets)
        return finish(half, cross, inverse, count, pairs)
    spectra = whiten(records, live_mask).reshape(count, windows * 8, LANES)
    slots = (depth + 1) * wide
    cross = pl.pallas_call(
        functools.partial(reach_kernel, (layers, columns, depth, pieces, windows, fold)),
        out_shape=jax.ShapeDtypeStruct((count, pairs, 8, LANES), jnp.float32),
        in_specs=[
            pl.BlockSpec(memory_space=pltpu.SMEM),
            pl.BlockSpec(memory_space=pltpu.VMEM),
        ],
        out_specs=pl.BlockSpec(memory_space=pltpu.VMEM),
        scratch_shapes=[
            pltpu.VMEM((slots + wide, count, windows * 8, LANES), jnp.bfloat16),
            pltpu.VMEM((slots * count, windows * 8, LANES), jnp.bfloat16),
            pltpu.VMEM((count, windows * 8, LANES), jnp.float32),
            pltpu.VMEM((count, windows * 8, LANES), jnp.float32),
            pltpu.VMEM((wide, count, 8, LANES), jnp.bfloat16),
            pltpu.VMEM((wide, count, 8, LANES), jnp.bfloat16),
        ]
        + [pltpu.SemaphoreType.DMA((depth + 2, pieces))] * 9
        + [pltpu.SemaphoreType.DMA((wide,))] * 2,
        compiler_params=pltpu.CompilerParams(
            vmem_limit_bytes=40 * 1024 * 1024, collective_id=0, has_side_effects=True
        ),
    )(offsets, spectra)
    return lags(cross.astype(jnp.bfloat16).reshape(count * pairs, 8 * LANES), count, pairs, length)


def lags(cross, count, pairs, length):
    result = jnp.dot(cross, jnp.asarray(inverse_table(length)), preferred_element_type=jnp.float32)
    result = result * (1.0 / math.sqrt(F))
    return result.reshape(count, pairs, LAGS).astype(jnp.bfloat16)


def solution(mesh):
    in_specs = (P(("day", "chan"), None, None), P(("day", "chan")), P())
    out_specs = P(("day", "chan"), None, None)
    columns = max(1, LAYER_CHIPS // mesh.shape["day"])
    body = functools.partial(shards, columns)
    return jax.shard_map(body, mesh=mesh, in_specs=in_specs, out_specs=out_specs, check_vma=False)
```

```python
import functools
import math

import jax
import jax.numpy as jnp
import numpy as np
from jax import lax
from jax.experimental import pallas as pl
from jax.experimental.pallas import tpu as pltpu
from jax.sharding import PartitionSpec as P

F = 512
F0 = 6
LAGS = 2048
LANES = 128
SPAN = 512
BAND = 512
PIECES = 4
LAYER_CHIPS = 4


def forward_table(length):
    samples = np.arange(length, dtype=np.int64)
    freqs = F0 + np.arange(F, dtype=np.int64)
    phase = np.mod(samples[:, None] * freqs[None, :], length)
    angle = 2.0 * math.pi / length * phase
    return np.concatenate([np.cos(angle), -np.sin(angle)], axis=1).astype(np.float32).astype(jnp.bfloat16)


def inverse_table(length):
    freqs = F0 + np.arange(F, dtype=np.int64)
    shifts = np.arange(LAGS, dtype=np.int64) - LAGS // 2
    phase = np.mod(freqs[:, None] * shifts[None, :], length)
    angle = 2.0 * math.pi / length * phase
    return np.concatenate([np.cos(angle), -np.sin(angle)], axis=0).astype(np.float32).astype(jnp.bfloat16)


def whiten(records, live_mask):
    count, windows, length = records.shape
    spectrum = jnp.dot(
        records.reshape(count * windows, length),
        jnp.asarray(forward_table(length)),
        preferred_element_type=jnp.float32,
    )
    power = jnp.mean(spectrum * spectrum, axis=1, keepdims=True)
    gain = jnp.repeat(live_mask.astype(jnp.float32), windows)[:, None]
    white = spectrum * (gain * lax.rsqrt(power + 1e-06))
    return white.astype(jnp.bfloat16)


def reach_kernel(shape, offsets_ref, white_ref, cross_ref, held, ext, own, swapped, made, back,
                 z_send, z_recv, c_send, c_recv, y_send, y_recv, d_send, d_recv, e_send, r_send, r_recv):
    layers, columns, depth, pieces, windows, fold = shape
    count, slab = white_ref.shape[0], white_ref.shape[1]
    pairs = offsets_ref.shape[0]
    wide = 2 * columns
    total = layers * wide * count
    me = lax.axis_index("chan")
    z, q = me // wide, me % wide
    y, c = q // 2, q % 2
    sibling = me + 1 - 2 * c
    sib_q = q + 1 - 2 * c
    mate = me + 2 - 4 * y
    mate_q = q + 2 - 4 * y
    far_q = sib_q + 2 - 4 * y
    step = count // pieces
    top, lifted = layers - 1, depth + 1

    barrier = pltpu.get_barrier_semaphore()

    def greet(device):
        pl.semaphore_signal(barrier, inc=1, device_id={"chan": device}, device_id_type=pl.DeviceIdType.MESH)

    greet(sibling)
    if columns == 2:
        greet(mate)

    @pl.when(z >= 1)
    def _():
        greet(me - wide)

    @pl.when(z < layers - 1)
    def _():
        greet(me + wide)

    below, above = jnp.minimum(z, 1), jnp.minimum(top - z, 1)
    peers = columns + below + above
    if fold:
        @pl.when(z == 0)
        def _():
            for i in range(wide):
                greet(top * wide + i)

        @pl.when(z == top)
        def _():
            for i in range(wide):
                greet(jnp.int32(i))

        peers = peers + wide * (2 - below - above)
    pl.semaphore_wait(barrier, peers)

    def rows(p):
        return pl.ds(p * step, step)

    def mine(dz, p):
        return white_ref.at[rows(p)] if dz == 0 else held.at[dz * wide + q, rows(p)]

    def copy(source, slot, p, send, recv, device):
        return pltpu.make_async_remote_copy(
            src_ref=source,
            dst_ref=held.at[slot, rows(p)],
            send_sem=send,
            recv_sem=recv,
            device_id={"chan": device},
            device_id_type=pl.DeviceIdType.MESH,
        )

    def down(dz, p):
        return copy(mine(dz, p), (dz + 1) * wide + q, p, z_send.at[dz, p], z_recv.at[dz + 1, p], me - wide)

    def from_above(dz, p):
        return copy(mine(dz, p), dz * wide + q, p, z_send.at[dz, p], z_recv.at[dz, p], me)

    def across(dz, p, slot):
        return copy(mine(dz, p), slot, p, c_send.at[dz, p], c_recv.at[dz, p], sibling)

    def over(dz, p, slot):
        return copy(mine(dz, p), slot, p, y_send.at[dz, p], y_recv.at[dz, p], mate)

    def onward(dz, p, slot):
        return copy(held.at[dz * wide + mate_q, rows(p)], slot, p, d_send.at[dz, p], d_recv.at[dz, p], sibling)

    def both(*conditions):
        joined = conditions[0]
        for condition in conditions[1:]:
            joined = jnp.logical_and(joined, condition)
        return joined

    def exists(dz):
        return z + dz < layers

    def goes(dz, at_start, at_end):
        if dz == lifted:
            return z == top
        if dz == 0:
            return at_start
        if fold and dz == depth:
            return both(exists(dz), at_end)
        return exists(dz)

    def z_tx(dz):
        if fold and dz + 1 == depth:
            return both(exists(dz), z >= 1, jnp.logical_or(z >= 2, q == 0))
        return both(exists(dz), z >= 1)

    def z_rx(dz):
        return goes(dz, None, q == 0)

    def c_tx(dz):
        return goes(dz, c == 1, q == 0)

    def c_rx(dz):
        return goes(dz, c == 0, q == 1)

    def y_tx(dz):
        return goes(dz, y == 1, q == 0)

    def y_rx(dz):
        return goes(dz, y == 0, q == 2)

    def detoured(dz, p):
        return fold and dz == depth - 1 and p == pieces - 1

    def over_tx(dz, p):
        if detoured(dz, p):
            return both(y_tx(dz), jnp.logical_or(z > 0, y == 0))
        if raised(dz, p):
            return both(y_tx(dz), y == 0)
        return y_tx(dz)

    def raised(dz, p):
        return fold and dz == lifted and p >= pieces // 2

    def lift_mate(p):
        return copy(held.at[mate_q, rows(p)], lifted * wide + mate_q, p,
                    e_send.at[lifted, p], y_recv.at[lifted, p], me + top * wide)

    def extra(dz, p):
        return copy(held.at[dz * wide + mate_q, rows(p)], (dz + 1) * wide + mate_q, p,
                    e_send.at[dz, p], y_recv.at[dz + 1, p], me - wide)

    def extra_tx():
        return both(z == 1, y == 0)

    def d_rx(dz):
        return goes(dz, y == 0, q == 3)

    def lift(p):
        return copy(white_ref.at[rows(p)], lifted * wide + q, p, z_send.at[lifted, p], z_recv.at[lifted, p],
                    me + top * wide)

    def sends(dz):
        for p in range(pieces):
            if dz > 0:
                @pl.when(z_rx(dz))
                def _():
                    from_above(dz, p).wait_recv()
            if dz < depth:
                @pl.when(z_tx(dz))
                def _():
                    down(dz, p).start()
            if columns == 2:
                @pl.when(over_tx(dz, p))
                def _():
                    over(dz, p, dz * wide + q).start()
            @pl.when(c_tx(dz))
            def _():
                across(dz, p, dz * wide + q).start()

    def passes(dz):
        if columns == 2:
            for p in range(pieces):
                @pl.when(y_rx(dz))
                def _():
                    over(dz, p, dz * wide + mate_q).wait_recv()
                    onward(dz, p, dz * wide + mate_q).start()
                if dz == 0 and raised(lifted, p):
                    @pl.when(both(z == 0, y == 0))
                    def _():
                        lift_mate(p).start()
                if detoured(dz + 1, p):
                    @pl.when(extra_tx())
                    def _():
                        extra(dz, p).start()

    def arrives(dz):
        for p in range(pieces):
            @pl.when(c_rx(dz))
            def _():
                across(dz, p, dz * wide + sib_q).wait_recv()
            if columns == 2:
                @pl.when(d_rx(dz))
                def _():
                    onward(dz, p, dz * wide + far_q).wait_recv()

    def finishes(dz):
        for p in range(pieces):
            if dz < depth:
                @pl.when(z_tx(dz))
                def _():
                    down(dz, p).wait_send()
            if columns == 2:
                @pl.when(over_tx(dz, p))
                def _():
                    over(dz, p, dz * wide + q).wait_send()
                if detoured(dz + 1, p):
                    @pl.when(extra_tx())
                    def _():
                        extra(dz, p).wait_send()
                @pl.when(y_rx(dz))
                def _():
                    onward(dz, p, dz * wide + mate_q).wait_send()
            @pl.when(c_tx(dz))
            def _():
                across(dz, p, dz * wide + q).wait_send()

    def answer(i):
        return pltpu.make_async_remote_copy(
            src_ref=made.at[i],
            dst_ref=back.at[q],
            send_sem=r_send.at[i],
            recv_sem=r_recv.at[q],
            device_id={"chan": jnp.int32(i)},
            device_id_type=pl.DeviceIdType.MESH,
        )

    def answered(i):
        return pltpu.make_async_remote_copy(
            src_ref=made.at[i],
            dst_ref=back.at[i],
            send_sem=r_send.at[i],
            recv_sem=r_recv.at[i],
            device_id={"chan": me},
            device_id_type=pl.DeviceIdType.MESH,
        )

    low = lax.broadcasted_iota(jnp.int32, (8, LANES), 0) < 4

    def prepare(i, carry):
        raw = white_ref[i]
        value = raw.astype(jnp.float32)
        own[i] = value
        ext[q * count + i] = raw
        for w in range(windows):
            swapped[i, w * 8 : w * 8 + 8] = pltpu.roll(value[w * 8 : w * 8 + 8], 4, 0)
        return carry

    def settle(dz):
        def one(l):
            def fill(i, carry):
                ext[(dz * wide + l) * count + i] = held[dz * wide + l, i]
                return carry
            lax.fori_loop(0, count, fill, 0, unroll=4)

        if dz == 0:
            for l in range(1, wide):
                @pl.when(q < l)
                def _():
                    one(l)
        else:
            @pl.when(exists(dz))
            def _():
                for l in range(1 if fold and dz == depth else wide):
                    one(l)

    live = jnp.minimum(layers * wide - me, pairs)

    def outside():
        def nothing(k, carry):
            for r in range(count):
                cross_ref[r, k] = jnp.zeros((8, LANES), jnp.float32)
            return carry

        lax.fori_loop(live, pairs, nothing, 0)

        @pl.when(layers - z <= depth)
        def _():
            def blank(i, carry):
                ext[(layers - z) * wide * count + i] = jnp.zeros((slab, LANES), jnp.bfloat16)
                return carry

            lax.fori_loop(0, 2 * count, blank, 0, unroll=4)

    def reached(dz):
        if dz < 0:
            return 0
        if dz == depth:
            return live
        return jnp.minimum((dz + 1) * wide - q - 1, live)

    def multiply(dz):
        def pair(k, carry):
            shift = offsets_ref[k]

            def channel(i, inner):
                place = me * count + i + shift
                keep = jnp.where(place < total, 1.0 / windows, 0.0)
                near = jnp.minimum(q * count + i + shift, ext.shape[0] - 1)
                partner = ext[near].astype(jnp.float32)
                straight = own[i, :8] * partner[:8]
                twisted = swapped[i, :8] * partner[:8]
                for w in range(1, windows):
                    part = slice(w * 8, w * 8 + 8)
                    straight += own[i, part] * partner[part]
                    twisted += swapped[i, part] * partner[part]
                joined = jnp.where(
                    low,
                    straight + pltpu.roll(straight, 4, 0),
                    pltpu.roll(twisted, 4, 0) - twisted,
                )
                cross_ref[i, k] = joined * keep
                return inner

            return lax.fori_loop(0, count, channel, carry, unroll=4)

        begin, end = reached(dz - 1), reached(dz)
        if fold and dz == depth:
            @pl.when(z == 0)
            def _():
                lax.fori_loop(begin, begin + 1, pair, 0)

            @pl.when(z > 0)
            def _():
                lax.fori_loop(begin, end, pair, 0)
        else:
            lax.fori_loop(begin, end, pair, 0)

    def reply():
        for i in range(wide):
            shift = offsets_ref[top * wide + q - i]

            def channel(r, carry):
                place = i * count + r + shift
                keep = jnp.where(place < total, 1.0 / windows, 0.0)
                near = jnp.clip(place - top * wide * count, 0, ext.shape[0] - 1)
                partner = ext[near].astype(jnp.float32)
                value = held[lifted * wide + i, r].astype(jnp.float32)
                straight = value[:8] * partner[:8]
                twisted = pltpu.roll(value[:8], 4, 0) * partner[:8]
                for w in range(1, windows):
                    part = slice(w * 8, w * 8 + 8)
                    straight += value[part] * partner[part]
                    twisted += pltpu.roll(value[part], 4, 0) * partner[part]
                joined = jnp.where(
                    low,
                    straight + pltpu.roll(straight, 4, 0),
                    pltpu.roll(twisted, 4, 0) - twisted,
                )
                made[i, r] = (joined * keep).astype(jnp.bfloat16)
                return carry

            lax.fori_loop(0, count, channel, 0, unroll=4)
        for i in range(wide):
            answer(i).start()

    sends(0)
    if fold:
        @pl.when(z == 0)
        def _():
            for p in range(pieces):
                lift(p).start()

    lax.fori_loop(0, count, prepare, 0)
    outside()
    for dz in range(depth + 1):
        if dz < depth:
            sends(dz + 1)
        if fold and dz == 0:
            sends(lifted)
        passes(dz)
        if fold and dz == 0:
            passes(lifted)
        arrives(dz)
        settle(dz)
        if fold and dz == 0:
            arrives(lifted)

            @pl.when(z == top)
            def _():
                reply()

        multiply(dz)

    if fold:
        @pl.when(z == 0)
        def _():
            for i in range(wide):
                answered(i).wait_recv()

                def take(r, carry):
                    cross_ref[r, top * wide - q + i] = back[i, r].astype(jnp.float32)
                    return carry

                lax.fori_loop(0, count, take, 0, unroll=4)
            for p in range(pieces):
                lift(p).wait_send()
                if raised(lifted, p):
                    @pl.when(y == 0)
                    def _():
                        lift_mate(p).wait_send()

        @pl.when(z == top)
        def _():
            for i in range(wide):
                answer(i).wait_send()

        finishes(lifted)
    for dz in range(depth + 1):
        finishes(dz)


def middle_kernel(shape, offsets_hbm, mask_hbm, records_hbm, table_hbm, inverse_hbm, half_ref, cross_ref, inverse,
                  offsets_ref, mask_ref, records, table, crossed, spectrum, square, white, gains, column, scales, held, spec, made, back, joined,
                  l_sem, x_send, f_send, g_send, n_send, n_recv, s_recv, r_send, r_recv):
    layers, wide, windows = shape
    pairs = offsets_ref.shape[0]
    count = records.shape[0] // windows
    chunks, width = table.shape[0], table.shape[2]
    rows = count * windows
    parts = layers * wide
    pitch = spec.shape[0] // (2 * windows)
    half, top, last = layers // 2, layers - 1, parts - 1
    me = lax.axis_index("chan")
    z, q = me // wide, me % wide
    c = q % 2
    first = z * wide
    base = half * wide
    sib_q = q + 1 - 2 * c
    mate_q = (q + 2) % wide
    far_q = (sib_q + 2) % wide
    near = c == 0

    def nearest(j):
        return jnp.where(j == 0, q, jnp.where(j == 1, sib_q, jnp.where(j == 2, mate_q, far_q)))

    def slowest(j):
        return jnp.where(j == 0, q, jnp.where(j == 1, mate_q, jnp.where(j == 2, sib_q, far_q)))

    def chunk(j):
        return pltpu.make_async_copy(table_hbm.at[slowest(j)], table.at[j], l_sem.at[j])

    load = [
        pltpu.make_async_copy(records_hbm, records, l_sem.at[chunks]),
        pltpu.make_async_copy(offsets_hbm, offsets_ref, l_sem.at[chunks + 1]),
        pltpu.make_async_copy(mask_hbm, mask_ref, l_sem.at[chunks + 2]),
    ]
    load[0].start()
    for n in range(chunks):
        chunk(n).start()
    for one in load[1:]:
        one.start()
    inner_low, inner_high = z == half - 1, z == half
    neighbour = jnp.where(
        jnp.logical_or(z == 0, jnp.logical_and(inner_low, c == 1)), me + wide, me - wide)
    own_end = jnp.where(
        z == 0, jnp.where(near, base, jnp.where(q < 2, wide + 2, wide)),
        jnp.where(jnp.logical_and(inner_low, c == 1), base + wide, parts + 1))
    barrier = pltpu.get_barrier_semaphore()

    def greet(device, condition):
        @pl.when(condition)
        def _():
            pl.semaphore_signal(barrier, inc=1, device_id={"chan": jnp.int32(device)},
                                device_id_type=pl.DeviceIdType.MESH)

    for col in (sib_q, mate_q, far_q):
        greet(first + col, z >= 0)
    for i in range(wide):
        odd = i % 2 == 1
        greet(wide + i, z == 0)
        if odd:
            greet(base + i, z < half)
        else:
            greet(base + i, jnp.logical_and(inner_low, q == i))
    greet(me - wide, jnp.logical_or(inner_low, jnp.logical_and(inner_high, c == 1)))
    greet(me + wide, inner_high)
    replies_far = jnp.where(inner_low, wide, jnp.where(jnp.logical_and(inner_high, c == 1), 2 * wide - 1, 0))
    ships_there = jnp.where(jnp.logical_and(inner_low, near), 0, 1)

    def remote(source, target, send, recv, device):
        return pltpu.make_async_remote_copy(
            src_ref=source, dst_ref=target, send_sem=send, recv_sem=recv,
            device_id={"chan": device}, device_id_type=pl.DeviceIdType.MESH,
        )

    def piece(ri, col):
        return white.at[ri * wide + col]

    def swap(ri, col):
        return remote(piece(ri, col), held.at[me, pl.ds(ri * rows, rows)], x_send, s_recv.at[me], first + col)

    def ship_own(ri):
        return remote(piece(ri, q), held.at[me, pl.ds(ri * rows, rows)], f_send, s_recv.at[me], neighbour)

    def ship(s):
        return remote(held.at[s], held.at[s], f_send, s_recv.at[s], neighbour)

    both_ways = jnp.logical_and(inner_low, c == 1)

    def drop_own(ri):
        return remote(piece(ri, q), held.at[me, pl.ds(ri * rows, rows)], g_send, s_recv.at[me], me - wide)

    def drop(s):
        return remote(held.at[s], held.at[s], g_send, s_recv.at[s], me - wide)

    def made_at(d, k):
        return made.at[d * pairs + k]

    def reply(d, k):
        return remote(made_at(d, k), back.at[k, q], r_send, r_recv.at[k], d)

    def shipped(slots, send):
        remote(held.at[0:slots], held.at[0:slots], send, s_recv.at[0], neighbour).wait_send()

    def gain_to(device):
        return remote(gains, scales.at[me], n_send, n_recv.at[me], device)

    def gain_on(s, device):
        return remote(scales.at[s], scales.at[s], n_send, n_recv.at[s], device)

    def clear(i, carry):
        joined[pl.ds(pl.multiple_of(i * 64, 64), 64), :] = jnp.zeros((64, LANES), jnp.float32)
        return carry

    lax.fori_loop(0, joined.shape[0] // 64, clear, 0)

    def blank(x, carry):
        spec[pl.ds(pl.multiple_of(x * pitch + parts * count, 8), count), :] = jnp.zeros((count, LANES), jnp.float32)
        return carry

    lax.fori_loop(0, 2 * windows, blank, 0)
    square[...] = jnp.zeros(square.shape, jnp.float32)
    load[0].wait()

    def transform(j, carry):
        col = slowest(j)
        chunk(j).wait()
        spectrum[...] = jnp.dot(records[...], table[j], preferred_element_type=jnp.float32)

        def narrow(i, inner):
            some = pl.ds(pl.multiple_of(i * 16, 16), 16)
            real, imag = spectrum[some, :LANES], spectrum[some, LANES:]
            white[col, some] = real.astype(jnp.bfloat16)
            white[wide + col, some] = imag.astype(jnp.bfloat16)
            square[some, :] += real * real + imag * imag
            return inner

        lax.fori_loop(0, rows // 16, narrow, 0, unroll=4)

        @pl.when(j == 0)
        def _():
            pl.semaphore_wait(barrier, wide - 1 + replies_far + ships_there)
            for ri in range(2):
                ship_own(ri).start()

            @pl.when(both_ways)
            def _():
                for ri in range(2):
                    drop_own(ri).start()

        @pl.when(j > 0)
        def _():
            for ri in range(2):
                swap(ri, col).start()
        return carry

    lax.fori_loop(0, chunks, transform, 0)
    for one in load[1:]:
        one.wait()
    place = lax.broadcasted_iota(jnp.int32, (16, LANES), 0)
    channel = lax.broadcasted_iota(jnp.int32, (8, LANES), 1) // windows
    terms = jnp.zeros((16, LANES), jnp.float32)
    for part in range(rows // LANES):
        total = jnp.sum(square[part * LANES:(part + 1) * LANES, :], axis=1, keepdims=True)
        scale = jnp.broadcast_to(lax.rsqrt(total * (1.0 / (2 * F)) + 1e-06), (LANES, LANES)).T[:8]
        alive = jnp.zeros((8, LANES), jnp.float32)
        for n in range(LANES // windows):
            alive = jnp.where(channel == n, mask_ref[part * (LANES // windows) + n].astype(jnp.float32), alive)
        rest = (scale * alive)[:1]
        for term in range(3):
            kept = rest.astype(jnp.bfloat16).astype(jnp.float32)
            terms = jnp.where(place == part * 3 + term, kept, terms)
            rest = rest - kept
    gains[...] = terms.astype(jnp.bfloat16)
    fetch = pltpu.make_async_copy(inverse_hbm, inverse, l_sem.at[0])
    fetch.start()

    def settle(s, gain, piece_of):
        for part in range(rows // LANES):
            scale = sum(gain[part * 3 + term:part * 3 + term + 1].astype(jnp.float32) for term in range(3))
            column[part * LANES:(part + 1) * LANES, :] = jnp.broadcast_to(scale, (LANES, LANES)).T

        def one(i, carry):
            some = pl.ds(pl.multiple_of(i * 2 * windows, 2 * windows), 2 * windows)
            factor = column[some, :]
            for ri in range(2):
                value = piece_of(ri, i).astype(jnp.float32) * factor
                for part in range(2):
                    row = ri * windows * pitch + s * count + 2 * i + part
                    spec[pl.ds(row, windows, stride=pitch), :] = value[part * windows:(part + 1) * windows]
            return carry

        lax.fori_loop(0, count // 2, one, 0, unroll=4)

    def own_rows(ri, i):
        return white[ri * wide + q, pl.ds(pl.multiple_of(i * 2 * windows, 2 * windows), 2 * windows)]

    def arrive(s, onward):
        ship(s).wait_recv()
        if onward is not None:
            @pl.when(onward)
            def _():
                ship(s).start()

    def unfold(s, onward):
        gain_on(s, me).wait_recv()
        if onward is not None:
            @pl.when(onward)
            def _():
                gain_on(s, neighbour).start()
        settle(
            s, scales[s],
            lambda ri, i: held[s, pl.ds(pl.multiple_of(ri * rows + i * 2 * windows, 2 * windows), 2 * windows)])

    def takes(start, begin, end, onward=None):
        def one(j, carry):
            arrive(start + nearest(j), onward)
            return carry

        def two(j, carry):
            unfold(start + nearest(j), onward)
            return carry

        lax.fori_loop(begin, end, one, 0)
        lax.fori_loop(begin, end, two, 0)

    def block(d, k):
        shift = offsets_ref[k]
        for g in range(count // 16):
            mine = d * count + g * 16
            real = imag = None
            for w in range(windows):
                cr = spec[pl.ds(pl.multiple_of(w * pitch + mine, 8), 16), :]
                ci = spec[pl.ds(pl.multiple_of((windows + w) * pitch + mine, 8), 16), :]
                pr = spec[pl.ds(w * pitch + mine + shift, 16), :]
                pi = spec[pl.ds((windows + w) * pitch + mine + shift, 16), :]
                re, im = cr * pr + ci * pi, ci * pr - cr * pi
                real, imag = (re, im) if w == 0 else (real + re, imag + im)
            rows = slice(g * 16, g * 16 + 16)
            made[d * pairs + k, 0, rows] = (real * (1.0 / windows)).astype(jnp.bfloat16)
            made[d * pairs + k, 1, rows] = (imag * (1.0 / windows)).astype(jnp.bfloat16)

    def spans(d_begin, d_end, u_begin, u_end, visit):
        def reach(u, carry):
            def one(d, inner):
                visit(d, u - 1 - d)
                return inner

            return lax.fori_loop(jnp.maximum(d_begin, u - pairs), jnp.minimum(d_end, u), one, carry)

        lax.fori_loop(u_begin, u_end, reach, 0)

    def give(d, k):
        @pl.when(d != me)
        def _():
            reply(d, k).start()

    def blocks(d_begin, d_end, u_begin, u_end):
        def reach(u, carry):
            spans(d_begin, d_end, u, u + 1, block)
            spans(d_begin, d_end, u, u + 1, give)
            return carry

        lax.fori_loop(u_begin, u_end, reach, 0)

    y = q // 2
    def reached_1(start, more=0):
        return jnp.where(y == 0, start, start + 3), jnp.where(y == 0, start + 2, start + wide + more)

    def reached_2(start, more=0):
        return jnp.where(y == 0, start + 2, start), jnp.where(y == 0, start + wide + more, start + 3)

    settle(me, gains[...], own_rows)
    gain_to(neighbour).start()
    for col in (sib_q, mate_q, far_q):
        gain_to(first + col).start()
    arrive(first + sib_q, z >= 0)

    @pl.when(both_ways)
    def _():
        drop(first + sib_q).start()
        gain_to(me - wide).start()
    unfold(first + sib_q, z >= 0)

    @pl.when(both_ways)
    def _():
        gain_on(first + sib_q, me - wide).start()
    takes(first, 2, wide, z >= 0)
    blocks(first, first + wide, first + 1, first + wide + jnp.where(z == top, 1, 0))

    @pl.when(z == 0)
    def _():
        takes(wide, 0, 2)
        blocks(0, wide, *reached_1(wide))

        @pl.when(near)
        def _():
            takes(wide, 2, wide)
            blocks(0, wide, *reached_2(wide))

    @pl.when(inner_low)
    def _():
        takes(0, 0, 2, jnp.logical_not(near))

        @pl.when(jnp.logical_not(near))
        def _():
            blocks(2 * y, 2 * y + 2, jnp.where(y == 0, wide + 2, wide + 1), jnp.where(y == 0, base, base - 1))
        takes(base, 0, 2)
        blocks(2 * y, 2 * y + 2, *reached_1(base))
        takes(0, 2, wide, jnp.logical_not(near))

        @pl.when(jnp.logical_not(near))
        def _():
            blocks(0, wide, wide, jnp.where(y == 0, wide, wide + 1))
            blocks(2 - 2 * y, wide - 2 * y, jnp.where(y == 0, wide + 2, wide + 1), jnp.where(y == 0, base, base - 1))
        blocks(2 - 2 * y, wide - 2 * y, *reached_1(base))
        blocks(wide, base, *reached_1(base))
        takes(base, 2, wide)
        blocks(0, wide, *reached_2(base))
        blocks(wide, base, *reached_2(base))

        @pl.when(near)
        def _():
            for begin, reached in ((0, reached_1), (2, reached_2)):
                takes(top * wide, begin, begin + 2)
                blocks(0, wide, *reached(top * wide, 1))
                blocks(wide, base, *reached(top * wide, 1))

    @pl.when(inner_high)
    def _():
        for begin, reached in ((0, reached_1), (2, reached_2)):
            takes(top * wide, begin, begin + 2, near)
            blocks(base, base + wide, *reached(top * wide, 1))

        @pl.when(jnp.logical_not(near))
        def _():
            takes(wide, 0, wide)
            blocks(wide, base, *reached_1(top * wide, 1))
            spans(wide, base, *reached_2(top * wide, 1), block)
            takes(0, 0, 2)
            blocks(2 * y, 2 * y + 2, top * wide, parts + 1)
            takes(0, 2, wide)
            blocks(2 - 2 * y, wide - 2 * y, top * wide, parts + 1)
            spans(wide, base, *reached_2(top * wide, 1), give)

    group = pairs // 2

    def unpack(source, k, col):
        for ri in range(2):
            for g in range(count // 16):
                value = source[ri, g * 16:g * 16 + 16].astype(jnp.float32)
                for part in range(2):
                    seg = (k // group) * 2 * wide + ri * wide + col
                    row = (seg * count + g * 16 + part * 8) * group + k % group
                    joined[pl.ds(row, 8, stride=group), :] = value[part * 8:part * 8 + 8]

    def collect(k, carry):
        u = me + k + 1
        kept = jnp.logical_and(jnp.logical_and(z == 0, q == wide - 1), u == base - 1)
        away = jnp.logical_and(u >= own_end, jnp.logical_not(kept))
        def received(cols):
            remote(back.at[k, 0:cols], back.at[k, 0:cols], r_send, r_recv.at[k], me).wait_recv()

        @pl.when(away)
        def _():
            received(wide)

        @pl.when(jnp.logical_not(away))
        def _():
            received(wide - 1)

        for col in range(wide):
            here = jnp.logical_and(q == col, jnp.logical_not(away))

            @pl.when(here)
            def _():
                unpack(made_at(me, k), k, col)

            @pl.when(jnp.logical_not(here))
            def _():
                unpack(back.at[k, col], k, col)
        return carry

    def pack(which, target):
        def one(i, carry):
            rows = pl.ds(pl.multiple_of(i * 16, 16), 16)
            for x in range(2 * wide):
                start = pl.multiple_of((which * 2 * wide + x) * count * group + i * 16, 16)
                target[rows, x * LANES:(x + 1) * LANES] = joined[pl.ds(start, 16), :].astype(jnp.bfloat16)
            return carry

        lax.fori_loop(0, count * group // 16, one, 0, unroll=2)

    lax.fori_loop(0, jnp.minimum(group, parts - me), collect, 0)
    pack(0, crossed)
    fetch.wait()
    for n in range(0, LAGS, SPAN):
        lagged = jnp.dot(crossed[...], inverse[:, n:n + SPAN], preferred_element_type=jnp.float32)
        half_ref[:, n:n + SPAN] = (lagged * (1.0 / math.sqrt(F))).astype(jnp.bfloat16)
    lax.fori_loop(group, parts - me, collect, 0)
    pack(1, cross_ref)

    shipped(wide - 1, x_send)
    forwards = jnp.logical_or(jnp.logical_and(inner_low, c == 1), jnp.logical_and(inner_high, near))

    def told(slots):
        remote(scales.at[0:slots], scales.at[0:slots], n_send, n_recv.at[0], me).wait_send()

    @pl.when(forwards)
    def _():
        shipped(2 * wide, f_send)

    @pl.when(both_ways)
    def _():
        shipped(2, g_send)
        told(3 * wide + 1)

    @pl.when(jnp.logical_and(inner_high, near))
    def _():
        told(3 * wide - 1)

    @pl.when(jnp.logical_not(forwards))
    def _():
        shipped(wide, f_send)
        told(2 * wide - 1)

    def owners(z, q, u):
        c, early = q % 2, u in ((wide, wide + 1) if q < 2 else (base - 1,))
        layer = min(u, last) // wide
        if z == 0:
            return (0,) if layer == 0 or (layer == 1 and (c == 0 or early)) else ()
        if z == half - 1:
            if layer == 1:
                return (1,) if c == 0 or early else (0, 1)
            return (0, 1) if layer == half or (layer == top and c == 0) else ()
        if z == half:
            return (0, 1, half) if layer == top and c == 1 else (half,) if layer >= half else ()
        return (top,) if layer == top else ()

    for i in range(parts):
        replies = sum(
            d // wide in owners(i // wide, i % wide, u) and d != i and 0 <= u - 1 - d < pairs
            for u in range(1, parts + 1) for d in range(parts))

        @pl.when(me == i)
        def _():
            done = made.at[0:replies]
            remote(done, done, r_send, r_recv.at[0], me).wait_send()


def meet(layers, wide, records, live_mask, offsets):
    pairs = offsets.shape[0]
    count, windows, length = records.shape
    parts = layers * wide
    pitch = (parts + 1) * count
    rows = count * windows
    width = 2 * LANES
    chunks = 2 * F // width
    table = np.ascontiguousarray(
        forward_table(length).reshape(length, 2, chunks, LANES).transpose(2, 0, 1, 3).reshape(chunks, length, width))
    return pl.pallas_call(
        functools.partial(middle_kernel, (layers, wide, windows)),
        out_shape=[
            jax.ShapeDtypeStruct((count * pairs // 2, LAGS), jnp.bfloat16),
            jax.ShapeDtypeStruct((count * pairs // 2, 2 * F), jnp.bfloat16),
            jax.ShapeDtypeStruct((2 * F, LAGS), jnp.bfloat16),
        ],
        in_specs=[
            pl.BlockSpec(memory_space=pltpu.HBM),
            pl.BlockSpec(memory_space=pltpu.HBM),
            pl.BlockSpec(memory_space=pltpu.HBM),
            pl.BlockSpec(memory_space=pltpu.HBM),
            pl.BlockSpec(memory_space=pltpu.HBM),
        ],
        out_specs=[pl.BlockSpec(memory_space=pltpu.VMEM)] * 3,
        scratch_shapes=[
            pltpu.SMEM((pairs,), jnp.int32),
            pltpu.SMEM((count,), jnp.int32),
            pltpu.VMEM((rows, length), jnp.bfloat16),
            pltpu.VMEM((chunks, length, width), jnp.bfloat16),
            pltpu.VMEM((count * pairs // 2, 2 * F), jnp.bfloat16),
            pltpu.VMEM((rows, width), jnp.float32),
            pltpu.VMEM((rows, LANES), jnp.float32),
            pltpu.VMEM((2 * wide, rows, LANES), jnp.bfloat16),
            pltpu.VMEM((16, LANES), jnp.bfloat16),
            pltpu.VMEM((rows, LANES), jnp.float32),
            pltpu.VMEM((parts, 16, LANES), jnp.bfloat16),
            pltpu.VMEM((parts, 2 * rows, LANES), jnp.bfloat16),
            pltpu.VMEM((2 * windows * pitch, LANES), jnp.float32),
            pltpu.VMEM((parts * pairs, 2, count, LANES), jnp.bfloat16),
            pltpu.VMEM((pairs, wide, 2, count, LANES), jnp.bfloat16),
            pltpu.VMEM((2 * wide * count * pairs, LANES), jnp.float32),
            pltpu.SemaphoreType.DMA((chunks + 3,)),
            pltpu.SemaphoreType.DMA,
            pltpu.SemaphoreType.DMA,
            pltpu.SemaphoreType.DMA,
            pltpu.SemaphoreType.DMA,
            pltpu.SemaphoreType.DMA((parts,)),
            pltpu.SemaphoreType.DMA((parts,)),
            pltpu.SemaphoreType.DMA,
            pltpu.SemaphoreType.DMA((pairs,)),
        ],
        compiler_params=pltpu.CompilerParams(
            vmem_limit_bytes=36 * 1024 * 1024, collective_id=1, has_side_effects=True
        ),
    )(*[
        pltpu.with_memory_space_constraint(x, pltpu.HBM)
        for x in (offsets, live_mask, records.reshape(rows, length), jnp.asarray(table),
                  jnp.asarray(inverse_table(length)))
    ])


def finish_kernel(half_ref, cross_ref, table_ref, out_hbm, stage, sem):
    group = out_hbm.shape[1] // 2
    copies = [pltpu.make_async_copy(half_ref, out_hbm.at[:, 0:group], sem.at[0])]
    copies[0].start()
    for i, n in enumerate(range(0, LAGS, SPAN)):
        lagged = jnp.dot(cross_ref[...], table_ref[:, n:n + SPAN], preferred_element_type=jnp.float32)
        lagged = (lagged * (1.0 / math.sqrt(F))).astype(jnp.bfloat16)
        stage[:, :, n:n + SPAN] = lagged.reshape(stage.shape[0], group, SPAN)
        copies.append(pltpu.make_async_copy(
            stage.at[:, :, n:n + SPAN], out_hbm.at[:, group:2 * group, n:n + SPAN], sem.at[i + 1]))
        copies[-1].start()
    for one in copies:
        one.wait()


def finish(half, cross, table, count, pairs):
    return pl.pallas_call(
        finish_kernel,
        out_shape=jax.ShapeDtypeStruct((count, pairs, LAGS), jnp.bfloat16),
        in_specs=[pl.BlockSpec(memory_space=pltpu.VMEM)] * 3,
        out_specs=pl.BlockSpec(memory_space=pltpu.HBM),
        scratch_shapes=[
            pltpu.VMEM((count, pairs // 2, LAGS), jnp.bfloat16),
            pltpu.SemaphoreType.DMA((LAGS // SPAN + 1,)),
        ],
        compiler_params=pltpu.CompilerParams(vmem_limit_bytes=16 * 1024 * 1024),
    )(half.reshape(count, pairs // 2, LAGS), cross, table)


def shards(columns, records, live_mask, offsets):
    count, windows, length = records.shape
    pairs = offsets.shape[0]
    wide = 2 * columns
    layers = lax.axis_size("chan") // wide
    reach = (BAND + count - 2) // count
    depth = min(layers - 1, (wide - 1 + reach) // wide)
    pieces = PIECES
    fold = columns == 2 and depth == layers - 1 and depth >= 2 and layers * wide == pairs and pairs * count == BAND
    if (
        columns == 2 and layers == 4 and layers * wide == pairs and pairs * count == BAND
        and F == wide * LANES and windows == 8 and count % 16 == 0
    ):
        half, cross, inverse = meet(layers, wide, records, live_mask, offsets)
        return finish(half, cross, inverse, count, pairs)
    spectra = whiten(records, live_mask).reshape(count, windows * 8, LANES)
    slots = (depth + 1) * wide
    cross = pl.pallas_call(
        functools.partial(reach_kernel, (layers, columns, depth, pieces, windows, fold)),
        out_shape=jax.ShapeDtypeStruct((count, pairs, 8, LANES), jnp.float32),
        in_specs=[
            pl.BlockSpec(memory_space=pltpu.SMEM),
            pl.BlockSpec(memory_space=pltpu.VMEM),
        ],
        out_specs=pl.BlockSpec(memory_space=pltpu.VMEM),
        scratch_shapes=[
            pltpu.VMEM((slots + wide, count, windows * 8, LANES), jnp.bfloat16),
            pltpu.VMEM((slots * count, windows * 8, LANES), jnp.bfloat16),
            pltpu.VMEM((count, windows * 8, LANES), jnp.float32),
            pltpu.VMEM((count, windows * 8, LANES), jnp.float32),
            pltpu.VMEM((wide, count, 8, LANES), jnp.bfloat16),
            pltpu.VMEM((wide, count, 8, LANES), jnp.bfloat16),
        ]
        + [pltpu.SemaphoreType.DMA((depth + 2, pieces))] * 9
        + [pltpu.SemaphoreType.DMA((wide,))] * 2,
        compiler_params=pltpu.CompilerParams(
            vmem_limit_bytes=40 * 1024 * 1024, collective_id=0, has_side_effects=True
        ),
    )(offsets, spectra)
    return lags(cross.astype(jnp.bfloat16).reshape(count * pairs, 8 * LANES), count, pairs, length)


def lags(cross, count, pairs, length):
    result = jnp.dot(cross, jnp.asarray(inverse_table(length)), preferred_element_type=jnp.float32)
    result = result * (1.0 / math.sqrt(F))
    return result.reshape(count, pairs, LAGS).astype(jnp.bfloat16)


def solution(mesh):
    in_specs = (P(("day", "chan"), None, None), P(("day", "chan")), P())
    out_specs = P(("day", "chan"), None, None)
    columns = max(1, LAYER_CHIPS // mesh.shape["day"])
    body = functools.partial(shards, columns)
    return jax.shard_map(body, mesh=mesh, in_specs=in_specs, out_specs=out_specs, check_vma=False)
```
